32 devices in a mesh: dp: 8 (over z, x), seq: 4 (over y, core).
Axes of the slice: x: 2, y: 2, z: 4, core: 2. Of those that a mesh axis runs over, the one named last changes fastest.
Arguments:
- inputs: bfloat16 [32, 1024, 1024], P('dp', 'seq'), may hold values from -6 to 6
- norm_gain: float32 [1024], replicated, may hold values from 0.1 to 1.9
- norm_shift: float32 [1024], replicated, may hold values from -3 to 3
- qkv_weight: bfloat16 [1024, 3072], replicated, may hold values from -0.1875 to 0.1875
- out_weight: bfloat16 [1024, 1024], replicated, may hold values from -0.75 to 0.75
- up_weight: bfloat16 [1024, 4096], replicated, may hold values from -0.1875 to 0.1875
- up_bias: float32 [4096], replicated, may hold values from -3 to 3
- down_weight: bfloat16 [4096, 1024], replicated, may hold values from -0.09375 to 0.09375
- down_bias: float32 [1024], replicated, may hold values from -3 to 3
- partners: int32 [32], P('dp'), may hold values from 0 to 31, as said below
- families: int32 [32, 1024], P('dp'), may hold values from 0 to 1023, as said below
- cotangent: bfloat16 [32, 1024, 1024], P('dp', 'seq'), may hold values from -6 to 6
Outputs:
- layer_out: bfloat16 [32, 1024, 1024], P('dp', 'seq')
- input_grad: float32 [32, 1024, 1024], P('dp', 'seq')
- gain_grad: float32 [1024], replicated
- shift_grad: float32 [1024], replicated
- qkv_grad: float32 [1024, 3072], P('dp', 'seq')
- out_grad: float32 [1024, 1024], P('dp', 'seq')
- up_grad: float32 [1024, 4096], P('dp', 'seq')
- up_bias_grad: float32 [4096], replicated
- down_grad: float32 [4096, 1024], P('dp', 'seq')
- down_bias_grad: float32 [1024], replicated
The draws below stay inside these ranges and needn't reach their ends.
Inputs may be any that keep to these rules, and one draw needn't show every extreme that they name: partners pairs the rows of each aligned block of 4 rows two by two: partners[partners[r]] = r, partners[r] != r, and partners[r] lies in the block of r. `families`: family ids never fall along a row and the last position of every row has id 1024 - 1; in each aligned block of 4 rows at least one row is a single group over all 1024 positions.
All inputs are finite; a program needn't handle non-finite values.
Results may differ from the reference program's by a relative error of at most 0.0099.
Values may be sent and summed in bfloat16 or wider, within the bound.
A program may use at most 256 MiB of HBM per device.

```python
import jax
import jax.numpy as jnp
from jax import lax

D = 1024
HEADS = 16
HEAD_DIM = 64
ROT = 32
FF = 4096
SEQ_LEN = 1024
ROWS_DEV = 4
ROWS = 32


def draw_partners(key, part):
    block_total = ROWS // ROWS_DEV
    base_key = jax.random.fold_in(key, 4711)

    def one_block(block_index):
        shuffled = jax.random.permutation(jax.random.fold_in(base_key, block_index), ROWS_DEV).astype(jnp.int32)
        partner_of_slot = shuffled.reshape(-1, 2)[:, ::-1].reshape(-1)
        result = jnp.zeros((ROWS_DEV,), jnp.int32).at[shuffled].set(partner_of_slot)
        return result + block_index * ROWS_DEV
    return jax.vmap(one_block)(jnp.arange(block_total).astype(jnp.int32)).reshape(-1).astype(jnp.int32)


def draw_families(key, part):
    block_total = ROWS // ROWS_DEV
    base_key = jax.random.fold_in(key, 9157)
    cut_key, whole_key = jax.random.split(base_key)
    cut_draw = jax.random.randint(cut_key, (ROWS, SEQ_LEN), 0, max(SEQ_LEN // 8, 2))
    cuts = (cut_draw == 0).astype(jnp.int32)
    cuts = cuts.at[:, 0].set(0)
    whole_slot = jax.random.randint(whole_key, (block_total,), 0, ROWS_DEV)
    whole_rows = (whole_slot + jnp.arange(block_total) * ROWS_DEV).astype(jnp.int32)
    row_ids = jnp.arange(ROWS).astype(jnp.int32)
    is_whole = jnp.any(row_ids[:, None] == whole_rows[None, :], 1)
    cuts = jnp.where(is_whole[:, None], 0, cuts)
    counted = jnp.cumsum(cuts, 1).astype(jnp.int32)
    lifted = counted + (SEQ_LEN - 1 - counted[:, -1:])
    return lifted.astype(jnp.int32)


def steps_of(key, dims, cuts, smallest, top_value):
    loudness, own = 1.0, jax.random.fold_in(key, 6)
    for position, blocks in cuts:
        heights = jnp.exp(jax.random.uniform(jax.random.fold_in(own, position), (blocks,), jnp.float32, smallest / len(cuts), top_value / len(cuts)))
        loudness = loudness * jnp.repeat(heights, dims[position] // blocks).reshape([-1 if axis == position else 1 for axis in range(len(dims))])
    return loudness


def centred(rng, extent, scale, reach, cuts=(), held_as=jnp.bfloat16):
    level = steps_of(rng, extent, cuts, -0.22, 0.18) if cuts else 1.0
    drawn = jax.random.normal(rng, extent, jnp.float32) * scale * level
    return jnp.minimum(jnp.maximum(drawn, -reach), reach).astype(held_as)


def setup_inputs(seed: int = 0) -> dict:
    key_of = jax.random.split(jax.random.key(seed), 13)
    return {
        "inputs": centred(key_of[0], (ROWS, SEQ_LEN, D), 1.0, 6.0, ((0, 8), (1, 4))),
        "norm_gain": jnp.clip(1.0 + 0.18 * jax.random.normal(key_of[1], (D,), jnp.float32), 0.1, 1.9),
        "norm_shift": centred(key_of[2], (D,), 0.5, 3.0, (), jnp.float32),
        "qkv_weight": centred(key_of[3], (D, 3 * D), D ** -0.5, 0.1875),
        "out_weight": centred(key_of[4], (D, D), (D // 16) ** -0.5, 0.75),
        "up_weight": centred(key_of[5], (D, FF), D ** -0.5, 0.1875),
        "up_bias": centred(key_of[6], (FF,), 0.5, 3.0, (), jnp.float32),
        "down_weight": centred(key_of[7], (FF, D), FF ** -0.5, 0.09375),
        "down_bias": centred(key_of[8], (D,), 0.5, 3.0, (), jnp.float32),
        "partners": draw_partners(jax.random.fold_in(key_of[12], 71), 0),
        "families": draw_families(jax.random.fold_in(key_of[12], 71), 0),
        "cotangent": centred(key_of[11], (ROWS, SEQ_LEN, D), 1.0, 6.0, ((0, 8), (1, 4))),
    }


EPS = 1e-05

@jax.custom_vjp
def low(v):
    return lax.optimization_barrier(v.astype(jnp.bfloat16)).astype(jnp.float32)

@jax.custom_vjp
def low_back(v):
    return v

def low_keep(v):
    return (low(v), None)

def low_pass(kept, grad):
    return (grad,)

def back_keep(v):
    return (v, None)

def back_low(kept, grad):
    return (low(grad),)
low.defvjp(low_keep, low_pass)
low_back.defvjp(back_keep, back_low)

def rotate(values, places):
    half_rot = ROT // 2
    inverse_freq = 10000.0 ** (-2.0 * jnp.arange(half_rot).astype(jnp.float32) / ROT)
    angles = places.astype(jnp.float32)[:, None] * inverse_freq[None, :]
    cosine_table = jnp.cos(angles)[:, None, :]
    sine_table = jnp.sin(angles)[:, None, :]
    first_half = values[..., :half_rot]
    second_half = values[..., half_rot:ROT]
    return jnp.concatenate([first_half * cosine_table - second_half * sine_table, second_half * cosine_table + first_half * sine_table, values[..., ROT:]], -1)

def attend_row(pieces):
    queries, key_rows, value_rows, family = pieces
    precise = lax.Precision.HIGHEST
    scores = jnp.einsum('qhd,khd->hqk', queries, key_rows, precision=precise) * HEAD_DIM ** (-0.5)
    scores = low_back(scores)
    places = jnp.arange(SEQ_LEN)
    allowed = (places[None, :] <= places[:, None]) & (family[:, None] == family[None, :])
    scores = jnp.where(allowed[None], scores, -1000000000.0)
    row_max = lax.optimization_barrier(jnp.max(scores, -1, keepdims=True))
    weights = jnp.exp(scores - row_max)
    prob_low = low(weights / lax.optimization_barrier(jnp.sum(weights, -1, keepdims=True)))
    mixed_heads = jnp.einsum('hqk,khd->qhd', prob_low, value_rows, precision=precise)
    return low_back(low(mixed_heads))

def layer_forward(values, norm_gain, norm_shift, qkv_weight, out_weight, up_weight, up_bias, down_weight, down_bias, families):
    row_count = values.shape[0]
    precise = lax.Precision.HIGHEST
    row_mean = lax.optimization_barrier(jnp.mean(values, -1, keepdims=True))
    centered = values - row_mean
    variance = lax.optimization_barrier(jnp.mean(centered * centered, -1, keepdims=True))
    normed = low(centered * lax.rsqrt(variance + EPS) * norm_gain + norm_shift)
    raw_qkv = low_back(jnp.einsum('bld,de->ble', normed, qkv_weight, precision=precise))
    raw_qkv = raw_qkv.reshape(row_count, SEQ_LEN, 3, HEADS, HEAD_DIM)
    places = jnp.arange(SEQ_LEN)
    queries = low_back(low(rotate(raw_qkv[:, :, 0], places)))
    key_rows = low_back(low(rotate(raw_qkv[:, :, 1], places)))
    value_rows = low_back(low(raw_qkv[:, :, 2]))
    mixed_heads = lax.map(jax.checkpoint(attend_row), (queries, key_rows, value_rows, families))
    attn_out = low_back(jnp.einsum('bld,de->ble', mixed_heads.reshape(row_count, SEQ_LEN, D), out_weight, precision=precise))
    hidden = low_back(jnp.einsum('bld,df->blf', normed, up_weight, precision=precise) + up_bias)
    active = low(jax.nn.gelu(hidden, approximate=True))
    mlp_out = low_back(jnp.einsum('blf,fd->bld', active, down_weight, precision=precise) + down_bias)
    return values + attn_out + mlp_out

def reference(inputs, norm_gain, norm_shift, qkv_weight, out_weight, up_weight, up_bias, down_weight, down_bias, partners, families, cotangent):
    weight_list = (norm_gain.astype(jnp.float32), norm_shift.astype(jnp.float32), qkv_weight.astype(jnp.float32), out_weight.astype(jnp.float32), up_weight.astype(jnp.float32), up_bias.astype(jnp.float32), down_weight.astype(jnp.float32), down_bias.astype(jnp.float32))
    row_total = inputs.shape[0]
    grads_in = cotangent[partners].astype(jnp.float32)
    per_step = 2
    step_count = row_total // per_step
    input_blocks = inputs.reshape(step_count, per_step, SEQ_LEN, D)
    family_blocks = families.reshape(step_count, per_step, SEQ_LEN)
    grad_blocks = grads_in.reshape(step_count, per_step, SEQ_LEN, D)

    def scan_step(summed, piece):
        input_piece, family_piece, grad_piece = piece

        def forward_only(values, gain, shift, wqkv, wout, wup, bup, wdown, bdown):
            return layer_forward(values, gain, shift, wqkv, wout, wup, bup, wdown, bdown, family_piece)
        output, pullback = jax.vjp(forward_only, input_piece.astype(jnp.float32), *weight_list)
        pulled = pullback(grad_piece)
        summed = tuple((left + right for left, right in zip(summed, pulled[1:])))
        return (summed, (output.astype(jnp.bfloat16), pulled[0]))
    initial = tuple((jnp.zeros_like(item) for item in weight_list))
    summed, (outputs, input_grads) = lax.scan(scan_step, initial, (input_blocks, family_blocks, grad_blocks))
    return (outputs.reshape(row_total, SEQ_LEN, D), input_grads.reshape(row_total, SEQ_LEN, D), summed[0], summed[1], summed[2], summed[3], summed[4], summed[5], summed[6], summed[7])
```

```python
import functools

import jax
import jax.numpy as jnp
from jax import lax
from jax.experimental import pallas as pl
from jax.experimental.pallas import tpu as pltpu
from jax.sharding import PartitionSpec as P

F32 = jnp.float32
BF16 = jnp.bfloat16
HEAD_DIM = 64
ROT = 32
EPS = 1e-05
C0 = 0.7978845608028654
C1 = C0 * 0.044715


def dot(a,b): return lax.dot_general(a,b,(((1,),(0,)),((),())),preferred_element_type=F32)
def dot_nt(a,b): return lax.dot_general(a,b,(((1,),(1,)),((),())),preferred_element_type=F32)
def dot_tn(a,b): return lax.dot_general(a,b,(((0,),(0,)),((),())),preferred_element_type=F32)

def turn(x, c, sa, sb, sign):
    left = pltpu.roll(x, 128 - ROT // 2, 1)
    right = pltpu.roll(x, ROT // 2, 1)
    return x * c + sign * (left * sa + right * sb)

def attn_kernel(x_ref, xt_ref, g_ref, wq_ref, wk_ref, wv_ref, wo_ref, famr_ref, famc_ref, c_ref, sa_ref, sb_ref,
                ao_ref, dn_ref, gq_ref, gk_ref, gv_ref, go_ref,
                q_s, k_s, v_s, do_s, kt_s, vt_s, ht_s, dqt_s, dk_s, dv_s, draw_s, ao_s, dn_s):
    step = pl.program_id(0)
    last = pl.num_programs(0) - 1
    n = x_ref.shape[0]
    tile = 256
    c, sa, sb = c_ref[...], sa_ref[...], sb_ref[...]
    x = x_ref[...]
    q_s[...] = (turn(dot(x, wq_ref[...]), c, sa, sb, 1.0) * HEAD_DIM ** -0.5).astype(BF16)
    k = turn(dot(x, wk_ref[...]), c, sa, sb, 1.0).astype(BF16)
    k_s[...] = k
    kt_s[...] = k.T
    v = dot(x, wv_ref[...]).astype(BF16)
    v_s[...] = v
    vt_s[...] = v.T
    do_s[...] = dot_nt(g_ref[...], wo_ref[...]).astype(BF16)
    lane = lax.broadcasted_iota(jnp.int32, (tile, 128), 1)
    for h in range(2):
        mine = (lane < HEAD_DIM) if h == 0 else (lane >= HEAD_DIM)
        rows = slice(h * HEAD_DIM, (h + 1) * HEAD_DIM)
        for i in reversed(range(n // tile)):
            span = (i + 1) * tile
            here = slice(i * tile, span)
            qh = jnp.where(mine, q_s[here, :], 0).astype(BF16)
            doh = jnp.where(mine, do_s[here, :], 0).astype(BF16)
            st = dot_nt(k_s[0:span, :], qh)
            allowed = famc_ref[0:span, :] == famr_ref[:, here]
            kpos = lax.broadcasted_iota(jnp.int32, (span, tile), 0)
            qpos = lax.broadcasted_iota(jnp.int32, (span, tile), 1) + i * tile
            allowed = allowed & (kpos <= qpos)
            st = jnp.where(allowed, st, -1e9)
            e = jnp.exp(st - jnp.max(st, 0, keepdims=True))
            p = e * (1.0 / jnp.sum(e, 0, keepdims=True))
            pb = p.astype(BF16)
            ht_s[rows, here] = dot(vt_s[rows, 0:span], pb).astype(BF16)
            dpt = dot_nt(v_s[0:span, :], doh)
            ds = (p * (dpt - jnp.sum(p * dpt, 0, keepdims=True))).astype(BF16)
            dqt_s[rows, here] = dot(kt_s[rows, 0:span], ds) * HEAD_DIM ** -0.5
            dv = dot(pb, doh)
            dk = dot(ds, qh)
            if h == 0 and i == n // tile - 1:
                dv_s[...] = dv
                dk_s[...] = dk
            else:
                dv_s[0:span, :] += dv
                dk_s[0:span, :] += dk
    draw_s[:, 0:128] = turn(dqt_s[...].T, c, sa, sb, -1.0).astype(BF16)
    draw_s[:, 128:256] = turn(dk_s[...], c, sa, sb, -1.0).astype(BF16)
    draw_s[:, 256:384] = dv_s[...].astype(BF16)
    grads = dot(xt_ref[...], draw_s[...])
    gq_ref[...] = grads[:, 0:128].astype(gq_ref.dtype)
    gk_ref[...] = grads[:, 128:256].astype(gq_ref.dtype)
    gv_ref[...] = grads[:, 256:384].astype(gq_ref.dtype)
    go_ref[...] = dot(ht_s[...], g_ref[...]).astype(go_ref.dtype)
    w = jnp.concatenate([wq_ref[...], wk_ref[...], wv_ref[...]], 1)
    heads = ht_s[...].T
    for m in range(n // tile):
        here = slice(m * tile, (m + 1) * tile)
        dn = dot_nt(draw_s[here, :], w)
        ao = dot(heads[here, :], wo_ref[...])
        @pl.when(step == 0)
        def _():
            dn_s[here, :] = dn
            ao_s[here, :] = ao
        @pl.when((step > 0) & (step < last))
        def _():
            dn_s[here, :] += dn
            ao_s[here, :] += ao
        @pl.when(step == last)
        def _():
            dn_ref[here, :] = (dn_s[here, :] + dn).astype(dn_ref.dtype)
            ao_ref[here, :] = (ao_s[here, :] + ao).astype(ao_ref.dtype)

def tables(n):
    half = ROT // 2
    inverse_freq = 10000.0 ** (-2.0 * jnp.arange(half).astype(F32) / ROT)
    angles = jnp.arange(n).astype(F32)[:, None] * inverse_freq[None, :]
    cosine, sine = jnp.cos(angles), jnp.sin(angles)
    ones, zeros = jnp.ones((n, HEAD_DIM - ROT), F32), jnp.zeros((n, HEAD_DIM - ROT), F32)
    z = jnp.zeros((n, half), F32)
    c = jnp.concatenate([cosine, cosine, ones], 1)
    sa = jnp.concatenate([-sine, z, zeros], 1)
    sb = jnp.concatenate([z, sine, zeros], 1)
    return tuple(jnp.concatenate([t, t], 1) for t in (c, sa, sb))

def attend(x, xt, g, wqkv, wo, family, tabs):
    n, d = x.shape
    pairs = d // 128
    whole = lambda s: pl.BlockSpec(s, lambda p: (0, 0), pipeline_mode=pl.Buffered(1))
    col = lambda k: pl.BlockSpec((d, 128), lambda p, k=k: (0, p + k * pairs))
    gcol = pl.BlockSpec((d, 128), lambda p: (0, p))
    bf = lambda s: jax.ShapeDtypeStruct(s, BF16)
    return pl.pallas_call(
        attn_kernel,
        out_shape=(bf((n, d)), bf((n, d)), bf((d, d)), bf((d, d)), bf((d, d)), bf((d, d))),
        grid=(pairs,),
        in_specs=[whole((n, d)), whole((d, n)), whole((n, d)), col(0), col(1), col(2), pl.BlockSpec((128, d), lambda p: (p, 0)),
                  whole((1, n)), whole((n, 1)), whole((n, 128)), whole((n, 128)), whole((n, 128))],
        out_specs=(whole((n, d)), whole((n, d)), gcol, gcol, gcol, pl.BlockSpec((128, d), lambda p: (p, 0))),
        scratch_shapes=[pltpu.VMEM((n, 128), BF16)] * 4 + [pltpu.VMEM((128, n), BF16)] * 3
        + [pltpu.VMEM((128, n), F32), pltpu.VMEM((n, 128), F32), pltpu.VMEM((n, 128), F32), pltpu.VMEM((n, 384), BF16),
           pltpu.VMEM((n, d), F32), pltpu.VMEM((n, d), F32)],
        compiler_params=pltpu.CompilerParams(vmem_limit_bytes=56 * 2**20),
        cost_estimate=pl.CostEstimate(flops=70_000_000_000, bytes_accessed=30_000_000, transcendentals=20_000_000),
    )(x, xt, g, wqkv, wqkv, wqkv, wo, family.reshape(1, n), family.reshape(n, 1), *tabs)

def mlp_kernel(x_ref, xt_ref, g_ref, wu_ref, b_ref, wd_ref, y_ref, dn_ref, gu_ref, gd_ref, gb_ref, act_s, dh_s, y_s, dn_s, *, tile):
    step = pl.program_id(0)
    last = pl.num_programs(0) - 1
    n = x_ref.shape[0]
    gb = None
    for m in range(n // tile):
        here = slice(m * tile, (m + 1) * tile)
        v = dot(x_ref[here, :], wu_ref[...]) + b_ref[...]
        vv = v * v
        a = 0.5 + 0.5 * jnp.tanh(v * (C0 + C1 * vv))
        act = v * a
        slope = a + act * (1.0 - a) * (2 * C0 + 6 * C1 * vv)
        act_s[here, :] = act.astype(BF16)
        dh = (dot_nt(g_ref[here, :], wd_ref[...]) * slope).astype(BF16)
        dh_s[here, :] = dh
        part = jnp.sum(dh.astype(F32), 0, keepdims=True)
        gb = part if gb is None else gb + part
    gb_ref[...] = gb
    gu_ref[...] = dot(xt_ref[...], dh_s[...]).astype(gu_ref.dtype)
    gd_ref[...] = dot_tn(act_s[...], g_ref[...]).astype(gd_ref.dtype)
    for m in range(n // tile):
        here = slice(m * tile, (m + 1) * tile)
        y = dot(act_s[here, :], wd_ref[...])
        dn = dot_nt(dh_s[here, :], wu_ref[...])
        @pl.when(step == 0)
        def _():
            y_s[here, :] = y
            dn_s[here, :] = dn
        @pl.when((step > 0) & (step < last))
        def _():
            y_s[here, :] += y
            dn_s[here, :] += dn
        @pl.when(step == last)
        def _():
            y_ref[here, :] = y_s[here, :] + y
            dn_ref[here, :] = dn_s[here, :] + dn
def mlp(x, xt, g, wu, b, wd, F=512, tile=256):
    n, d = x.shape
    f = wu.shape[1]
    whole = lambda s: pl.BlockSpec(s, lambda p: (0, 0), pipeline_mode=pl.Buffered(1))
    sd = jax.ShapeDtypeStruct
    return pl.pallas_call(
        functools.partial(mlp_kernel, tile=tile),
        out_shape=(sd((n, d), F32), sd((n, d), F32), sd((d, f), BF16), sd((f, d), BF16), sd((1, f), F32)),
        grid=(f // F,),
        in_specs=[whole((n, d)), whole((d, n)), whole((n, d)), pl.BlockSpec((d, F), lambda p: (0, p)), pl.BlockSpec((1, F), lambda p: (0, p)),
                  pl.BlockSpec((F, d), lambda p: (p, 0))],
        out_specs=(whole((n, d)), whole((n, d)), pl.BlockSpec((d, F), lambda p: (0, p)), pl.BlockSpec((F, d), lambda p: (p, 0)), pl.BlockSpec((1, F), lambda p: (0, p))),
        scratch_shapes=[pltpu.VMEM((n, F), BF16)] * 2 + [pltpu.VMEM((n, d), F32)] * 2,
        compiler_params=pltpu.CompilerParams(vmem_limit_bytes=56 * 2**20),
        cost_estimate=pl.CostEstimate(flops=52_000_000_000, bytes_accessed=50_000_000, transcendentals=4_000_000),
    )(x, xt, g, wu, b.reshape(1, f), wd)

def normalize(values):
    centered = values - jnp.mean(values, -1, keepdims=True)
    scale = lax.rsqrt(jnp.mean(centered * centered, -1, keepdims=True) + EPS)
    return centered * scale, scale


def on_device(inputs, norm_gain, norm_shift, qkv_weight, out_weight, up_weight, up_bias, down_weight, down_bias,
              partners, families, cotangent):
    row_count, place_count, width = inputs.shape
    tokens = row_count * place_count
    local_rows = partners - lax.axis_index("dp") * row_count
    grad = jnp.take(cotangent, local_rows, axis=0)
    to_rows = functools.partial(lax.all_to_all, axis_name="seq", split_axis=0, concat_axis=1, tiled=True)
    to_places = functools.partial(lax.all_to_all, axis_name="seq", split_axis=1, concat_axis=0, tiled=True)
    row_inputs = to_rows(inputs)
    row_grad = to_rows(grad)
    values = inputs.astype(F32).reshape(tokens, width)
    grad = grad.reshape(tokens, width)
    xhat, scale = normalize(values)
    normed = (xhat * norm_gain + norm_shift).astype(BF16)
    mlp_out, d_normed, up_grad, down_grad, up_bias_grad = mlp(normed, normed.T, grad, up_weight, up_bias, down_weight)
    row_xhat, _ = normalize(row_inputs[0].astype(F32))
    row_normed = (row_xhat * norm_gain + norm_shift).astype(BF16)
    family = lax.dynamic_index_in_dim(families, lax.axis_index("seq"), 0, keepdims=False)
    full = row_normed.shape[0]
    attn_out, d_attn, q_grad, k_grad, v_grad, out_grad = attend(
        row_normed, row_normed.T, row_grad[0], qkv_weight, out_weight, family, tables(full))
    attn_back = to_places(attn_out[None]).reshape(tokens, width).astype(F32)
    d_back = to_places(d_attn[None]).reshape(tokens, width).astype(F32)
    layer_out = (values + attn_back + (mlp_out + down_bias)).astype(BF16).reshape(inputs.shape)
    d_total = d_normed + d_back
    grad32 = grad.astype(F32)
    dx = d_total * norm_gain
    input_grad = grad32 + (dx - jnp.mean(dx, -1, keepdims=True) - xhat * jnp.mean(dx * xhat, -1, keepdims=True)) * scale
    small = (jnp.sum(d_total * xhat, 0), jnp.sum(d_total, 0), up_bias_grad[0], jnp.sum(grad32, 0))
    gain_sum, shift_sum, up_bias_sum, down_bias_sum = lax.psum(small, ("dp", "seq"))

    def scatter(whole):
        part = lax.psum_scatter(whole, "seq", scatter_dimension=1, tiled=True)
        return lax.psum_scatter(part, "dp", scatter_dimension=0, tiled=True).astype(F32)

    down_sum = scatter(down_grad)
    up_sum = scatter(up_grad)
    out_sum = scatter(out_grad)
    qkv_sum = scatter(jnp.concatenate([q_grad, k_grad, v_grad], 1))
    return (layer_out, input_grad.reshape(inputs.shape), gain_sum, shift_sum, qkv_sum, out_sum, up_sum, up_bias_sum,
            down_sum, down_bias_sum)


def solution(mesh):
    rows = P("dp", "seq", None)
    placed = (rows,) + (P(),) * 8 + (P("dp"), P("dp", None), rows)
    grads = P("dp", "seq")
    return jax.shard_map(on_device, mesh=mesh, in_specs=placed,
                         out_specs=(rows, rows, P(), P(), grads, grads, grads, P(), grads, P()), check_vma=False)
```

```python
import functools

import jax
import jax.numpy as jnp
from jax import lax
from jax.experimental import pallas as pl
from jax.experimental.pallas import tpu as pltpu
from jax.sharding import PartitionSpec as P

F32 = jnp.float32
BF16 = jnp.bfloat16
HEAD_DIM = 64
ROT = 32
EPS = 1e-05
C0 = 0.7978845608028654
C1 = C0 * 0.044715

MESH_ID = pl.DeviceIdType.MESH

class Place:
    def __init__(self):
        dp, seq = lax.axis_index("dp"), lax.axis_index("seq")
        self.z, self.x, self.y, self.c = dp // 2, dp % 2, seq // 2, seq % 2
        self.twin = (dp, self.y * 2 + 1 - self.c)
        self.beside_y = (dp, (1 - self.y) * 2 + self.c)
        self.beside_x = (self.z * 2 + 1 - self.x, seq)
        self.along_z = [(((self.z + j) % 4) * 2 + self.x, seq) for j in (1, 2, 3)]
    def greet(self):
        barrier = pltpu.get_barrier_semaphore()
        partners = [self.twin, self.beside_y, self.beside_x] + self.along_z
        for partner in partners:
            pl.semaphore_signal(barrier, inc=1, device_id=partner, device_id_type=MESH_ID)
        pl.semaphore_wait(barrier, len(partners))

def add_into(dst, src, lead):
    rows, w = src.shape[-2:]
    band = rows
    while band * w > 32768:
        band //= 2
    count = 1
    for n in lead:
        count *= n
    def body(t, carry):
        block, part = t // (rows // band), t % (rows // band)
        index = []
        for n in reversed(lead):
            index.insert(0, block % n)
            block = block // n
        at = tuple(index) + (pl.ds(pl.multiple_of(part * band, band), band), slice(None))
        dst[at] = dst[at] + src[at]
        return carry
    lax.fori_loop(0, count * (rows // band), body, 0)

def piece_scratch(r, w, ra):
    return [pltpu.VMEM((2, 4, 2, r, w), BF16), pltpu.VMEM((2, 4, 2, r, w), BF16),
            pltpu.VMEM((4, 2, ra, w), BF16), pltpu.VMEM((2, 4, r - ra, w), BF16),
            pltpu.VMEM((4, ra, w), BF16), pltpu.VMEM((4, r - ra, w), BF16), pltpu.VMEM((3, r, w), BF16),
            pltpu.SemaphoreType.DMA((9,)), pltpu.SemaphoreType.DMA((9,)), pltpu.SemaphoreType.DMA((2,))]

class Piece:
    def __init__(self, place, src, out, scratch, ra, row0, col0, stride):
        self.p, self.src, self.out, self.ra, self.row0, self.col0, self.stride = place, src, out, ra, row0, col0, stride
        self.a, self.twin, self.r1p, self.r1q, self.r2p, self.r2q, self.r3, self.ss, self.rs, self.ls = scratch
        self.r, self.w = self.a.shape[-2:]
    def part(self, y, c):
        col = pl.multiple_of((y * 2 + c) * self.stride + self.col0, 128)
        return self.src.at[:, :, pl.ds(self.row0, self.r), pl.ds(col, self.w)]
    def send(self, k, src, dst, to):
        return pltpu.make_async_remote_copy(src_ref=src, dst_ref=dst, send_sem=self.ss.at[k], recv_sem=self.rs.at[k],
                                            device_id=to, device_id_type=MESH_ID)
    def copies(self, stage):
        p, a, ra, r = self.p, self.a, self.ra, self.r
        low, high = pl.ds(0, ra), pl.ds(ra, r - ra)
        if stage == 0:
            return [self.send(k, self.part(k, 1 - p.c), self.twin.at[k], p.twin) for k in (0, 1)]
        if stage == 1:
            return [self.send(2, a.at[1 - p.y, :, :, low, :], self.r1p, p.beside_y),
                    self.send(3, a.at[:, :, 1 - p.x, high, :], self.r1q, p.beside_x)]
        if stage == 2:
            return [self.send(4, a.at[p.y, :, 1 - p.x, low, :], self.r2p, p.beside_x),
                    self.send(5, a.at[1 - p.y, :, p.x, high, :], self.r2q, p.beside_y)]
        return [self.send(6 + j, a.at[p.y, (p.z + 1 + j) % 4, p.x], self.r3.at[j], p.along_z[j]) for j in range(3)]
    def own(self):
        return [pltpu.make_async_copy(self.part(k, self.p.c), self.a.at[k], self.ls.at[k]) for k in (0, 1)]
    def start(self, stage):
        for copy in self.copies(stage): copy.start()
        if stage == 0:
            for copy in self.own(): copy.start()
    def finish(self, stage):
        p, a, ra, r = self.p, self.a, self.ra, self.r
        low, high = pl.ds(0, ra), pl.ds(ra, r - ra)
        for copy in self.copies(stage): copy.wait()
        if stage == 0:
            for copy in self.own(): copy.wait()
            add_into(a, self.twin, (2, 4, 2))
        if stage == 1:
            add_into(a.at[p.y, :, :, low, :], self.r1p, (4, 2))
            add_into(a.at[:, :, p.x, high, :], self.r1q, (2, 4))
        if stage == 2:
            add_into(a.at[p.y, :, p.x, low, :], self.r2p, (4,))
            add_into(a.at[p.y, :, p.x, high, :], self.r2q, (4,))
        if stage == 3:
            self.out[...] = (a[p.y, p.z, p.x].astype(F32) + self.r3[0].astype(F32) + self.r3[1].astype(F32)
                             + self.r3[2].astype(F32))
    def tick(self, t):
        if t > 0: self.finish(t - 1)
        if t < 4: self.start(t)


def dot(a,b): return lax.dot_general(a,b,(((1,),(0,)),((),())),preferred_element_type=F32)
def dot_nt(a,b): return lax.dot_general(a,b,(((1,),(1,)),((),())),preferred_element_type=F32)
def dot_tn(a,b): return lax.dot_general(a,b,(((0,),(0,)),((),())),preferred_element_type=F32)

def turn(x, c, sa, sb, sign):
    left = pltpu.roll(x, 128 - ROT // 2, 1)
    right = pltpu.roll(x, ROT // 2, 1)
    return x * c + sign * (left * sa + right * sb)

def attn_kernel(x_ref, xt_ref, g_ref, wq_ref, wk_ref, wv_ref, wo_ref, famr_ref, famc_ref, c_ref, sa_ref, sb_ref,
                *rest, pieces):
    count = len(pieces)
    sources = rest[:2 if count else 0]
    rest = rest[len(sources):]
    ao_ref, dn_ref, gqkv_ref, go_ref = rest[:4]
    sums, rest = rest[4:4 + count], rest[4 + count:]
    q_s, k_s, v_s, do_s, kt_s, vt_s, ht_s, dqt_s, dk_s, dv_s, draw_s, ao_s, dn_s, out_s, out_sem = rest[:15]
    rest = rest[15:]
    step = pl.program_id(0)
    if count:
        place = Place()
        pl.when(step == 0)(place.greet)
        for i, (src, r, w, *where) in enumerate(pieces):
            piece = Piece(place, sources[src], sums[i], rest[i * 10:(i + 1) * 10], *where)
            for t in range(5):
                pl.when(step == i + t)(functools.partial(piece.tick, t))
    d = x_ref.shape[1]

    def put(k, at):
        cols = pl.multiple_of(k * d + at * 128, 128)
        return pltpu.make_async_copy(out_s.at[k], gqkv_ref.at[:, pl.ds(cols, 128)], out_sem.at[k])

    last = pl.num_programs(0) - 1
    n = x_ref.shape[0]
    tile = 256
    c, sa, sb = c_ref[...], sa_ref[...], sb_ref[...]
    x = x_ref[...]
    q_s[...] = (turn(dot(x, wq_ref[...]), c, sa, sb, 1.0) * HEAD_DIM ** -0.5).astype(BF16)
    k = turn(dot(x, wk_ref[...]), c, sa, sb, 1.0).astype(BF16)
    k_s[...] = k
    kt_s[...] = k.T
    v = dot(x, wv_ref[...]).astype(BF16)
    v_s[...] = v
    vt_s[...] = v.T
    do_s[...] = dot_nt(g_ref[...], wo_ref[...]).astype(BF16)
    lane = lax.broadcasted_iota(jnp.int32, (tile, 128), 1)
    for h in range(2):
        mine = (lane < HEAD_DIM) if h == 0 else (lane >= HEAD_DIM)
        rows = slice(h * HEAD_DIM, (h + 1) * HEAD_DIM)
        for i in reversed(range(n // tile)):
            span = (i + 1) * tile
            here = slice(i * tile, span)
            qh = jnp.where(mine, q_s[here, :], 0).astype(BF16)
            doh = jnp.where(mine, do_s[here, :], 0).astype(BF16)
            st = dot_nt(k_s[0:span, :], qh)
            allowed = famc_ref[0:span, :] == famr_ref[:, here]
            kpos = lax.broadcasted_iota(jnp.int32, (span, tile), 0)
            qpos = lax.broadcasted_iota(jnp.int32, (span, tile), 1) + i * tile
            allowed = allowed & (kpos <= qpos)
            st = jnp.where(allowed, st, -1e9)
            e = jnp.exp(st - jnp.max(st, 0, keepdims=True))
            p = e * (1.0 / jnp.sum(e, 0, keepdims=True))
            pb = p.astype(BF16)
            ht_s[rows, here] = dot(vt_s[rows, 0:span], pb).astype(BF16)
            dpt = dot_nt(v_s[0:span, :], doh)
            ds = (p * (dpt - jnp.sum(p * dpt, 0, keepdims=True))).astype(BF16)
            dqt_s[rows, here] = dot(kt_s[rows, 0:span], ds) * HEAD_DIM ** -0.5
            dv = dot(pb, doh)
            dk = dot(ds, qh)
            if h == 0 and i == n // tile - 1:
                dv_s[...] = dv
                dk_s[...] = dk
            else:
                dv_s[0:span, :] += dv
                dk_s[0:span, :] += dk
    draw_s[:, 0:128] = turn(dqt_s[...].T, c, sa, sb, -1.0).astype(BF16)
    draw_s[:, 128:256] = turn(dk_s[...], c, sa, sb, -1.0).astype(BF16)
    draw_s[:, 256:384] = dv_s[...].astype(BF16)
    grads = dot(xt_ref[...], draw_s[...])

    @pl.when(step > 0)
    def _():
        for k in range(3):
            put(k, step - 1).wait()
    for k in range(3):
        out_s[k] = grads[:, k * 128:(k + 1) * 128].astype(BF16)
        put(k, step).start()

    @pl.when(step == last)
    def _():
        for k in range(3):
            put(k, step).wait()
    go_ref[...] = dot(ht_s[...], g_ref[...]).astype(go_ref.dtype)
    w = jnp.concatenate([wq_ref[...], wk_ref[...], wv_ref[...]], 1)
    heads = ht_s[...].T
    for m in range(n // tile):
        here = slice(m * tile, (m + 1) * tile)
        dn = dot_nt(draw_s[here, :], w)
        ao = dot(heads[here, :], wo_ref[...])
        @pl.when(step == 0)
        def _():
            dn_s[here, :] = dn
            ao_s[here, :] = ao
        @pl.when((step > 0) & (step < last))
        def _():
            dn_s[here, :] += dn
            ao_s[here, :] += ao
        @pl.when(step == last)
        def _():
            dn_ref[here, :] = (dn_s[here, :] + dn).astype(dn_ref.dtype)
            ao_ref[here, :] = (ao_s[here, :] + ao).astype(ao_ref.dtype)

def tables(n):
    half = ROT // 2
    inverse_freq = 10000.0 ** (-2.0 * jnp.arange(half).astype(F32) / ROT)
    angles = jnp.arange(n).astype(F32)[:, None] * inverse_freq[None, :]
    cosine, sine = jnp.cos(angles), jnp.sin(angles)
    ones, zeros = jnp.ones((n, HEAD_DIM - ROT), F32), jnp.zeros((n, HEAD_DIM - ROT), F32)
    z = jnp.zeros((n, half), F32)
    c = jnp.concatenate([cosine, cosine, ones], 1)
    sa = jnp.concatenate([-sine, z, zeros], 1)
    sb = jnp.concatenate([z, sine, zeros], 1)
    return tuple(jnp.concatenate([t, t], 1) for t in (c, sa, sb))

def attend(x, xt, g, wqkv, wo, family, tabs, sources, pieces):
    n, d = x.shape
    pairs = d // 128
    whole = lambda s: pl.BlockSpec(s, lambda p: (0, 0), pipeline_mode=pl.Buffered(1))
    col = lambda k: pl.BlockSpec((d, 128), lambda p, k=k: (0, p + k * pairs))
    row = pl.BlockSpec((128, d), lambda p: (p, 0))
    anywhere = pl.BlockSpec(memory_space=pl.ANY)
    bf = lambda s: jax.ShapeDtypeStruct(s, BF16)
    vm = pltpu.VMEM
    extra = [item for piece in pieces for item in piece_scratch(*piece[1:4])]
    own_barrier = dict(collective_id=1, has_side_effects=True) if pieces else {}
    return pl.pallas_call(
        functools.partial(attn_kernel, pieces=pieces),
        out_shape=[bf((n, d)), bf((n, d)), bf((d, 3 * d)), bf((d, d))]
        + [jax.ShapeDtypeStruct((p[1], p[2]), F32) for p in pieces],
        grid=(pairs,),
        in_specs=[whole((n, d)), whole((d, n)), whole((n, d)), col(0), col(1), col(2), row,
                  whole((1, n)), whole((n, 1)), whole((n, 128)), whole((n, 128)), whole((n, 128))]
        + [anywhere] * len(sources),
        out_specs=[whole((n, d)), whole((n, d)), anywhere, row] + [whole((p[1], p[2])) for p in pieces],
        scratch_shapes=[vm((n, 128), BF16)] * 4 + [vm((128, n), BF16)] * 3
        + [vm((128, n), F32), vm((n, 128), F32), vm((n, 128), F32), vm((n, 384), BF16), vm((n, d), F32), vm((n, d), F32),
           vm((3, d, 128), BF16), pltpu.SemaphoreType.DMA((3,))] + extra,
        compiler_params=pltpu.CompilerParams(vmem_limit_bytes=60 * 2**20, **own_barrier),
        cost_estimate=pl.CostEstimate(flops=70_000_000_000, bytes_accessed=30_000_000, transcendentals=20_000_000),
    )(x, xt, g, wqkv, wqkv, wqkv, wo, family.reshape(1, n), family.reshape(n, 1), *tabs, *sources)

def mlp_kernel(x_ref, xt_ref, g_ref, wu_ref, b_ref, wd_ref, y_ref, dn_ref, gu_ref, gd_ref, gb_ref, act_s, dh_s, y_s, dn_s, *, tile):
    step = pl.program_id(0)
    last = pl.num_programs(0) - 1
    n = x_ref.shape[0]
    gb = None
    for m in range(n // tile):
        here = slice(m * tile, (m + 1) * tile)
        v = dot(x_ref[here, :], wu_ref[...]) + b_ref[...]
        vv = v * v
        a = 0.5 + 0.5 * jnp.tanh(v * (C0 + C1 * vv))
        act = v * a
        slope = a + act * (1.0 - a) * (2 * C0 + 6 * C1 * vv)
        act_s[here, :] = act.astype(BF16)
        dh = (dot_nt(g_ref[here, :], wd_ref[...]) * slope).astype(BF16)
        dh_s[here, :] = dh
        part = jnp.sum(dh.astype(F32), 0, keepdims=True)
        gb = part if gb is None else gb + part
    gb_ref[...] = gb
    gu_ref[...] = dot(xt_ref[...], dh_s[...]).astype(gu_ref.dtype)
    gd_ref[...] = dot_tn(act_s[...], g_ref[...]).astype(gd_ref.dtype)
    for m in range(n // tile):
        here = slice(m * tile, (m + 1) * tile)
        y = dot(act_s[here, :], wd_ref[...])
        dn = dot_nt(dh_s[here, :], wu_ref[...])
        @pl.when(step == 0)
        def _():
            y_s[here, :] = y
            dn_s[here, :] = dn
        @pl.when((step > 0) & (step < last))
        def _():
            y_s[here, :] += y
            dn_s[here, :] += dn
        @pl.when(step == last)
        def _():
            y_ref[here, :] = y_s[here, :] + y
            dn_ref[here, :] = dn_s[here, :] + dn
def mlp(x, xt, g, wu, b, wd, F=512, tile=256):
    n, d = x.shape
    f = wu.shape[1]
    whole = lambda s: pl.BlockSpec(s, lambda p: (0, 0), pipeline_mode=pl.Buffered(1))
    sd = jax.ShapeDtypeStruct
    return pl.pallas_call(
        functools.partial(mlp_kernel, tile=tile),
        out_shape=(sd((n, d), F32), sd((n, d), F32), sd((d, f), BF16), sd((f, d), BF16), sd((1, f), F32)),
        grid=(f // F,),
        in_specs=[whole((n, d)), whole((d, n)), whole((n, d)), pl.BlockSpec((d, F), lambda p: (0, p)), pl.BlockSpec((1, F), lambda p: (0, p)),
                  pl.BlockSpec((F, d), lambda p: (p, 0))],
        out_specs=(whole((n, d)), whole((n, d)), pl.BlockSpec((d, F), lambda p: (0, p)), pl.BlockSpec((F, d), lambda p: (p, 0)), pl.BlockSpec((1, F), lambda p: (0, p))),
        scratch_shapes=[pltpu.VMEM((n, F), BF16)] * 2 + [pltpu.VMEM((n, d), F32)] * 2,
        compiler_params=pltpu.CompilerParams(vmem_limit_bytes=56 * 2**20),
        cost_estimate=pl.CostEstimate(flops=52_000_000_000, bytes_accessed=50_000_000, transcendentals=4_000_000),
    )(x, xt, g, wu, b.reshape(1, f), wd)

def sum_kernel(*refs, pieces, sources):
    count = len(pieces)
    outs, scratch = refs[sources:sources + count], refs[sources + count:]
    place = Place()
    place.greet()
    made = [Piece(place, refs[p[0]], outs[i], scratch[i * 10:(i + 1) * 10], *p[3:]) for i, p in enumerate(pieces)]
    for t in range(count + 4):
        for i, piece in enumerate(made):
            if 0 <= t - i <= 4:
                piece.tick(t - i)


def sum_up(sources, pieces):
    return pl.pallas_call(
        functools.partial(sum_kernel, pieces=pieces, sources=len(sources)),
        out_shape=[jax.ShapeDtypeStruct((p[1], p[2]), F32) for p in pieces],
        in_specs=[pl.BlockSpec(memory_space=pl.ANY)] * len(sources),
        out_specs=[pl.BlockSpec(memory_space=pltpu.VMEM)] * len(pieces),
        scratch_shapes=[item for p in pieces for item in piece_scratch(*p[1:4])],
        compiler_params=pltpu.CompilerParams(collective_id=2, has_side_effects=True, vmem_limit_bytes=56 * 2**20),
    )(*sources)


def normalize(values):
    centered = values - jnp.mean(values, -1, keepdims=True)
    scale = lax.rsqrt(jnp.mean(centered * centered, -1, keepdims=True) + EPS)
    return centered * scale, scale


def by_chip(grad):
    return grad.reshape(4, 2, grad.shape[0] // 8, grad.shape[1])


def on_device(inputs, norm_gain, norm_shift, qkv_weight, out_weight, up_weight, up_bias, down_weight, down_bias,
              partners, families, cotangent, small_slice):
    row_count, place_count, width = inputs.shape
    tokens = row_count * place_count
    hidden = up_bias.shape[0]
    local_rows = partners - lax.axis_index("dp") * row_count
    grad = jnp.take(cotangent, local_rows, axis=0)
    swap = functools.partial(lax.all_to_all, axis_name="seq", split_axis=0, concat_axis=0, tiled=True)
    row_inputs = swap(inputs).reshape(tokens, width)
    row_grad = swap(grad).reshape(tokens, width)
    values = inputs.astype(F32).reshape(tokens, width)
    grad = grad.reshape(tokens, width)
    xhat, scale = normalize(values)
    normed = (xhat * norm_gain + norm_shift).astype(BF16)
    mlp_out, d_normed, up_grad, down_grad, up_bias_grad = mlp(normed, normed.T, grad, up_weight, up_bias, down_weight)
    row_xhat, _ = normalize(row_inputs.astype(F32))
    row_normed = (row_xhat * norm_gain + norm_shift).astype(BF16)
    family = lax.dynamic_index_in_dim(families, lax.axis_index("seq"), 0, keepdims=False)
    branch = functools.partial(attend, row_normed, row_normed.T, row_grad, qkv_weight, out_weight, family, tables(tokens))
    if small_slice:
        half, eighth, quarter = hidden // 8, hidden // 16, width // 4
        up_rows = width // 8
        pieces = ((0, up_rows, half, up_rows // 2, 0, 0, 2 * half), (0, up_rows, half, up_rows // 2, 0, half, 2 * half),
                  (1, eighth, quarter, eighth // 2, 0, 0, quarter), (1, eighth, quarter, eighth // 2, eighth, 0, quarter))
        attn_out, d_attn, qkv_grad, out_grad, up_a, up_b, down_a, down_b = branch((by_chip(up_grad), by_chip(down_grad)), pieces)
        up_sum = jnp.concatenate([up_a, up_b], 1)
        down_sum = jnp.concatenate([down_a, down_b], 0)
        third = 3 * width // 8
        pieces = ((1, up_rows, quarter, up_rows // 2, 0, 0, quarter), (0, up_rows, third, up_rows // 2, 0, 0, 2 * third),
                  (0, up_rows, third, up_rows // 2, 0, third, 2 * third))
        out_sum, qkv_a, qkv_b = sum_up((by_chip(qkv_grad), by_chip(out_grad)), pieces)
        qkv_sum = jnp.concatenate([qkv_a, qkv_b], 1)
    else:
        attn_out, d_attn, qkv_grad, out_grad = branch((), ())

        def scatter(whole):
            part = lax.psum_scatter(whole, "seq", scatter_dimension=1, tiled=True)
            return lax.psum_scatter(part, "dp", scatter_dimension=0, tiled=True).astype(F32)

        qkv_sum, out_sum, up_sum, down_sum = scatter(qkv_grad), scatter(out_grad), scatter(up_grad), scatter(down_grad)
    attn_back = swap(attn_out.reshape(inputs.shape)).reshape(tokens, width).astype(F32)
    d_back = swap(d_attn.reshape(inputs.shape)).reshape(tokens, width).astype(F32)
    layer_out = (values + attn_back + (mlp_out + down_bias)).astype(BF16).reshape(inputs.shape)
    d_total = d_normed + d_back
    grad32 = grad.astype(F32)
    dx = d_total * norm_gain
    input_grad = grad32 + (dx - jnp.mean(dx, -1, keepdims=True) - xhat * jnp.mean(dx * xhat, -1, keepdims=True)) * scale
    small = (jnp.sum(d_total * xhat, 0), jnp.sum(d_total, 0), up_bias_grad[0], jnp.sum(grad32, 0))
    gain_sum, shift_sum, up_bias_sum, down_bias_sum = lax.psum(small, ("dp", "seq"))
    return (layer_out, input_grad.reshape(inputs.shape), gain_sum, shift_sum, qkv_sum, out_sum, up_sum, up_bias_sum,
            down_sum, down_bias_sum)


def solution(mesh):
    rows = P("dp", "seq", None)
    placed = (rows,) + (P(),) * 8 + (P("dp"), P("dp", None), rows)
    grads = P("dp", "seq")
    small_slice = (mesh.shape["dp"], mesh.shape["seq"]) == (8, 4)
    return jax.shard_map(functools.partial(on_device, small_slice=small_slice), mesh=mesh, in_specs=placed,
                         out_specs=(rows, rows, P(), P(), grads, grads, grads, P(), grads, P()), check_vma=False)
```

```python
import functools

import jax
import jax.numpy as jnp
import numpy as np
from jax import lax
from jax.experimental import pallas as pl
from jax.experimental.pallas import tpu as pltpu
from jax.sharding import PartitionSpec as P

F32 = jnp.float32
BF16 = jnp.bfloat16
HEAD_DIM = 64
ROT = 32
EPS = 1e-05
C0 = 0.7978845608028654
C1 = C0 * 0.044715
TILE = 256
TAIL_UP = 32
ORDER = ((0, 3), (4, 7), (1, 2), (5, 6))
MESH_ID = pl.DeviceIdType.MESH
ANYWHERE = pl.BlockSpec(memory_space=pl.ANY)
DMA = pltpu.SemaphoreType.DMA


def dot(a, b):
    return lax.dot_general(a, b, (((1,), (0,)), ((), ())), preferred_element_type=F32)


def dot_nt(a, b):
    return lax.dot_general(a, b, (((1,), (1,)), ((), ())), preferred_element_type=F32)


def dot_tn(a, b):
    return lax.dot_general(a, b, (((0,), (0,)), ((), ())), preferred_element_type=F32)


def whole(shape):
    return pl.BlockSpec(shape, lambda p: (0,) * len(shape), pipeline_mode=pl.Buffered(1))


def pick(step, values):
    out = jnp.int32(values[0])
    for i, value in enumerate(values[1:], 1):
        out = jnp.where(step == i, value, out)
    return out


def normalize(values):
    centered = values - jnp.mean(values, -1, keepdims=True)
    scale = lax.rsqrt(jnp.mean(centered * centered, -1, keepdims=True) + EPS)
    return centered * scale, scale


def local_copy(src, dst, sem):
    return pltpu.make_async_copy(src, dst, sem)


def remote_copy(src, dst, send, recv, to):
    return pltpu.make_async_remote_copy(src_ref=src, dst_ref=dst, send_sem=send, recv_sem=recv, device_id=to,
                                        device_id_type=MESH_ID)


class Place:
    def __init__(self):
        self.dp, self.seq = lax.axis_index("dp"), lax.axis_index("seq")
        self.z, self.x, self.y, self.c = self.dp // 2, self.dp % 2, self.seq // 2, self.seq % 2
        self.twin = (self.dp, self.y * 2 + 1 - self.c)
        self.beside_y = (self.dp, (1 - self.y) * 2 + self.c)
        self.across = (self.dp, (1 - self.y) * 2 + 1 - self.c)
        self.beside_x = (self.z * 2 + 1 - self.x, self.seq)
        self.along_z = [(((self.z + j) % 4) * 2 + self.x, self.seq) for j in (1, 2, 3)]
        self.peers = [((self.seq + j) % 4, (self.dp, (self.seq + j) % 4)) for j in (1, 2, 3)]
        self.partners = [self.twin, self.beside_y, self.beside_x] + self.along_z

    def greet(self):
        barrier = pltpu.get_barrier_semaphore()
        for partner in self.partners + [self.across]:
            pl.semaphore_signal(barrier, inc=1, device_id=partner, device_id_type=MESH_ID)
        pl.semaphore_wait(barrier, len(self.partners) + 1)


def add_into(dst, src, lead):
    rows, w = src.shape[-2:]
    band = rows
    while band * w > 32768:
        band //= 2
    count = 1
    for n in lead:
        count *= n

    def body(t, carry):
        block, part = t // (rows // band), t % (rows // band)
        index = []
        for n in reversed(lead):
            index.insert(0, block % n)
            block = block // n
        at = tuple(index) + (pl.ds(pl.multiple_of(part * band, band), band), slice(None))
        dst[at] = dst[at] + src[at]
        return carry

    lax.fori_loop(0, count * (rows // band), body, 0)


def piece_scratch(r, w, ra=None):
    ra = r // 2 if ra is None else ra
    vm = pltpu.VMEM
    return [vm((2, 4, 2, r, w), BF16), vm((2, 4, 2, r, w), BF16), vm((4, 2, ra, w), BF16), vm((2, 4, r - ra, w), BF16),
            vm((4, ra, w), BF16), vm((4, r - ra, w), BF16), vm((3, r, w), BF16), DMA((9,)), DMA((9,)), DMA((2,))]


class Piece:
    def __init__(self, place, part, done, scratch):
        self.p, self.part, self.done = place, part, done
        self.a, self.from_twin, self.r1p, self.r1q, self.r2p, self.r2q, self.r3, self.ss, self.rs, self.ls = scratch
        self.r, self.w = self.a.shape[-2:]
        self.ra = self.r1p.shape[-2]

    def send(self, k, src, dst, to):
        return remote_copy(src, dst, self.ss.at[k], self.rs.at[k], to)

    def copies(self, stage):
        p, a = self.p, self.a
        low, high = pl.ds(0, self.ra), pl.ds(self.ra, self.r - self.ra)
        if stage == 0:
            return [self.send(k, self.part(k, 1 - p.c), self.from_twin.at[k], p.twin) for k in (0, 1)]
        if stage == 1:
            return [self.send(2, a.at[1 - p.y, :, :, low, :], self.r1p, p.beside_y),
                    self.send(3, a.at[:, :, 1 - p.x, high, :], self.r1q, p.beside_x)]
        if stage == 2:
            return [self.send(4, a.at[p.y, :, 1 - p.x, low, :], self.r2p, p.beside_x),
                    self.send(5, a.at[1 - p.y, :, p.x, high, :], self.r2q, p.beside_y)]
        return [self.send(6 + j, a.at[p.y, (p.z + 1 + j) % 4, p.x], self.r3.at[j], p.along_z[j]) for j in range(3)]

    def own(self):
        return [local_copy(self.part(k, self.p.c), self.a.at[k], self.ls.at[k]) for k in (0, 1)]

    def tick(self, t):
        p, a = self.p, self.a
        low, high = pl.ds(0, self.ra), pl.ds(self.ra, self.r - self.ra)
        if t > 0:
            for copy in self.copies(t - 1):
                copy.wait()
        if t == 0:
            for copy in self.copies(0) + self.own():
                copy.start()
        if t == 1:
            for copy in self.own():
                copy.wait()
            add_into(a, self.from_twin, (2, 4, 2))
        if t == 2:
            add_into(a.at[p.y, :, :, low, :], self.r1p, (4, 2))
            add_into(a.at[:, :, p.x, high, :], self.r1q, (2, 4))
        if t == 3:
            add_into(a.at[p.y, :, p.x, low, :], self.r2p, (4,))
            add_into(a.at[p.y, :, p.x, high, :], self.r2q, (4,))
        if t in (1, 2, 3):
            for copy in self.copies(t):
                copy.start()
        if t == 4:
            self.done(a[p.y, p.z, p.x].astype(F32) + self.r3[0].astype(F32) + self.r3[1].astype(F32) + self.r3[2].astype(F32))


class Credit:
    def __init__(self, place, sem):
        self.p, self.sem = place, sem

    def give(self):
        for partner in self.p.partners:
            pl.semaphore_signal(self.sem, inc=1, device_id=partner, device_id_type=MESH_ID)

    def take(self):
        pl.semaphore_wait(self.sem, len(self.p.partners))


def ff_kernel(inp_ref, g_ref, gain_ref, shift_ref, bias_ref, wu_ref, wd_ref, *rest, linked):
    hand, rest = (rest[:2], rest[2:]) if linked else ((), rest)
    y_ref, dn_ref, sums_ref, ub_ref = rest[:4]
    outs, rest = (rest[4:9], rest[9:]) if linked else (rest[4:6], rest[6:])
    x_s, xt_s, act_s, dh_s, wu_s, wd_s, gu_s, gd_s, wu_sem, wd_sem, gu_sem, gd_sem = rest[:12]
    rest = rest[12:]
    step = pl.program_id(0)
    last = pl.num_programs(0) - 1
    n, d = x_s.shape
    hidden = bias_ref.shape[1]
    group = hidden // 8
    tile = 512
    slot = step % 2

    def places(at):
        k, j = at // 2, at % 2
        return [(s, (2 * s + j) * group + k * 128) for s in range(4)]

    def weights(at, slot):
        out = []
        for s, f in places(at):
            f = pl.multiple_of(f, 128)
            out.append(local_copy(wu_ref.at[:, pl.ds(f, 128)], wu_s.at[slot, :, pl.ds(s * 128, 128)], wu_sem.at[slot, s]))
            out.append(local_copy(wd_ref.at[pl.ds(f, 128), :], wd_s.at[slot, pl.ds(s * 128, 128), :], wd_sem.at[slot, s]))
        return out

    def results(at):
        out = []
        k, j = at // 2, at % 2
        for s, f in places(at):
            f = pl.multiple_of(f, 128)
            up, down = gu_s.at[:, :, :, pl.ds(s * 128, 128)], gd_s.at[pl.ds(s * 128, 128), :]
            if linked:
                col = pl.multiple_of(s * 256 + j * 128, 128)
                to = outs[0].at[k, :, :, pl.ds(0, 128), pl.ds(col, 128)], outs[0].at[k, s, j, pl.ds(128, 128), :]
            else:
                to = outs[0].at[:, :, :, pl.ds(f, 128)], outs[1].at[pl.ds(f, 128), :]
            out.append(local_copy(up, to[0], gu_sem.at[s]))
            out.append(local_copy(down, to[1], gd_sem.at[s]))
        return out

    if linked:
        place = Place()
        row_send, row_recv, own_sem = rest[:3]
        rest = rest[3:]

        def swaps():
            out = []
            for a in range(2):
                for j, (to, device) in enumerate(place.peers):
                    out.append(remote_copy(hand[a].at[to], outs[1 + a].at[place.seq], row_send.at[a, j], row_recv.at[a, j], device))
                out.append(local_copy(hand[a].at[place.seq], outs[1 + a].at[place.seq], own_sem.at[a]))
            return out

        up_ref, down_ref = outs[3], outs[4]

        def part(y, c):
            return outs[0].at[0, :, :, :, pl.ds(pl.multiple_of((y * 2 + c) * 256, 256), 256)]

        def done(total):
            up_ref[...] = total[0:128]
            down_ref[...] = total[128:256]

        piece = Piece(place, part, done, rest)

    @pl.when(step == 0)
    def _():
        for copy in weights(0, 0):
            copy.start()
        if linked:
            place.greet()
            for copy in swaps():
                copy.start()
        for m in range(n // 256):
            rows = slice(m * 256, m * 256 + 256)
            xhat, _ = normalize(inp_ref[rows, :].astype(F32))
            normed = (xhat * gain_ref[...] + shift_ref[...]).astype(BF16)
            x_s[rows, :] = normed
            xt_s[:, rows] = normed.T
            total = jnp.sum(g_ref[rows, :].astype(F32), 0, keepdims=True)
            if m == 0:
                sums_ref[2:3, :] = total
            else:
                sums_ref[2:3, :] += total

    @pl.when(step < last)
    def _():
        for copy in weights(step + 1, 1 - slot):
            copy.start()
    for copy in weights(step, slot):
        copy.wait()
    w_up, w_down = wu_s.at[slot], wd_s.at[slot]
    bias = jnp.concatenate([bias_ref[:, pl.ds(pl.multiple_of(f, 128), 128)] for _, f in places(step)], 1)
    unit_sums = None
    for m in range(n // tile):
        here = slice(m * tile, (m + 1) * tile)
        v = dot(x_s[here, :], w_up[...]) + bias
        vv = v * v
        a = 0.5 + 0.5 * jnp.tanh(v * (C0 + C1 * vv))
        act = v * a
        slope = a + act * (1.0 - a) * (2 * C0 + 6 * C1 * vv)
        act_s[here, :] = act.astype(BF16)
        dh = (dot_nt(g_ref[here, :], w_down[...]) * slope).astype(BF16)
        dh_s[here, :] = dh
        total = jnp.sum(dh.astype(F32), 0, keepdims=True)
        unit_sums = total if unit_sums is None else unit_sums + total
    for s, f in places(step):
        ub_ref[:, pl.ds(pl.multiple_of(f, 128), 128)] = unit_sums[:, s * 128:(s + 1) * 128]

    @pl.when(step > 0)
    def _():
        for copy in results(step - 1):
            copy.wait()
    if linked:
        for t, at in enumerate((2, 3, 5, 6, 7)):
            pl.when(step == at)(functools.partial(piece.tick, t))
    for m in range(d // 256):
        grads = dot(xt_s[m * 256:(m + 1) * 256, :], dh_s[...]).astype(BF16)
        gu_s[m, 0] = grads[0:128]
        gu_s[m, 1] = grads[128:256]
    gd_s[...] = dot_tn(act_s[...], g_ref[...]).astype(BF16)
    for copy in results(step):
        copy.start()
    for m in range(n // tile):
        here = slice(m * tile, (m + 1) * tile)
        y = dot(act_s[here, :], w_down[...])
        dn = dot_nt(dh_s[here, :], w_up[...])

        @pl.when(step == 0)
        def _():
            y_ref[here, :] = y
            dn_ref[here, :] = dn

        @pl.when(step > 0)
        def _():
            y_ref[here, :] += y
            dn_ref[here, :] += dn

    @pl.when(step == last)
    def _():
        for m in range(n // 256):
            here = slice(m * 256, (m + 1) * 256)
            total = dn_ref[here, :]
            xhat, _ = normalize(inp_ref[here, :].astype(F32))
            gain_part = jnp.sum(total * xhat, 0, keepdims=True)
            shift_part = jnp.sum(total, 0, keepdims=True)
            if m == 0:
                sums_ref[0:1, :] = gain_part
                sums_ref[1:2, :] = shift_part
            else:
                sums_ref[0:1, :] += gain_part
                sums_ref[1:2, :] += shift_part
        for copy in results(step):
            copy.wait()
        if linked:
            for copy in swaps():
                copy.wait()


def feed_forward(inp, g, gain, shift, bias, wu, wd, linked):
    rows, span, d = inp.shape
    n, hidden = rows * span, bias.shape[0]
    sd, vm = jax.ShapeDtypeStruct, pltpu.VMEM
    out_shape = [sd((n, d), F32), sd((n, d), F32), sd((8, d), F32), sd((1, hidden), F32)]
    out_specs = [whole((n, d)), whole((n, d)), whole((8, d)), whole((1, hidden))]
    scratch = [vm((n, d), BF16), vm((d, n), BF16), vm((n, 512), BF16), vm((n, 512), BF16), vm((2, d, 512), BF16), vm((2, 512, d), BF16),
               vm((4, 2, 128, 512), BF16), vm((512, d), BF16), DMA((2, 4)), DMA((2, 4)), DMA((4,)), DMA((4,))]
    more, params = [], {}
    if linked:
        more = [inp, g]
        out_shape += [sd((4, 4, 2, 256, d), BF16), sd(inp.shape, BF16), sd(inp.shape, BF16), sd((128, 256), F32), sd((128, 256), F32)]
        out_specs += [ANYWHERE] * 3 + [whole((128, 256))] * 2
        scratch += [DMA((2, 3)), DMA((2, 3)), DMA((2,))] + piece_scratch(256, 256)
        params = dict(collective_id=0, has_side_effects=True)
    else:
        out_shape += [sd((4, 2, 128, hidden), BF16), sd((hidden, d), BF16)]
        out_specs += [ANYWHERE] * 2
    return pl.pallas_call(
        functools.partial(ff_kernel, linked=linked), out_shape=out_shape, grid=(hidden // 512,),
        in_specs=[whole((n, d)), whole((n, d)), whole((1, d)), whole((1, d)), whole((1, hidden)), ANYWHERE, ANYWHERE] + [ANYWHERE] * len(more),
        out_specs=out_specs, scratch_shapes=scratch,
        compiler_params=pltpu.CompilerParams(vmem_limit_bytes=58 * 2**20, **params),
        cost_estimate=pl.CostEstimate(flops=52_000_000_000, bytes_accessed=50_000_000, transcendentals=4_000_000),
    )(inp.reshape(n, d), g.reshape(n, d), gain.reshape(1, d), shift.reshape(1, d), bias.reshape(1, hidden), wu, wd, *more)


def turn(x, c, s, sign):
    lanes = x.shape[1]
    lane = lax.broadcasted_iota(jnp.int32, x.shape, 1) % HEAD_DIM
    other = jnp.where(lane < ROT // 2, pltpu.roll(x, lanes - ROT // 2, 1), pltpu.roll(x, ROT // 2, 1))
    return x * c + (sign * other) * s


def tile_place(tile):
    early = [kind * 8 + pair for two in ORDER[:2] for pair in two for kind in range(3)]
    block = tile // 6
    mates = sorted(t for t in range(24) if t // 6 == block and (t in early) == (tile in early))
    return block, mates.index(tile)


def attn_kernel(raw_ref, g_ref, gain_ref, shift_ref, famr_ref, famc_ref, tab_ref, wqkv_ref, wo_ref, *rest, linked):
    hand, rest = (rest[:1], rest[1:]) if linked else ((), rest)
    dn_ref, sums_ref, gqkv_ref, go_ref, heads_ref = rest[:5]
    outs, rest = (rest[5:12], rest[12:]) if linked else ((), rest[5:])
    (x_s, xt_s, c_s, s_s, w_s, wo_s, q_s, k_s, v_s, do_s, kt_s, vt_s, ht_s, dqt_s, dk_s, dv_s, draw_s, dn_s, gq_s, go_s, heads_s,
     w_sem, wo_sem, gq_sem, go_sem, h_sem) = rest[:26]
    rest = rest[26:]
    step = pl.program_id(0)
    steps = len(ORDER)
    last = steps - 1
    n, d = raw_ref.shape
    lanes = 256
    pairs = d // 128
    slot = step % 2

    def weights(at, slot):
        out = []
        for half in range(2):
            pair = pick(at, [o[half] for o in ORDER])
            for kind in range(3):
                col = pl.multiple_of((kind * pairs + pair) * 128, 128)
                j = kind * 2 + half
                out.append(local_copy(wqkv_ref.at[:, pl.ds(col, 128)], w_s.at[slot, :, pl.ds(j * 128, 128)], w_sem.at[slot, j]))
            row = pl.multiple_of(pair * 128, 128)
            out.append(local_copy(wo_ref.at[pl.ds(row, 128), :], wo_s.at[slot, pl.ds(half * 128, 128), :], wo_sem.at[slot, half]))
        return out

    def results(at):
        out = []
        for half in range(2):
            pair = pick(at, [o[half] for o in ORDER])
            for kind in range(3):
                j = kind * 2 + half
                if linked:
                    col = pick(at, [block * 384 + rank * 128 for block, rank in (tile_place(kind * 8 + o[half]) for o in ORDER)])
                    to = gqkv_ref.at[at // 2, :, :, :, pl.ds(pl.multiple_of(col, 128), 128)]
                else:
                    to = gqkv_ref.at[:, :, :, pl.ds(pl.multiple_of((kind * pairs + pair) * 128, 128), 128)]
                out.append(local_copy(gq_s.at[:, :, :, pl.ds(j * 128, 128)], to, gq_sem.at[j]))
            out.append(local_copy(go_s.at[pl.ds(half * 128, 128), :], go_ref.at[pair // 2, pair % 2], go_sem.at[half]))
        return out

    if linked:
        place = Place()
        head_send, head_recv, free_sem = rest[:3]
        rest = rest[3:]

        def heads_out(at):
            cols = pl.ds(pl.multiple_of(at * lanes, lanes), lanes)
            span = n // 4
            out = []
            for j, (to, device) in enumerate(place.peers):
                src = heads_s.at[pl.ds(pl.multiple_of(to * span, span), span), :]
                out.append(remote_copy(src, heads_ref.at[place.seq, :, cols], head_send.at[at, j], head_recv.at[at, j], device))
            mine = heads_s.at[pl.ds(pl.multiple_of(place.seq * span, span), span), :]
            return out, local_copy(mine, heads_ref.at[place.seq, :, cols], h_sem.at[0])

        def part_of(source, k, w):
            return lambda y, c: source.at[k, :, :, :, pl.ds(pl.multiple_of((y * 2 + c) * w, 128), w)]

        def done_at(k):
            def done(total):
                if k == 3:
                    outs[6][...] = total
                else:
                    outs[2 * k][...] = total[0:128]
                    outs[2 * k + 1][...] = total[128:256]
            return done

        buffers = [rest[0:10], rest[10:20], rest[20:30]]
        made = [Piece(place, part_of(hand[0], 1, 256), done_at(0), buffers[0]),
                Piece(place, part_of(hand[0], 2, 256), done_at(1), buffers[1]),
                Piece(place, part_of(hand[0], 3, 256), done_at(2), buffers[0]),
                Piece(place, part_of(gqkv_ref, 0, 384), done_at(3), buffers[2])]
        credit = Credit(place, free_sem)
        plan = {}
        for which, start in ((0, 0), (1, 3), (2, 10), (3, 11)):
            for t, off in enumerate((0, 1, 4, 6, 9)):
                plan.setdefault(min(start + off, 20), []).append((which, t))
    else:
        plan = {}

    def tick(position):
        for at, what in sorted(plan.items()):
            if min(at // 5, last) * 5 + position == at:
                def run(what=what):
                    for which, t in sorted(what, key=lambda w: (-w[1], w[0])):
                        if which == 2 and t == 0:
                            credit.take()
                        made[which].tick(t)
                        if which == 0 and t == 4:
                            credit.give()
                pl.when(step == min(at // 5, last))(run)

    @pl.when(step == 0)
    def _():
        for copy in weights(0, 0):
            copy.start()
        if linked:
            place.greet()

    @pl.when(step > 0)
    def _():
        for copy in results(step - 1):
            copy.wait()

    tick(0)

    @pl.when(step == 0)
    def _():
        for a in range(n // 32):
            rows = slice(a * 32, a * 32 + 32)
            ca, sa = tab_ref[0, a:a + 1, :], tab_ref[1, a:a + 1, :]
            cb, sb = tab_ref[2], tab_ref[3]
            c1 = ca * cb - sa * sb
            s1 = sa * cb + ca * sb
            lane = lax.broadcasted_iota(jnp.int32, c1.shape, 1) % HEAD_DIM
            c_s[rows, :] = jnp.where(lane < ROT, c1, 1.0)
            s_s[rows, :] = jnp.where(lane < ROT // 2, -s1, jnp.where(lane < ROT, s1, 0.0))
        for m in range(n // 256):
            rows = slice(m * 256, m * 256 + 256)
            xhat, _ = normalize(raw_ref[rows, :].astype(F32))
            normed = (xhat * gain_ref[...] + shift_ref[...]).astype(BF16)
            x_s[rows, :] = normed
            xt_s[:, rows] = normed.T

    @pl.when(step < last)
    def _():
        for copy in weights(step + 1, 1 - slot):
            copy.start()
    for copy in weights(step, slot):
        copy.wait()

    w_ref, wo1_ref = w_s.at[slot], wo_s.at[slot]
    scaling = HEAD_DIM ** -0.5

    def both(rows):
        c, s = c_s[rows, :], s_s[rows, :]
        return jnp.concatenate([c, c], 1), jnp.concatenate([s, s], 1)

    for m in range(n // 256):
        rows = slice(m * 256, m * 256 + 256)
        raw = dot(x_s[rows, :], w_ref[...])
        c, s = both(rows)
        q_s[rows, :] = (turn(raw[:, 0:lanes], c, s, 1.0) * scaling).astype(BF16)
        keys = turn(raw[:, lanes:2 * lanes], c, s, 1.0).astype(BF16)
        k_s[rows, :] = keys
        kt_s[:, rows] = keys.T
        vals = raw[:, 2 * lanes:].astype(BF16)
        v_s[rows, :] = vals
        vt_s[:, rows] = vals.T
        do_s[rows, :] = dot_nt(g_ref[rows, :], wo1_ref[...]).astype(BF16)

    tile = TILE
    lane = lax.broadcasted_iota(jnp.int32, (tile, 128), 1)
    work = [(h, i) for i in reversed(range(n // tile)) for h in range(4)]

    def first(h, i):
        span = (i + 1) * tile
        here = slice(i * tile, span)
        cols = slice(h // 2 * 128, h // 2 * 128 + 128)
        mine = (lane < HEAD_DIM) if h % 2 == 0 else (lane >= HEAD_DIM)
        qh = jnp.where(mine, q_s[here, cols], 0).astype(BF16)
        doh = jnp.where(mine, do_s[here, cols], 0).astype(BF16)
        return qh, doh, dot_nt(k_s[0:span, cols], qh), dot_nt(v_s[0:span, cols], doh)

    def second(h, i, qh, doh, st, dpt):
        span = (i + 1) * tile
        here = slice(i * tile, span)
        cols = slice(h // 2 * 128, h // 2 * 128 + 128)
        rows = slice(h * HEAD_DIM, (h + 1) * HEAD_DIM)
        allowed = famc_ref[0:span, :] == famr_ref[:, here]
        key_place = lax.broadcasted_iota(jnp.int32, (span, tile), 0)
        query_place = lax.broadcasted_iota(jnp.int32, (span, tile), 1) + i * tile
        st = jnp.where(allowed & (key_place <= query_place), st, -1e9)
        e = jnp.exp(st - jnp.max(st, 0, keepdims=True))
        p = e * (1.0 / jnp.sum(e, 0, keepdims=True))
        pb = p.astype(BF16)
        ds = (p * (dpt - jnp.sum(p * dpt, 0, keepdims=True))).astype(BF16)
        ht_s[rows, here] = dot(vt_s[rows, 0:span], pb).astype(BF16)
        dqt_s[rows, here] = dot(kt_s[rows, 0:span], ds) * scaling
        dv = dot(pb, doh)
        dk = dot(ds, qh)
        if h % 2 == 0 and i == n // tile - 1:
            dv_s[:, cols] = dv
            dk_s[:, cols] = dk
        else:
            dv_s[0:span, cols] += dv
            dk_s[0:span, cols] += dk

    made_first = first(*work[0])
    for j, (h, i) in enumerate(work):
        later = first(*work[j + 1]) if j + 1 < len(work) else None
        second(h, i, *made_first)
        made_first = later
        if h == 3:
            tick(n // tile - i)

    @pl.when(step > 0)
    def _():
        if linked:
            sent, mine = heads_out(step - 1)
            for copy in sent:
                copy.wait_send()
            mine.wait()
        else:
            local_copy(heads_s, heads_ref.at[:, pl.ds(pl.multiple_of((step - 1) * lanes, lanes), lanes)], h_sem.at[0]).wait()
    heads_s[...] = ht_s[...].T
    if linked:
        sent, mine = heads_out(step)
        for copy in sent:
            copy.start()
        mine.start()
    else:
        local_copy(heads_s, heads_ref.at[:, pl.ds(pl.multiple_of(step * lanes, lanes), lanes)], h_sem.at[0]).start()

    for m in range(n // 256):
        rows = slice(m * 256, m * 256 + 256)
        c, s = both(rows)
        draw_s[rows, 0:lanes] = turn(dqt_s[:, rows].T, c, s, -1.0).astype(BF16)
        draw_s[rows, lanes:2 * lanes] = turn(dk_s[rows, :], c, s, -1.0).astype(BF16)
        draw_s[rows, 2 * lanes:] = dv_s[rows, :].astype(BF16)

    for m in range(d // 256):
        grads = dot(xt_s[m * 256:(m + 1) * 256, :], draw_s[...]).astype(BF16)
        gq_s[m, 0] = grads[0:128]
        gq_s[m, 1] = grads[128:256]
    go_s[...] = dot(ht_s[...], g_ref[...]).astype(BF16)
    for copy in results(step):
        copy.start()
    for m in range(n // 256):
        here = slice(m * 256, (m + 1) * 256)
        dn = dot_nt(draw_s[here, :], w_ref[...])

        @pl.when(step == 0)
        def _():
            dn_s[here, :] = dn

        @pl.when((step > 0) & (step < last))
        def _():
            dn_s[here, :] += dn

        @pl.when(step == last)
        def _():
            total = dn_s[here, :] + dn
            xhat, _ = normalize(raw_ref[here, :].astype(F32))
            gain_part = jnp.sum(total * xhat, 0, keepdims=True)
            shift_part = jnp.sum(total, 0, keepdims=True)
            if m == 0:
                sums_ref[0:1, :] = gain_part
                sums_ref[1:2, :] = shift_part
            else:
                sums_ref[0:1, :] += gain_part
                sums_ref[1:2, :] += shift_part
            dn_ref[here, :] = total.astype(BF16)

    tick(5)

    @pl.when(step == last)
    def _():
        for copy in results(step):
            copy.wait()
        if linked:
            for at in range(steps):
                for copy in heads_out(at)[0]:
                    copy.wait_recv()
            for copy in heads_out(step)[0]:
                copy.wait_send()
            heads_out(step)[1].wait()
        else:
            local_copy(heads_s, heads_ref.at[:, pl.ds(pl.multiple_of(step * lanes, lanes), lanes)], h_sem.at[0]).wait()


def attend(raw, g, gain, shift, wqkv, wo, family, linked, grads=None):
    n, d = raw.shape
    pair_lane = np.arange(128) % HEAD_DIM % (ROT // 2)
    freq = 10000.0 ** (-2.0 * pair_lane / ROT)
    high, low = np.arange(n // 32)[:, None] * 32.0 * freq, np.arange(32)[:, None] * freq
    tab = jnp.asarray(np.stack([np.cos(high), np.sin(high), np.cos(low), np.sin(low)]), F32)
    sd, vm = jax.ShapeDtypeStruct, pltpu.VMEM
    out_shape = [sd((n, d), BF16), sd((8, d), F32), sd((2, 4, 2, 128, 3 * d // 2) if linked else (4, 2, 128, 3 * d), BF16),
                 sd((4, 2, 128, d), BF16), sd((4, n // 4, d) if linked else (n, d), BF16)]
    out_specs = [whole((n, d)), whole((8, d))] + [ANYWHERE] * 3
    scratch = [vm((n, d), BF16), vm((d, n), BF16), vm((n, 128), F32), vm((n, 128), F32), vm((2, d, 768), BF16), vm((2, 256, d), BF16)]
    scratch += [vm((n, 256), BF16)] * 4 + [vm((256, n), BF16)] * 3
    scratch += [vm((256, n), F32), vm((n, 256), F32), vm((n, 256), F32), vm((n, 768), BF16), vm((n, d), F32), vm((4, 2, 128, 768), BF16),
                vm((256, d), BF16), vm((n, 256), BF16), DMA((2, 6)), DMA((2, 2)), DMA((6,)), DMA((2,)), DMA((1,))]
    params, more = {}, []
    if linked:
        more = [grads]
        out_shape += [sd((128, 256), F32)] * 6 + [sd((128, 384), F32)]
        out_specs += [whole((128, 256))] * 6 + [whole((128, 384))]
        scratch += [DMA((4, 3)), DMA((4, 3)), pltpu.SemaphoreType.REGULAR]
        scratch += piece_scratch(256, 256) * 2 + piece_scratch(128, 384)
        params = dict(collective_id=1, has_side_effects=True)
    return pl.pallas_call(
        functools.partial(attn_kernel, linked=linked), out_shape=out_shape, grid=(len(ORDER),),
        in_specs=[whole((n, d)), whole((n, d)), whole((1, d)), whole((1, d)), whole((1, n)), whole((n, 1)), whole((4, 32, 128)), ANYWHERE, ANYWHERE]
        + [ANYWHERE] * len(more),
        out_specs=out_specs, scratch_shapes=scratch,
        compiler_params=pltpu.CompilerParams(vmem_limit_bytes=60 * 2**20, **params),
        cost_estimate=pl.CostEstimate(flops=70_000_000_000, bytes_accessed=30_000_000, transcendentals=20_000_000),
    )(raw, g, gain.reshape(1, d), shift.reshape(1, d), family.reshape(1, n), family.reshape(n, 1), tab, wqkv, wo, *more)


class SmallSum:
    def __init__(self, place, held, heard, by_z, send, recv):
        self.p, self.held, self.heard, self.by_z, self.send, self.recv = place, held, heard, by_z, send, recv

    def copies(self, t):
        p = self.p
        if t < 3:
            to = (p.twin, p.beside_y, p.beside_x)[t]
            return [remote_copy(self.held, self.heard.at[t], self.send.at[t], self.recv.at[t], to)]
        return [remote_copy(self.by_z.at[p.z], self.by_z.at[p.z], self.send.at[3 + j], self.recv.at[3 + j], to)
                for j, to in enumerate(p.along_z)]

    def tick(self, t):
        if t > 0:
            for copy in self.copies(t - 1):
                copy.wait()
        if 0 < t < 4:
            total = self.held[...] + self.heard[t - 1]
            if t < 3:
                self.held[...] = total
            else:
                self.by_z[self.p.z] = total
        if t < 4:
            for copy in self.copies(t):
                copy.start()
        return None if t < 4 else self.by_z[0] + self.by_z[1] + self.by_z[2] + self.by_z[3]


def tail_kernel(dat_ref, heads_ref, gq_ref, go_ref, inp_ref, g_ref, y_ref, dn_ref, wo_ref, gain_ref, dbias_ref, sums_ff_ref, sums_at_ref,
                ub_ref, early_ref, lo_ref, ig_ref, qkv_ref, out_ref, gain_o, shift_o, ub_o, db_o,
                back_s, inp_s, g_s, heads_s, y_s, dn_s, wo_s, lo_s, ig_s, small_s, heard_s, by_z_s,
                load_sem, wo_sem, back_send, back_recv, own_sem, small_send, small_recv, lo_sem, ig_sem, *pieces):
    place = Place()
    d = wo_s.shape[0]
    place.greet()
    swaps = [remote_copy(dat_ref.at[to], back_s.at[place.seq], back_send.at[j], back_recv.at[j], device)
             for j, (to, device) in enumerate(place.peers)]
    own = local_copy(dat_ref.at[place.seq], back_s.at[place.seq], own_sem.at[0])
    blocks = {}

    def part(source, w):
        return lambda y, c: source.at[:, :, :, pl.ds(pl.multiple_of((y * 2 + c) * w, 128), w)]

    def out_done(total):
        out_ref[...] = total

    def qkv_done(total):
        early = early_ref[...]
        first = jnp.where(place.c == 0, early, total)
        second = jnp.where(place.c == 0, total, early)
        order = ((first, 0), (second, 0), (second, 1), (first, 1), (first, 2), (second, 2))
        for k, (source, at) in enumerate(order):
            qkv_ref[:, k * 128:(k + 1) * 128] = source[:, at * 128:(at + 1) * 128]

    made = [Piece(place, part(go_ref, 256), out_done, pieces[:10]), Piece(place, part(gq_ref.at[1], 384), qkv_done, pieces[10:])]
    small = SmallSum(place, small_s, heard_s, by_z_s, small_send, small_recv)
    small_s[0:3, :] = sums_ff_ref[0:3, :]
    small_s[0:2, :] += sums_at_ref[0:2, :]
    small_s[3:4, :] = jnp.zeros((1, d), F32)
    for k in range(4):
        small_s[4 + k:5 + k, :] = ub_ref[:, k * d:(k + 1) * d]
    for piece in made:
        piece.tick(0)
    for copy in swaps:
        copy.start()
    small.tick(0)
    loads = [local_copy(a, b, load_sem.at[k]) for k, (a, b) in enumerate(
        ((heads_ref, heads_s), (inp_ref, inp_s), (y_ref, y_s), (g_ref, g_s), (dn_ref, dn_s)))]
    for pair in range(d // 128):
        at = [p for two in ORDER for p in two].index(pair)
        blocks[at] = local_copy(wo_ref.at[pl.ds(pair * 128, 128), :], wo_s.at[pl.ds(at * 128, 128), :], wo_sem.at[at])
    for copy in [loads[0]] + list(blocks.values()) + loads[1:] + [own]:
        copy.start()
    for copy in list(blocks.values()) + loads:
        copy.wait()

    def lo_out(r):
        return local_copy(lo_s.at[r], lo_ref.at[r], lo_sem.at[r])

    def ig_out(r):
        return local_copy(ig_s.at[r], ig_ref.at[r], ig_sem.at[r])

    def forward(r):
        total = inp_s[r].astype(F32) + dot(heads_s[r], wo_s[...]) + (y_s[r] + dbias_ref[...])
        lo_s[r] = total.astype(BF16)
        lo_out(r).start()

    def backward(r):
        xhat, scale = normalize(inp_s[r].astype(F32))
        dx = (dn_s[r] + back_s[r].astype(F32)) * gain_ref[...]
        ig_s[r] = g_s[r].astype(F32) + (dx - jnp.mean(dx, -1, keepdims=True) - xhat * jnp.mean(dx * xhat, -1, keepdims=True)) * scale
        ig_out(r).start()

    forward(0)
    forward(1)
    for piece in made:
        piece.tick(1)
    small.tick(1)
    forward(2)
    forward(3)
    for piece in made:
        piece.tick(2)
    small.tick(2)
    own.wait()
    backward(place.seq)
    for piece in made:
        piece.tick(3)
    small.tick(3)
    for j, (to, _) in enumerate(place.peers):
        swaps[j].wait_send()
    for j in (2, 1, 0):
        swaps[j].wait_recv()
        backward((place.seq + 3 - j) % 4)
    for piece in made:
        piece.tick(4)
    total = small.tick(4)
    gain_o[...] = total[0:1]
    shift_o[...] = total[1:2]
    db_o[...] = total[2:3]
    for k in range(4):
        ub_o[:, k * d:(k + 1) * d] = total[4 + k:5 + k]
    for r in range(4):
        lo_out(r).wait()
        ig_out(r).wait()


def finish(dat, heads, gq, go, inp, g, y, dn, wo, gain, dbias, sums_ff, sums_at, ub, early):
    sd, vm = jax.ShapeDtypeStruct, pltpu.VMEM
    shape, d = inp.shape, inp.shape[2]
    vmem = pl.BlockSpec(memory_space=pltpu.VMEM)
    return pl.pallas_call(
        tail_kernel,
        out_shape=[sd(shape, BF16), sd(shape, F32), sd((128, 768), F32), sd((128, 256), F32), sd((1, d), F32), sd((1, d), F32), sd((1, 4 * d), F32),
                   sd((1, d), F32)],
        in_specs=[ANYWHERE] * 9 + [vmem] * 6, out_specs=[ANYWHERE] * 2 + [vmem] * 6,
        scratch_shapes=[vm(shape, BF16)] * 4 + [vm(shape, F32)] * 2 + [vm((d, d), BF16), vm(shape, BF16), vm(shape, F32),
                        vm((8, d), F32), vm((3, 8, d), F32), vm((4, 8, d), F32),
                        DMA((5,)), DMA((8,)), DMA((3,)), DMA((3,)), DMA((1,)), DMA((6,)), DMA((6,)), DMA((4,)), DMA((4,))]
        + piece_scratch(128, 256, TAIL_UP) + piece_scratch(128, 384, TAIL_UP),
        compiler_params=pltpu.CompilerParams(collective_id=2, has_side_effects=True, vmem_limit_bytes=56 * 2**20),
    )(dat.reshape(shape), heads, gq, go, inp, g, y.reshape(shape), dn.reshape(shape), wo, gain.reshape(1, d), dbias.reshape(1, d), sums_ff, sums_at,
      ub, early)


def on_device(inputs, norm_gain, norm_shift, qkv_weight, out_weight, up_weight, up_bias, down_weight, down_bias, partners, families, cotangent, linked):
    row_count, place_count, width = inputs.shape
    tokens = row_count * place_count
    local_rows = partners - lax.axis_index("dp") * row_count
    grad = jnp.take(cotangent, local_rows, axis=0, mode="clip")
    family = lax.dynamic_index_in_dim(families, lax.axis_index("seq"), 0, keepdims=False)
    branch_args = norm_gain, norm_shift, qkv_weight, out_weight, family, linked
    if linked:
        y, dn, sums_ff, ub, grads, row_inputs, row_grad, up0, down0 = feed_forward(inputs, grad, norm_gain, norm_shift, up_bias, up_weight, down_weight, True)
        dat, sums_at, gq, go, heads, up1, down1, up2, down2, up3, down3, early = attend(
            row_inputs.reshape(tokens, width), row_grad.reshape(tokens, width), *branch_args, grads)
        layer_out, input_grad, qkv_sum, out_sum, gain_sum, shift_sum, ub_sum, db_sum = finish(
            dat, heads, gq, go, inputs, grad, y, dn, out_weight, norm_gain, down_bias, sums_ff, sums_at, ub, early)
        ups = (up0, up1, up2, up3)
        up_sum = jnp.concatenate([u[:, :128] for u in ups] + [u[:, 128:] for u in ups], 1)
        down_sum = jnp.concatenate([down0, down1, down2, down3], 0)
        return (layer_out, input_grad, gain_sum.reshape(width), shift_sum.reshape(width), qkv_sum, out_sum, up_sum, ub_sum.reshape(-1), down_sum,
                db_sum.reshape(width))
    swap = functools.partial(lax.all_to_all, axis_name="seq", split_axis=0, concat_axis=0, tiled=True)
    row_inputs, row_grad = swap(inputs).reshape(tokens, width), swap(grad).reshape(tokens, width)
    y, dn, sums_ff, ub, up_grad, down_grad = feed_forward(inputs, grad, norm_gain, norm_shift, up_bias, up_weight, down_weight, False)
    dat, sums_at, qkv_grad, out_grad, heads = attend(row_inputs, row_grad, *branch_args)

    def scatter(parts, columns):
        part = lax.psum_scatter(parts.reshape(-1, columns), "seq", scatter_dimension=1, tiled=True)
        return lax.psum_scatter(part, "dp", scatter_dimension=0, tiled=True).astype(F32)

    qkv_sum, out_sum = scatter(qkv_grad, 3 * width), scatter(out_grad, width)
    up_sum, down_sum = scatter(up_grad, up_bias.shape[0]), scatter(down_grad, width)
    heads = swap(heads.reshape(inputs.shape)).reshape(tokens, width)
    order = np.array([p for two in ORDER for p in two])
    attn_out = dot(heads, out_weight.reshape(-1, 128, width)[order].reshape(width, width))
    values = inputs.astype(F32).reshape(tokens, width)
    layer_out = (values + attn_out + (y + down_bias)).astype(BF16).reshape(inputs.shape)
    xhat, scale = normalize(values)
    dx = (dn + swap(dat.reshape(inputs.shape)).reshape(tokens, width).astype(F32)) * norm_gain
    input_grad = grad.reshape(tokens, width).astype(F32) + (dx - jnp.mean(dx, -1, keepdims=True) - xhat * jnp.mean(dx * xhat, -1, keepdims=True)) * scale
    gain_sum, shift_sum, up_bias_sum, down_bias_sum = lax.psum((sums_ff[0] + sums_at[0], sums_ff[1] + sums_at[1], ub[0], sums_ff[2]), ("dp", "seq"))
    return (layer_out, input_grad.reshape(inputs.shape), gain_sum, shift_sum, qkv_sum, out_sum, up_sum, up_bias_sum, down_sum, down_bias_sum)


def solution(mesh):
    rows = P("dp", "seq", None)
    placed = (rows,) + (P(),) * 8 + (P("dp"), P("dp", None), rows)
    grads = P("dp", "seq")
    linked = (mesh.shape["dp"], mesh.shape["seq"]) == (8, 4)
    return jax.shard_map(functools.partial(on_device, linked=linked), mesh=mesh, in_specs=placed,
                         out_specs=(rows, rows, P(), P(), grads, grads, grads, P(), grads, P()), check_vma=False)
```

```python
import functools

import jax
import jax.numpy as jnp
import numpy as np
from jax import lax
from jax.experimental import pallas as pl
from jax.experimental.pallas import tpu as pltpu
from jax.sharding import PartitionSpec as P

F32 = jnp.float32
BF16 = jnp.bfloat16
HEAD_DIM = 64
ROT = 32
EPS = 1e-05
C0 = 0.7978845608028654
C1 = C0 * 0.044715
TILE = 256
FF_SPLITS = (0, 176, 80), (96, 112, 48)
AT_SPLIT = 96, 112, 48
EARLY_SPLIT = 48, 64, 16
TAIL_SPLITS = (0, 80, 48), (0, 48, 16), (0, 32, 32)
FF_TICKS = (6, 9, 15, 18, 22), (12, 15, 20, 22, 24)
AT_TICKS = (0, 2, 7, 10, 14), (4, 7, 12, 15, 19), (13, 15, 19, 21, 24)
ORDER = ((0, 3), (4, 7), (1, 2), (5, 6))
MESH_ID = pl.DeviceIdType.MESH
ANYWHERE = pl.BlockSpec(memory_space=pl.ANY)
DMA = pltpu.SemaphoreType.DMA


def dot(a, b):
    return lax.dot_general(a, b, (((1,), (0,)), ((), ())), preferred_element_type=F32)


def dot_nt(a, b):
    return lax.dot_general(a, b, (((1,), (1,)), ((), ())), preferred_element_type=F32)


def dot_tn(a, b):
    return lax.dot_general(a, b, (((0,), (0,)), ((), ())), preferred_element_type=F32)


def whole(shape):
    return pl.BlockSpec(shape, lambda p: (0,) * len(shape), pipeline_mode=pl.Buffered(1))


def pick(step, values):
    out = jnp.int32(values[0])
    for i, value in enumerate(values[1:], 1):
        out = jnp.where(step == i, value, out)
    return out


def normalize(values):
    centered = values - jnp.mean(values, -1, keepdims=True)
    scale = lax.rsqrt(jnp.mean(centered * centered, -1, keepdims=True) + EPS)
    return centered * scale, scale


def each_band(count, body):
    def step(m, carry):
        body(pl.ds(pl.multiple_of(m * 256, 256), 256), m)
        return carry

    lax.fori_loop(0, count, step, 0)


def local_copy(src, dst, sem):
    return pltpu.make_async_copy(src, dst, sem)


def remote_copy(src, dst, send, recv, to):
    return pltpu.make_async_remote_copy(src_ref=src, dst_ref=dst, send_sem=send, recv_sem=recv, device_id=to,
                                        device_id_type=MESH_ID)


class Place:
    def __init__(self):
        self.dp, self.seq = lax.axis_index("dp"), lax.axis_index("seq")
        self.z, self.x, self.y, self.c = self.dp // 2, self.dp % 2, self.seq // 2, self.seq % 2
        self.twin = (self.dp, self.y * 2 + 1 - self.c)
        self.beside_y = (self.dp, (1 - self.y) * 2 + self.c)
        self.across = (self.dp, (1 - self.y) * 2 + 1 - self.c)
        self.beside_x = (self.z * 2 + 1 - self.x, self.seq)
        self.along_z = [(((self.z + j) % 4) * 2 + self.x, self.seq) for j in (1, 2, 3)]
        self.peers = [((self.seq + j) % 4, (self.dp, (self.seq + j) % 4)) for j in (1, 2, 3)]
        self.partners = [self.twin, self.beside_y, self.beside_x] + self.along_z

    def greet(self):
        barrier = pltpu.get_barrier_semaphore()
        for partner in self.partners + [self.across]:
            pl.semaphore_signal(barrier, inc=1, device_id=partner, device_id_type=MESH_ID)
        pl.semaphore_wait(barrier, len(self.partners) + 1)


def add_into(dst, src, lead):
    rows, w = src.shape[-2:]
    band = rows
    while band * w > 65536 and band % 32 == 0:
        band //= 2
    count = 1
    for n in lead:
        count *= n

    def body(t, carry):
        block, part = t // (rows // band), t % (rows // band)
        index = []
        for n in reversed(lead):
            index.insert(0, block % n)
            block = block // n
        at = tuple(index) + (pl.ds(pl.multiple_of(part * band, band), band), slice(None))
        dst[at] = dst[at] + src[at]
        return carry

    lax.fori_loop(0, count * (rows // band), body, 0)


def piece_scratch(w, split):
    ra, rb, rc = split
    r = sum(split)
    out = [((2, 4, 2, r), 1), ((2, 4, 2, r), 1), ((4, 2, ra), ra), ((2, 4, rb), rb), ((3, 2, 2, rc), rc), ((4, ra), ra), ((4, rb), rb), ((2, rc), rc),
           ((3, ra + rb), ra + rb), ((rc,), rc)]
    return [pltpu.VMEM(shape + (w,), BF16) for shape, used in out if used] + [DMA((14,)), DMA((14,)), DMA((2,))]


def piece_count(split):
    return len(piece_scratch(128, split))


class Piece:
    def __init__(self, place, part, done, split, scratch):
        self.p, self.part, self.done, self.split = place, part, done, split
        ra, rb, rc = split
        names = [("a", 1), ("from_twin", 1), ("ya", ra), ("xb", rb), ("zc", rc), ("xa", ra), ("yb", rb), ("xc", rc), ("zab", ra + rb), ("yc", rc)]
        scratch = list(scratch)
        for name, used in names:
            setattr(self, name, scratch.pop(0) if used else None)
        self.ss, self.rs, self.ls = scratch
        self.rows_a, self.rows_b, self.rows_ab, self.rows_c = pl.ds(0, ra), pl.ds(ra, rb), pl.ds(0, ra + rb), pl.ds(ra + rb, rc)

    def copies(self, stage):
        p, a, (ra, rb, rc) = self.p, self.a, self.split
        out = []
        slot = (0, 2, 7, 10)[stage]

        def send(src, dst, to):
            k = slot + len(out)
            out.append(remote_copy(src, dst, self.ss.at[k], self.rs.at[k], to))

        zs = [((p.z + 1 + j) % 4, p.along_z[j]) for j in range(3)]
        if stage == 0:
            for k in (0, 1):
                send(self.part(k, 1 - p.c), self.from_twin.at[k], p.twin)
        if stage == 1:
            if ra:
                send(a.at[1 - p.y, :, :, self.rows_a, :], self.ya, p.beside_y)
            if rb:
                send(a.at[:, :, 1 - p.x, self.rows_b, :], self.xb, p.beside_x)
            for j in range(3 if rc else 0):
                send(a.at[:, zs[j][0], :, self.rows_c, :], self.zc.at[j], zs[j][1])
        if stage == 2:
            if ra:
                send(a.at[p.y, :, 1 - p.x, self.rows_a, :], self.xa, p.beside_x)
            if rb:
                send(a.at[1 - p.y, :, p.x, self.rows_b, :], self.yb, p.beside_y)
            if rc:
                send(a.at[:, p.z, 1 - p.x, self.rows_c, :], self.xc, p.beside_x)
        if stage == 3:
            for j in range(3 if ra + rb else 0):
                send(a.at[p.y, zs[j][0], p.x, self.rows_ab, :], self.zab.at[j], zs[j][1])
            if rc:
                send(a.at[1 - p.y, p.z, p.x, self.rows_c, :], self.yc, p.beside_y)
        return out

    def own(self):
        return [local_copy(self.part(k, self.p.c), self.a.at[k], self.ls.at[k]) for k in (0, 1)]

    def tick(self, t):
        p, a, (ra, rb, rc) = self.p, self.a, self.split
        if t > 0:
            for copy in self.copies(t - 1):
                copy.wait()
        if t == 0:
            for copy in self.copies(0) + self.own():
                copy.start()
        if t == 1:
            for copy in self.own():
                copy.wait()
            add_into(a, self.from_twin, (2, 4, 2))
        if t == 2:
            if ra:
                add_into(a.at[p.y, :, :, self.rows_a, :], self.ya, (4, 2))
            if rb:
                add_into(a.at[:, :, p.x, self.rows_b, :], self.xb, (2, 4))
            for j in range(3 if rc else 0):
                add_into(a.at[:, p.z, :, self.rows_c, :], self.zc.at[j], (2, 2))
        if t == 3:
            if ra:
                add_into(a.at[p.y, :, p.x, self.rows_a, :], self.xa, (4,))
            if rb:
                add_into(a.at[p.y, :, p.x, self.rows_b, :], self.yb, (4,))
            if rc:
                add_into(a.at[:, p.z, p.x, self.rows_c, :], self.xc, (2,))
        if t in (1, 2, 3):
            for copy in self.copies(t):
                copy.start()
        if t == 4:
            mine = a.at[p.y, p.z, p.x]
            parts = []
            if ra + rb:
                total = mine[self.rows_ab, :].astype(F32)
                for j in range(3):
                    total += self.zab[j].astype(F32)
                parts.append(total)
            if rc:
                parts.append(mine[self.rows_c, :].astype(F32) + self.yc[...].astype(F32))
            self.done(jnp.concatenate(parts, 0) if len(parts) > 1 else parts[0])


def ff_kernel(inp_ref, g_ref, gain_ref, shift_ref, bias_ref, wu_ref, wd_ref, *rest, linked):
    hand, rest = (rest[:2], rest[2:]) if linked else ((), rest)
    y_ref, dn_ref, sums_ref, ub_ref = rest[:4]
    outs, rest = (rest[4:11], rest[11:]) if linked else (rest[4:6], rest[6:])
    x_s, xt_s, act_s, dh_s, wu_s, wd_s, gu_s, gd_s, wu_sem, wd_sem, gu_sem, gd_sem = rest[:12]
    rest = rest[12:]
    step = pl.program_id(0)
    last = pl.num_programs(0) - 1
    n, d = x_s.shape
    hidden = bias_ref.shape[1]
    group = hidden // 8
    tile = 512
    slot = step % 2

    def places(at):
        k, j = at // 2, at % 2
        return [(s, (2 * s + j) * group + k * 128) for s in range(4)]

    def weights(at, slot):
        out = []
        for s, f in places(at):
            f = pl.multiple_of(f, 128)
            out.append(local_copy(wu_ref.at[:, pl.ds(f, 128)], wu_s.at[slot, :, pl.ds(s * 128, 128)], wu_sem.at[slot, s]))
            out.append(local_copy(wd_ref.at[pl.ds(f, 128), :], wd_s.at[slot, pl.ds(s * 128, 128), :], wd_sem.at[slot, s]))
        return out

    def results(at):
        out = []
        k, j = at // 2, at % 2
        for s, f in places(at):
            f = pl.multiple_of(f, 128)
            up, down = gu_s.at[:, :, :, pl.ds(s * 128, 128)], gd_s.at[pl.ds(s * 128, 128), :]
            if linked:
                col = pl.multiple_of(s * 256 + j * 128, 128)
                to = outs[0].at[k, :, :, pl.ds(0, 128), pl.ds(col, 128)], outs[0].at[k, s, j, pl.ds(128, 128), :]
            else:
                to = outs[0].at[:, :, :, pl.ds(f, 128)], outs[1].at[pl.ds(f, 128), :]
            out.append(local_copy(up, to[0], gu_sem.at[s]))
            out.append(local_copy(down, to[1], gd_sem.at[s]))
        return out

    if linked:
        place = Place()
        row_send, row_recv, own_sem = rest[:3]
        rest = rest[3:]

        def swaps():
            out = []
            for a in range(2):
                for j, (to, device) in enumerate(place.peers):
                    out.append(remote_copy(hand[a].at[to], outs[1 + a].at[place.seq], row_send.at[a, j], row_recv.at[a, j], device))
                out.append(local_copy(hand[a].at[place.seq], outs[1 + a].at[place.seq], own_sem.at[a]))
            return out

        def part_of(k):
            return lambda y, c: outs[0].at[k, :, :, :, pl.ds(pl.multiple_of((y * 2 + c) * 256, 256), 256)]

        def done_at(k):
            def done(total):
                outs[3 + 2 * k][...] = total[0:128]
                outs[4 + 2 * k][...] = total[128:256]
            return done

        cut = piece_count(FF_SPLITS[0])
        made = [Piece(place, part_of(k), done_at(k), FF_SPLITS[k], (rest[:cut], rest[cut:])[k]) for k in range(2)]

    def tick(position):
        for which, times in enumerate(FF_TICKS if linked else ()):
            for t, at in enumerate(times):
                if min(at // 3, 7) * 3 + position == at:
                    pl.when(step == min(at // 3, 7))(functools.partial(made[which].tick, t))

    @pl.when(step == 0)
    def _():
        for copy in weights(0, 0):
            copy.start()
        if linked:
            place.greet()
            for copy in swaps():
                copy.start()
        sums_ref[...] = jnp.zeros_like(sums_ref)

        @functools.partial(each_band, n // 256)
        def _(rows, m):
            xhat, _ = normalize(inp_ref[rows, :].astype(F32))
            normed = (xhat * gain_ref[...] + shift_ref[...]).astype(BF16)
            x_s[rows, :] = normed
            xt_s[:, rows] = normed.T
            sums_ref[2:3, :] += jnp.sum(g_ref[rows, :].astype(F32), 0, keepdims=True)

    @pl.when(step > 0)
    def _():
        for copy in results(step - 1):
            copy.wait()

    tick(0)

    @pl.when(step < last)
    def _():
        for copy in weights(step + 1, 1 - slot):
            copy.start()
    for copy in weights(step, slot):
        copy.wait()
    w_up, w_down = wu_s.at[slot], wd_s.at[slot]
    bias = jnp.concatenate([bias_ref[:, pl.ds(pl.multiple_of(f, 128), 128)] for _, f in places(step)], 1)
    unit_sums = None
    for m in range(n // tile):
        here = slice(m * tile, (m + 1) * tile)
        v = dot(x_s[here, :], w_up[...]) + bias
        vv = v * v
        a = 0.5 + 0.5 * jnp.tanh(v * (C0 + C1 * vv))
        act = v * a
        slope = a + act * (1.0 - a) * (2 * C0 + 6 * C1 * vv)
        act_s[here, :] = act.astype(BF16)
        dh = (dot_nt(g_ref[here, :], w_down[...]) * slope).astype(BF16)
        dh_s[here, :] = dh
        total = jnp.sum(dh.astype(F32), 0, keepdims=True)
        unit_sums = total if unit_sums is None else unit_sums + total
    for s, f in places(step):
        ub_ref[:, pl.ds(pl.multiple_of(f, 128), 128)] = unit_sums[:, s * 128:(s + 1) * 128]

    tick(1)
    for m in range(d // 256):
        grads = dot(xt_s[m * 256:(m + 1) * 256, :], dh_s[...]).astype(BF16)
        gu_s[m, 0] = grads[0:128]
        gu_s[m, 1] = grads[128:256]
    gd_s[...] = dot_tn(act_s[...], g_ref[...]).astype(BF16)
    for copy in results(step):
        copy.start()
    tick(2)
    for m in range(n // tile):
        here = slice(m * tile, (m + 1) * tile)
        y = dot(act_s[here, :], w_down[...])
        dn = dot_nt(dh_s[here, :], w_up[...])

        @pl.when(step == 0)
        def _():
            y_ref[here, :] = y
            dn_ref[here, :] = dn

        @pl.when(step > 0)
        def _():
            y_ref[here, :] += y
            dn_ref[here, :] += dn

    tick(3)

    @pl.when(step == last)
    def _():
        @functools.partial(each_band, n // 256)
        def _(here, m):
            total = dn_ref[here, :]
            xhat, _ = normalize(inp_ref[here, :].astype(F32))
            sums_ref[0:1, :] += jnp.sum(total * xhat, 0, keepdims=True)
            sums_ref[1:2, :] += jnp.sum(total, 0, keepdims=True)

        for copy in results(step):
            copy.wait()
        if linked:
            for copy in swaps():
                copy.wait()


def feed_forward(inp, g, gain, shift, bias, wu, wd, linked):
    rows, span, d = inp.shape
    n, hidden = rows * span, bias.shape[0]
    sd, vm = jax.ShapeDtypeStruct, pltpu.VMEM
    out_shape = [sd((n, d), F32), sd((n, d), F32), sd((8, d), F32), sd((1, hidden), F32)]
    out_specs = [whole((n, d)), whole((n, d)), whole((8, d)), whole((1, hidden))]
    scratch = [vm((n, d), BF16), vm((d, n), BF16), vm((n, 512), BF16), vm((n, 512), BF16), vm((2, d, 512), BF16), vm((2, 512, d), BF16),
               vm((4, 2, 128, 512), BF16), vm((512, d), BF16), DMA((2, 4)), DMA((2, 4)), DMA((4,)), DMA((4,))]
    more, params = [], {}
    if linked:
        more = [inp, g]
        out_shape += [sd((4, 4, 2, 256, d), BF16), sd(inp.shape, BF16), sd(inp.shape, BF16), *[sd((128, 256), F32)] * 4]
        out_specs += [ANYWHERE] * 3 + [whole((128, 256))] * 4
        scratch += [DMA((2, 3)), DMA((2, 3)), DMA((2,))] + piece_scratch(256, FF_SPLITS[0]) + piece_scratch(256, FF_SPLITS[1])
        params = dict(collective_id=0, has_side_effects=True)
    else:
        out_shape += [sd((4, 2, 128, hidden), BF16), sd((hidden, d), BF16)]
        out_specs += [ANYWHERE] * 2
    return pl.pallas_call(
        functools.partial(ff_kernel, linked=linked), out_shape=out_shape, grid=(hidden // 512,),
        in_specs=[whole((n, d)), whole((n, d)), whole((1, d)), whole((1, d)), whole((1, hidden)), ANYWHERE, ANYWHERE] + [ANYWHERE] * len(more),
        out_specs=out_specs, scratch_shapes=scratch,
        compiler_params=pltpu.CompilerParams(vmem_limit_bytes=58 * 2**20, **params),
        cost_estimate=pl.CostEstimate(flops=52_000_000_000, bytes_accessed=50_000_000, transcendentals=4_000_000),
    )(inp.reshape(n, d), g.reshape(n, d), gain.reshape(1, d), shift.reshape(1, d), bias.reshape(1, hidden), wu, wd, *more)


def turn(x, c, s, sign):
    lanes = x.shape[1]
    lane = lax.broadcasted_iota(jnp.int32, x.shape, 1) % HEAD_DIM
    other = jnp.where(lane < ROT // 2, pltpu.roll(x, lanes - ROT // 2, 1), pltpu.roll(x, ROT // 2, 1))
    return x * c + (sign * other) * s


def tile_place(tile):
    early = [kind * 8 + pair for two in ORDER[:2] for pair in two for kind in range(3)]
    block = tile // 6
    mates = sorted(t for t in range(24) if t // 6 == block and (t in early) == (tile in early))
    return block, mates.index(tile)


def attn_kernel(raw_ref, g_ref, gain_ref, shift_ref, fam_ref, tab_ref, wqkv_ref, wo_ref, *rest, linked):
    hand, rest = (rest[:1], rest[1:]) if linked else ((), rest)
    dn_ref, sums_ref, gqkv_ref, go_ref, heads_ref = rest[:5]
    outs, rest = (rest[5:10], rest[10:]) if linked else ((), rest[5:])
    (x_s, xt_s, c_s, s_s, w_s, wo_s, q_s, k_s, v_s, do_s, kt_s, vt_s, ht_s, dqt_s, dk_s, dv_s, draw_s, dn_s, gq_s, go_s, heads_s,
     famr_s, famc_s, w_sem, wo_sem, gq_sem, go_sem, h_sem) = rest[:28]
    rest = rest[28:]
    step = pl.program_id(0)
    steps = len(ORDER)
    last = steps - 1
    n, d = raw_ref.shape
    lanes = 256
    pairs = d // 128
    slot = step % 2

    def weights(at, slot):
        out = []
        for half in range(2):
            pair = pick(at, [o[half] for o in ORDER])
            for kind in range(3):
                col = pl.multiple_of((kind * pairs + pair) * 128, 128)
                j = kind * 2 + half
                out.append(local_copy(wqkv_ref.at[:, pl.ds(col, 128)], w_s.at[slot, :, pl.ds(j * 128, 128)], w_sem.at[slot, j]))
            row = pl.multiple_of(pair * 128, 128)
            out.append(local_copy(wo_ref.at[pl.ds(row, 128), :], wo_s.at[slot, pl.ds(half * 128, 128), :], wo_sem.at[slot, half]))
        return out

    def results(at):
        out = []
        for half in range(2):
            pair = pick(at, [o[half] for o in ORDER])
            for kind in range(3):
                j = kind * 2 + half
                if linked:
                    col = pick(at, [block * 384 + rank * 128 for block, rank in (tile_place(kind * 8 + o[half]) for o in ORDER)])
                    to = gqkv_ref.at[at // 2, :, :, :, pl.ds(pl.multiple_of(col, 128), 128)]
                else:
                    to = gqkv_ref.at[:, :, :, pl.ds(pl.multiple_of((kind * pairs + pair) * 128, 128), 128)]
                out.append(local_copy(gq_s.at[:, :, :, pl.ds(j * 128, 128)], to, gq_sem.at[j]))
            out.append(local_copy(go_s.at[pl.ds(half * 128, 128), :], go_ref.at[pair // 2, pair % 2], go_sem.at[half]))
        return out

    if linked:
        place = Place()
        head_send, head_recv = rest[:2]
        rest = rest[2:]

        def heads_out(at):
            cols = pl.ds(pl.multiple_of(at * lanes, lanes), lanes)
            span = n // 4
            out = []
            for j, (to, device) in enumerate(place.peers):
                src = heads_s.at[pl.ds(pl.multiple_of(to * span, span), span), :]
                out.append(remote_copy(src, heads_ref.at[place.seq, :, cols], head_send.at[at, j], head_recv.at[at, j], device))
            mine = heads_s.at[pl.ds(pl.multiple_of(place.seq * span, span), span), :]
            return out, local_copy(mine, heads_ref.at[place.seq, :, cols], h_sem.at[0])

        def part_of(source, k, w):
            return lambda y, c: source.at[k, :, :, :, pl.ds(pl.multiple_of((y * 2 + c) * w, 128), w)]

        def done_at(k):
            def done(total):
                if k == 2:
                    outs[4][...] = total
                else:
                    outs[2 * k][...] = total[0:128]
                    outs[2 * k + 1][...] = total[128:256]
            return done

        cut = piece_count(AT_SPLIT)
        made = [Piece(place, part_of(hand[0], 2, 256), done_at(0), AT_SPLIT, rest[:cut]),
                Piece(place, part_of(hand[0], 3, 256), done_at(1), AT_SPLIT, rest[cut:2 * cut]),
                Piece(place, part_of(gqkv_ref, 0, 384), done_at(2), EARLY_SPLIT, rest[2 * cut:])]
        plan = {}
        for which, times in enumerate(AT_TICKS):
            for t, at in enumerate(times):
                plan.setdefault(at, []).append((which, t))
    else:
        plan = {}

    def tick(position):
        for at, what in sorted(plan.items()):
            if min(at // 6, last) * 6 + position == at:
                def run(what=what):
                    for which, t in sorted(what, key=lambda w: (-w[1], w[0])):
                        made[which].tick(t)
                pl.when(step == min(at // 6, last))(run)

    @pl.when(step == 0)
    def _():
        for copy in weights(0, 0):
            copy.start()
        if linked:
            place.greet()

    @pl.when(step > 0)
    def _():
        for copy in results(step - 1):
            copy.wait()

    tick(0)

    @pl.when(step == 0)
    def _():
        family = fam_ref[pl.ds(lax.axis_index("seq"), 1), :].astype(F32)
        famr_s[...] = family
        for m in range(n // 128):
            rows = slice(m * 128, m * 128 + 128)
            famc_s[rows, :] = jnp.broadcast_to(family[:, rows], (128, 128)).T
        for a in range(n // 32):
            rows = slice(a * 32, a * 32 + 32)
            ca, sa = tab_ref[0, a:a + 1, :], tab_ref[1, a:a + 1, :]
            cb, sb = tab_ref[2], tab_ref[3]
            c1 = ca * cb - sa * sb
            s1 = sa * cb + ca * sb
            lane = lax.broadcasted_iota(jnp.int32, c1.shape, 1) % HEAD_DIM
            c_s[rows, :] = jnp.where(lane < ROT, c1, 1.0)
            s_s[rows, :] = jnp.where(lane < ROT // 2, -s1, jnp.where(lane < ROT, s1, 0.0))
        @functools.partial(each_band, n // 256)
        def _(rows, m):
            xhat, _ = normalize(raw_ref[rows, :].astype(F32))
            normed = (xhat * gain_ref[...] + shift_ref[...]).astype(BF16)
            x_s[rows, :] = normed
            xt_s[:, rows] = normed.T

    @pl.when(step < last)
    def _():
        for copy in weights(step + 1, 1 - slot):
            copy.start()
    for copy in weights(step, slot):
        copy.wait()

    w_ref, wo1_ref = w_s.at[slot], wo_s.at[slot]
    scaling = HEAD_DIM ** -0.5

    def both(rows):
        c, s = c_s[rows, :], s_s[rows, :]
        return jnp.concatenate([c, c], 1), jnp.concatenate([s, s], 1)

    for m in range(n // 256):
        rows = slice(m * 256, m * 256 + 256)
        raw = dot(x_s[rows, :], w_ref[...])
        c, s = both(rows)
        q_s[rows, :] = (turn(raw[:, 0:lanes], c, s, 1.0) * scaling).astype(BF16)
        keys = turn(raw[:, lanes:2 * lanes], c, s, 1.0).astype(BF16)
        k_s[rows, :] = keys
        kt_s[:, rows] = keys.T
        vals = raw[:, 2 * lanes:].astype(BF16)
        v_s[rows, :] = vals
        vt_s[:, rows] = vals.T
        do_s[rows, :] = dot_nt(g_ref[rows, :], wo1_ref[...]).astype(BF16)

    tick(1)
    tile = TILE
    lane = lax.broadcasted_iota(jnp.int32, (tile, 128), 1)
    work = [(h, i) for i in reversed(range(n // tile)) for h in range(4)]

    def first(h, i):
        span = (i + 1) * tile
        here = slice(i * tile, span)
        cols = slice(h // 2 * 128, h // 2 * 128 + 128)
        mine = (lane < HEAD_DIM) if h % 2 == 0 else (lane >= HEAD_DIM)
        qh = jnp.where(mine, q_s[here, cols], 0).astype(BF16)
        doh = jnp.where(mine, do_s[here, cols], 0).astype(BF16)
        return qh, doh, dot_nt(k_s[0:span, cols], qh), dot_nt(v_s[0:span, cols], doh)

    def second(h, i, qh, doh, st, dpt):
        span = (i + 1) * tile
        here = slice(i * tile, span)
        cols = slice(h // 2 * 128, h // 2 * 128 + 128)
        rows = slice(h * HEAD_DIM, (h + 1) * HEAD_DIM)
        family = famc_s[0:span, :]
        allowed = jnp.concatenate([family] * (tile // 128), 1) == famr_s[:, here]
        key_place = lax.broadcasted_iota(jnp.int32, (span, tile), 0)
        query_place = lax.broadcasted_iota(jnp.int32, (span, tile), 1) + i * tile
        st = jnp.where(allowed & (key_place <= query_place), st, -1e9)
        e = jnp.exp(st - jnp.max(st, 0, keepdims=True))
        p = e * (1.0 / jnp.sum(e, 0, keepdims=True))
        pb = p.astype(BF16)
        ds = (p * (dpt - jnp.sum(p * dpt, 0, keepdims=True))).astype(BF16)
        ht_s[rows, here] = dot(vt_s[rows, 0:span], pb).astype(BF16)
        dqt_s[rows, here] = dot(kt_s[rows, 0:span], ds) * scaling
        dv = dot(pb, doh)
        dk = dot(ds, qh)
        if h % 2 == 0 and i == n // tile - 1:
            dv_s[:, cols] = dv
            dk_s[:, cols] = dk
        else:
            dv_s[0:span, cols] += dv
            dk_s[0:span, cols] += dk

    made_first = first(*work[0])
    for j, (h, i) in enumerate(work):
        later = first(*work[j + 1]) if j + 1 < len(work) else None
        second(h, i, *made_first)
        made_first = later
        if h == 3 and i != 1:
            tick({3: 2, 2: 3, 0: 4}[i])

    @pl.when(step > 0)
    def _():
        if linked:
            sent, mine = heads_out(step - 1)
            for copy in sent:
                copy.wait_send()
            mine.wait()
        else:
            local_copy(heads_s, heads_ref.at[:, pl.ds(pl.multiple_of((step - 1) * lanes, lanes), lanes)], h_sem.at[0]).wait()
    heads_s[...] = ht_s[...].T
    if linked:
        sent, mine = heads_out(step)
        for copy in sent:
            copy.start()
        mine.start()
    else:
        local_copy(heads_s, heads_ref.at[:, pl.ds(pl.multiple_of(step * lanes, lanes), lanes)], h_sem.at[0]).start()

    @functools.partial(each_band, n // 256)
    def _(rows, m):
        c, s = both(rows)
        draw_s[rows, 0:lanes] = turn(dqt_s[:, rows].T, c, s, -1.0).astype(BF16)
        draw_s[rows, lanes:2 * lanes] = turn(dk_s[rows, :], c, s, -1.0).astype(BF16)
        draw_s[rows, 2 * lanes:] = dv_s[rows, :].astype(BF16)

    for m in range(d // 256):
        grads = dot(xt_s[m * 256:(m + 1) * 256, :], draw_s[...]).astype(BF16)
        gq_s[m, 0] = grads[0:128]
        gq_s[m, 1] = grads[128:256]
    go_s[...] = dot(ht_s[...], g_ref[...]).astype(BF16)
    for copy in results(step):
        copy.start()
    tick(5)
    for m in range(n // 256):
        here = slice(m * 256, (m + 1) * 256)
        dn = dot_nt(draw_s[here, :], w_ref[...])

        @pl.when(step == 0)
        def _():
            dn_s[here, :] = dn

        @pl.when(step > 0)
        def _():
            dn_s[here, :] += dn

    @pl.when(step == last)
    def _():
        sums_ref[...] = jnp.zeros_like(sums_ref)

        @functools.partial(each_band, n // 256)
        def _(here, m):
            total = dn_s[here, :]
            xhat, _ = normalize(raw_ref[here, :].astype(F32))
            sums_ref[0:1, :] += jnp.sum(total * xhat, 0, keepdims=True)
            sums_ref[1:2, :] += jnp.sum(total, 0, keepdims=True)
            dn_ref[here, :] = total.astype(BF16)

    tick(6)

    @pl.when(step == last)
    def _():
        for copy in results(step):
            copy.wait()
        if linked:
            for at in range(steps):
                for copy in heads_out(at)[0]:
                    copy.wait_recv()
            for copy in heads_out(step)[0]:
                copy.wait_send()
            heads_out(step)[1].wait()
        else:
            local_copy(heads_s, heads_ref.at[:, pl.ds(pl.multiple_of(step * lanes, lanes), lanes)], h_sem.at[0]).wait()


def attend(raw, g, gain, shift, wqkv, wo, families, linked, grads=None):
    n, d = raw.shape
    pair_lane = np.arange(128) % HEAD_DIM % (ROT // 2)
    freq = 10000.0 ** (-2.0 * pair_lane / ROT)
    high, low = np.arange(n // 32)[:, None] * 32.0 * freq, np.arange(32)[:, None] * freq
    tab = jnp.asarray(np.stack([np.cos(high), np.sin(high), np.cos(low), np.sin(low)]), F32)
    sd, vm = jax.ShapeDtypeStruct, pltpu.VMEM
    out_shape = [sd((n, d), BF16), sd((8, d), F32), sd((2, 4, 2, 128, 3 * d // 2) if linked else (4, 2, 128, 3 * d), BF16),
                 sd((4, 2, 128, d), BF16), sd((4, n // 4, d) if linked else (n, d), BF16)]
    out_specs = [whole((n, d)), whole((8, d))] + [ANYWHERE] * 3
    scratch = [vm((n, d), BF16), vm((d, n), BF16), vm((n, 128), F32), vm((n, 128), F32), vm((2, d, 768), BF16), vm((2, 256, d), BF16)]
    scratch += [vm((n, 256), BF16)] * 4 + [vm((256, n), BF16)] * 3
    scratch += [vm((256, n), F32), vm((n, 256), F32), vm((n, 256), F32), vm((n, 768), BF16), vm((n, d), F32), vm((4, 2, 128, 768), BF16),
                vm((256, d), BF16), vm((n, 256), BF16), vm((1, n), F32), vm((n, 128), F32), DMA((2, 6)), DMA((2, 2)), DMA((6,)), DMA((2,)), DMA((1,))]
    params, more = {}, []
    if linked:
        more = [grads]
        out_shape += [sd((128, 256), F32)] * 4 + [sd((128, 384), F32)]
        out_specs += [whole((128, 256))] * 4 + [whole((128, 384))]
        scratch += [DMA((4, 3)), DMA((4, 3))]
        scratch += piece_scratch(256, AT_SPLIT) * 2 + piece_scratch(384, EARLY_SPLIT)
        params = dict(collective_id=1, has_side_effects=True)
    return pl.pallas_call(
        functools.partial(attn_kernel, linked=linked), out_shape=out_shape, grid=(len(ORDER),),
        in_specs=[whole((n, d)), whole((n, d)), whole((1, d)), whole((1, d)), whole(families.shape), whole((4, 32, 128)), ANYWHERE, ANYWHERE]
        + [ANYWHERE] * len(more),
        out_specs=out_specs, scratch_shapes=scratch,
        compiler_params=pltpu.CompilerParams(vmem_limit_bytes=60 * 2**20, **params),
        cost_estimate=pl.CostEstimate(flops=70_000_000_000, bytes_accessed=30_000_000, transcendentals=20_000_000),
    )(raw, g, gain.reshape(1, d), shift.reshape(1, d), families, tab, wqkv, wo, *more)


class SmallSum:
    def __init__(self, place, held, heard, by_z, send, recv):
        self.p, self.held, self.heard, self.by_z, self.send, self.recv = place, held, heard, by_z, send, recv

    def copies(self, t):
        p = self.p
        if t < 3:
            to = (p.twin, p.beside_y, p.beside_x)[t]
            return [remote_copy(self.held, self.heard.at[t], self.send.at[t], self.recv.at[t], to)]
        return [remote_copy(self.by_z.at[p.z], self.by_z.at[p.z], self.send.at[3 + j], self.recv.at[3 + j], to)
                for j, to in enumerate(p.along_z)]

    def tick(self, t):
        if t > 0:
            for copy in self.copies(t - 1):
                copy.wait()
        if 0 < t < 4:
            total = self.held[...] + self.heard[t - 1]
            if t < 3:
                self.held[...] = total
            else:
                self.by_z[self.p.z] = total
        if t < 4:
            for copy in self.copies(t):
                copy.start()
        return None if t < 4 else self.by_z[0] + self.by_z[1] + self.by_z[2] + self.by_z[3]


def tail_kernel(dat_ref, heads_ref, gq_ref, go_ref, inp_ref, g_ref, y_ref, dn_ref, wo_ref, gain_ref, dbias_ref, sums_ff_ref, sums_at_ref,
                ub_ref, early_ref, lo_ref, ig_ref, qkv_ref, out_ref, gain_o, shift_o, ub_o, db_o,
                back_s, inp_s, g_s, heads_s, y_s, dn_s, wo_s, lo_s, ig_s, small_s, heard_s, by_z_s,
                load_sem, wo_sem, back_send, back_recv, own_sem, small_send, small_recv, lo_sem, ig_sem, *pieces):
    place = Place()
    d = wo_s.shape[0]
    place.greet()
    swaps = [remote_copy(dat_ref.at[to], back_s.at[place.seq], back_send.at[j], back_recv.at[j], device)
             for j, (to, device) in enumerate(place.peers)]
    own = local_copy(dat_ref.at[place.seq], back_s.at[place.seq], own_sem.at[0])
    blocks = {}

    def part(source, w, row0, rows):
        return lambda y, c: source.at[:, :, pl.ds(row0, rows), pl.ds(pl.multiple_of((y * 2 + c) * w, 128), w)]

    def out_done(total):
        out_ref[...] = total

    def qkv_done(row0):
        def done(total):
            rows = slice(row0, row0 + total.shape[0])
            early = early_ref[rows, :]
            first = jnp.where(place.c == 0, early, total)
            second = jnp.where(place.c == 0, total, early)
            order = ((first, 0), (second, 0), (second, 1), (first, 1), (first, 2), (second, 2))
            for k, (source, at) in enumerate(order):
                qkv_ref[rows, k * 128:(k + 1) * 128] = source[:, at * 128:(at + 1) * 128]
        return done

    cuts = [0, piece_count(TAIL_SPLITS[0])]
    for split in TAIL_SPLITS[1:]:
        cuts.append(cuts[-1] + piece_count(split))
    late = gq_ref.at[1]
    row1 = sum(TAIL_SPLITS[1])
    made = [Piece(place, part(go_ref, 256, 0, 128), out_done, TAIL_SPLITS[0], pieces[:cuts[1]]),
            Piece(place, part(late, 384, 0, row1), qkv_done(0), TAIL_SPLITS[1], pieces[cuts[1]:cuts[2]]),
            Piece(place, part(late, 384, row1, 128 - row1), qkv_done(row1), TAIL_SPLITS[2], pieces[cuts[2]:])]
    small = SmallSum(place, small_s, heard_s, by_z_s, small_send, small_recv)
    small_s[0:3, :] = sums_ff_ref[0:3, :]
    small_s[0:2, :] += sums_at_ref[0:2, :]
    small_s[3:4, :] = jnp.zeros((1, d), F32)
    for k in range(4):
        small_s[4 + k:5 + k, :] = ub_ref[:, k * d:(k + 1) * d]
    for piece in made:
        piece.tick(0)
    for copy in swaps:
        copy.start()
    small.tick(0)
    loads = [local_copy(a, b, load_sem.at[k]) for k, (a, b) in enumerate(
        ((heads_ref, heads_s), (inp_ref, inp_s), (y_ref, y_s), (g_ref, g_s), (dn_ref, dn_s)))]
    for pair in range(d // 128):
        at = [p for two in ORDER for p in two].index(pair)
        blocks[at] = local_copy(wo_ref.at[pl.ds(pair * 128, 128), :], wo_s.at[pl.ds(at * 128, 128), :], wo_sem.at[at])
    for copy in [loads[0]] + list(blocks.values()) + loads[1:] + [own]:
        copy.start()

    def lo_out(r):
        return local_copy(lo_s.at[r], lo_ref.at[r], lo_sem.at[r])

    def ig_out(r):
        return local_copy(ig_s.at[r], ig_ref.at[r], ig_sem.at[r])

    def forward(r):
        total = inp_s[r].astype(F32) + dot(heads_s[r], wo_s[...]) + (y_s[r] + dbias_ref[...])
        lo_s[r] = total.astype(BF16)
        lo_out(r).start()

    def backward(r):
        xhat, scale = normalize(inp_s[r].astype(F32))
        dx = (dn_s[r] + back_s[r].astype(F32)) * gain_ref[...]
        ig_s[r] = g_s[r].astype(F32) + (dx - jnp.mean(dx, -1, keepdims=True) - xhat * jnp.mean(dx * xhat, -1, keepdims=True)) * scale
        ig_out(r).start()

    made[0].tick(1)
    small.tick(1)
    for copy in list(blocks.values()) + loads[:3]:
        copy.wait()
    forward(0)
    forward(1)
    made[1].tick(1)
    forward(2)
    forward(3)
    made[0].tick(2)
    made[2].tick(1)
    small.tick(2)
    loads[3].wait()
    loads[4].wait()
    own.wait()
    backward(place.seq)
    made[1].tick(2)
    made[0].tick(3)
    small.tick(3)
    for j in range(3):
        swaps[j].wait_send()
    swaps[2].wait_recv()
    backward((place.seq + 1) % 4)
    made[2].tick(2)
    made[1].tick(3)
    swaps[1].wait_recv()
    backward((place.seq + 2) % 4)
    made[2].tick(3)
    swaps[0].wait_recv()
    backward((place.seq + 3) % 4)
    total = small.tick(4)
    for piece in made:
        piece.tick(4)
    gain_o[...] = total[0:1]
    shift_o[...] = total[1:2]
    db_o[...] = total[2:3]
    for k in range(4):
        ub_o[:, k * d:(k + 1) * d] = total[4 + k:5 + k]
    for r in range(4):
        lo_out(r).wait()
        ig_out(r).wait()


def finish(dat, heads, gq, go, inp, g, y, dn, wo, gain, dbias, sums_ff, sums_at, ub, early):
    sd, vm = jax.ShapeDtypeStruct, pltpu.VMEM
    shape, d = inp.shape, inp.shape[2]
    vmem = pl.BlockSpec(memory_space=pltpu.VMEM)
    return pl.pallas_call(
        tail_kernel,
        out_shape=[sd(shape, BF16), sd(shape, F32), sd((128, 768), F32), sd((128, 256), F32), sd((1, d), F32), sd((1, d), F32), sd((1, 4 * d), F32),
                   sd((1, d), F32)],
        in_specs=[ANYWHERE] * 9 + [vmem] * 6, out_specs=[ANYWHERE] * 2 + [vmem] * 6,
        scratch_shapes=[vm(shape, BF16)] * 4 + [vm(shape, F32)] * 2 + [vm((d, d), BF16), vm(shape, BF16), vm(shape, F32),
                        vm((8, d), F32), vm((3, 8, d), F32), vm((4, 8, d), F32),
                        DMA((5,)), DMA((8,)), DMA((3,)), DMA((3,)), DMA((1,)), DMA((6,)), DMA((6,)), DMA((4,)), DMA((4,))]
        + piece_scratch(256, TAIL_SPLITS[0]) + piece_scratch(384, TAIL_SPLITS[1]) + piece_scratch(384, TAIL_SPLITS[2]),
        compiler_params=pltpu.CompilerParams(collective_id=2, has_side_effects=True, vmem_limit_bytes=56 * 2**20),
    )(dat.reshape(shape), heads, gq, go, inp, g, y.reshape(shape), dn.reshape(shape), wo, gain.reshape(1, d), dbias.reshape(1, d), sums_ff, sums_at,
      ub, early)


def on_device(inputs, norm_gain, norm_shift, qkv_weight, out_weight, up_weight, up_bias, down_weight, down_bias, partners, families, cotangent, linked):
    row_count, place_count, width = inputs.shape
    tokens = row_count * place_count
    local_rows = partners - lax.axis_index("dp") * row_count
    grad = jnp.take(cotangent, local_rows, axis=0, mode="clip")
    branch_args = norm_gain, norm_shift, qkv_weight, out_weight, families, linked
    if linked:
        y, dn, sums_ff, ub, grads, row_inputs, row_grad, up0, down0, up1, down1 = feed_forward(inputs, grad, norm_gain, norm_shift, up_bias, up_weight, down_weight, True)
        dat, sums_at, gq, go, heads, up2, down2, up3, down3, early = attend(
            row_inputs.reshape(tokens, width), row_grad.reshape(tokens, width), *branch_args, grads)
        layer_out, input_grad, qkv_sum, out_sum, gain_sum, shift_sum, ub_sum, db_sum = finish(
            dat, heads, gq, go, inputs, grad, y, dn, out_weight, norm_gain, down_bias, sums_ff, sums_at, ub, early)
        ups = (up0, up1, up2, up3)
        up_sum = jnp.concatenate([u[:, :128] for u in ups] + [u[:, 128:] for u in ups], 1)
        down_sum = jnp.concatenate([down0, down1, down2, down3], 0)
        return (layer_out, input_grad, gain_sum.reshape(width), shift_sum.reshape(width), qkv_sum, out_sum, up_sum, ub_sum.reshape(-1), down_sum,
                db_sum.reshape(width))
    swap = functools.partial(lax.all_to_all, axis_name="seq", split_axis=0, concat_axis=0, tiled=True)
    row_inputs, row_grad = swap(inputs).reshape(tokens, width), swap(grad).reshape(tokens, width)
    y, dn, sums_ff, ub, up_grad, down_grad = feed_forward(inputs, grad, norm_gain, norm_shift, up_bias, up_weight, down_weight, False)
    dat, sums_at, qkv_grad, out_grad, heads = attend(row_inputs, row_grad, *branch_args)

    def scatter(parts, columns):
        part = lax.psum_scatter(parts.reshape(-1, columns), "seq", scatter_dimension=1, tiled=True)
        return lax.psum_scatter(part, "dp", scatter_dimension=0, tiled=True).astype(F32)

    qkv_sum, out_sum = scatter(qkv_grad, 3 * width), scatter(out_grad, width)
    up_sum, down_sum = scatter(up_grad, up_bias.shape[0]), scatter(down_grad, width)
    heads = swap(heads.reshape(inputs.shape)).reshape(tokens, width)
    order = np.array([p for two in ORDER for p in two])
    attn_out = dot(heads, out_weight.reshape(-1, 128, width)[order].reshape(width, width))
    values = inputs.astype(F32).reshape(tokens, width)
    layer_out = (values + attn_out + (y + down_bias)).astype(BF16).reshape(inputs.shape)
    xhat, scale = normalize(values)
    dx = (dn + swap(dat.reshape(inputs.shape)).reshape(tokens, width).astype(F32)) * norm_gain
    input_grad = grad.reshape(tokens, width).astype(F32) + (dx - jnp.mean(dx, -1, keepdims=True) - xhat * jnp.mean(dx * xhat, -1, keepdims=True)) * scale
    gain_sum, shift_sum, up_bias_sum, down_bias_sum = lax.psum((sums_ff[0] + sums_at[0], sums_ff[1] + sums_at[1], ub[0], sums_ff[2]), ("dp", "seq"))
    return (layer_out, input_grad.reshape(inputs.shape), gain_sum, shift_sum, qkv_sum, out_sum, up_sum, up_bias_sum, down_sum, down_bias_sum)


def solution(mesh):
    rows = P("dp", "seq", None)
    placed = (rows,) + (P(),) * 8 + (P("dp"), P("dp", None), rows)
    grads = P("dp", "seq")
    linked = (mesh.shape["dp"], mesh.shape["seq"]) == (8, 4)
    return jax.shard_map(functools.partial(on_device, linked=linked), mesh=mesh, in_specs=placed,
                         out_specs=(rows, rows, P(), P(), grads, grads, grads, P(), grads, P()), check_vma=False)
```

```python
import functools

import jax
import jax.numpy as jnp
import numpy as np
from jax import lax
from jax.experimental import pallas as pl
from jax.experimental.pallas import tpu as pltpu
from jax.sharding import PartitionSpec as P

F32 = jnp.float32
BF16 = jnp.bfloat16
HEAD_DIM = 64
ROT = 32
EPS = 1e-05
C0 = 0.7978845608028654
C1 = C0 * 0.044715
TILE = 256
FF_SPLITS = (0, 176, 80), (96, 112, 48)
AT_SPLIT = 96, 112, 48
EARLY_SPLIT = 48, 64, 16
TAIL_SPLITS = (0, 80, 48), (0, 48, 16), (0, 32, 32)
FF_TICKS = (6, 9, 15, 18, 22), (12, 15, 20, 22, 24)
AT_TICKS = (0, 2, 7, 10, 14), (4, 7, 12, 15, 19), (13, 15, 19, 21, 24)
ORDER = ((0, 3), (4, 7), (1, 2), (5, 6))
MESH_ID = pl.DeviceIdType.MESH
ANYWHERE = pl.BlockSpec(memory_space=pl.ANY)
DMA = pltpu.SemaphoreType.DMA


def dot(a, b):
    return lax.dot_general(a, b, (((1,), (0,)), ((), ())), preferred_element_type=F32)


def dot_nt(a, b):
    return lax.dot_general(a, b, (((1,), (1,)), ((), ())), preferred_element_type=F32)


def dot_tn(a, b):
    return lax.dot_general(a, b, (((0,), (0,)), ((), ())), preferred_element_type=F32)


def whole(shape):
    return pl.BlockSpec(shape, lambda p: (0,) * len(shape), pipeline_mode=pl.Buffered(1))


def pick(step, values):
    out = jnp.int32(values[0])
    for i, value in enumerate(values[1:], 1):
        out = jnp.where(step == i, value, out)
    return out


def normalize(values):
    centered = values - jnp.mean(values, -1, keepdims=True)
    scale = lax.rsqrt(jnp.mean(centered * centered, -1, keepdims=True) + EPS)
    return centered * scale, scale


def each_band(count, body):
    def step(m, carry):
        body(pl.ds(pl.multiple_of(m * 256, 256), 256), m)
        return carry

    lax.fori_loop(0, count, step, 0)


def local_copy(src, dst, sem):
    return pltpu.make_async_copy(src, dst, sem)


def remote_copy(src, dst, send, recv, to):
    return pltpu.make_async_remote_copy(src_ref=src, dst_ref=dst, send_sem=send, recv_sem=recv, device_id=to,
                                        device_id_type=MESH_ID)


class Place:
    def __init__(self):
        self.dp, self.seq = lax.axis_index("dp"), lax.axis_index("seq")
        self.z, self.x, self.y, self.c = self.dp // 2, self.dp % 2, self.seq // 2, self.seq % 2
        self.twin = (self.dp, self.y * 2 + 1 - self.c)
        self.beside_y = (self.dp, (1 - self.y) * 2 + self.c)
        self.across = (self.dp, (1 - self.y) * 2 + 1 - self.c)
        self.beside_x = (self.z * 2 + 1 - self.x, self.seq)
        self.along_z = [(((self.z + j) % 4) * 2 + self.x, self.seq) for j in (1, 2, 3)]
        self.peers = [((self.seq + j) % 4, (self.dp, (self.seq + j) % 4)) for j in (1, 2, 3)]
        self.partners = [self.twin, self.beside_y, self.beside_x] + self.along_z

    def greet(self):
        barrier = pltpu.get_barrier_semaphore()
        for partner in self.partners + [self.across]:
            pl.semaphore_signal(barrier, inc=1, device_id=partner, device_id_type=MESH_ID)
        pl.semaphore_wait(barrier, len(self.partners) + 1)


def add_into(dst, src, lead):
    rows, w = src.shape[-2:]
    band = rows
    while band * w > 65536 and band % 32 == 0:
        band //= 2
    count = 1
    for n in lead:
        count *= n

    def body(t, carry):
        block, part = t // (rows // band), t % (rows // band)
        index = []
        for n in reversed(lead):
            index.insert(0, block % n)
            block = block // n
        at = tuple(index) + (pl.ds(pl.multiple_of(part * band, band), band), slice(None))
        dst[at] = dst[at] + src[at]
        return carry

    lax.fori_loop(0, count * (rows // band), body, 0)


def piece_scratch(w, split):
    ra, rb, rc = split
    r = sum(split)
    out = [((2, 4, 2, r), 1), ((2, 4, 2, r), 1), ((4, 2, ra), ra), ((2, 4, rb), rb), ((3, 2, 2, rc), rc), ((4, ra), ra), ((4, rb), rb), ((2, rc), rc),
           ((3, ra + rb), ra + rb), ((rc,), rc)]
    return [pltpu.VMEM(shape + (w,), BF16) for shape, used in out if used] + [DMA((14,)), DMA((14,)), DMA((2,))]


def piece_count(split):
    return len(piece_scratch(128, split))


class Piece:
    def __init__(self, place, part, done, split, scratch):
        self.p, self.part, self.done, self.split = place, part, done, split
        ra, rb, rc = split
        names = [("a", 1), ("from_twin", 1), ("ya", ra), ("xb", rb), ("zc", rc), ("xa", ra), ("yb", rb), ("xc", rc), ("zab", ra + rb), ("yc", rc)]
        scratch = list(scratch)
        for name, used in names:
            setattr(self, name, scratch.pop(0) if used else None)
        self.ss, self.rs, self.ls = scratch
        self.rows_a, self.rows_b, self.rows_ab, self.rows_c = pl.ds(0, ra), pl.ds(ra, rb), pl.ds(0, ra + rb), pl.ds(ra + rb, rc)

    def copies(self, stage):
        p, a, (ra, rb, rc) = self.p, self.a, self.split
        out = []
        slot = (0, 2, 7, 10)[stage]

        def send(src, dst, to):
            k = slot + len(out)
            out.append(remote_copy(src, dst, self.ss.at[k], self.rs.at[k], to))

        zs = [((p.z + 1 + j) % 4, p.along_z[j]) for j in range(3)]
        if stage == 0:
            for k in (0, 1):
                send(self.part(k, 1 - p.c), self.from_twin.at[k], p.twin)
        if stage == 1:
            if ra:
                send(a.at[1 - p.y, :, :, self.rows_a, :], self.ya, p.beside_y)
            if rb:
                send(a.at[:, :, 1 - p.x, self.rows_b, :], self.xb, p.beside_x)
            for j in range(3 if rc else 0):
                send(a.at[:, zs[j][0], :, self.rows_c, :], self.zc.at[j], zs[j][1])
        if stage == 2:
            if ra:
                send(a.at[p.y, :, 1 - p.x, self.rows_a, :], self.xa, p.beside_x)
            if rb:
                send(a.at[1 - p.y, :, p.x, self.rows_b, :], self.yb, p.beside_y)
            if rc:
                send(a.at[:, p.z, 1 - p.x, self.rows_c, :], self.xc, p.beside_x)
        if stage == 3:
            for j in range(3 if ra + rb else 0):
                send(a.at[p.y, zs[j][0], p.x, self.rows_ab, :], self.zab.at[j], zs[j][1])
            if rc:
                send(a.at[1 - p.y, p.z, p.x, self.rows_c, :], self.yc, p.beside_y)
        return out

    def own(self):
        return [local_copy(self.part(k, self.p.c), self.a.at[k], self.ls.at[k]) for k in (0, 1)]

    def tick(self, t):
        p, a, (ra, rb, rc) = self.p, self.a, self.split
        if t > 0:
            for copy in self.copies(t - 1):
                copy.wait()
        if t == 0:
            for copy in self.copies(0) + self.own():
                copy.start()
        if t == 1:
            for copy in self.own():
                copy.wait()
            add_into(a, self.from_twin, (2, 4, 2))
        if t == 2:
            if ra:
                add_into(a.at[p.y, :, :, self.rows_a, :], self.ya, (4, 2))
            if rb:
                add_into(a.at[:, :, p.x, self.rows_b, :], self.xb, (2, 4))
            for j in range(3 if rc else 0):
                add_into(a.at[:, p.z, :, self.rows_c, :], self.zc.at[j], (2, 2))
        if t == 3:
            if ra:
                add_into(a.at[p.y, :, p.x, self.rows_a, :], self.xa, (4,))
            if rb:
                add_into(a.at[p.y, :, p.x, self.rows_b, :], self.yb, (4,))
            if rc:
                add_into(a.at[:, p.z, p.x, self.rows_c, :], self.xc, (2,))
        if t in (1, 2, 3):
            for copy in self.copies(t):
                copy.start()
        if t == 4:
            mine = a.at[p.y, p.z, p.x]
            parts = []
            if ra + rb:
                total = mine[self.rows_ab, :].astype(F32)
                for j in range(3):
                    total += self.zab[j].astype(F32)
                parts.append(total)
            if rc:
                parts.append(mine[self.rows_c, :].astype(F32) + self.yc[...].astype(F32))
            self.done(jnp.concatenate(parts, 0) if len(parts) > 1 else parts[0])


def ff_kernel(part_ref, inp_ref, cot_ref, gain_ref, shift_ref, bias_ref, wu_ref, wd_ref, *rest, linked):
    hand, rest = (rest[:1], rest[1:]) if linked else ((), rest)
    y_ref, dn_ref, sums_ref, ub_ref = rest[:4]
    outs, rest = (rest[4:11], rest[11:]) if linked else (rest[4:6], rest[6:])
    x_s, xt_s, act_s, dh_s, wu_s, wd_s, gu_s, gd_s, g_ref, wu_sem, wd_sem, gu_sem, gd_sem = rest[:13]
    rest = rest[13:]
    step = pl.program_id(0)
    last = pl.num_programs(0) - 1
    n, d = x_s.shape
    hidden = bias_ref.shape[1]
    group = hidden // 8
    tile = 512
    slot = step % 2

    def places(at):
        k, j = at // 2, at % 2
        return [(s, (2 * s + j) * group + k * 128) for s in range(4)]

    def weights(at, slot):
        out = []
        for s, f in places(at):
            f = pl.multiple_of(f, 128)
            out.append(local_copy(wu_ref.at[:, pl.ds(f, 128)], wu_s.at[slot, :, pl.ds(s * 128, 128)], wu_sem.at[slot, s]))
            out.append(local_copy(wd_ref.at[pl.ds(f, 128), :], wd_s.at[slot, pl.ds(s * 128, 128), :], wd_sem.at[slot, s]))
        return out

    def results(at):
        out = []
        k, j = at // 2, at % 2
        for s, f in places(at):
            f = pl.multiple_of(f, 128)
            up, down = gu_s.at[:, :, :, pl.ds(s * 128, 128)], gd_s.at[pl.ds(s * 128, 128), :]
            if linked:
                col = pl.multiple_of(s * 256 + j * 128, 128)
                to = outs[0].at[k, :, :, pl.ds(0, 128), pl.ds(col, 128)], outs[0].at[k, s, j, pl.ds(128, 128), :]
            else:
                to = outs[0].at[:, :, :, pl.ds(f, 128)], outs[1].at[pl.ds(f, 128), :]
            out.append(local_copy(up, to[0], gu_sem.at[s]))
            out.append(local_copy(down, to[1], gd_sem.at[s]))
        return out

    if linked:
        place = Place()
        row_send, row_recv, own_sem = rest[:3]
        rest = rest[3:]

        def swaps(a):
            span = n // 4

            def row(at):
                return g_ref.at[pl.ds(pl.multiple_of(at * span, span), span), :] if a else hand[0].at[at]

            out = [remote_copy(row(to), outs[1 + a].at[place.seq], row_send.at[a, j], row_recv.at[a, j], device)
                   for j, (to, device) in enumerate(place.peers)]
            return out + [local_copy(row(place.seq), outs[1 + a].at[place.seq], own_sem.at[a])]

        def part_of(k):
            return lambda y, c: outs[0].at[k, :, :, :, pl.ds(pl.multiple_of((y * 2 + c) * 256, 256), 256)]

        def done_at(k):
            def done(total):
                outs[3 + 2 * k][...] = total[0:128]
                outs[4 + 2 * k][...] = total[128:256]
            return done

        cut = piece_count(FF_SPLITS[0])
        made = [Piece(place, part_of(k), done_at(k), FF_SPLITS[k], (rest[:cut], rest[cut:])[k]) for k in range(2)]

    def tick(position):
        for which, times in enumerate(FF_TICKS if linked else ()):
            for t, at in enumerate(times):
                if min(at // 3, 7) * 3 + position == at:
                    pl.when(step == min(at // 3, 7))(functools.partial(made[which].tick, t))

    @pl.when(step == 0)
    def _():
        for copy in weights(0, 0):
            copy.start()
        if linked:
            place.greet()
            for copy in swaps(0):
                copy.start()
        count, span, _ = cot_ref.shape
        for r in range(count):
            g_ref[r * span:(r + 1) * span, :] = cot_ref[lax.rem(part_ref[r], count)]
        if linked:
            for copy in swaps(1):
                copy.start()
        sums_ref[...] = jnp.zeros_like(sums_ref)

        @functools.partial(each_band, n // 256)
        def _(rows, m):
            xhat, _ = normalize(inp_ref[rows, :].astype(F32))
            normed = (xhat * gain_ref[...] + shift_ref[...]).astype(BF16)
            x_s[rows, :] = normed
            xt_s[:, rows] = normed.T
            sums_ref[2:3, :] += jnp.sum(g_ref[rows, :].astype(F32), 0, keepdims=True)

    @pl.when(step > 0)
    def _():
        for copy in results(step - 1):
            copy.wait()

    tick(0)

    @pl.when(step < last)
    def _():
        for copy in weights(step + 1, 1 - slot):
            copy.start()
    for copy in weights(step, slot):
        copy.wait()
    w_up, w_down = wu_s.at[slot], wd_s.at[slot]
    bias = jnp.concatenate([bias_ref[:, pl.ds(pl.multiple_of(f, 128), 128)] for _, f in places(step)], 1)
    unit_sums = None
    for m in range(n // tile):
        here = slice(m * tile, (m + 1) * tile)
        v = dot(x_s[here, :], w_up[...]) + bias
        vv = v * v
        a = 0.5 + 0.5 * jnp.tanh(v * (C0 + C1 * vv))
        act = v * a
        slope = a + act * (1.0 - a) * (2 * C0 + 6 * C1 * vv)
        act_s[here, :] = act.astype(BF16)
        dh = (dot_nt(g_ref[here, :], w_down[...]) * slope).astype(BF16)
        dh_s[here, :] = dh
        total = jnp.sum(dh.astype(F32), 0, keepdims=True)
        unit_sums = total if unit_sums is None else unit_sums + total
    for s, f in places(step):
        ub_ref[:, pl.ds(pl.multiple_of(f, 128), 128)] = unit_sums[:, s * 128:(s + 1) * 128]

    tick(1)
    for m in range(d // 256):
        grads = dot(xt_s[m * 256:(m + 1) * 256, :], dh_s[...]).astype(BF16)
        gu_s[m, 0] = grads[0:128]
        gu_s[m, 1] = grads[128:256]
    gd_s[...] = dot_tn(act_s[...], g_ref[...]).astype(BF16)
    for copy in results(step):
        copy.start()
    tick(2)
    for m in range(n // tile):
        here = slice(m * tile, (m + 1) * tile)
        y = dot(act_s[here, :], w_down[...])
        dn = dot_nt(dh_s[here, :], w_up[...])

        @pl.when(step == 0)
        def _():
            y_ref[here, :] = y
            dn_ref[here, :] = dn

        @pl.when(step > 0)
        def _():
            y_ref[here, :] += y
            dn_ref[here, :] += dn

    tick(3)

    @pl.when(step == last)
    def _():
        @functools.partial(each_band, n // 256)
        def _(here, m):
            total = dn_ref[here, :]
            xhat, _ = normalize(inp_ref[here, :].astype(F32))
            sums_ref[0:1, :] += jnp.sum(total * xhat, 0, keepdims=True)
            sums_ref[1:2, :] += jnp.sum(total, 0, keepdims=True)

        for copy in results(step):
            copy.wait()
        if linked:
            for copy in swaps(0) + swaps(1):
                copy.wait()


def feed_forward(inp, cot, partners, gain, shift, bias, wu, wd, linked):
    rows, span, d = inp.shape
    n, hidden = rows * span, bias.shape[0]
    sd, vm = jax.ShapeDtypeStruct, pltpu.VMEM
    out_shape = [sd((n, d), F32), sd((n, d), F32), sd((8, d), F32), sd((1, hidden), F32)]
    out_specs = [whole((n, d)), whole((n, d)), whole((8, d)), whole((1, hidden))]
    scratch = [vm((n, d), BF16), vm((d, n), BF16), vm((n, 512), BF16), vm((n, 512), BF16), vm((2, d, 512), BF16), vm((2, 512, d), BF16),
               vm((4, 2, 128, 512), BF16), vm((512, d), BF16), vm((n, d), BF16), DMA((2, 4)), DMA((2, 4)), DMA((4,)), DMA((4,))]
    more, params = [], {}
    if linked:
        more = [inp]
        out_shape += [sd((4, 4, 2, 256, d), BF16), sd(inp.shape, BF16), sd(inp.shape, BF16), *[sd((128, 256), F32)] * 4]
        out_specs += [ANYWHERE] * 3 + [whole((128, 256))] * 4
        scratch += [DMA((2, 3)), DMA((2, 3)), DMA((2,))] + piece_scratch(256, FF_SPLITS[0]) + piece_scratch(256, FF_SPLITS[1])
        params = dict(collective_id=0, has_side_effects=True)
    else:
        out_shape += [sd((4, 2, 128, hidden), BF16), sd((hidden, d), BF16)]
        out_specs += [ANYWHERE] * 2
    return pl.pallas_call(
        functools.partial(ff_kernel, linked=linked), out_shape=out_shape, grid=(hidden // 512,),
        in_specs=[pl.BlockSpec(memory_space=pltpu.SMEM), whole((n, d)), whole(cot.shape), whole((1, d)), whole((1, d)), whole((1, hidden)), ANYWHERE, ANYWHERE] + [ANYWHERE] * len(more),
        out_specs=out_specs, scratch_shapes=scratch,
        compiler_params=pltpu.CompilerParams(vmem_limit_bytes=58 * 2**20, **params),
        cost_estimate=pl.CostEstimate(flops=52_000_000_000, bytes_accessed=50_000_000, transcendentals=4_000_000),
    )(partners, inp.reshape(n, d), cot, gain.reshape(1, d), shift.reshape(1, d), bias.reshape(1, hidden), wu, wd, *more)


def turn(x, c, s, sign):
    lanes = x.shape[1]
    lane = lax.broadcasted_iota(jnp.int32, x.shape, 1) % HEAD_DIM
    other = jnp.where(lane < ROT // 2, pltpu.roll(x, lanes - ROT // 2, 1), pltpu.roll(x, ROT // 2, 1))
    return x * c + (sign * other) * s


def tile_place(tile):
    early = [kind * 8 + pair for two in ORDER[:2] for pair in two for kind in range(3)]
    block = tile // 6
    mates = sorted(t for t in range(24) if t // 6 == block and (t in early) == (tile in early))
    return block, mates.index(tile)


def attn_kernel(raw_ref, g_ref, gain_ref, shift_ref, fam_ref, tab_ref, wqkv_ref, wo_ref, *rest, linked):
    hand, rest = (rest[:1], rest[1:]) if linked else ((), rest)
    dn_ref, sums_ref, gqkv_ref, go_ref, heads_ref = rest[:5]
    outs, rest = (rest[5:10], rest[10:]) if linked else ((), rest[5:])
    (x_s, xt_s, c_s, s_s, w_s, wo_s, q_s, k_s, v_s, do_s, kt_s, vt_s, ht_s, dqt_s, dk_s, dv_s, draw_s, dn_s, gq_s, go_s, heads_s,
     famr_s, famc_s, w_sem, wo_sem, gq_sem, go_sem, h_sem) = rest[:28]
    rest = rest[28:]
    step = pl.program_id(0)
    steps = len(ORDER)
    last = steps - 1
    n, d = raw_ref.shape
    lanes = 256
    pairs = d // 128
    slot = step % 2

    def weights(at, slot):
        out = []
        for half in range(2):
            pair = pick(at, [o[half] for o in ORDER])
            for kind in range(3):
                col = pl.multiple_of((kind * pairs + pair) * 128, 128)
                j = kind * 2 + half
                out.append(local_copy(wqkv_ref.at[:, pl.ds(col, 128)], w_s.at[slot, :, pl.ds(j * 128, 128)], w_sem.at[slot, j]))
            row = pl.multiple_of(pair * 128, 128)
            out.append(local_copy(wo_ref.at[pl.ds(row, 128), :], wo_s.at[slot, pl.ds(half * 128, 128), :], wo_sem.at[slot, half]))
        return out

    def results(at):
        out = []
        for half in range(2):
            pair = pick(at, [o[half] for o in ORDER])
            for kind in range(3):
                j = kind * 2 + half
                if linked:
                    col = pick(at, [block * 384 + rank * 128 for block, rank in (tile_place(kind * 8 + o[half]) for o in ORDER)])
                    to = gqkv_ref.at[at // 2, :, :, :, pl.ds(pl.multiple_of(col, 128), 128)]
                else:
                    to = gqkv_ref.at[:, :, :, pl.ds(pl.multiple_of((kind * pairs + pair) * 128, 128), 128)]
                out.append(local_copy(gq_s.at[:, :, :, pl.ds(j * 128, 128)], to, gq_sem.at[j]))
            out.append(local_copy(go_s.at[pl.ds(half * 128, 128), :], go_ref.at[pair // 2, pair % 2], go_sem.at[half]))
        return out

    if linked:
        place = Place()
        head_send, head_recv = rest[:2]
        rest = rest[2:]

        def heads_out(at):
            cols = pl.ds(pl.multiple_of(at * lanes, lanes), lanes)
            span = n // 4
            out = []
            for j, (to, device) in enumerate(place.peers):
                src = heads_s.at[pl.ds(pl.multiple_of(to * span, span), span), :]
                out.append(remote_copy(src, heads_ref.at[place.seq, :, cols], head_send.at[at, j], head_recv.at[at, j], device))
            mine = heads_s.at[pl.ds(pl.multiple_of(place.seq * span, span), span), :]
            return out, local_copy(mine, heads_ref.at[place.seq, :, cols], h_sem.at[0])

        def part_of(source, k, w):
            return lambda y, c: source.at[k, :, :, :, pl.ds(pl.multiple_of((y * 2 + c) * w, 128), w)]

        def done_at(k):
            def done(total):
                if k == 2:
                    outs[4][...] = total
                else:
                    outs[2 * k][...] = total[0:128]
                    outs[2 * k + 1][...] = total[128:256]
            return done

        cut = piece_count(AT_SPLIT)
        made = [Piece(place, part_of(hand[0], 2, 256), done_at(0), AT_SPLIT, rest[:cut]),
                Piece(place, part_of(hand[0], 3, 256), done_at(1), AT_SPLIT, rest[cut:2 * cut]),
                Piece(place, part_of(gqkv_ref, 0, 384), done_at(2), EARLY_SPLIT, rest[2 * cut:])]
        plan = {}
        for which, times in enumerate(AT_TICKS):
            for t, at in enumerate(times):
                plan.setdefault(at, []).append((which, t))
    else:
        plan = {}

    def tick(position):
        for at, what in sorted(plan.items()):
            if min(at // 6, last) * 6 + position == at:
                def run(what=what):
                    for which, t in sorted(what, key=lambda w: (-w[1], w[0])):
                        made[which].tick(t)
                pl.when(step == min(at // 6, last))(run)

    @pl.when(step == 0)
    def _():
        for copy in weights(0, 0):
            copy.start()
        if linked:
            place.greet()

    @pl.when(step > 0)
    def _():
        for copy in results(step - 1):
            copy.wait()

    tick(0)

    @pl.when(step == 0)
    def _():
        family = fam_ref[pl.ds(lax.axis_index("seq"), 1), :].astype(F32)
        famr_s[...] = family
        for m in range(n // 128):
            rows = slice(m * 128, m * 128 + 128)
            famc_s[rows, :] = jnp.broadcast_to(family[:, rows], (128, 128)).T
        for a in range(n // 32):
            rows = slice(a * 32, a * 32 + 32)
            ca, sa = tab_ref[0, a:a + 1, :], tab_ref[1, a:a + 1, :]
            cb, sb = tab_ref[2], tab_ref[3]
            c1 = ca * cb - sa * sb
            s1 = sa * cb + ca * sb
            lane = lax.broadcasted_iota(jnp.int32, c1.shape, 1) % HEAD_DIM
            c_s[rows, :] = jnp.where(lane < ROT, c1, 1.0)
            s_s[rows, :] = jnp.where(lane < ROT // 2, -s1, jnp.where(lane < ROT, s1, 0.0))
        @functools.partial(each_band, n // 256)
        def _(rows, m):
            xhat, _ = normalize(raw_ref[rows, :].astype(F32))
            normed = (xhat * gain_ref[...] + shift_ref[...]).astype(BF16)
            x_s[rows, :] = normed
            xt_s[:, rows] = normed.T

    @pl.when(step < last)
    def _():
        for copy in weights(step + 1, 1 - slot):
            copy.start()
    for copy in weights(step, slot):
        copy.wait()

    w_ref, wo1_ref = w_s.at[slot], wo_s.at[slot]
    scaling = HEAD_DIM ** -0.5

    def both(rows):
        c, s = c_s[rows, :], s_s[rows, :]
        return jnp.concatenate([c, c], 1), jnp.concatenate([s, s], 1)

    for m in range(n // 256):
        rows = slice(m * 256, m * 256 + 256)
        raw = dot(x_s[rows, :], w_ref[...])
        c, s = both(rows)
        q_s[rows, :] = (turn(raw[:, 0:lanes], c, s, 1.0) * scaling).astype(BF16)
        keys = turn(raw[:, lanes:2 * lanes], c, s, 1.0).astype(BF16)
        k_s[rows, :] = keys
        kt_s[:, rows] = keys.T
        vals = raw[:, 2 * lanes:].astype(BF16)
        v_s[rows, :] = vals
        vt_s[:, rows] = vals.T
        do_s[rows, :] = dot_nt(g_ref[rows, :], wo1_ref[...]).astype(BF16)

    tick(1)
    tile = TILE
    lane = lax.broadcasted_iota(jnp.int32, (tile, 128), 1)
    work = [(h, i) for i in reversed(range(n // tile)) for h in range(4)]

    def first(h, i):
        span = (i + 1) * tile
        here = slice(i * tile, span)
        cols = slice(h // 2 * 128, h // 2 * 128 + 128)
        mine = (lane < HEAD_DIM) if h % 2 == 0 else (lane >= HEAD_DIM)
        qh = jnp.where(mine, q_s[here, cols], 0).astype(BF16)
        doh = jnp.where(mine, do_s[here, cols], 0).astype(BF16)
        return qh, doh, dot_nt(k_s[0:span, cols], qh), dot_nt(v_s[0:span, cols], doh)

    def second(h, i, qh, doh, st, dpt):
        span = (i + 1) * tile
        here = slice(i * tile, span)
        cols = slice(h // 2 * 128, h // 2 * 128 + 128)
        rows = slice(h * HEAD_DIM, (h + 1) * HEAD_DIM)
        family = famc_s[0:span, :]
        allowed = jnp.concatenate([family] * (tile // 128), 1) == famr_s[:, here]
        key_place = lax.broadcasted_iota(jnp.int32, (span, tile), 0)
        query_place = lax.broadcasted_iota(jnp.int32, (span, tile), 1) + i * tile
        st = jnp.where(allowed & (key_place <= query_place), st, -1e9)
        e = jnp.exp(st - jnp.max(st, 0, keepdims=True))
        p = e * (1.0 / jnp.sum(e, 0, keepdims=True))
        pb = p.astype(BF16)
        ds = (p * (dpt - jnp.sum(p * dpt, 0, keepdims=True))).astype(BF16)
        ht_s[rows, here] = dot(vt_s[rows, 0:span], pb).astype(BF16)
        dqt_s[rows, here] = dot(kt_s[rows, 0:span], ds) * scaling
        dv = dot(pb, doh)
        dk = dot(ds, qh)
        if h % 2 == 0 and i == n // tile - 1:
            dv_s[:, cols] = dv
            dk_s[:, cols] = dk
        else:
            dv_s[0:span, cols] += dv
            dk_s[0:span, cols] += dk

    made_first = first(*work[0])
    for j, (h, i) in enumerate(work):
        later = first(*work[j + 1]) if j + 1 < len(work) else None
        second(h, i, *made_first)
        made_first = later
        if h == 3 and i != 1:
            tick({3: 2, 2: 3, 0: 4}[i])

    @pl.when(step > 0)
    def _():
        if linked:
            sent, mine = heads_out(step - 1)
            for copy in sent:
                copy.wait_send()
            mine.wait()
        else:
            local_copy(heads_s, heads_ref.at[:, pl.ds(pl.multiple_of((step - 1) * lanes, lanes), lanes)], h_sem.at[0]).wait()
    heads_s[...] = ht_s[...].T
    if linked:
        sent, mine = heads_out(step)
        for copy in sent:
            copy.start()
        mine.start()
    else:
        local_copy(heads_s, heads_ref.at[:, pl.ds(pl.multiple_of(step * lanes, lanes), lanes)], h_sem.at[0]).start()

    for m in range(n // 256):
        rows = slice(m * 256, m * 256 + 256)
        c, s = both(rows)
        draw_s[rows, 0:lanes] = turn(dqt_s[:, rows].T, c, s, -1.0).astype(BF16)
        draw_s[rows, lanes:2 * lanes] = turn(dk_s[rows, :], c, s, -1.0).astype(BF16)
        draw_s[rows, 2 * lanes:] = dv_s[rows, :].astype(BF16)

    for m in range(d // 256):
        grads = dot(xt_s[m * 256:(m + 1) * 256, :], draw_s[...]).astype(BF16)
        gq_s[m, 0] = grads[0:128]
        gq_s[m, 1] = grads[128:256]
    go_s[...] = dot(ht_s[...], g_ref[...]).astype(BF16)
    for copy in results(step):
        copy.start()
    tick(5)
    for m in range(n // 256):
        here = slice(m * 256, (m + 1) * 256)
        dn = dot_nt(draw_s[here, :], w_ref[...])

        @pl.when(step == 0)
        def _():
            dn_s[here, :] = dn

        @pl.when(step > 0)
        def _():
            dn_s[here, :] += dn

    @pl.when(step == last)
    def _():
        sums_ref[...] = jnp.zeros_like(sums_ref)

        @functools.partial(each_band, n // 256)
        def _(here, m):
            total = dn_s[here, :]
            xhat, _ = normalize(raw_ref[here, :].astype(F32))
            sums_ref[0:1, :] += jnp.sum(total * xhat, 0, keepdims=True)
            sums_ref[1:2, :] += jnp.sum(total, 0, keepdims=True)
            dn_ref[here, :] = total.astype(BF16)

    tick(6)

    @pl.when(step == last)
    def _():
        for copy in results(step):
            copy.wait()
        if linked:
            for at in range(steps):
                for copy in heads_out(at)[0]:
                    copy.wait_recv()
            for copy in heads_out(step)[0]:
                copy.wait_send()
            heads_out(step)[1].wait()
        else:
            local_copy(heads_s, heads_ref.at[:, pl.ds(pl.multiple_of(step * lanes, lanes), lanes)], h_sem.at[0]).wait()


def attend(raw, g, gain, shift, wqkv, wo, families, linked, grads=None):
    n, d = raw.shape
    pair_lane = np.arange(128) % HEAD_DIM % (ROT // 2)
    freq = 10000.0 ** (-2.0 * pair_lane / ROT)
    high, low = np.arange(n // 32)[:, None] * 32.0 * freq, np.arange(32)[:, None] * freq
    tab = jnp.asarray(np.stack([np.cos(high), np.sin(high), np.cos(low), np.sin(low)]), F32)
    sd, vm = jax.ShapeDtypeStruct, pltpu.VMEM
    out_shape = [sd((n, d), BF16), sd((8, d), F32), sd((2, 4, 2, 128, 3 * d // 2) if linked else (4, 2, 128, 3 * d), BF16),
                 sd((4, 2, 128, d), BF16), sd((4, n // 4, d) if linked else (n, d), BF16)]
    out_specs = [whole((n, d)), whole((8, d))] + [ANYWHERE] * 3
    scratch = [vm((n, d), BF16), vm((d, n), BF16), vm((n, 128), F32), vm((n, 128), F32), vm((2, d, 768), BF16), vm((2, 256, d), BF16)]
    scratch += [vm((n, 256), BF16)] * 4 + [vm((256, n), BF16)] * 3
    scratch += [vm((256, n), F32), vm((n, 256), F32), vm((n, 256), F32), vm((n, 768), BF16), vm((n, d), F32), vm((4, 2, 128, 768), BF16),
                vm((256, d), BF16), vm((n, 256), BF16), vm((1, n), F32), vm((n, 128), F32), DMA((2, 6)), DMA((2, 2)), DMA((6,)), DMA((2,)), DMA((1,))]
    params, more = {}, []
    if linked:
        more = [grads]
        out_shape += [sd((128, 256), F32)] * 4 + [sd((128, 384), F32)]
        out_specs += [whole((128, 256))] * 4 + [whole((128, 384))]
        scratch += [DMA((4, 3)), DMA((4, 3))]
        scratch += piece_scratch(256, AT_SPLIT) * 2 + piece_scratch(384, EARLY_SPLIT)
        params = dict(collective_id=1, has_side_effects=True)
    return pl.pallas_call(
        functools.partial(attn_kernel, linked=linked), out_shape=out_shape, grid=(len(ORDER),),
        in_specs=[whole((n, d)), whole((n, d)), whole((1, d)), whole((1, d)), whole(families.shape), whole((4, 32, 128)), ANYWHERE, ANYWHERE]
        + [ANYWHERE] * len(more),
        out_specs=out_specs, scratch_shapes=scratch,
        compiler_params=pltpu.CompilerParams(vmem_limit_bytes=60 * 2**20, **params),
        cost_estimate=pl.CostEstimate(flops=70_000_000_000, bytes_accessed=30_000_000, transcendentals=20_000_000),
    )(raw, g, gain.reshape(1, d), shift.reshape(1, d), families, tab, wqkv, wo, *more)


class SmallSum:
    def __init__(self, place, held, heard, by_z, send, recv):
        self.p, self.held, self.heard, self.by_z, self.send, self.recv = place, held, heard, by_z, send, recv

    def copies(self, t):
        p = self.p
        if t < 3:
            to = (p.twin, p.beside_y, p.beside_x)[t]
            return [remote_copy(self.held, self.heard.at[t], self.send.at[t], self.recv.at[t], to)]
        return [remote_copy(self.by_z.at[p.z], self.by_z.at[p.z], self.send.at[3 + j], self.recv.at[3 + j], to)
                for j, to in enumerate(p.along_z)]

    def tick(self, t):
        if t > 0:
            for copy in self.copies(t - 1):
                copy.wait()
        if 0 < t < 4:
            total = self.held[...] + self.heard[t - 1]
            if t < 3:
                self.held[...] = total
            else:
                self.by_z[self.p.z] = total
        if t < 4:
            for copy in self.copies(t):
                copy.start()
        return None if t < 4 else self.by_z[0] + self.by_z[1] + self.by_z[2] + self.by_z[3]


def tail_kernel(dat_ref, heads_ref, gq_ref, go_ref, inp_ref, cot_ref, y_ref, dn_ref, wo_ref, part_ref, gain_ref, dbias_ref, sums_ff_ref, sums_at_ref,
                ub_ref, early_ref, lo_ref, ig_ref, qkv_ref, out_ref, gain_o, shift_o, ub_o, db_o,
                back_s, inp_s, g_s, heads_s, y_s, dn_s, wo_s, lo_s, ig_s, small_s, heard_s, by_z_s,
                load_sem, wo_sem, back_send, back_recv, own_sem, small_send, small_recv, lo_sem, ig_sem, *pieces):
    place = Place()
    d = wo_s.shape[0]
    place.greet()
    swaps = [remote_copy(dat_ref.at[to], back_s.at[place.seq], back_send.at[j], back_recv.at[j], device)
             for j, (to, device) in enumerate(place.peers)]
    own = local_copy(dat_ref.at[place.seq], back_s.at[place.seq], own_sem.at[0])
    blocks = {}

    def part(source, w, row0, rows):
        return lambda y, c: source.at[:, :, pl.ds(row0, rows), pl.ds(pl.multiple_of((y * 2 + c) * w, 128), w)]

    def out_done(total):
        out_ref[...] = total

    def qkv_done(row0):
        def done(total):
            rows = slice(row0, row0 + total.shape[0])
            early = early_ref[rows, :]
            first = jnp.where(place.c == 0, early, total)
            second = jnp.where(place.c == 0, total, early)
            order = ((first, 0), (second, 0), (second, 1), (first, 1), (first, 2), (second, 2))
            for k, (source, at) in enumerate(order):
                qkv_ref[rows, k * 128:(k + 1) * 128] = source[:, at * 128:(at + 1) * 128]
        return done

    cuts = [0, piece_count(TAIL_SPLITS[0])]
    for split in TAIL_SPLITS[1:]:
        cuts.append(cuts[-1] + piece_count(split))
    late = gq_ref.at[1]
    row1 = sum(TAIL_SPLITS[1])
    made = [Piece(place, part(go_ref, 256, 0, 128), out_done, TAIL_SPLITS[0], pieces[:cuts[1]]),
            Piece(place, part(late, 384, 0, row1), qkv_done(0), TAIL_SPLITS[1], pieces[cuts[1]:cuts[2]]),
            Piece(place, part(late, 384, row1, 128 - row1), qkv_done(row1), TAIL_SPLITS[2], pieces[cuts[2]:])]
    small = SmallSum(place, small_s, heard_s, by_z_s, small_send, small_recv)
    small_s[0:3, :] = sums_ff_ref[0:3, :]
    small_s[0:2, :] += sums_at_ref[0:2, :]
    small_s[3:4, :] = jnp.zeros((1, d), F32)
    for k in range(4):
        small_s[4 + k:5 + k, :] = ub_ref[:, k * d:(k + 1) * d]
    for piece in made:
        piece.tick(0)
    for copy in swaps:
        copy.start()
    small.tick(0)
    loads = [local_copy(a, b, load_sem.at[k]) for k, (a, b) in enumerate(
        ((heads_ref, heads_s), (inp_ref, inp_s), (y_ref, y_s), (cot_ref, g_s), (dn_ref, dn_s)))]
    for pair in range(d // 128):
        at = [p for two in ORDER for p in two].index(pair)
        blocks[at] = local_copy(wo_ref.at[pl.ds(pair * 128, 128), :], wo_s.at[pl.ds(at * 128, 128), :], wo_sem.at[at])
    for copy in [loads[0]] + list(blocks.values()) + loads[1:] + [own]:
        copy.start()

    def lo_out(r):
        return local_copy(lo_s.at[r], lo_ref.at[r], lo_sem.at[r])

    def ig_out(r):
        return local_copy(ig_s.at[r], ig_ref.at[r], ig_sem.at[r])

    def forward(r, carry):
        total = inp_s[r].astype(F32) + dot(heads_s[r], wo_s[...]) + (y_s[r] + dbias_ref[...])
        lo_s[r] = total.astype(BF16)
        lo_out(r).start()
        return carry

    def backward(r):
        xhat, scale = normalize(inp_s[r].astype(F32))
        dx = (dn_s[r] + back_s[r].astype(F32)) * gain_ref[...]
        ig_s[r] = g_s[lax.rem(part_ref[r], 4)].astype(F32) + (dx - jnp.mean(dx, -1, keepdims=True) - xhat * jnp.mean(dx * xhat, -1, keepdims=True)) * scale
        ig_out(r).start()

    made[0].tick(1)
    small.tick(1)
    for copy in list(blocks.values()) + loads[:3]:
        copy.wait()
    lax.fori_loop(0, 2, forward, 0)
    made[1].tick(1)
    lax.fori_loop(2, 4, forward, 0)
    made[0].tick(2)
    made[2].tick(1)
    small.tick(2)
    loads[3].wait()
    loads[4].wait()
    own.wait()
    backward(place.seq)
    made[1].tick(2)
    made[0].tick(3)
    small.tick(3)
    for j in range(3):
        swaps[j].wait_send()
    swaps[2].wait_recv()
    backward((place.seq + 1) % 4)
    made[2].tick(2)
    made[1].tick(3)
    swaps[1].wait_recv()
    backward((place.seq + 2) % 4)
    made[2].tick(3)
    swaps[0].wait_recv()
    backward((place.seq + 3) % 4)
    total = small.tick(4)
    for piece in made:
        piece.tick(4)
    gain_o[...] = total[0:1]
    shift_o[...] = total[1:2]
    db_o[...] = total[2:3]
    for k in range(4):
        ub_o[:, k * d:(k + 1) * d] = total[4 + k:5 + k]
    for r in range(4):
        lo_out(r).wait()
        ig_out(r).wait()


def finish(dat, heads, gq, go, inp, cot, y, dn, wo, partners, gain, dbias, sums_ff, sums_at, ub, early):
    sd, vm = jax.ShapeDtypeStruct, pltpu.VMEM
    shape, d = inp.shape, inp.shape[2]
    vmem = pl.BlockSpec(memory_space=pltpu.VMEM)
    return pl.pallas_call(
        tail_kernel,
        out_shape=[sd(shape, BF16), sd(shape, F32), sd((128, 768), F32), sd((128, 256), F32), sd((1, d), F32), sd((1, d), F32), sd((1, 4 * d), F32),
                   sd((1, d), F32)],
        in_specs=[ANYWHERE] * 9 + [pl.BlockSpec(memory_space=pltpu.SMEM)] + [vmem] * 6, out_specs=[ANYWHERE] * 2 + [vmem] * 6,
        scratch_shapes=[vm(shape, BF16)] * 4 + [vm(shape, F32)] * 2 + [vm((d, d), BF16), vm(shape, BF16), vm(shape, F32),
                        vm((8, d), F32), vm((3, 8, d), F32), vm((4, 8, d), F32),
                        DMA((5,)), DMA((8,)), DMA((3,)), DMA((3,)), DMA((1,)), DMA((6,)), DMA((6,)), DMA((4,)), DMA((4,))]
        + piece_scratch(256, TAIL_SPLITS[0]) + piece_scratch(384, TAIL_SPLITS[1]) + piece_scratch(384, TAIL_SPLITS[2]),
        compiler_params=pltpu.CompilerParams(collective_id=2, has_side_effects=True, vmem_limit_bytes=56 * 2**20),
    )(dat.reshape(shape), heads, gq, go, inp, cot, y.reshape(shape), dn.reshape(shape), wo, partners, gain.reshape(1, d), dbias.reshape(1, d), sums_ff, sums_at,
      ub, early)


def copy_kernel(*refs, moves):
    count = len(refs) - 1
    refs, sem = refs[:count], refs[count]
    copies = [local_copy(refs[a].at[at], refs[b].at[to], sem.at[k]) for k, (a, at, b, to) in enumerate(moves)]
    for copy in copies:
        copy.start()
    for copy in copies:
        copy.wait()


def gather_up(layer_out, input_grad, qkv_sum, out_sum, small, ups, downs):
    sd, everything = jax.ShapeDtypeStruct, slice(None)
    ins = [layer_out, input_grad, qkv_sum, out_sum, *small, *ups, *downs]
    shapes = [sd(layer_out.shape, BF16), sd(input_grad.shape, F32), sd(qkv_sum.shape, F32), sd(out_sum.shape, F32), *[sd(v.shape, F32) for v in small],
              sd((128, 1024), F32), sd((512, 256), F32)]
    first = len(ins)
    moves = [(a, r, first + a, r) for a in (1, 0) for r in range(4)]
    moves += [(a, (everything, everything), first + a, (everything, everything)) for a in range(2, 8)]
    for k in range(4):
        for half in range(2):
            moves.append((8 + k, (everything, slice(half * 128, half * 128 + 128)), first + 8,
                          (everything, slice(half * 512 + k * 128, half * 512 + k * 128 + 128))))
        moves.append((12 + k, (everything, everything), first + 9, (slice(k * 128, k * 128 + 128), everything)))
    return pl.pallas_call(functools.partial(copy_kernel, moves=moves), out_shape=shapes, in_specs=[ANYWHERE] * first, out_specs=[ANYWHERE] * len(shapes),
                          scratch_shapes=[DMA((len(moves),))])(*ins)


def on_device(inputs, norm_gain, norm_shift, qkv_weight, out_weight, up_weight, up_bias, down_weight, down_bias, partners, families, cotangent, linked):
    row_count, place_count, width = inputs.shape
    tokens = row_count * place_count
    branch_args = norm_gain, norm_shift, qkv_weight, out_weight, families, linked
    if linked:
        y, dn, sums_ff, ub, grads, row_inputs, row_grad, up0, down0, up1, down1 = feed_forward(
            inputs, cotangent, partners, norm_gain, norm_shift, up_bias, up_weight, down_weight, True)
        dat, sums_at, gq, go, heads, up2, down2, up3, down3, early = attend(
            row_inputs.reshape(tokens, width), row_grad.reshape(tokens, width), *branch_args, grads)
        layer_out, input_grad, qkv_sum, out_sum, gain_sum, shift_sum, ub_sum, db_sum = finish(
            dat, heads, gq, go, inputs, cotangent, y, dn, out_weight, partners, norm_gain, down_bias, sums_ff, sums_at, ub, early)
        layer_out, input_grad, qkv_sum, out_sum, gain_sum, shift_sum, ub_sum, db_sum, up_sum, down_sum = gather_up(
            layer_out, input_grad, qkv_sum, out_sum, (gain_sum, shift_sum, ub_sum, db_sum), (up0, up1, up2, up3), (down0, down1, down2, down3))
        return (layer_out, input_grad, gain_sum.reshape(width), shift_sum.reshape(width), qkv_sum, out_sum, up_sum, ub_sum.reshape(-1), down_sum,
                db_sum.reshape(width))
    local_rows = partners - lax.axis_index("dp") * row_count
    grad = jnp.take(cotangent, local_rows, axis=0, mode="clip")
    swap = functools.partial(lax.all_to_all, axis_name="seq", split_axis=0, concat_axis=0, tiled=True)
    row_inputs, row_grad = swap(inputs).reshape(tokens, width), swap(grad).reshape(tokens, width)
    y, dn, sums_ff, ub, up_grad, down_grad = feed_forward(
        inputs, cotangent, partners, norm_gain, norm_shift, up_bias, up_weight, down_weight, False)
    dat, sums_at, qkv_grad, out_grad, heads = attend(row_inputs, row_grad, *branch_args)

    def scatter(parts, columns):
        part = lax.psum_scatter(parts.reshape(-1, columns), "seq", scatter_dimension=1, tiled=True)
        return lax.psum_scatter(part, "dp", scatter_dimension=0, tiled=True).astype(F32)

    qkv_sum, out_sum = scatter(qkv_grad, 3 * width), scatter(out_grad, width)
    up_sum, down_sum = scatter(up_grad, up_bias.shape[0]), scatter(down_grad, width)
    heads = swap(heads.reshape(inputs.shape)).reshape(tokens, width)
    order = np.array([p for two in ORDER for p in two])
    attn_out = dot(heads, out_weight.reshape(-1, 128, width)[order].reshape(width, width))
    values = inputs.astype(F32).reshape(tokens, width)
    layer_out = (values + attn_out + (y + down_bias)).astype(BF16).reshape(inputs.shape)
    xhat, scale = normalize(values)
    dx = (dn + swap(dat.reshape(inputs.shape)).reshape(tokens, width).astype(F32)) * norm_gain
    input_grad = grad.reshape(tokens, width).astype(F32) + (dx - jnp.mean(dx, -1, keepdims=True) - xhat * jnp.mean(dx * xhat, -1, keepdims=True)) * scale
    gain_sum, shift_sum, up_bias_sum, down_bias_sum = lax.psum((sums_ff[0] + sums_at[0], sums_ff[1] + sums_at[1], ub[0], sums_ff[2]), ("dp", "seq"))
    return (layer_out, input_grad.reshape(inputs.shape), gain_sum, shift_sum, qkv_sum, out_sum, up_sum, up_bias_sum, down_sum, down_bias_sum)


def solution(mesh):
    rows = P("dp", "seq", None)
    placed = (rows,) + (P(),) * 8 + (P("dp"), P("dp", None), rows)
    grads = P("dp", "seq")
    linked = (mesh.shape["dp"], mesh.shape["seq"]) == (8, 4)
    return jax.shard_map(functools.partial(on_device, linked=linked), mesh=mesh, in_specs=placed,
                         out_specs=(rows, rows, P(), P(), grads, grads, grads, P(), grads, P()), check_vma=False)
```

```python
import functools

import jax
import jax.numpy as jnp
import numpy as np
from jax import lax
from jax.experimental import pallas as pl
from jax.experimental.pallas import tpu as pltpu
from jax.sharding import PartitionSpec as P

F32 = jnp.float32
BF16 = jnp.bfloat16
HEAD_DIM = 64
ROT = 32
EPS = 1e-05
C0 = 0.7978845608028654
C1 = C0 * 0.044715
TILE = 256
FF_SPLITS = (0, 176, 80), (96, 112, 48)
AT_SPLIT = 96, 112, 48
EARLY_SPLIT = 48, 64, 16
TAIL_SPLITS = (0, 80, 48), (0, 48, 16), (0, 32, 32)
FF_TICKS = (6, 9, 15, 18, 22), (12, 15, 20, 22, 24)
AT_TICKS = (0, 2, 7, 10, 14), (4, 7, 12, 15, 19), (13, 15, 19, 21, 24)
ORDER = ((0, 3), (4, 7), (1, 2), (5, 6))
MESH_ID = pl.DeviceIdType.MESH
ANYWHERE = pl.BlockSpec(memory_space=pl.ANY)
DMA = pltpu.SemaphoreType.DMA


def dot(a, b):
    return lax.dot_general(a, b, (((1,), (0,)), ((), ())), preferred_element_type=F32)


def dot_nt(a, b):
    return lax.dot_general(a, b, (((1,), (1,)), ((), ())), preferred_element_type=F32)


def dot_tn(a, b):
    return lax.dot_general(a, b, (((0,), (0,)), ((), ())), preferred_element_type=F32)


def whole(shape):
    return pl.BlockSpec(shape, lambda p: (0,) * len(shape), pipeline_mode=pl.Buffered(1))


def pick(step, values):
    out = jnp.int32(values[0])
    for i, value in enumerate(values[1:], 1):
        out = jnp.where(step == i, value, out)
    return out


def normalize(values):
    centered = values - jnp.mean(values, -1, keepdims=True)
    scale = lax.rsqrt(jnp.mean(centered * centered, -1, keepdims=True) + EPS)
    return centered * scale, scale


def each_band(count, body):
    def step(m, carry):
        body(pl.ds(pl.multiple_of(m * 256, 256), 256), m)
        return carry

    lax.fori_loop(0, count, step, 0)


def local_copy(src, dst, sem):
    return pltpu.make_async_copy(src, dst, sem)


def remote_copy(src, dst, send, recv, to):
    return pltpu.make_async_remote_copy(src_ref=src, dst_ref=dst, send_sem=send, recv_sem=recv, device_id=to,
                                        device_id_type=MESH_ID)


class Place:
    def __init__(self):
        self.dp, self.seq = lax.axis_index("dp"), lax.axis_index("seq")
        self.z, self.x, self.y, self.c = self.dp // 2, self.dp % 2, self.seq // 2, self.seq % 2
        self.twin = (self.dp, self.y * 2 + 1 - self.c)
        self.beside_y = (self.dp, (1 - self.y) * 2 + self.c)
        self.across = (self.dp, (1 - self.y) * 2 + 1 - self.c)
        self.beside_x = (self.z * 2 + 1 - self.x, self.seq)
        self.along_z = [(((self.z + j) % 4) * 2 + self.x, self.seq) for j in (1, 2, 3)]
        self.peers = [((self.seq + j) % 4, (self.dp, (self.seq + j) % 4)) for j in (1, 2, 3)]
        self.partners = [self.twin, self.beside_y, self.beside_x] + self.along_z

    def greet(self):
        barrier = pltpu.get_barrier_semaphore()
        for partner in self.partners + [self.across]:
            pl.semaphore_signal(barrier, inc=1, device_id=partner, device_id_type=MESH_ID)
        pl.semaphore_wait(barrier, len(self.partners) + 1)


def add_into(dst, src, lead):
    rows, w = src.shape[-2:]
    band = rows
    while band * w > 65536 and band % 32 == 0:
        band //= 2
    count = 1
    for n in lead:
        count *= n

    def body(t, carry):
        block, part = t // (rows // band), t % (rows // band)
        index = []
        for n in reversed(lead):
            index.insert(0, block % n)
            block = block // n
        at = tuple(index) + (pl.ds(pl.multiple_of(part * band, band), band), slice(None))
        dst[at] = dst[at] + src[at]
        return carry

    lax.fori_loop(0, count * (rows // band), body, 0)


def piece_scratch(w, split):
    ra, rb, rc = split
    r = sum(split)
    out = [((2, 4, 2, r), 1), ((2, 4, 2, r), 1), ((4, 2, ra), ra), ((2, 4, rb), rb), ((3, 2, 2, rc), rc), ((4, ra), ra), ((4, rb), rb), ((2, rc), rc),
           ((3, ra + rb), ra + rb), ((rc,), rc)]
    return [pltpu.VMEM(shape + (w,), BF16) for shape, used in out if used] + [DMA((14,)), DMA((14,)), DMA((2,))]


def piece_count(split):
    return len(piece_scratch(128, split))


class Piece:
    def __init__(self, place, part, done, split, scratch):
        self.p, self.part, self.done, self.split = place, part, done, split
        ra, rb, rc = split
        names = [("a", 1), ("from_twin", 1), ("ya", ra), ("xb", rb), ("zc", rc), ("xa", ra), ("yb", rb), ("xc", rc), ("zab", ra + rb), ("yc", rc)]
        scratch = list(scratch)
        for name, used in names:
            setattr(self, name, scratch.pop(0) if used else None)
        self.ss, self.rs, self.ls = scratch
        self.rows_a, self.rows_b, self.rows_ab, self.rows_c = pl.ds(0, ra), pl.ds(ra, rb), pl.ds(0, ra + rb), pl.ds(ra + rb, rc)

    def copies(self, stage):
        p, a, (ra, rb, rc) = self.p, self.a, self.split
        out = []
        slot = (0, 2, 7, 10)[stage]

        def send(src, dst, to):
            k = slot + len(out)
            out.append(remote_copy(src, dst, self.ss.at[k], self.rs.at[k], to))

        zs = [((p.z + 1 + j) % 4, p.along_z[j]) for j in range(3)]
        if stage == 0:
            for k in (0, 1):
                send(self.part(k, 1 - p.c), self.from_twin.at[k], p.twin)
        if stage == 1:
            if ra:
                send(a.at[1 - p.y, :, :, self.rows_a, :], self.ya, p.beside_y)
            if rb:
                send(a.at[:, :, 1 - p.x, self.rows_b, :], self.xb, p.beside_x)
            for j in range(3 if rc else 0):
                send(a.at[:, zs[j][0], :, self.rows_c, :], self.zc.at[j], zs[j][1])
        if stage == 2:
            if ra:
                send(a.at[p.y, :, 1 - p.x, self.rows_a, :], self.xa, p.beside_x)
            if rb:
                send(a.at[1 - p.y, :, p.x, self.rows_b, :], self.yb, p.beside_y)
            if rc:
                send(a.at[:, p.z, 1 - p.x, self.rows_c, :], self.xc, p.beside_x)
        if stage == 3:
            for j in range(3 if ra + rb else 0):
                send(a.at[p.y, zs[j][0], p.x, self.rows_ab, :], self.zab.at[j], zs[j][1])
            if rc:
                send(a.at[1 - p.y, p.z, p.x, self.rows_c, :], self.yc, p.beside_y)
        return out

    def own(self):
        return [local_copy(self.part(k, self.p.c), self.a.at[k], self.ls.at[k]) for k in (0, 1)]

    def tick(self, t):
        p, a, (ra, rb, rc) = self.p, self.a, self.split
        if t > 0:
            for copy in self.copies(t - 1):
                copy.wait()
        if t == 0:
            for copy in self.copies(0) + self.own():
                copy.start()
        if t == 1:
            for copy in self.own():
                copy.wait()
            add_into(a, self.from_twin, (2, 4, 2))
        if t == 2:
            if ra:
                add_into(a.at[p.y, :, :, self.rows_a, :], self.ya, (4, 2))
            if rb:
                add_into(a.at[:, :, p.x, self.rows_b, :], self.xb, (2, 4))
            for j in range(3 if rc else 0):
                add_into(a.at[:, p.z, :, self.rows_c, :], self.zc.at[j], (2, 2))
        if t == 3:
            if ra:
                add_into(a.at[p.y, :, p.x, self.rows_a, :], self.xa, (4,))
            if rb:
                add_into(a.at[p.y, :, p.x, self.rows_b, :], self.yb, (4,))
            if rc:
                add_into(a.at[:, p.z, p.x, self.rows_c, :], self.xc, (2,))
        if t in (1, 2, 3):
            for copy in self.copies(t):
                copy.start()
        if t == 4:
            mine = a.at[p.y, p.z, p.x]
            parts = []
            if ra + rb:
                total = mine[self.rows_ab, :].astype(F32)
                for j in range(3):
                    total += self.zab[j].astype(F32)
                parts.append(total)
            if rc:
                parts.append(mine[self.rows_c, :].astype(F32) + self.yc[...].astype(F32))
            self.done(jnp.concatenate(parts, 0) if len(parts) > 1 else parts[0])


def ff_kernel(part_ref, inp_ref, cot_ref, gain_ref, shift_ref, bias_ref, wu_ref, wd_ref, *rest, linked):
    hand, rest = (rest[:1], rest[1:]) if linked else ((), rest)
    y_ref, dn_ref, sums_ref, ub_ref = rest[:4]
    outs, rest = (rest[4:11], rest[11:]) if linked else (rest[4:6], rest[6:])
    x_s, xt_s, act_s, dh_s, wu_s, wd_s, gu_s, gd_s, g_ref, wu_sem, wd_sem, gu_sem, gd_sem = rest[:13]
    rest = rest[13:]
    step = pl.program_id(0)
    last = pl.num_programs(0) - 1
    n, d = x_s.shape
    hidden = bias_ref.shape[1]
    group = hidden // 8
    tile = 512
    slot = step % 2

    def places(at):
        k, j = at // 2, at % 2
        return [(s, (2 * s + j) * group + k * 128) for s in range(4)]

    def weights(at, slot):
        out = []
        for s, f in places(at):
            f = pl.multiple_of(f, 128)
            out.append(local_copy(wu_ref.at[:, pl.ds(f, 128)], wu_s.at[slot, :, pl.ds(s * 128, 128)], wu_sem.at[slot, s]))
            out.append(local_copy(wd_ref.at[pl.ds(f, 128), :], wd_s.at[slot, pl.ds(s * 128, 128), :], wd_sem.at[slot, s]))
        return out

    def results(at):
        out = []
        k, j = at // 2, at % 2
        for s, f in places(at):
            f = pl.multiple_of(f, 128)
            up, down = gu_s.at[:, :, :, pl.ds(s * 128, 128)], gd_s.at[pl.ds(s * 128, 128), :]
            if linked:
                col = pl.multiple_of(s * 256 + j * 128, 128)
                to = outs[0].at[k, :, :, pl.ds(0, 128), pl.ds(col, 128)], outs[0].at[k, s, j, pl.ds(128, 128), :]
            else:
                to = outs[0].at[:, :, :, pl.ds(f, 128)], outs[1].at[pl.ds(f, 128), :]
            out.append(local_copy(up, to[0], gu_sem.at[s]))
            out.append(local_copy(down, to[1], gd_sem.at[s]))
        return out

    if linked:
        place = Place()
        row_send, row_recv, own_sem = rest[:3]
        rest = rest[3:]

        def swaps(a):
            span = n // 4

            def row(at):
                return g_ref.at[pl.ds(pl.multiple_of(at * span, span), span), :] if a else hand[0].at[at]

            out = [remote_copy(row(to), outs[1 + a].at[place.seq], row_send.at[a, j], row_recv.at[a, j], device)
                   for j, (to, device) in enumerate(place.peers)]
            return out + [local_copy(row(place.seq), outs[1 + a].at[place.seq], own_sem.at[a])]

        def part_of(k):
            return lambda y, c: outs[0].at[k, :, :, :, pl.ds(pl.multiple_of((y * 2 + c) * 256, 256), 256)]

        def done_at(k):
            def done(total):
                outs[3 + 2 * k][...] = total[0:128]
                outs[4 + 2 * k][...] = total[128:256]
            return done

        cut = piece_count(FF_SPLITS[0])
        made = [Piece(place, part_of(k), done_at(k), FF_SPLITS[k], (rest[:cut], rest[cut:])[k]) for k in range(2)]

    def tick(position):
        for which, times in enumerate(FF_TICKS if linked else ()):
            for t, at in enumerate(times):
                if min(at // 3, 7) * 3 + position == at:
                    pl.when(step == min(at // 3, 7))(functools.partial(made[which].tick, t))

    @pl.when(step == 0)
    def _():
        for copy in weights(0, 0):
            copy.start()
        if linked:
            place.greet()
            for copy in swaps(0):
                copy.start()
        count, span, _ = cot_ref.shape
        for r in range(count):
            g_ref[r * span:(r + 1) * span, :] = cot_ref[lax.rem(part_ref[r], count)]
        if linked:
            for copy in swaps(1):
                copy.start()
        sums_ref[...] = jnp.zeros_like(sums_ref)

        @functools.partial(each_band, n // 256)
        def _(rows, m):
            xhat, _ = normalize(inp_ref[rows, :].astype(F32))
            normed = (xhat * gain_ref[...] + shift_ref[...]).astype(BF16)
            x_s[rows, :] = normed
            xt_s[:, rows] = normed.T
            sums_ref[2:3, :] += jnp.sum(g_ref[rows, :].astype(F32), 0, keepdims=True)

    @pl.when(step > 0)
    def _():
        for copy in results(step - 1):
            copy.wait()

    tick(0)

    @pl.when(step < last)
    def _():
        for copy in weights(step + 1, 1 - slot):
            copy.start()
    for copy in weights(step, slot):
        copy.wait()
    w_up, w_down = wu_s.at[slot], wd_s.at[slot]
    bias = jnp.concatenate([bias_ref[:, pl.ds(pl.multiple_of(f, 128), 128)] for _, f in places(step)], 1)
    unit_sums = None
    for m in range(n // tile):
        here = slice(m * tile, (m + 1) * tile)
        v = dot(x_s[here, :], w_up[...]) + bias
        vv = v * v
        a = 0.5 + 0.5 * jnp.tanh(v * (C0 + C1 * vv))
        act = v * a
        slope = a + act * (1.0 - a) * (2 * C0 + 6 * C1 * vv)
        act_s[here, :] = act.astype(BF16)
        dh = (dot_nt(g_ref[here, :], w_down[...]) * slope).astype(BF16)
        dh_s[here, :] = dh
        total = jnp.sum(dh.astype(F32), 0, keepdims=True)
        unit_sums = total if unit_sums is None else unit_sums + total
    for s, f in places(step):
        ub_ref[:, pl.ds(pl.multiple_of(f, 128), 128)] = unit_sums[:, s * 128:(s + 1) * 128]

    tick(1)
    for m in range(d // 256):
        grads = dot(xt_s[m * 256:(m + 1) * 256, :], dh_s[...]).astype(BF16)
        gu_s[m, 0] = grads[0:128]
        gu_s[m, 1] = grads[128:256]
    gd_s[...] = dot_tn(act_s[...], g_ref[...]).astype(BF16)
    for copy in results(step):
        copy.start()
    tick(2)
    for m in range(n // tile):
        here = slice(m * tile, (m + 1) * tile)
        y = dot(act_s[here, :], w_down[...])
        dn = dot_nt(dh_s[here, :], w_up[...])

        @pl.when(step == 0)
        def _():
            y_ref[here, :] = y
            dn_ref[here, :] = dn

        @pl.when(step > 0)
        def _():
            y_ref[here, :] += y
            dn_ref[here, :] += dn

    tick(3)

    @pl.when(step == last)
    def _():
        @functools.partial(each_band, n // 256)
        def _(here, m):
            total = dn_ref[here, :]
            xhat, _ = normalize(inp_ref[here, :].astype(F32))
            sums_ref[0:1, :] += jnp.sum(total * xhat, 0, keepdims=True)
            sums_ref[1:2, :] += jnp.sum(total, 0, keepdims=True)

        for copy in results(step):
            copy.wait()
        if linked:
            for copy in swaps(0) + swaps(1):
                copy.wait()


def feed_forward(inp, cot, partners, gain, shift, bias, wu, wd, linked):
    rows, span, d = inp.shape
    n, hidden = rows * span, bias.shape[0]
    sd, vm = jax.ShapeDtypeStruct, pltpu.VMEM
    out_shape = [sd((n, d), F32), sd((n, d), F32), sd((8, d), F32), sd((1, hidden), F32)]
    out_specs = [whole((n, d)), whole((n, d)), whole((8, d)), whole((1, hidden))]
    scratch = [vm((n, d), BF16), vm((d, n), BF16), vm((n, 512), BF16), vm((n, 512), BF16), vm((2, d, 512), BF16), vm((2, 512, d), BF16),
               vm((4, 2, 128, 512), BF16), vm((512, d), BF16), vm((n, d), BF16), DMA((2, 4)), DMA((2, 4)), DMA((4,)), DMA((4,))]
    more, params = [], {}
    if linked:
        more = [inp]
        out_shape += [sd((4, 4, 2, 256, d), BF16), sd(inp.shape, BF16), sd(inp.shape, BF16), *[sd((128, 256), F32)] * 4]
        out_specs += [ANYWHERE] * 3 + [whole((128, 256))] * 4
        scratch += [DMA((2, 3)), DMA((2, 3)), DMA((2,))] + piece_scratch(256, FF_SPLITS[0]) + piece_scratch(256, FF_SPLITS[1])
        params = dict(collective_id=0, has_side_effects=True)
    else:
        out_shape += [sd((4, 2, 128, hidden), BF16), sd((hidden, d), BF16)]
        out_specs += [ANYWHERE] * 2
    return pl.pallas_call(
        functools.partial(ff_kernel, linked=linked), out_shape=out_shape, grid=(hidden // 512,),
        in_specs=[pl.BlockSpec(memory_space=pltpu.SMEM), whole((n, d)), whole(cot.shape), whole((1, d)), whole((1, d)), whole((1, hidden)), ANYWHERE, ANYWHERE] + [ANYWHERE] * len(more),
        out_specs=out_specs, scratch_shapes=scratch,
        compiler_params=pltpu.CompilerParams(vmem_limit_bytes=58 * 2**20, **params),
        cost_estimate=pl.CostEstimate(flops=52_000_000_000, bytes_accessed=50_000_000, transcendentals=4_000_000),
    )(partners, inp.reshape(n, d), cot, gain.reshape(1, d), shift.reshape(1, d), bias.reshape(1, hidden), wu, wd, *more)


def turn(x, c, s, sign):
    lanes = x.shape[1]
    lane = lax.broadcasted_iota(jnp.int32, x.shape, 1) % HEAD_DIM
    other = jnp.where(lane < ROT // 2, pltpu.roll(x, lanes - ROT // 2, 1), pltpu.roll(x, ROT // 2, 1))
    return x * c + (sign * other) * s


def tile_place(tile):
    early = [kind * 8 + pair for two in ORDER[:2] for pair in two for kind in range(3)]
    block = tile // 6
    mates = sorted(t for t in range(24) if t // 6 == block and (t in early) == (tile in early))
    return block, mates.index(tile)


def attn_kernel(raw_ref, g_ref, gain_ref, shift_ref, fam_ref, tab_ref, wqkv_ref, wo_ref, *rest, linked):
    hand, rest = (rest[:1], rest[1:]) if linked else ((), rest)
    dn_ref, sums_ref, gqkv_ref, go_ref, heads_ref = rest[:5]
    outs, rest = (rest[5:10], rest[10:]) if linked else ((), rest[5:])
    (x_s, xt_s, c_s, s_s, w_s, wo_s, q_s, k_s, v_s, do_s, kt_s, vt_s, ht_s, dqt_s, dk_s, dv_s, draw_s, dn_s, gq_s, go_s, heads_s,
     famr_s, famc_s, w_sem, wo_sem, gq_sem, go_sem, h_sem) = rest[:28]
    rest = rest[28:]
    step = pl.program_id(0)
    steps = len(ORDER)
    last = steps - 1
    n, d = raw_ref.shape
    lanes = 256
    pairs = d // 128
    slot = step % 2

    def weights(at, slot):
        out = []
        for half in range(2):
            pair = pick(at, [o[half] for o in ORDER])
            for kind in range(3):
                col = pl.multiple_of((kind * pairs + pair) * 128, 128)
                j = kind * 2 + half
                out.append(local_copy(wqkv_ref.at[:, pl.ds(col, 128)], w_s.at[slot, :, pl.ds(j * 128, 128)], w_sem.at[slot, j]))
            row = pl.multiple_of(pair * 128, 128)
            out.append(local_copy(wo_ref.at[pl.ds(row, 128), :], wo_s.at[slot, pl.ds(half * 128, 128), :], wo_sem.at[slot, half]))
        return out

    def results(at):
        out = []
        for half in range(2):
            pair = pick(at, [o[half] for o in ORDER])
            for kind in range(3):
                j = kind * 2 + half
                if linked:
                    col = pick(at, [block * 384 + rank * 128 for block, rank in (tile_place(kind * 8 + o[half]) for o in ORDER)])
                    to = gqkv_ref.at[at // 2, :, :, :, pl.ds(pl.multiple_of(col, 128), 128)]
                else:
                    to = gqkv_ref.at[:, :, :, pl.ds(pl.multiple_of((kind * pairs + pair) * 128, 128), 128)]
                out.append(local_copy(gq_s.at[:, :, :, pl.ds(j * 128, 128)], to, gq_sem.at[j]))
            out.append(local_copy(go_s.at[pl.ds(half * 128, 128), :], go_ref.at[pair // 2, pair % 2], go_sem.at[half]))
        return out

    if linked:
        place = Place()
        head_send, head_recv = rest[:2]
        rest = rest[2:]

        def heads_out(at):
            cols = pl.ds(pl.multiple_of(at * lanes, lanes), lanes)
            span = n // 4
            out = []
            for j, (to, device) in enumerate(place.peers):
                src = heads_s.at[pl.ds(pl.multiple_of(to * span, span), span), :]
                out.append(remote_copy(src, heads_ref.at[place.seq, :, cols], head_send.at[at, j], head_recv.at[at, j], device))
            mine = heads_s.at[pl.ds(pl.multiple_of(place.seq * span, span), span), :]
            return out, local_copy(mine, heads_ref.at[place.seq, :, cols], h_sem.at[0])

        def part_of(source, k, w):
            return lambda y, c: source.at[k, :, :, :, pl.ds(pl.multiple_of((y * 2 + c) * w, 128), w)]

        def done_at(k):
            def done(total):
                if k == 2:
                    outs[4][...] = total
                else:
                    outs[2 * k][...] = total[0:128]
                    outs[2 * k + 1][...] = total[128:256]
            return done

        cut = piece_count(AT_SPLIT)
        made = [Piece(place, part_of(hand[0], 2, 256), done_at(0), AT_SPLIT, rest[:cut]),
                Piece(place, part_of(hand[0], 3, 256), done_at(1), AT_SPLIT, rest[cut:2 * cut]),
                Piece(place, part_of(gqkv_ref, 0, 384), done_at(2), EARLY_SPLIT, rest[2 * cut:])]
        plan = {}
        for which, times in enumerate(AT_TICKS):
            for t, at in enumerate(times):
                plan.setdefault(at, []).append((which, t))
    else:
        plan = {}

    def tick(position):
        for at, what in sorted(plan.items()):
            if min(at // 6, last) * 6 + position == at:
                def run(what=what):
                    for which, t in sorted(what, key=lambda w: (-w[1], w[0])):
                        made[which].tick(t)
                pl.when(step == min(at // 6, last))(run)

    @pl.when(step == 0)
    def _():
        for copy in weights(0, 0):
            copy.start()
        if linked:
            place.greet()

    @pl.when(step > 0)
    def _():
        for copy in results(step - 1):
            copy.wait()

    tick(0)

    @pl.when(step == 0)
    def _():
        family = fam_ref[pl.ds(lax.axis_index("seq"), 1), :].astype(F32)
        famr_s[...] = family
        for m in range(n // 128):
            rows = slice(m * 128, m * 128 + 128)
            famc_s[rows, :] = jnp.broadcast_to(family[:, rows], (128, 128)).T
        for a in range(n // 32):
            rows = slice(a * 32, a * 32 + 32)
            ca, sa = tab_ref[0, a:a + 1, :], tab_ref[1, a:a + 1, :]
            cb, sb = tab_ref[2], tab_ref[3]
            c1 = ca * cb - sa * sb
            s1 = sa * cb + ca * sb
            lane = lax.broadcasted_iota(jnp.int32, c1.shape, 1) % HEAD_DIM
            c_s[rows, :] = jnp.where(lane < ROT, c1, 1.0)
            s_s[rows, :] = jnp.where(lane < ROT // 2, -s1, jnp.where(lane < ROT, s1, 0.0))
        @functools.partial(each_band, n // 256)
        def _(rows, m):
            xhat, _ = normalize(raw_ref[rows, :].astype(F32))
            normed = (xhat * gain_ref[...] + shift_ref[...]).astype(BF16)
            x_s[rows, :] = normed
            xt_s[:, rows] = normed.T

    @pl.when(step < last)
    def _():
        for copy in weights(step + 1, 1 - slot):
            copy.start()
    for copy in weights(step, slot):
        copy.wait()

    w_ref, wo1_ref = w_s.at[slot], wo_s.at[slot]
    scaling = HEAD_DIM ** -0.5

    def both(rows):
        c, s = c_s[rows, :], s_s[rows, :]
        return jnp.concatenate([c, c], 1), jnp.concatenate([s, s], 1)

    for m in range(n // 256):
        rows = slice(m * 256, m * 256 + 256)
        raw = dot(x_s[rows, :], w_ref[...])
        c, s = both(rows)
        q_s[rows, :] = (turn(raw[:, 0:lanes], c, s, 1.0) * scaling).astype(BF16)
        keys = turn(raw[:, lanes:2 * lanes], c, s, 1.0).astype(BF16)
        k_s[rows, :] = keys
        kt_s[:, rows] = keys.T
        vals = raw[:, 2 * lanes:].astype(BF16)
        v_s[rows, :] = vals
        vt_s[:, rows] = vals.T
        do_s[rows, :] = dot_nt(g_ref[rows, :], wo1_ref[...]).astype(BF16)

    tick(1)
    tile = TILE
    lane = lax.broadcasted_iota(jnp.int32, (tile, 128), 1)
    work = [(h, i) for i in reversed(range(n // tile)) for h in range(4)]

    def first(h, i):
        span = (i + 1) * tile
        here = slice(i * tile, span)
        cols = slice(h // 2 * 128, h // 2 * 128 + 128)
        mine = (lane < HEAD_DIM) if h % 2 == 0 else (lane >= HEAD_DIM)
        qh = jnp.where(mine, q_s[here, cols], 0).astype(BF16)
        doh = jnp.where(mine, do_s[here, cols], 0).astype(BF16)
        return qh, doh, dot_nt(k_s[0:span, cols], qh), dot_nt(v_s[0:span, cols], doh)

    def second(h, i, qh, doh, st, dpt):
        span = (i + 1) * tile
        here = slice(i * tile, span)
        cols = slice(h // 2 * 128, h // 2 * 128 + 128)
        rows = slice(h * HEAD_DIM, (h + 1) * HEAD_DIM)
        family = famc_s[0:span, :]
        allowed = jnp.concatenate([family] * (tile // 128), 1) == famr_s[:, here]
        key_place = lax.broadcasted_iota(jnp.int32, (span, tile), 0)
        query_place = lax.broadcasted_iota(jnp.int32, (span, tile), 1) + i * tile
        st = jnp.where(allowed & (key_place <= query_place), st, -1e9)
        e = jnp.exp(st - jnp.max(st, 0, keepdims=True))
        p = e * (1.0 / jnp.sum(e, 0, keepdims=True))
        pb = p.astype(BF16)
        ds = (p * (dpt - jnp.sum(p * dpt, 0, keepdims=True))).astype(BF16)
        ht_s[rows, here] = dot(vt_s[rows, 0:span], pb).astype(BF16)
        dqt_s[rows, here] = dot(kt_s[rows, 0:span], ds) * scaling
        dv = dot(pb, doh)
        dk = dot(ds, qh)
        if h % 2 == 0 and i == n // tile - 1:
            dv_s[:, cols] = dv
            dk_s[:, cols] = dk
        else:
            dv_s[0:span, cols] += dv
            dk_s[0:span, cols] += dk

    made_first = first(*work[0])
    for j, (h, i) in enumerate(work):
        later = first(*work[j + 1]) if j + 1 < len(work) else None
        second(h, i, *made_first)
        made_first = later
        if h == 3 and i != 1:
            tick({3: 2, 2: 3, 0: 4}[i])

    @pl.when(step > 0)
    def _():
        if linked:
            sent, mine = heads_out(step - 1)
            for copy in sent:
                copy.wait_send()
            mine.wait()
        else:
            local_copy(heads_s, heads_ref.at[:, pl.ds(pl.multiple_of((step - 1) * lanes, lanes), lanes)], h_sem.at[0]).wait()
    heads_s[...] = ht_s[...].T
    if linked:
        sent, mine = heads_out(step)
        for copy in sent:
            copy.start()
        mine.start()
    else:
        local_copy(heads_s, heads_ref.at[:, pl.ds(pl.multiple_of(step * lanes, lanes), lanes)], h_sem.at[0]).start()

    for m in range(n // 256):
        rows = slice(m * 256, m * 256 + 256)
        c, s = both(rows)
        draw_s[rows, 0:lanes] = turn(dqt_s[:, rows].T, c, s, -1.0).astype(BF16)
        draw_s[rows, lanes:2 * lanes] = turn(dk_s[rows, :], c, s, -1.0).astype(BF16)
        draw_s[rows, 2 * lanes:] = dv_s[rows, :].astype(BF16)

    for m in range(d // 256):
        grads = dot(xt_s[m * 256:(m + 1) * 256, :], draw_s[...]).astype(BF16)
        gq_s[m, 0] = grads[0:128]
        gq_s[m, 1] = grads[128:256]
    go_s[...] = dot(ht_s[...], g_ref[...]).astype(BF16)
    for copy in results(step):
        copy.start()
    tick(5)
    for m in range(n // 256):
        here = slice(m * 256, (m + 1) * 256)
        dn = dot_nt(draw_s[here, :], w_ref[...])

        @pl.when(step == 0)
        def _():
            dn_s[here, :] = dn

        @pl.when(step > 0)
        def _():
            dn_s[here, :] += dn

    @pl.when(step == last)
    def _():
        sums_ref[...] = jnp.zeros_like(sums_ref)

        @functools.partial(each_band, n // 256)
        def _(here, m):
            total = dn_s[here, :]
            xhat, _ = normalize(raw_ref[here, :].astype(F32))
            sums_ref[0:1, :] += jnp.sum(total * xhat, 0, keepdims=True)
            sums_ref[1:2, :] += jnp.sum(total, 0, keepdims=True)
            dn_ref[here, :] = total.astype(BF16)

    tick(6)

    @pl.when(step == last)
    def _():
        for copy in results(step):
            copy.wait()
        if linked:
            for at in range(steps):
                for copy in heads_out(at)[0]:
                    copy.wait_recv()
            for copy in heads_out(step)[0]:
                copy.wait_send()
            heads_out(step)[1].wait()
        else:
            local_copy(heads_s, heads_ref.at[:, pl.ds(pl.multiple_of(step * lanes, lanes), lanes)], h_sem.at[0]).wait()


def attend(raw, g, gain, shift, wqkv, wo, families, linked, grads=None):
    n, d = raw.shape
    pair_lane = np.arange(128) % HEAD_DIM % (ROT // 2)
    freq = 10000.0 ** (-2.0 * pair_lane / ROT)
    high, low = np.arange(n // 32)[:, None] * 32.0 * freq, np.arange(32)[:, None] * freq
    tab = jnp.asarray(np.stack([np.cos(high), np.sin(high), np.cos(low), np.sin(low)]), F32)
    sd, vm = jax.ShapeDtypeStruct, pltpu.VMEM
    out_shape = [sd((n, d), BF16), sd((8, d), F32), sd((2, 4, 2, 128, 3 * d // 2) if linked else (4, 2, 128, 3 * d), BF16),
                 sd((4, 2, 128, d), BF16), sd((4, n // 4, d) if linked else (n, d), BF16)]
    out_specs = [whole((n, d)), whole((8, d))] + [ANYWHERE] * 3
    scratch = [vm((n, d), BF16), vm((d, n), BF16), vm((n, 128), F32), vm((n, 128), F32), vm((2, d, 768), BF16), vm((2, 256, d), BF16)]
    scratch += [vm((n, 256), BF16)] * 4 + [vm((256, n), BF16)] * 3
    scratch += [vm((256, n), F32), vm((n, 256), F32), vm((n, 256), F32), vm((n, 768), BF16), vm((n, d), F32), vm((4, 2, 128, 768), BF16),
                vm((256, d), BF16), vm((n, 256), BF16), vm((1, n), F32), vm((n, 128), F32), DMA((2, 6)), DMA((2, 2)), DMA((6,)), DMA((2,)), DMA((1,))]
    params, more = {}, []
    if linked:
        more = [grads]
        out_shape += [sd((128, 256), F32)] * 4 + [sd((128, 384), F32)]
        out_specs += [whole((128, 256))] * 4 + [whole((128, 384))]
        scratch += [DMA((4, 3)), DMA((4, 3))]
        scratch += piece_scratch(256, AT_SPLIT) * 2 + piece_scratch(384, EARLY_SPLIT)
        params = dict(collective_id=1, has_side_effects=True)
    return pl.pallas_call(
        functools.partial(attn_kernel, linked=linked), out_shape=out_shape, grid=(len(ORDER),),
        in_specs=[whole((n, d)), whole((n, d)), whole((1, d)), whole((1, d)), whole(families.shape), whole((4, 32, 128)), ANYWHERE, ANYWHERE]
        + [ANYWHERE] * len(more),
        out_specs=out_specs, scratch_shapes=scratch,
        compiler_params=pltpu.CompilerParams(vmem_limit_bytes=60 * 2**20, **params),
        cost_estimate=pl.CostEstimate(flops=70_000_000_000, bytes_accessed=30_000_000, transcendentals=20_000_000),
    )(raw, g, gain.reshape(1, d), shift.reshape(1, d), families, tab, wqkv, wo, *more)


class SmallSum:
    def __init__(self, place, held, heard, by_z, send, recv):
        self.p, self.held, self.heard, self.by_z, self.send, self.recv = place, held, heard, by_z, send, recv

    def copies(self, t):
        p = self.p
        if t < 3:
            to = (p.twin, p.beside_y, p.beside_x)[t]
            return [remote_copy(self.held, self.heard.at[t], self.send.at[t], self.recv.at[t], to)]
        return [remote_copy(self.by_z.at[p.z], self.by_z.at[p.z], self.send.at[3 + j], self.recv.at[3 + j], to)
                for j, to in enumerate(p.along_z)]

    def tick(self, t):
        if t > 0:
            for copy in self.copies(t - 1):
                copy.wait()
        if 0 < t < 4:
            total = self.held[...] + self.heard[t - 1]
            if t < 3:
                self.held[...] = total
            else:
                self.by_z[self.p.z] = total
        if t < 4:
            for copy in self.copies(t):
                copy.start()
        return None if t < 4 else self.by_z[0] + self.by_z[1] + self.by_z[2] + self.by_z[3]


def tail_kernel(dat_ref, heads_ref, gq_ref, go_ref, inp_ref, cot_ref, y_ref, dn_ref, wo_ref, part_ref, gain_ref, dbias_ref, sums_ff_ref, sums_at_ref,
                ub_ref, early_ref, lo_ref, ig_ref, qkv_ref, out_ref, gain_o, shift_o, ub_o, db_o,
                back_s, inp_s, g_s, heads_s, y_s, dn_s, wo_s, lo_s, ig_s, small_s, heard_s, by_z_s,
                load_sem, wo_sem, back_send, back_recv, own_sem, small_send, small_recv, lo_sem, ig_sem, *pieces):
    place = Place()
    d = wo_s.shape[0]
    place.greet()
    swaps = [remote_copy(dat_ref.at[to], back_s.at[place.seq], back_send.at[j], back_recv.at[j], device)
             for j, (to, device) in enumerate(place.peers)]
    own = local_copy(dat_ref.at[place.seq], back_s.at[place.seq], own_sem.at[0])
    blocks = {}

    def part(source, w, row0, rows):
        return lambda y, c: source.at[:, :, pl.ds(row0, rows), pl.ds(pl.multiple_of((y * 2 + c) * w, 128), w)]

    def out_done(total):
        out_ref[...] = total

    def qkv_done(row0):
        def done(total):
            rows = slice(row0, row0 + total.shape[0])
            early = early_ref[rows, :]
            first = jnp.where(place.c == 0, early, total)
            second = jnp.where(place.c == 0, total, early)
            order = ((first, 0), (second, 0), (second, 1), (first, 1), (first, 2), (second, 2))
            for k, (source, at) in enumerate(order):
                qkv_ref[rows, k * 128:(k + 1) * 128] = source[:, at * 128:(at + 1) * 128]
        return done

    cuts = [0, piece_count(TAIL_SPLITS[0])]
    for split in TAIL_SPLITS[1:]:
        cuts.append(cuts[-1] + piece_count(split))
    late = gq_ref.at[1]
    row1 = sum(TAIL_SPLITS[1])
    made = [Piece(place, part(go_ref, 256, 0, 128), out_done, TAIL_SPLITS[0], pieces[:cuts[1]]),
            Piece(place, part(late, 384, 0, row1), qkv_done(0), TAIL_SPLITS[1], pieces[cuts[1]:cuts[2]]),
            Piece(place, part(late, 384, row1, 128 - row1), qkv_done(row1), TAIL_SPLITS[2], pieces[cuts[2]:])]
    small = SmallSum(place, small_s, heard_s, by_z_s, small_send, small_recv)
    small_s[0:3, :] = sums_ff_ref[0:3, :]
    small_s[0:2, :] += sums_at_ref[0:2, :]
    small_s[3:4, :] = jnp.zeros((1, d), F32)
    for k in range(4):
        small_s[4 + k:5 + k, :] = ub_ref[:, k * d:(k + 1) * d]
    for piece in made:
        piece.tick(0)
    for copy in swaps:
        copy.start()
    small.tick(0)
    loads = [local_copy(a, b, load_sem.at[k]) for k, (a, b) in enumerate(
        ((heads_ref, heads_s), (inp_ref, inp_s), (y_ref, y_s), (cot_ref, g_s), (dn_ref, dn_s)))]
    for pair in range(d // 128):
        at = [p for two in ORDER for p in two].index(pair)
        blocks[at] = local_copy(wo_ref.at[pl.ds(pair * 128, 128), :], wo_s.at[pl.ds(at * 128, 128), :], wo_sem.at[at])
    for copy in [loads[0]] + list(blocks.values()) + loads[1:] + [own]:
        copy.start()

    def lo_out(r):
        return local_copy(lo_s.at[r], lo_ref.at[r], lo_sem.at[r])

    def ig_out(r):
        return local_copy(ig_s.at[r], ig_ref.at[r], ig_sem.at[r])

    def forward(r, carry):
        total = inp_s[r].astype(F32) + dot(heads_s[r], wo_s[...]) + (y_s[r] + dbias_ref[...])
        lo_s[r] = total.astype(BF16)
        lo_out(r).start()
        return carry

    def backward(r):
        xhat, scale = normalize(inp_s[r].astype(F32))
        dx = (dn_s[r] + back_s[r].astype(F32)) * gain_ref[...]
        ig_s[r] = g_s[lax.rem(part_ref[r], 4)].astype(F32) + (dx - jnp.mean(dx, -1, keepdims=True) - xhat * jnp.mean(dx * xhat, -1, keepdims=True)) * scale
        ig_out(r).start()

    made[0].tick(1)
    small.tick(1)
    for copy in list(blocks.values()) + loads[:3]:
        copy.wait()
    lax.fori_loop(0, 2, forward, 0)
    made[1].tick(1)
    lax.fori_loop(2, 4, forward, 0)
    made[0].tick(2)
    made[2].tick(1)
    small.tick(2)
    loads[3].wait()
    loads[4].wait()
    own.wait()
    backward(place.seq)
    made[1].tick(2)
    made[0].tick(3)
    small.tick(3)
    for j in range(3):
        swaps[j].wait_send()
    swaps[2].wait_recv()
    backward((place.seq + 1) % 4)
    made[2].tick(2)
    made[1].tick(3)
    swaps[1].wait_recv()
    backward((place.seq + 2) % 4)
    made[2].tick(3)
    swaps[0].wait_recv()
    backward((place.seq + 3) % 4)
    total = small.tick(4)
    for piece in made:
        piece.tick(4)
    gain_o[...] = total[0:1]
    shift_o[...] = total[1:2]
    db_o[...] = total[2:3]
    for k in range(4):
        ub_o[:, k * d:(k + 1) * d] = total[4 + k:5 + k]
    for r in range(4):
        lo_out(r).wait()
        ig_out(r).wait()


def finish(dat, heads, gq, go, inp, cot, y, dn, wo, partners, gain, dbias, sums_ff, sums_at, ub, early):
    sd, vm = jax.ShapeDtypeStruct, pltpu.VMEM
    shape, d = inp.shape, inp.shape[2]
    vmem = pl.BlockSpec(memory_space=pltpu.VMEM)
    return pl.pallas_call(
        tail_kernel,
        out_shape=[sd(shape, BF16), sd(shape, F32), sd((128, 768), F32), sd((128, 256), F32), sd((1, d), F32), sd((1, d), F32), sd((1, 4 * d), F32),
                   sd((1, d), F32)],
        in_specs=[ANYWHERE] * 9 + [pl.BlockSpec(memory_space=pltpu.SMEM)] + [vmem] * 6, out_specs=[ANYWHERE] * 2 + [vmem] * 6,
        scratch_shapes=[vm(shape, BF16)] * 4 + [vm(shape, F32)] * 2 + [vm((d, d), BF16), vm(shape, BF16), vm(shape, F32),
                        vm((8, d), F32), vm((3, 8, d), F32), vm((4, 8, d), F32),
                        DMA((5,)), DMA((8,)), DMA((3,)), DMA((3,)), DMA((1,)), DMA((6,)), DMA((6,)), DMA((4,)), DMA((4,))]
        + piece_scratch(256, TAIL_SPLITS[0]) + piece_scratch(384, TAIL_SPLITS[1]) + piece_scratch(384, TAIL_SPLITS[2]),
        compiler_params=pltpu.CompilerParams(collective_id=2, has_side_effects=True, vmem_limit_bytes=56 * 2**20),
    )(dat.reshape(shape), heads, gq, go, inp, cot, y.reshape(shape), dn.reshape(shape), wo, partners, gain.reshape(1, d), dbias.reshape(1, d), sums_ff, sums_at,
      ub, early)


def copy_kernel(*refs):
    (lo, ig, qkv, out, gain, shift, ub, db), ups, downs = refs[:8], refs[8:12], refs[12:16]
    lo_o, ig_o, qkv_o, out_o, gain_o, shift_o, ub_o, db_o, up_o, down_o = refs[16:]
    lo_o[...] = lo[...]
    ig_o[...] = ig[...]

    @pl.when(pl.program_id(0) == 0)
    def _():
        for to, source in ((qkv_o, qkv), (out_o, out), (gain_o, gain), (shift_o, shift), (ub_o, ub), (db_o, db)):
            to[...] = source[...]
        for k in range(4):
            up_o[:, k * 128:(k + 1) * 128] = ups[k][:, 0:128]
            up_o[:, 512 + k * 128:512 + (k + 1) * 128] = ups[k][:, 128:256]
            down_o[k * 128:(k + 1) * 128, :] = downs[k][...]


def gather_up(*parts):
    sd, shape = jax.ShapeDtypeStruct, parts[0].shape
    flat = [(shape[0] * shape[1], shape[2])] * 2 + [p.shape for p in parts[2:]]
    band = pl.BlockSpec((128, shape[2]), lambda p: (p, 0))
    outs = flat[:8] + [(128, 1024), (512, 256)]
    return pl.pallas_call(
        copy_kernel, out_shape=[sd(s, BF16 if k == 0 else F32) for k, s in enumerate(outs)], grid=(flat[0][0] // 128,),
        in_specs=[band, band] + [whole(s) for s in flat[2:]], out_specs=[band, band] + [whole(s) for s in outs[2:]],
        compiler_params=pltpu.CompilerParams(vmem_limit_bytes=32 * 2**20),
    )(*[p.reshape(s) for p, s in zip(parts, flat)])


def on_device(inputs, norm_gain, norm_shift, qkv_weight, out_weight, up_weight, up_bias, down_weight, down_bias, partners, families, cotangent, linked):
    row_count, place_count, width = inputs.shape
    tokens = row_count * place_count
    branch_args = norm_gain, norm_shift, qkv_weight, out_weight, families, linked
    if linked:
        y, dn, sums_ff, ub, grads, row_inputs, row_grad, up0, down0, up1, down1 = feed_forward(
            inputs, cotangent, partners, norm_gain, norm_shift, up_bias, up_weight, down_weight, True)
        dat, sums_at, gq, go, heads, up2, down2, up3, down3, early = attend(
            row_inputs.reshape(tokens, width), row_grad.reshape(tokens, width), *branch_args, grads)
        layer_out, input_grad, qkv_sum, out_sum, gain_sum, shift_sum, ub_sum, db_sum = finish(
            dat, heads, gq, go, inputs, cotangent, y, dn, out_weight, partners, norm_gain, down_bias, sums_ff, sums_at, ub, early)
        layer_out, input_grad, qkv_sum, out_sum, gain_sum, shift_sum, ub_sum, db_sum, up_sum, down_sum = gather_up(
            layer_out, input_grad, qkv_sum, out_sum, gain_sum, shift_sum, ub_sum, db_sum, up0, up1, up2, up3, down0, down1, down2, down3)
        return (layer_out.reshape(inputs.shape), input_grad.reshape(inputs.shape), gain_sum.reshape(width), shift_sum.reshape(width), qkv_sum, out_sum,
                up_sum, ub_sum.reshape(-1), down_sum, db_sum.reshape(width))
    local_rows = partners - lax.axis_index("dp") * row_count
    grad = jnp.take(cotangent, local_rows, axis=0, mode="clip")
    swap = functools.partial(lax.all_to_all, axis_name="seq", split_axis=0, concat_axis=0, tiled=True)
    row_inputs, row_grad = swap(inputs).reshape(tokens, width), swap(grad).reshape(tokens, width)
    y, dn, sums_ff, ub, up_grad, down_grad = feed_forward(
        inputs, cotangent, partners, norm_gain, norm_shift, up_bias, up_weight, down_weight, False)
    dat, sums_at, qkv_grad, out_grad, heads = attend(row_inputs, row_grad, *branch_args)

    def scatter(parts, columns):
        part = lax.psum_scatter(parts.reshape(-1, columns), "seq", scatter_dimension=1, tiled=True)
        return lax.psum_scatter(part, "dp", scatter_dimension=0, tiled=True).astype(F32)

    qkv_sum, out_sum = scatter(qkv_grad, 3 * width), scatter(out_grad, width)
    up_sum, down_sum = scatter(up_grad, up_bias.shape[0]), scatter(down_grad, width)
    heads = swap(heads.reshape(inputs.shape)).reshape(tokens, width)
    order = np.array([p for two in ORDER for p in two])
    attn_out = dot(heads, out_weight.reshape(-1, 128, width)[order].reshape(width, width))
    values = inputs.astype(F32).reshape(tokens, width)
    layer_out = (values + attn_out + (y + down_bias)).astype(BF16).reshape(inputs.shape)
    xhat, scale = normalize(values)
    dx = (dn + swap(dat.reshape(inputs.shape)).reshape(tokens, width).astype(F32)) * norm_gain
    input_grad = grad.reshape(tokens, width).astype(F32) + (dx - jnp.mean(dx, -1, keepdims=True) - xhat * jnp.mean(dx * xhat, -1, keepdims=True)) * scale
    gain_sum, shift_sum, up_bias_sum, down_bias_sum = lax.psum((sums_ff[0] + sums_at[0], sums_ff[1] + sums_at[1], ub[0], sums_ff[2]), ("dp", "seq"))
    return (layer_out, input_grad.reshape(inputs.shape), gain_sum, shift_sum, qkv_sum, out_sum, up_sum, up_bias_sum, down_sum, down_bias_sum)


def solution(mesh):
    rows = P("dp", "seq", None)
    placed = (rows,) + (P(),) * 8 + (P("dp"), P("dp", None), rows)
    grads = P("dp", "seq")
    linked = (mesh.shape["dp"], mesh.shape["seq"]) == (8, 4)
    return jax.shard_map(functools.partial(on_device, linked=linked), mesh=mesh, in_specs=placed,
                         out_specs=(rows, rows, P(), P(), grads, grads, grads, P(), grads, P()), check_vma=False)
```

```python
import functools

import jax
import jax.numpy as jnp
import numpy as np
from jax import lax
from jax.experimental import pallas as pl
from jax.experimental.pallas import tpu as pltpu
from jax.sharding import PartitionSpec as P

F32 = jnp.float32
BF16 = jnp.bfloat16
HEAD_DIM = 64
ROT = 32
EPS = 1e-05
C0 = 0.7978845608028654
C1 = C0 * 0.044715
TILE = 256
FF_SPLITS = (0, 176, 80), (96, 112, 48)
AT_SPLIT = 96, 112, 48
EARLY_SPLIT = 48, 64, 16
TAIL_SPLITS = (0, 80, 48), (0, 48, 16), (0, 32, 32)
FF_TICKS = (6, 9, 15, 18, 22), (12, 15, 20, 22, 24)
AT_TICKS = (0, 2, 7, 10, 14), (4, 7, 12, 15, 19), (13, 15, 19, 21, 24)
ORDER = ((0, 3), (4, 7), (1, 2), (5, 6))
MESH_ID = pl.DeviceIdType.MESH
ANYWHERE = pl.BlockSpec(memory_space=pl.ANY)
DMA = pltpu.SemaphoreType.DMA


def dot(a, b):
    return lax.dot_general(a, b, (((1,), (0,)), ((), ())), preferred_element_type=F32)


def dot_nt(a, b):
    return lax.dot_general(a, b, (((1,), (1,)), ((), ())), preferred_element_type=F32)


def dot_tn(a, b):
    return lax.dot_general(a, b, (((0,), (0,)), ((), ())), preferred_element_type=F32)


def whole(shape):
    return pl.BlockSpec(shape, lambda p: (0,) * len(shape), pipeline_mode=pl.Buffered(1))


def pick(step, values):
    out = jnp.int32(values[0])
    for i, value in enumerate(values[1:], 1):
        out = jnp.where(step == i, value, out)
    return out


def normalize(values):
    centered = values - jnp.mean(values, -1, keepdims=True)
    scale = lax.rsqrt(jnp.mean(centered * centered, -1, keepdims=True) + EPS)
    return centered * scale, scale


def each_band(count, body):
    def step(m, carry):
        body(pl.ds(pl.multiple_of(m * 256, 256), 256), m)
        return carry

    lax.fori_loop(0, count, step, 0)


def local_copy(src, dst, sem):
    return pltpu.make_async_copy(src, dst, sem)


def remote_copy(src, dst, send, recv, to):
    return pltpu.make_async_remote_copy(src_ref=src, dst_ref=dst, send_sem=send, recv_sem=recv, device_id=to,
                                        device_id_type=MESH_ID)


class Place:
    def __init__(self):
        self.dp, self.seq = lax.axis_index("dp"), lax.axis_index("seq")
        self.z, self.x, self.y, self.c = self.dp // 2, self.dp % 2, self.seq // 2, self.seq % 2
        self.twin = (self.dp, self.y * 2 + 1 - self.c)
        self.beside_y = (self.dp, (1 - self.y) * 2 + self.c)
        self.across = (self.dp, (1 - self.y) * 2 + 1 - self.c)
        self.beside_x = (self.z * 2 + 1 - self.x, self.seq)
        self.along_z = [(((self.z + j) % 4) * 2 + self.x, self.seq) for j in (1, 2, 3)]
        self.peers = [((self.seq + j) % 4, (self.dp, (self.seq + j) % 4)) for j in (1, 2, 3)]
        self.partners = [self.twin, self.beside_y, self.beside_x] + self.along_z

    def greet(self):
        barrier = pltpu.get_barrier_semaphore()
        for partner in self.partners + [self.across]:
            pl.semaphore_signal(barrier, inc=1, device_id=partner, device_id_type=MESH_ID)
        pl.semaphore_wait(barrier, len(self.partners) + 1)


def add_into(dst, src, lead):
    rows, w = src.shape[-2:]
    band = rows
    while band * w > 65536 and band % 32 == 0:
        band //= 2
    count = 1
    for n in lead:
        count *= n

    def body(t, carry):
        block, part = t // (rows // band), t % (rows // band)
        index = []
        for n in reversed(lead):
            index.insert(0, block % n)
            block = block // n
        at = tuple(index) + (pl.ds(pl.multiple_of(part * band, band), band), slice(None))
        dst[at] = dst[at] + src[at]
        return carry

    lax.fori_loop(0, count * (rows // band), body, 0)


def piece_scratch(w, split):
    ra, rb, rc = split
    r = sum(split)
    out = [((2, 4, 2, r), 1), ((2, 4, 2, r), 1), ((4, 2, ra), ra), ((2, 4, rb), rb), ((3, 2, 2, rc), rc), ((4, ra), ra), ((4, rb), rb), ((2, rc), rc),
           ((3, ra + rb), ra + rb), ((rc,), rc)]
    return [pltpu.VMEM(shape + (w,), BF16) for shape, used in out if used] + [DMA((14,)), DMA((14,)), DMA((2,))]


def piece_count(split):
    return len(piece_scratch(128, split))


class Piece:
    def __init__(self, place, part, done, split, scratch):
        self.p, self.part, self.done, self.split = place, part, done, split
        ra, rb, rc = split
        names = [("a", 1), ("from_twin", 1), ("ya", ra), ("xb", rb), ("zc", rc), ("xa", ra), ("yb", rb), ("xc", rc), ("zab", ra + rb), ("yc", rc)]
        scratch = list(scratch)
        for name, used in names:
            setattr(self, name, scratch.pop(0) if used else None)
        self.ss, self.rs, self.ls = scratch
        self.rows_a, self.rows_b, self.rows_ab, self.rows_c = pl.ds(0, ra), pl.ds(ra, rb), pl.ds(0, ra + rb), pl.ds(ra + rb, rc)

    def copies(self, stage):
        p, a, (ra, rb, rc) = self.p, self.a, self.split
        out = []
        slot = (0, 2, 7, 10)[stage]

        def send(src, dst, to):
            k = slot + len(out)
            out.append(remote_copy(src, dst, self.ss.at[k], self.rs.at[k], to))

        zs = [((p.z + 1 + j) % 4, p.along_z[j]) for j in range(3)]
        if stage == 0:
            for k in (0, 1):
                send(self.part(k, 1 - p.c), self.from_twin.at[k], p.twin)
        if stage == 1:
            if ra:
                send(a.at[1 - p.y, :, :, self.rows_a, :], self.ya, p.beside_y)
            if rb:
                send(a.at[:, :, 1 - p.x, self.rows_b, :], self.xb, p.beside_x)
            for j in range(3 if rc else 0):
                send(a.at[:, zs[j][0], :, self.rows_c, :], self.zc.at[j], zs[j][1])
        if stage == 2:
            if ra:
                send(a.at[p.y, :, 1 - p.x, self.rows_a, :], self.xa, p.beside_x)
            if rb:
                send(a.at[1 - p.y, :, p.x, self.rows_b, :], self.yb, p.beside_y)
            if rc:
                send(a.at[:, p.z, 1 - p.x, self.rows_c, :], self.xc, p.beside_x)
        if stage == 3:
            for j in range(3 if ra + rb else 0):
                send(a.at[p.y, zs[j][0], p.x, self.rows_ab, :], self.zab.at[j], zs[j][1])
            if rc:
                send(a.at[1 - p.y, p.z, p.x, self.rows_c, :], self.yc, p.beside_y)
        return out

    def own(self):
        return [local_copy(self.part(k, self.p.c), self.a.at[k], self.ls.at[k]) for k in (0, 1)]

    def tick(self, t):
        p, a, (ra, rb, rc) = self.p, self.a, self.split
        if t > 0:
            for copy in self.copies(t - 1):
                copy.wait()
        if t == 0:
            for copy in self.copies(0) + self.own():
                copy.start()
        if t == 1:
            for copy in self.own():
                copy.wait()
            add_into(a, self.from_twin, (2, 4, 2))
        if t == 2:
            if ra:
                add_into(a.at[p.y, :, :, self.rows_a, :], self.ya, (4, 2))
            if rb:
                add_into(a.at[:, :, p.x, self.rows_b, :], self.xb, (2, 4))
            for j in range(3 if rc else 0):
                add_into(a.at[:, p.z, :, self.rows_c, :], self.zc.at[j], (2, 2))
        if t == 3:
            if ra:
                add_into(a.at[p.y, :, p.x, self.rows_a, :], self.xa, (4,))
            if rb:
                add_into(a.at[p.y, :, p.x, self.rows_b, :], self.yb, (4,))
            if rc:
                add_into(a.at[:, p.z, p.x, self.rows_c, :], self.xc, (2,))
        if t in (1, 2, 3):
            for copy in self.copies(t):
                copy.start()
        if t == 4:
            mine = a.at[p.y, p.z, p.x]
            parts = []
            if ra + rb:
                total = mine[self.rows_ab, :].astype(F32)
                for j in range(3):
                    total += self.zab[j].astype(F32)
                parts.append(total)
            if rc:
                parts.append(mine[self.rows_c, :].astype(F32) + self.yc[...].astype(F32))
            self.done(jnp.concatenate(parts, 0) if len(parts) > 1 else parts[0])


def ff_kernel(part_ref, inp_ref, cot_ref, gain_ref, shift_ref, bias_ref, wu_ref, wd_ref, *rest, linked):
    hand, rest = (rest[:1], rest[1:]) if linked else ((), rest)
    y_ref, dn_ref, sums_ref, ub_ref = rest[:4]
    outs, rest = (rest[4:11], rest[11:]) if linked else (rest[4:6], rest[6:])
    x_s, xt_s, act_s, dh_s, wu_s, wd_s, gu_s, gd_s, g_ref, wu_sem, wd_sem, gu_sem, gd_sem = rest[:13]
    rest = rest[13:]
    step = pl.program_id(0)
    last = pl.num_programs(0) - 1
    n, d = x_s.shape
    hidden = bias_ref.shape[1]
    group = hidden // 8
    tile = 512
    slot = step % 2

    def places(at):
        k, j = at // 2, at % 2
        return [(s, (2 * s + j) * group + k * 128) for s in range(4)]

    def weights(at, slot):
        out = []
        for s, f in places(at):
            f = pl.multiple_of(f, 128)
            out.append(local_copy(wu_ref.at[:, pl.ds(f, 128)], wu_s.at[slot, :, pl.ds(s * 128, 128)], wu_sem.at[slot, s]))
            out.append(local_copy(wd_ref.at[pl.ds(f, 128), :], wd_s.at[slot, pl.ds(s * 128, 128), :], wd_sem.at[slot, s]))
        return out

    def results(at):
        out = []
        k, j = at // 2, at % 2
        for s, f in places(at):
            f = pl.multiple_of(f, 128)
            up, down = gu_s.at[:, :, :, pl.ds(s * 128, 128)], gd_s.at[pl.ds(s * 128, 128), :]
            if linked:
                col = pl.multiple_of(s * 256 + j * 128, 128)
                to = outs[0].at[k, :, :, pl.ds(0, 128), pl.ds(col, 128)], outs[0].at[k, s, j, pl.ds(128, 128), :]
            else:
                to = outs[0].at[:, :, :, pl.ds(f, 128)], outs[1].at[pl.ds(f, 128), :]
            out.append(local_copy(up, to[0], gu_sem.at[s]))
            out.append(local_copy(down, to[1], gd_sem.at[s]))
        return out

    if linked:
        place = Place()
        row_send, row_recv, own_sem = rest[:3]
        rest = rest[3:]

        def swaps(a):
            span = n // 4

            def row(at):
                return g_ref.at[pl.ds(pl.multiple_of(at * span, span), span), :] if a else hand[0].at[at]

            out = [remote_copy(row(to), outs[1 + a].at[place.seq], row_send.at[a, j], row_recv.at[a, j], device)
                   for j, (to, device) in enumerate(place.peers)]
            return out + [local_copy(row(place.seq), outs[1 + a].at[place.seq], own_sem.at[a])]

        def part_of(k):
            return lambda y, c: outs[0].at[k, :, :, :, pl.ds(pl.multiple_of((y * 2 + c) * 256, 256), 256)]

        def done_at(k):
            def done(total):
                outs[3 + 2 * k][...] = total[0:128]
                outs[4 + 2 * k][...] = total[128:256]
            return done

        cut = piece_count(FF_SPLITS[0])
        made = [Piece(place, part_of(k), done_at(k), FF_SPLITS[k], (rest[:cut], rest[cut:])[k]) for k in range(2)]

    def tick(position):
        for which, times in enumerate(FF_TICKS if linked else ()):
            for t, at in enumerate(times):
                if min(at // 3, 7) * 3 + position == at:
                    pl.when(step == min(at // 3, 7))(functools.partial(made[which].tick, t))

    @pl.when(step == 0)
    def _():
        for copy in weights(0, 0):
            copy.start()
        if linked:
            place.greet()
            for copy in swaps(0):
                copy.start()
        count, span, _ = cot_ref.shape
        for r in range(count):
            g_ref[r * span:(r + 1) * span, :] = cot_ref[lax.rem(part_ref[r], count)]
        if linked:
            for copy in swaps(1):
                copy.start()
        sums_ref[...] = jnp.zeros_like(sums_ref)

        @functools.partial(each_band, n // 256)
        def _(rows, m):
            xhat, _ = normalize(inp_ref[rows, :].astype(F32))
            normed = (xhat * gain_ref[...] + shift_ref[...]).astype(BF16)
            x_s[rows, :] = normed
            xt_s[:, rows] = normed.T
            sums_ref[2:3, :] += jnp.sum(g_ref[rows, :].astype(F32), 0, keepdims=True)

    @pl.when(step > 0)
    def _():
        for copy in results(step - 1):
            copy.wait()

    tick(0)

    @pl.when(step < last)
    def _():
        for copy in weights(step + 1, 1 - slot):
            copy.start()
    for copy in weights(step, slot):
        copy.wait()
    w_up, w_down = wu_s.at[slot], wd_s.at[slot]
    bias = jnp.concatenate([bias_ref[:, pl.ds(pl.multiple_of(f, 128), 128)] for _, f in places(step)], 1)
    unit_sums = None
    for m in range(n // tile):
        here = slice(m * tile, (m + 1) * tile)
        v = dot(x_s[here, :], w_up[...]) + bias
        vv = v * v
        a = 0.5 + 0.5 * jnp.tanh(v * (C0 + C1 * vv))
        act = v * a
        slope = a + act * (1.0 - a) * (2 * C0 + 6 * C1 * vv)
        act_s[here, :] = act.astype(BF16)
        dh = (dot_nt(g_ref[here, :], w_down[...]) * slope).astype(BF16)
        dh_s[here, :] = dh
        total = jnp.sum(dh.astype(F32), 0, keepdims=True)
        unit_sums = total if unit_sums is None else unit_sums + total
    for s, f in places(step):
        ub_ref[:, pl.ds(pl.multiple_of(f, 128), 128)] = unit_sums[:, s * 128:(s + 1) * 128]

    tick(1)
    for m in range(d // 256):
        grads = dot(xt_s[m * 256:(m + 1) * 256, :], dh_s[...]).astype(BF16)
        gu_s[m, 0] = grads[0:128]
        gu_s[m, 1] = grads[128:256]
    gd_s[...] = dot_tn(act_s[...], g_ref[...]).astype(BF16)
    for copy in results(step):
        copy.start()
    tick(2)
    for m in range(n // tile):
        here = slice(m * tile, (m + 1) * tile)
        y = dot(act_s[here, :], w_down[...])
        dn = dot_nt(dh_s[here, :], w_up[...])

        @pl.when(step == 0)
        def _():
            y_ref[here, :] = y
            dn_ref[here, :] = dn

        @pl.when(step > 0)
        def _():
            y_ref[here, :] += y
            dn_ref[here, :] += dn

    tick(3)

    @pl.when(step == last)
    def _():
        @functools.partial(each_band, n // 256)
        def _(here, m):
            total = dn_ref[here, :]
            xhat, _ = normalize(inp_ref[here, :].astype(F32))
            sums_ref[0:1, :] += jnp.sum(total * xhat, 0, keepdims=True)
            sums_ref[1:2, :] += jnp.sum(total, 0, keepdims=True)

        for copy in results(step):
            copy.wait()
        if linked:
            for copy in swaps(0) + swaps(1):
                copy.wait()


def feed_forward(inp, cot, partners, gain, shift, bias, wu, wd, linked):
    rows, span, d = inp.shape
    n, hidden = rows * span, bias.shape[0]
    sd, vm = jax.ShapeDtypeStruct, pltpu.VMEM
    out_shape = [sd((n, d), F32), sd((n, d), F32), sd((8, d), F32), sd((1, hidden), F32)]
    out_specs = [whole((n, d)), whole((n, d)), whole((8, d)), whole((1, hidden))]
    scratch = [vm((n, d), BF16), vm((d, n), BF16), vm((n, 512), BF16), vm((n, 512), BF16), vm((2, d, 512), BF16), vm((2, 512, d), BF16),
               vm((4, 2, 128, 512), BF16), vm((512, d), BF16), vm((n, d), BF16), DMA((2, 4)), DMA((2, 4)), DMA((4,)), DMA((4,))]
    more, params = [], {}
    if linked:
        more = [inp]
        out_shape += [sd((4, 4, 2, 256, d), BF16), sd(inp.shape, BF16), sd(inp.shape, BF16), *[sd((128, 256), F32)] * 4]
        out_specs += [ANYWHERE] * 3 + [whole((128, 256))] * 4
        scratch += [DMA((2, 3)), DMA((2, 3)), DMA((2,))] + piece_scratch(256, FF_SPLITS[0]) + piece_scratch(256, FF_SPLITS[1])
        params = dict(collective_id=0, has_side_effects=True)
    else:
        out_shape += [sd((4, 2, 128, hidden), BF16), sd((hidden, d), BF16)]
        out_specs += [ANYWHERE] * 2
    return pl.pallas_call(
        functools.partial(ff_kernel, linked=linked), out_shape=out_shape, grid=(hidden // 512,),
        in_specs=[pl.BlockSpec(memory_space=pltpu.SMEM), whole((n, d)), whole(cot.shape), whole((1, d)), whole((1, d)), whole((1, hidden)), ANYWHERE, ANYWHERE] + [ANYWHERE] * len(more),
        out_specs=out_specs, scratch_shapes=scratch,
        compiler_params=pltpu.CompilerParams(vmem_limit_bytes=58 * 2**20, **params),
        cost_estimate=pl.CostEstimate(flops=52_000_000_000, bytes_accessed=50_000_000, transcendentals=4_000_000),
    )(partners, inp.reshape(n, d), cot, gain.reshape(1, d), shift.reshape(1, d), bias.reshape(1, hidden), wu, wd, *more)


def turn(x, c, s, sign):
    lanes = x.shape[1]
    lane = lax.broadcasted_iota(jnp.int32, x.shape, 1) % HEAD_DIM
    other = jnp.where(lane < ROT // 2, pltpu.roll(x, lanes - ROT // 2, 1), pltpu.roll(x, ROT // 2, 1))
    return x * c + (sign * other) * s


def tile_place(tile):
    early = [kind * 8 + pair for two in ORDER[:2] for pair in two for kind in range(3)]
    block = tile // 6
    mates = sorted(t for t in range(24) if t // 6 == block and (t in early) == (tile in early))
    return block, mates.index(tile)


def attn_kernel(raw_ref, g_ref, gain_ref, shift_ref, fam_ref, tab_ref, wqkv_ref, wo_ref, *rest, linked):
    hand, rest = (rest[:1], rest[1:]) if linked else ((), rest)
    dn_ref, sums_ref, gqkv_ref, go_ref, heads_ref = rest[:5]
    outs, rest = (rest[5:10], rest[10:]) if linked else ((), rest[5:])
    (x_s, xt_s, c_s, s_s, w_s, wo_s, q_s, k_s, v_s, do_s, kt_s, vt_s, ht_s, dqt_s, dk_s, dv_s, draw_s, dn_s, gq_s, go_s, heads_s,
     famr_s, famc_s, w_sem, wo_sem, gq_sem, go_sem, h_sem) = rest[:28]
    rest = rest[28:]
    step = pl.program_id(0)
    steps = len(ORDER)
    last = steps - 1
    n, d = raw_ref.shape
    lanes = 256
    pairs = d // 128
    slot = step % 2

    def weights(at, slot):
        out = []
        for half in range(2):
            pair = pick(at, [o[half] for o in ORDER])
            for kind in range(3):
                col = pl.multiple_of((kind * pairs + pair) * 128, 128)
                j = kind * 2 + half
                out.append(local_copy(wqkv_ref.at[:, pl.ds(col, 128)], w_s.at[slot, :, pl.ds(j * 128, 128)], w_sem.at[slot, j]))
            row = pl.multiple_of(pair * 128, 128)
            out.append(local_copy(wo_ref.at[pl.ds(row, 128), :], wo_s.at[slot, pl.ds(half * 128, 128), :], wo_sem.at[slot, half]))
        return out

    def results(at):
        out = []
        for half in range(2):
            pair = pick(at, [o[half] for o in ORDER])
            for kind in range(3):
                j = kind * 2 + half
                if linked:
                    col = pick(at, [block * 384 + rank * 128 for block, rank in (tile_place(kind * 8 + o[half]) for o in ORDER)])
                    to = gqkv_ref.at[at // 2, :, :, :, pl.ds(pl.multiple_of(col, 128), 128)]
                else:
                    to = gqkv_ref.at[:, :, :, pl.ds(pl.multiple_of((kind * pairs + pair) * 128, 128), 128)]
                out.append(local_copy(gq_s.at[:, :, :, pl.ds(j * 128, 128)], to, gq_sem.at[j]))
            out.append(local_copy(go_s.at[pl.ds(half * 128, 128), :], go_ref.at[pair // 2, pair % 2], go_sem.at[half]))
        return out

    if linked:
        place = Place()
        head_send, head_recv = rest[:2]
        rest = rest[2:]

        def heads_out(at):
            cols = pl.ds(pl.multiple_of(at * lanes, lanes), lanes)
            span = n // 4
            out = []
            for j, (to, device) in enumerate(place.peers):
                src = heads_s.at[pl.ds(pl.multiple_of(to * span, span), span), :]
                out.append(remote_copy(src, heads_ref.at[place.seq, :, cols], head_send.at[at, j], head_recv.at[at, j], device))
            mine = heads_s.at[pl.ds(pl.multiple_of(place.seq * span, span), span), :]
            return out, local_copy(mine, heads_ref.at[place.seq, :, cols], h_sem.at[0])

        def part_of(source, k, w):
            return lambda y, c: source.at[k, :, :, :, pl.ds(pl.multiple_of((y * 2 + c) * w, 128), w)]

        def done_at(k):
            def done(total):
                if k == 2:
                    outs[4][...] = total
                else:
                    outs[2 * k][...] = total[0:128]
                    outs[2 * k + 1][...] = total[128:256]
            return done

        cut = piece_count(AT_SPLIT)
        made = [Piece(place, part_of(hand[0], 2, 256), done_at(0), AT_SPLIT, rest[:cut]),
                Piece(place, part_of(hand[0], 3, 256), done_at(1), AT_SPLIT, rest[cut:2 * cut]),
                Piece(place, part_of(gqkv_ref, 0, 384), done_at(2), EARLY_SPLIT, rest[2 * cut:])]
        plan = {}
        for which, times in enumerate(AT_TICKS):
            for t, at in enumerate(times):
                plan.setdefault(at, []).append((which, t))
    else:
        plan = {}

    def tick(position):
        for at, what in sorted(plan.items()):
            if min(at // 6, last) * 6 + position == at:
                def run(what=what):
                    for which, t in sorted(what, key=lambda w: (-w[1], w[0])):
                        made[which].tick(t)
                pl.when(step == min(at // 6, last))(run)

    @pl.when(step == 0)
    def _():
        for copy in weights(0, 0):
            copy.start()
        if linked:
            place.greet()

    @pl.when(step > 0)
    def _():
        for copy in results(step - 1):
            copy.wait()

    tick(0)

    @pl.when(step == 0)
    def _():
        family = fam_ref[pl.ds(lax.axis_index("seq"), 1), :].astype(F32)
        famr_s[...] = family
        for m in range(n // 128):
            rows = slice(m * 128, m * 128 + 128)
            famc_s[rows, :] = jnp.broadcast_to(family[:, rows], (128, 128)).T
        for a in range(n // 32):
            rows = slice(a * 32, a * 32 + 32)
            ca, sa = tab_ref[0, a:a + 1, :], tab_ref[1, a:a + 1, :]
            cb, sb = tab_ref[2], tab_ref[3]
            c1 = ca * cb - sa * sb
            s1 = sa * cb + ca * sb
            lane = lax.broadcasted_iota(jnp.int32, c1.shape, 1) % HEAD_DIM
            c_s[rows, :] = jnp.where(lane < ROT, c1, 1.0)
            s_s[rows, :] = jnp.where(lane < ROT // 2, -s1, jnp.where(lane < ROT, s1, 0.0))
        @functools.partial(each_band, n // 256)
        def _(rows, m):
            xhat, _ = normalize(raw_ref[rows, :].astype(F32))
            normed = (xhat * gain_ref[...] + shift_ref[...]).astype(BF16)
            x_s[rows, :] = normed
            xt_s[:, rows] = normed.T

    @pl.when(step < last)
    def _():
        for copy in weights(step + 1, 1 - slot):
            copy.start()
    for copy in weights(step, slot):
        copy.wait()

    w_ref, wo1_ref = w_s.at[slot], wo_s.at[slot]
    scaling = HEAD_DIM ** -0.5

    def both(rows):
        c, s = c_s[rows, :], s_s[rows, :]
        return jnp.concatenate([c, c], 1), jnp.concatenate([s, s], 1)

    for m in range(n // 256):
        rows = slice(m * 256, m * 256 + 256)
        raw = dot(x_s[rows, :], w_ref[...])
        c, s = both(rows)
        q_s[rows, :] = (turn(raw[:, 0:lanes], c, s, 1.0) * scaling).astype(BF16)
        keys = turn(raw[:, lanes:2 * lanes], c, s, 1.0).astype(BF16)
        k_s[rows, :] = keys
        kt_s[:, rows] = keys.T
        vals = raw[:, 2 * lanes:].astype(BF16)
        v_s[rows, :] = vals
        vt_s[:, rows] = vals.T
        do_s[rows, :] = dot_nt(g_ref[rows, :], wo1_ref[...]).astype(BF16)

    tick(1)
    tile = TILE
    lane = lax.broadcasted_iota(jnp.int32, (tile, 128), 1)
    work = [(h, i) for i in reversed(range(n // tile)) for h in range(4)]

    def first(h, i):
        span = (i + 1) * tile
        here = slice(i * tile, span)
        cols = slice(h // 2 * 128, h // 2 * 128 + 128)
        mine = (lane < HEAD_DIM) if h % 2 == 0 else (lane >= HEAD_DIM)
        qh = jnp.where(mine, q_s[here, cols], 0).astype(BF16)
        doh = jnp.where(mine, do_s[here, cols], 0).astype(BF16)
        return qh, doh, dot_nt(k_s[0:span, cols], qh), dot_nt(v_s[0:span, cols], doh)

    def second(h, i, qh, doh, st, dpt):
        span = (i + 1) * tile
        here = slice(i * tile, span)
        cols = slice(h // 2 * 128, h // 2 * 128 + 128)
        rows = slice(h * HEAD_DIM, (h + 1) * HEAD_DIM)
        family = famc_s[0:span, :]
        allowed = jnp.concatenate([family] * (tile // 128), 1) == famr_s[:, here]
        key_place = lax.broadcasted_iota(jnp.int32, (span, tile), 0)
        query_place = lax.broadcasted_iota(jnp.int32, (span, tile), 1) + i * tile
        st = jnp.where(allowed & (key_place <= query_place), st, -1e9)
        e = jnp.exp(st - jnp.max(st, 0, keepdims=True))
        p = e * (1.0 / jnp.sum(e, 0, keepdims=True))
        pb = p.astype(BF16)
        ds = (p * (dpt - jnp.sum(p * dpt, 0, keepdims=True))).astype(BF16)
        ht_s[rows, here] = dot(vt_s[rows, 0:span], pb).astype(BF16)
        dqt_s[rows, here] = dot(kt_s[rows, 0:span], ds) * scaling
        dv = dot(pb, doh)
        dk = dot(ds, qh)
        if h % 2 == 0 and i == n // tile - 1:
            dv_s[:, cols] = dv
            dk_s[:, cols] = dk
        else:
            dv_s[0:span, cols] += dv
            dk_s[0:span, cols] += dk

    made_first = first(*work[0])
    for j, (h, i) in enumerate(work):
        later = first(*work[j + 1]) if j + 1 < len(work) else None
        second(h, i, *made_first)
        made_first = later
        if h == 3 and i != 1:
            tick({3: 2, 2: 3, 0: 4}[i])

    @pl.when(step > 0)
    def _():
        if linked:
            sent, mine = heads_out(step - 1)
            for copy in sent:
                copy.wait_send()
            mine.wait()
        else:
            local_copy(heads_s, heads_ref.at[:, pl.ds(pl.multiple_of((step - 1) * lanes, lanes), lanes)], h_sem.at[0]).wait()
    heads_s[...] = ht_s[...].T
    if linked:
        sent, mine = heads_out(step)
        for copy in sent:
            copy.start()
        mine.start()
    else:
        local_copy(heads_s, heads_ref.at[:, pl.ds(pl.multiple_of(step * lanes, lanes), lanes)], h_sem.at[0]).start()

    for m in range(n // 256):
        rows = slice(m * 256, m * 256 + 256)
        c, s = both(rows)
        draw_s[rows, 0:lanes] = turn(dqt_s[:, rows].T, c, s, -1.0).astype(BF16)
        draw_s[rows, lanes:2 * lanes] = turn(dk_s[rows, :], c, s, -1.0).astype(BF16)
        draw_s[rows, 2 * lanes:] = dv_s[rows, :].astype(BF16)

    for m in range(d // 256):
        grads = dot(xt_s[m * 256:(m + 1) * 256, :], draw_s[...]).astype(BF16)
        gq_s[m, 0] = grads[0:128]
        gq_s[m, 1] = grads[128:256]
    go_s[...] = dot(ht_s[...], g_ref[...]).astype(BF16)
    for copy in results(step):
        copy.start()
    tick(5)
    for m in range(n // 256):
        here = slice(m * 256, (m + 1) * 256)
        dn = dot_nt(draw_s[here, :], w_ref[...])

        @pl.when(step == 0)
        def _():
            dn_s[here, :] = dn

        @pl.when(step > 0)
        def _():
            dn_s[here, :] += dn

    @pl.when(step == last)
    def _():
        sums_ref[...] = jnp.zeros_like(sums_ref)

        @functools.partial(each_band, n // 256)
        def _(here, m):
            total = dn_s[here, :]
            xhat, _ = normalize(raw_ref[here, :].astype(F32))
            sums_ref[0:1, :] += jnp.sum(total * xhat, 0, keepdims=True)
            sums_ref[1:2, :] += jnp.sum(total, 0, keepdims=True)
            dn_ref[here, :] = total.astype(BF16)

    tick(6)

    @pl.when(step == last)
    def _():
        for copy in results(step):
            copy.wait()
        if linked:
            for at in range(steps):
                for copy in heads_out(at)[0]:
                    copy.wait_recv()
            for copy in heads_out(step)[0]:
                copy.wait_send()
            heads_out(step)[1].wait()
        else:
            local_copy(heads_s, heads_ref.at[:, pl.ds(pl.multiple_of(step * lanes, lanes), lanes)], h_sem.at[0]).wait()


def attend(raw, g, gain, shift, wqkv, wo, families, linked, grads=None):
    n, d = raw.shape
    pair_lane = np.arange(128) % HEAD_DIM % (ROT // 2)
    freq = 10000.0 ** (-2.0 * pair_lane / ROT)
    high, low = np.arange(n // 32)[:, None] * 32.0 * freq, np.arange(32)[:, None] * freq
    tab = jnp.asarray(np.stack([np.cos(high), np.sin(high), np.cos(low), np.sin(low)]), F32)
    sd, vm = jax.ShapeDtypeStruct, pltpu.VMEM
    out_shape = [sd((n, d), BF16), sd((8, d), F32), sd((2, 4, 2, 128, 3 * d // 2) if linked else (4, 2, 128, 3 * d), BF16),
                 sd((4, 2, 128, d), BF16), sd((4, n // 4, d) if linked else (n, d), BF16)]
    out_specs = [whole((n, d)), whole((8, d))] + [ANYWHERE] * 3
    scratch = [vm((n, d), BF16), vm((d, n), BF16), vm((n, 128), F32), vm((n, 128), F32), vm((2, d, 768), BF16), vm((2, 256, d), BF16)]
    scratch += [vm((n, 256), BF16)] * 4 + [vm((256, n), BF16)] * 3
    scratch += [vm((256, n), F32), vm((n, 256), F32), vm((n, 256), F32), vm((n, 768), BF16), vm((n, d), F32), vm((4, 2, 128, 768), BF16),
                vm((256, d), BF16), vm((n, 256), BF16), vm((1, n), F32), vm((n, 128), F32), DMA((2, 6)), DMA((2, 2)), DMA((6,)), DMA((2,)), DMA((1,))]
    params, more = {}, []
    if linked:
        more = [grads]
        out_shape += [sd((128, 256), F32)] * 4 + [sd((128, 384), F32)]
        out_specs += [whole((128, 256))] * 4 + [whole((128, 384))]
        scratch += [DMA((4, 3)), DMA((4, 3))]
        scratch += piece_scratch(256, AT_SPLIT) * 2 + piece_scratch(384, EARLY_SPLIT)
        params = dict(collective_id=1, has_side_effects=True)
    return pl.pallas_call(
        functools.partial(attn_kernel, linked=linked), out_shape=out_shape, grid=(len(ORDER),),
        in_specs=[whole((n, d)), whole((n, d)), whole((1, d)), whole((1, d)), whole(families.shape), whole((4, 32, 128)), ANYWHERE, ANYWHERE]
        + [ANYWHERE] * len(more),
        out_specs=out_specs, scratch_shapes=scratch,
        compiler_params=pltpu.CompilerParams(vmem_limit_bytes=60 * 2**20, **params),
        cost_estimate=pl.CostEstimate(flops=70_000_000_000, bytes_accessed=30_000_000, transcendentals=20_000_000),
    )(raw, g, gain.reshape(1, d), shift.reshape(1, d), families, tab, wqkv, wo, *more)


class SmallSum:
    def __init__(self, place, held, heard, by_z, send, recv):
        self.p, self.held, self.heard, self.by_z, self.send, self.recv = place, held, heard, by_z, send, recv

    def copies(self, t):
        p = self.p
        if t < 3:
            to = (p.twin, p.beside_y, p.beside_x)[t]
            return [remote_copy(self.held, self.heard.at[t], self.send.at[t], self.recv.at[t], to)]
        return [remote_copy(self.by_z.at[p.z], self.by_z.at[p.z], self.send.at[3 + j], self.recv.at[3 + j], to)
                for j, to in enumerate(p.along_z)]

    def tick(self, t):
        if t > 0:
            for copy in self.copies(t - 1):
                copy.wait()
        if 0 < t < 4:
            total = self.held[...] + self.heard[t - 1]
            if t < 3:
                self.held[...] = total
            else:
                self.by_z[self.p.z] = total
        if t < 4:
            for copy in self.copies(t):
                copy.start()
        return None if t < 4 else self.by_z[0] + self.by_z[1] + self.by_z[2] + self.by_z[3]


def tail_kernel(dat_ref, heads_ref, gq_ref, go_ref, inp_ref, cot_ref, y_ref, dn_ref, wo_ref, part_ref, gain_ref, dbias_ref, sums_ff_ref, sums_at_ref,
                ub_ref, early_ref, lo_ref, ig_ref, qkv_ref, out_ref, gain_o, shift_o, ub_o, db_o,
                back_s, inp_s, g_s, heads_s, y_s, dn_s, wo_s, lo_s, ig_s, small_s, heard_s, by_z_s,
                load_sem, wo_sem, back_send, back_recv, own_sem, small_send, small_recv, lo_sem, ig_sem, *pieces):
    place = Place()
    d = wo_s.shape[0]
    place.greet()
    swaps = [remote_copy(dat_ref.at[to], back_s.at[place.seq], back_send.at[j], back_recv.at[j], device)
             for j, (to, device) in enumerate(place.peers)]
    own = local_copy(dat_ref.at[place.seq], back_s.at[place.seq], own_sem.at[0])
    blocks = {}

    def part(source, w, row0, rows):
        return lambda y, c: source.at[:, :, pl.ds(row0, rows), pl.ds(pl.multiple_of((y * 2 + c) * w, 128), w)]

    def out_done(total):
        out_ref[...] = total

    def qkv_done(row0):
        def done(total):
            rows = slice(row0, row0 + total.shape[0])
            early = early_ref[rows, :]
            first = jnp.where(place.c == 0, early, total)
            second = jnp.where(place.c == 0, total, early)
            order = ((first, 0), (second, 0), (second, 1), (first, 1), (first, 2), (second, 2))
            for k, (source, at) in enumerate(order):
                qkv_ref[rows, k * 128:(k + 1) * 128] = source[:, at * 128:(at + 1) * 128]
        return done

    cuts = [0, piece_count(TAIL_SPLITS[0])]
    for split in TAIL_SPLITS[1:]:
        cuts.append(cuts[-1] + piece_count(split))
    late = gq_ref.at[1]
    row1 = sum(TAIL_SPLITS[1])
    made = [Piece(place, part(go_ref, 256, 0, 128), out_done, TAIL_SPLITS[0], pieces[:cuts[1]]),
            Piece(place, part(late, 384, 0, row1), qkv_done(0), TAIL_SPLITS[1], pieces[cuts[1]:cuts[2]]),
            Piece(place, part(late, 384, row1, 128 - row1), qkv_done(row1), TAIL_SPLITS[2], pieces[cuts[2]:])]
    small = SmallSum(place, small_s, heard_s, by_z_s, small_send, small_recv)
    small_s[0:3, :] = sums_ff_ref[0:3, :]
    small_s[0:2, :] += sums_at_ref[0:2, :]
    small_s[3:4, :] = jnp.zeros((1, d), F32)
    for k in range(4):
        small_s[4 + k:5 + k, :] = ub_ref[:, k * d:(k + 1) * d]
    for piece in made:
        piece.tick(0)
    for copy in swaps:
        copy.start()
    small.tick(0)
    loads = [local_copy(a, b, load_sem.at[k]) for k, (a, b) in enumerate(
        ((heads_ref, heads_s), (inp_ref, inp_s), (y_ref, y_s), (cot_ref, g_s), (dn_ref, dn_s)))]
    for pair in range(d // 128):
        at = [p for two in ORDER for p in two].index(pair)
        blocks[at] = local_copy(wo_ref.at[pl.ds(pair * 128, 128), :], wo_s.at[pl.ds(at * 128, 128), :], wo_sem.at[at])
    for copy in [loads[0]] + list(blocks.values()) + loads[1:] + [own]:
        copy.start()

    def lo_out(r):
        return local_copy(lo_s.at[r], lo_ref.at[r], lo_sem.at[r])

    def ig_out(r):
        return local_copy(ig_s.at[r], ig_ref.at[r], ig_sem.at[r])

    def forward(r, carry):
        total = inp_s[r].astype(F32) + dot(heads_s[r], wo_s[...]) + (y_s[r] + dbias_ref[...])
        lo_s[r] = total.astype(BF16)
        lo_out(r).start()
        return carry

    def backward(r):
        xhat, scale = normalize(inp_s[r].astype(F32))
        dx = (dn_s[r] + back_s[r].astype(F32)) * gain_ref[...]
        ig_s[r] = g_s[lax.rem(part_ref[r], 4)].astype(F32) + (dx - jnp.mean(dx, -1, keepdims=True) - xhat * jnp.mean(dx * xhat, -1, keepdims=True)) * scale
        ig_out(r).start()

    made[0].tick(1)
    small.tick(1)
    for copy in list(blocks.values()) + loads[:3]:
        copy.wait()
    lax.fori_loop(0, 2, forward, 0)
    made[1].tick(1)
    lax.fori_loop(2, 4, forward, 0)
    made[0].tick(2)
    made[2].tick(1)
    small.tick(2)
    loads[3].wait()
    loads[4].wait()
    own.wait()
    backward(place.seq)
    made[1].tick(2)
    made[0].tick(3)
    small.tick(3)
    for j in range(3):
        swaps[j].wait_send()
    swaps[2].wait_recv()
    backward((place.seq + 1) % 4)
    made[2].tick(2)
    made[1].tick(3)
    swaps[1].wait_recv()
    backward((place.seq + 2) % 4)
    made[2].tick(3)
    swaps[0].wait_recv()
    backward((place.seq + 3) % 4)
    total = small.tick(4)
    for piece in made:
        piece.tick(4)
    gain_o[...] = total[0:1]
    shift_o[...] = total[1:2]
    db_o[...] = total[2:3]
    for k in range(4):
        ub_o[:, k * d:(k + 1) * d] = total[4 + k:5 + k]
    for r in range(4):
        lo_out(r).wait()
        ig_out(r).wait()


def finish(dat, heads, gq, go, inp, cot, y, dn, wo, partners, gain, dbias, sums_ff, sums_at, ub, early):
    sd, vm = jax.ShapeDtypeStruct, pltpu.VMEM
    shape, d = inp.shape, inp.shape[2]
    vmem = pl.BlockSpec(memory_space=pltpu.VMEM)
    return pl.pallas_call(
        tail_kernel,
        out_shape=[sd(shape, BF16), sd(shape, F32), sd((128, 768), F32), sd((128, 256), F32), sd((1, d), F32), sd((1, d), F32), sd((1, 4 * d), F32),
                   sd((1, d), F32)],
        in_specs=[ANYWHERE] * 9 + [pl.BlockSpec(memory_space=pltpu.SMEM)] + [vmem] * 6, out_specs=[ANYWHERE] * 2 + [vmem] * 6,
        scratch_shapes=[vm(shape, BF16)] * 4 + [vm(shape, F32)] * 2 + [vm((d, d), BF16), vm(shape, BF16), vm(shape, F32),
                        vm((8, d), F32), vm((3, 8, d), F32), vm((4, 8, d), F32),
                        DMA((5,)), DMA((8,)), DMA((3,)), DMA((3,)), DMA((1,)), DMA((6,)), DMA((6,)), DMA((4,)), DMA((4,))]
        + piece_scratch(256, TAIL_SPLITS[0]) + piece_scratch(384, TAIL_SPLITS[1]) + piece_scratch(384, TAIL_SPLITS[2]),
        compiler_params=pltpu.CompilerParams(collective_id=2, has_side_effects=True, vmem_limit_bytes=56 * 2**20),
    )(dat.reshape(shape), heads, gq, go, inp, cot, y.reshape(shape), dn.reshape(shape), wo, partners, gain.reshape(1, d), dbias.reshape(1, d), sums_ff, sums_at,
      ub, early)


def copy_kernel(*refs):
    (lo, ig, qkv, out, gain, shift, ub, db), ups, downs = refs[:8], refs[8:12], refs[12:16]
    lo_o, ig_o, qkv_o, out_o, gain_o, shift_o, ub_o, db_o, up_o, down_o = refs[16:]
    lo_o[...] = lo[...]
    ig_o[...] = ig[...]

    @pl.when(pl.program_id(0) == 0)
    def _():
        for to, source in ((qkv_o, qkv), (out_o, out), (gain_o, gain), (shift_o, shift), (ub_o, ub), (db_o, db)):
            to[...] = source[...]
        for k in range(4):
            up_o[:, k * 128:(k + 1) * 128] = ups[k][:, 0:128]
            up_o[:, 512 + k * 128:512 + (k + 1) * 128] = ups[k][:, 128:256]
            down_o[k * 128:(k + 1) * 128, :] = downs[k][...]


def gather_up(*parts):
    sd, shape = jax.ShapeDtypeStruct, parts[0].shape
    flat = [(shape[0] * shape[1], shape[2])] * 2 + [p.shape for p in parts[2:]]
    band = pl.BlockSpec((128, shape[2]), lambda p: (p, 0))
    outs = flat[:8] + [(128, 1024), (512, 256)]
    return pl.pallas_call(
        copy_kernel, out_shape=[sd(s, BF16 if k == 0 else F32) for k, s in enumerate(outs)], grid=(flat[0][0] // 128,),
        in_specs=[band, band] + [whole(s) for s in flat[2:]], out_specs=[band, band] + [whole(s) for s in outs[2:]],
        compiler_params=pltpu.CompilerParams(vmem_limit_bytes=60 * 2**20),
    )(*[p.reshape(s) for p, s in zip(parts, flat)])


def on_device(inputs, norm_gain, norm_shift, qkv_weight, out_weight, up_weight, up_bias, down_weight, down_bias, partners, families, cotangent, linked):
    row_count, place_count, width = inputs.shape
    tokens = row_count * place_count
    branch_args = norm_gain, norm_shift, qkv_weight, out_weight, families, linked
    if linked:
        y, dn, sums_ff, ub, grads, row_inputs, row_grad, up0, down0, up1, down1 = feed_forward(
            inputs, cotangent, partners, norm_gain, norm_shift, up_bias, up_weight, down_weight, True)
        dat, sums_at, gq, go, heads, up2, down2, up3, down3, early = attend(
            row_inputs.reshape(tokens, width), row_grad.reshape(tokens, width), *branch_args, grads)
        layer_out, input_grad, qkv_sum, out_sum, gain_sum, shift_sum, ub_sum, db_sum = finish(
            dat, heads, gq, go, inputs, cotangent, y, dn, out_weight, partners, norm_gain, down_bias, sums_ff, sums_at, ub, early)
        layer_out, input_grad, qkv_sum, out_sum, gain_sum, shift_sum, ub_sum, db_sum, up_sum, down_sum = gather_up(
            layer_out, input_grad, qkv_sum, out_sum, gain_sum, shift_sum, ub_sum, db_sum, up0, up1, up2, up3, down0, down1, down2, down3)
        return (layer_out.reshape(inputs.shape), input_grad.reshape(inputs.shape), gain_sum.reshape(width), shift_sum.reshape(width), qkv_sum, out_sum,
                up_sum, ub_sum.reshape(-1), down_sum, db_sum.reshape(width))
    local_rows = partners - lax.axis_index("dp") * row_count
    grad = jnp.take(cotangent, local_rows, axis=0, mode="clip")
    swap = functools.partial(lax.all_to_all, axis_name="seq", split_axis=0, concat_axis=0, tiled=True)
    row_inputs, row_grad = swap(inputs).reshape(tokens, width), swap(grad).reshape(tokens, width)
    y, dn, sums_ff, ub, up_grad, down_grad = feed_forward(
        inputs, cotangent, partners, norm_gain, norm_shift, up_bias, up_weight, down_weight, False)
    dat, sums_at, qkv_grad, out_grad, heads = attend(row_inputs, row_grad, *branch_args)

    def scatter(parts, columns):
        part = lax.psum_scatter(parts.reshape(-1, columns), "seq", scatter_dimension=1, tiled=True)
        return lax.psum_scatter(part, "dp", scatter_dimension=0, tiled=True).astype(F32)

    qkv_sum, out_sum = scatter(qkv_grad, 3 * width), scatter(out_grad, width)
    up_sum, down_sum = scatter(up_grad, up_bias.shape[0]), scatter(down_grad, width)
    heads = swap(heads.reshape(inputs.shape)).reshape(tokens, width)
    order = np.array([p for two in ORDER for p in two])
    attn_out = dot(heads, out_weight.reshape(-1, 128, width)[order].reshape(width, width))
    values = inputs.astype(F32).reshape(tokens, width)
    layer_out = (values + attn_out + (y + down_bias)).astype(BF16).reshape(inputs.shape)
    xhat, scale = normalize(values)
    dx = (dn + swap(dat.reshape(inputs.shape)).reshape(tokens, width).astype(F32)) * norm_gain
    input_grad = grad.reshape(tokens, width).astype(F32) + (dx - jnp.mean(dx, -1, keepdims=True) - xhat * jnp.mean(dx * xhat, -1, keepdims=True)) * scale
    gain_sum, shift_sum, up_bias_sum, down_bias_sum = lax.psum((sums_ff[0] + sums_at[0], sums_ff[1] + sums_at[1], ub[0], sums_ff[2]), ("dp", "seq"))
    return (layer_out, input_grad.reshape(inputs.shape), gain_sum, shift_sum, qkv_sum, out_sum, up_sum, up_bias_sum, down_sum, down_bias_sum)


def solution(mesh):
    rows = P("dp", "seq", None)
    placed = (rows,) + (P(),) * 8 + (P("dp"), P("dp", None), rows)
    grads = P("dp", "seq")
    linked = (mesh.shape["dp"], mesh.shape["seq"]) == (8, 4)
    return jax.shard_map(functools.partial(on_device, linked=linked), mesh=mesh, in_specs=placed,
                         out_specs=(rows, rows, P(), P(), grads, grads, grads, P(), grads, P()), check_vma=False)
```

```python
import functools

import jax
import jax.numpy as jnp
import numpy as np
from jax import lax
from jax.experimental import pallas as pl
from jax.experimental.pallas import tpu as pltpu
from jax.sharding import PartitionSpec as P

F32 = jnp.float32
BF16 = jnp.bfloat16
HEAD_DIM = 64
ROT = 32
EPS = 1e-05
C0 = 0.7978845608028654
C1 = C0 * 0.044715
TILE = 256
FF_SPLIT = 0, 176, 80
AT_SPLIT = 64, 128, 64
EARLY_SPLIT = 48, 64, 16
TAIL_FIRST = 2
TAIL_SPLITS = (0, 80, 48), (0, 48, 16), (0, 32, 32)
FF_TICKS = 6, 10, 18, 21, 24
AT_TICKS = (0, 2, 7, 10, 14), (4, 7, 12, 15, 19), (8, 12, 17, 20, 23), (13, 17, 21, 23, 24)
ORDER = ((0, 3), (4, 7), (1, 2), (5, 6))
MESH_ID = pl.DeviceIdType.MESH
ANYWHERE = pl.BlockSpec(memory_space=pl.ANY)
DMA = pltpu.SemaphoreType.DMA


def dot(a, b):
    return lax.dot_general(a, b, (((1,), (0,)), ((), ())), preferred_element_type=F32)


def dot_nt(a, b):
    return lax.dot_general(a, b, (((1,), (1,)), ((), ())), preferred_element_type=F32)


def dot_tn(a, b):
    return lax.dot_general(a, b, (((0,), (0,)), ((), ())), preferred_element_type=F32)


def whole(shape):
    return pl.BlockSpec(shape, lambda p: (0,) * len(shape), pipeline_mode=pl.Buffered(1))


def pick(step, values):
    out = jnp.int32(values[0])
    for i, value in enumerate(values[1:], 1):
        out = jnp.where(step == i, value, out)
    return out


def normalize(values):
    centered = values - jnp.mean(values, -1, keepdims=True)
    scale = lax.rsqrt(jnp.mean(centered * centered, -1, keepdims=True) + EPS)
    return centered * scale, scale


def each_band(count, body):
    def step(m, carry):
        body(pl.ds(pl.multiple_of(m * 256, 256), 256), m)
        return carry

    lax.fori_loop(0, count, step, 0)


def local_copy(src, dst, sem):
    return pltpu.make_async_copy(src, dst, sem)


def remote_copy(src, dst, send, recv, to):
    return pltpu.make_async_remote_copy(src_ref=src, dst_ref=dst, send_sem=send, recv_sem=recv, device_id=to,
                                        device_id_type=MESH_ID)


class Place:
    def __init__(self):
        self.dp, self.seq = lax.axis_index("dp"), lax.axis_index("seq")
        self.z, self.x, self.y, self.c = self.dp // 2, self.dp % 2, self.seq // 2, self.seq % 2
        self.twin = (self.dp, self.y * 2 + 1 - self.c)
        self.beside_y = (self.dp, (1 - self.y) * 2 + self.c)
        self.across = (self.dp, (1 - self.y) * 2 + 1 - self.c)
        self.beside_x = (self.z * 2 + 1 - self.x, self.seq)
        self.along_z = [(((self.z + j) % 4) * 2 + self.x, self.seq) for j in (1, 2, 3)]
        self.peers = [((self.seq + j) % 4, (self.dp, (self.seq + j) % 4)) for j in (1, 2, 3)]
        self.partners = [self.twin, self.beside_y, self.beside_x] + self.along_z

    def greet(self):
        barrier = pltpu.get_barrier_semaphore()
        for partner in self.partners + [self.across]:
            pl.semaphore_signal(barrier, inc=1, device_id=partner, device_id_type=MESH_ID)
        pl.semaphore_wait(barrier, len(self.partners) + 1)


def add_into(dst, src, lead):
    rows, w = src.shape[-2:]
    band = rows
    while band * w > 65536 and band % 32 == 0:
        band //= 2
    count = 1
    for n in lead:
        count *= n

    def body(t, carry):
        block, part = t // (rows // band), t % (rows // band)
        index = []
        for n in reversed(lead):
            index.insert(0, block % n)
            block = block // n
        at = tuple(index) + (pl.ds(pl.multiple_of(part * band, band), band), slice(None))
        dst[at] = dst[at] + src[at]
        return carry

    lax.fori_loop(0, count * (rows // band), body, 0)


def piece_scratch(w, split):
    ra, rb, rc = split
    r = sum(split)
    out = [((2, 4, 2, r), 1), ((2, 4, 2, r), 1), ((4, 2, ra), ra), ((2, 4, rb), rb), ((3, 2, 2, rc), rc), ((4, ra), ra), ((4, rb), rb), ((2, rc), rc),
           ((3, ra + rb), ra + rb), ((rc,), rc)]
    return [pltpu.VMEM(shape + (w,), BF16) for shape, used in out if used] + [DMA((14,)), DMA((14,)), DMA((2,))]


def piece_count(split):
    return len(piece_scratch(128, split))


class Piece:
    def __init__(self, place, part, done, split, scratch):
        self.p, self.part, self.done, self.split = place, part, done, split
        ra, rb, rc = split
        names = [("a", 1), ("from_twin", 1), ("ya", ra), ("xb", rb), ("zc", rc), ("xa", ra), ("yb", rb), ("xc", rc), ("zab", ra + rb), ("yc", rc)]
        scratch = list(scratch)
        for name, used in names:
            setattr(self, name, scratch.pop(0) if used else None)
        self.ss, self.rs, self.ls = scratch
        self.rows_a, self.rows_b, self.rows_ab, self.rows_c = pl.ds(0, ra), pl.ds(ra, rb), pl.ds(0, ra + rb), pl.ds(ra + rb, rc)

    def copies(self, stage):
        p, a, (ra, rb, rc) = self.p, self.a, self.split
        out = []
        slot = (0, 2, 7, 10)[stage]

        def send(src, dst, to):
            k = slot + len(out)
            out.append(remote_copy(src, dst, self.ss.at[k], self.rs.at[k], to))

        zs = [((p.z + 1 + j) % 4, p.along_z[j]) for j in range(3)]
        if stage == 0:
            for k in (0, 1):
                send(self.part(k, 1 - p.c), self.from_twin.at[k], p.twin)
        if stage == 1:
            if ra:
                send(a.at[1 - p.y, :, :, self.rows_a, :], self.ya, p.beside_y)
            if rb:
                send(a.at[:, :, 1 - p.x, self.rows_b, :], self.xb, p.beside_x)
            for j in range(3 if rc else 0):
                send(a.at[:, zs[j][0], :, self.rows_c, :], self.zc.at[j], zs[j][1])
        if stage == 2:
            if ra:
                send(a.at[p.y, :, 1 - p.x, self.rows_a, :], self.xa, p.beside_x)
            if rb:
                send(a.at[1 - p.y, :, p.x, self.rows_b, :], self.yb, p.beside_y)
            if rc:
                send(a.at[:, p.z, 1 - p.x, self.rows_c, :], self.xc, p.beside_x)
        if stage == 3:
            for j in range(3 if ra + rb else 0):
                send(a.at[p.y, zs[j][0], p.x, self.rows_ab, :], self.zab.at[j], zs[j][1])
            if rc:
                send(a.at[1 - p.y, p.z, p.x, self.rows_c, :], self.yc, p.beside_y)
        return out

    def own(self):
        return [local_copy(self.part(k, self.p.c), self.a.at[k], self.ls.at[k]) for k in (0, 1)]

    def tick(self, t):
        p, a, (ra, rb, rc) = self.p, self.a, self.split
        if t > 0:
            for copy in self.copies(t - 1):
                copy.wait()
        if t == 0:
            for copy in self.copies(0) + self.own():
                copy.start()
        if t == 1:
            for copy in self.own():
                copy.wait()
            add_into(a, self.from_twin, (2, 4, 2))
        if t == 2:
            if ra:
                add_into(a.at[p.y, :, :, self.rows_a, :], self.ya, (4, 2))
            if rb:
                add_into(a.at[:, :, p.x, self.rows_b, :], self.xb, (2, 4))
            for j in range(3 if rc else 0):
                add_into(a.at[:, p.z, :, self.rows_c, :], self.zc.at[j], (2, 2))
        if t == 3:
            if ra:
                add_into(a.at[p.y, :, p.x, self.rows_a, :], self.xa, (4,))
            if rb:
                add_into(a.at[p.y, :, p.x, self.rows_b, :], self.yb, (4,))
            if rc:
                add_into(a.at[:, p.z, p.x, self.rows_c, :], self.xc, (2,))
        if t in (1, 2, 3):
            for copy in self.copies(t):
                copy.start()
        if t == 4:
            mine = a.at[p.y, p.z, p.x]
            parts = []
            if ra + rb:
                total = mine[self.rows_ab, :].astype(F32)
                for j in range(3):
                    total += self.zab[j].astype(F32)
                parts.append(total)
            if rc:
                parts.append(mine[self.rows_c, :].astype(F32) + self.yc[...].astype(F32))
            self.done(jnp.concatenate(parts, 0) if len(parts) > 1 else parts[0])


def hidden_runs(at, hidden):
    return [(s, (2 * s + at % 2) * (hidden // 8) + at // 2 * 128) for s in range(4)]


def ff_kernel(part_ref, inp_ref, cot_ref, gain_ref, shift_ref, bias_ref, wu_ref, wd_ref, *rest, linked):
    hand, rest = (rest[:1], rest[1:]) if linked else ((), rest)
    y_ref, dn_ref, sums_ref, ub_ref = rest[:4]
    outs, rest = (rest[4:9], rest[9:]) if linked else (rest[4:6], rest[6:])
    x_s, xt_s, act_s, dh_s, wu_s, wd_s, gu_s, gd_s, g_ref, wu_sem, wd_sem, gu_sem, gd_sem, act_sem = rest[:14]
    rest = rest[14:]
    step = pl.program_id(0)
    last = pl.num_programs(0) - 1
    n, d = x_s.shape
    hidden = bias_ref.shape[1]
    tile = 512
    slot = step % 2

    def places(at):
        return hidden_runs(at, hidden)

    def weights(at, slot):
        out = []
        for s, f in places(at):
            f = pl.multiple_of(f, 128)
            out.append(local_copy(wu_ref.at[:, pl.ds(f, 128)], wu_s.at[slot, :, pl.ds(s * 128, 128)], wu_sem.at[slot, s]))
            out.append(local_copy(wd_ref.at[pl.ds(f, 128), :], wd_s.at[slot, pl.ds(s * 128, 128), :], wd_sem.at[slot, s]))
        return out

    def results(at):
        out = []
        k, j = at // 2, at % 2
        for s, f in places(at):
            f = pl.multiple_of(f, 128)
            up, down = gu_s.at[:, :, :, pl.ds(s * 128, 128)], gd_s.at[pl.ds(s * 128, 128), :]
            if linked:
                col = pl.multiple_of(s * 256 + j * 128, 128)
                to = outs[0].at[k, :, :, pl.ds(0, 128), pl.ds(col, 128)], outs[0].at[k, s, j, pl.ds(128, 128), :]
            else:
                to = outs[0].at[:, :, :, pl.ds(f, 128)], outs[1].at[pl.ds(f, 128), :]
            out.append(local_copy(up, to[0], gu_sem.at[s]))
            out.append(local_copy(down, to[1], gd_sem.at[s]))
        return out

    def keep(at):
        return [local_copy(act_s, y_ref.at[at], act_sem.at[0])] if linked else []

    if linked:
        place = Place()
        row_send, row_recv, own_sem = rest[:3]
        rest = rest[3:]

        def swaps(a):
            span = n // 4

            def row(at):
                return g_ref.at[pl.ds(pl.multiple_of(at * span, span), span), :] if a else hand[0].at[at]

            out = [remote_copy(row(to), outs[1 + a].at[place.seq], row_send.at[a, j], row_recv.at[a, j], device)
                   for j, (to, device) in enumerate(place.peers)]
            return out + [local_copy(row(place.seq), outs[1 + a].at[place.seq], own_sem.at[a])]

        def part_of(k):
            return lambda y, c: outs[0].at[k, :, :, :, pl.ds(pl.multiple_of((y * 2 + c) * 256, 256), 256)]

        def done_at(k):
            def done(total):
                outs[3 + 2 * k][...] = total[0:128]
                outs[4 + 2 * k][...] = total[128:256]
            return done

        made = [Piece(place, part_of(0), done_at(0), FF_SPLIT, rest)]

    def tick(position):
        for which, times in enumerate((FF_TICKS,) if linked else ()):
            for t, at in enumerate(times):
                if min(at // 3, 7) * 3 + position == at:
                    pl.when(step == min(at // 3, 7))(functools.partial(made[which].tick, t))

    @pl.when(step == 0)
    def _():
        for copy in weights(0, 0):
            copy.start()
        if linked:
            place.greet()
            for copy in swaps(0):
                copy.start()
        count, span, _ = cot_ref.shape
        for r in range(count):
            g_ref[r * span:(r + 1) * span, :] = cot_ref[lax.rem(part_ref[r], count)]
        if linked:
            for copy in swaps(1):
                copy.start()
        sums_ref[...] = jnp.zeros_like(sums_ref)

        @functools.partial(each_band, n // 256)
        def _(rows, m):
            xhat, _ = normalize(inp_ref[rows, :].astype(F32))
            normed = (xhat * gain_ref[...] + shift_ref[...]).astype(BF16)
            x_s[rows, :] = normed
            xt_s[:, rows] = normed.T
            sums_ref[2:3, :] += jnp.sum(g_ref[rows, :].astype(F32), 0, keepdims=True)

    @pl.when(step > 0)
    def _():
        for copy in results(step - 1) + keep(step - 1):
            copy.wait()

    tick(0)

    @pl.when(step < last)
    def _():
        for copy in weights(step + 1, 1 - slot):
            copy.start()
    for copy in weights(step, slot):
        copy.wait()
    w_up, w_down = wu_s.at[slot], wd_s.at[slot]
    bias = jnp.concatenate([bias_ref[:, pl.ds(pl.multiple_of(f, 128), 128)] for _, f in places(step)], 1)
    unit_sums = None
    for m in range(n // tile):
        here = slice(m * tile, (m + 1) * tile)
        v = dot(x_s[here, :], w_up[...]) + bias
        vv = v * v
        a = 0.5 + 0.5 * jnp.tanh(v * (C0 + C1 * vv))
        act = v * a
        slope = a + act * (1.0 - a) * (2 * C0 + 6 * C1 * vv)
        act_s[here, :] = act.astype(BF16)
        dh = (dot_nt(g_ref[here, :], w_down[...]) * slope).astype(BF16)
        dh_s[here, :] = dh
        total = jnp.sum(dh.astype(F32), 0, keepdims=True)
        unit_sums = total if unit_sums is None else unit_sums + total
    for copy in keep(step):
        copy.start()
    for s, f in places(step):
        ub_ref[:, pl.ds(pl.multiple_of(f, 128), 128)] = unit_sums[:, s * 128:(s + 1) * 128]

    tick(1)
    for m in range(d // 256):
        grads = dot(xt_s[m * 256:(m + 1) * 256, :], dh_s[...]).astype(BF16)
        gu_s[m, 0] = grads[0:128]
        gu_s[m, 1] = grads[128:256]
    gd_s[...] = dot_tn(act_s[...], g_ref[...]).astype(BF16)
    for copy in results(step):
        copy.start()
    tick(2)
    for m in range(n // tile):
        here = slice(m * tile, (m + 1) * tile)
        y = None if linked else dot(act_s[here, :], w_down[...])
        dn = dot_nt(dh_s[here, :], w_up[...])

        @pl.when(step == 0)
        def _():
            if not linked:
                y_ref[here, :] = y
            dn_ref[here, :] = dn

        @pl.when(step > 0)
        def _():
            if not linked:
                y_ref[here, :] += y
            dn_ref[here, :] += dn

    tick(3)

    @pl.when(step == last)
    def _():
        @functools.partial(each_band, n // 256)
        def _(here, m):
            total = dn_ref[here, :]
            xhat, _ = normalize(inp_ref[here, :].astype(F32))
            sums_ref[0:1, :] += jnp.sum(total * xhat, 0, keepdims=True)
            sums_ref[1:2, :] += jnp.sum(total, 0, keepdims=True)

        for copy in results(step) + keep(step):
            copy.wait()
        if linked:
            for copy in swaps(0) + swaps(1):
                copy.wait()


def feed_forward(inp, cot, partners, gain, shift, bias, wu, wd, linked):
    rows, span, d = inp.shape
    n, hidden = rows * span, bias.shape[0]
    sd, vm = jax.ShapeDtypeStruct, pltpu.VMEM
    out_shape = [sd((hidden // 512, n, 512), BF16) if linked else sd((n, d), F32), sd((n, d), F32), sd((8, d), F32), sd((1, hidden), F32)]
    out_specs = [ANYWHERE if linked else whole((n, d)), whole((n, d)), whole((8, d)), whole((1, hidden))]
    scratch = [vm((n, d), BF16), vm((d, n), BF16), vm((n, 512), BF16), vm((n, 512), BF16), vm((2, d, 512), BF16), vm((2, 512, d), BF16),
               vm((4, 2, 128, 512), BF16), vm((512, d), BF16), vm((n, d), BF16), DMA((2, 4)), DMA((2, 4)), DMA((4,)), DMA((4,)), DMA((1,))]
    more, params = [], {}
    if linked:
        more = [inp]
        out_shape += [sd((4, 4, 2, 256, d), BF16), sd(inp.shape, BF16), sd(inp.shape, BF16), *[sd((128, 256), F32)] * 2]
        out_specs += [ANYWHERE] * 3 + [whole((128, 256))] * 2
        scratch += [DMA((2, 3)), DMA((2, 3)), DMA((2,))] + piece_scratch(256, FF_SPLIT)
        params = dict(collective_id=0, has_side_effects=True)
    else:
        out_shape += [sd((4, 2, 128, hidden), BF16), sd((hidden, d), BF16)]
        out_specs += [ANYWHERE] * 2
    return pl.pallas_call(
        functools.partial(ff_kernel, linked=linked), out_shape=out_shape, grid=(hidden // 512,),
        in_specs=[pl.BlockSpec(memory_space=pltpu.SMEM), whole((n, d)), whole(cot.shape), whole((1, d)), whole((1, d)), whole((1, hidden)), ANYWHERE, ANYWHERE] + [ANYWHERE] * len(more),
        out_specs=out_specs, scratch_shapes=scratch,
        compiler_params=pltpu.CompilerParams(vmem_limit_bytes=58 * 2**20, **params),
        cost_estimate=pl.CostEstimate(flops=52_000_000_000, bytes_accessed=50_000_000, transcendentals=4_000_000),
    )(partners, inp.reshape(n, d), cot, gain.reshape(1, d), shift.reshape(1, d), bias.reshape(1, hidden), wu, wd, *more)


def turn(x, c, s, sign):
    lanes = x.shape[1]
    lane = lax.broadcasted_iota(jnp.int32, x.shape, 1) % HEAD_DIM
    other = jnp.where(lane < ROT // 2, pltpu.roll(x, lanes - ROT // 2, 1), pltpu.roll(x, ROT // 2, 1))
    return x * c + (sign * other) * s


def tile_place(tile):
    early = [kind * 8 + pair for two in ORDER[:2] for pair in two for kind in range(3)]
    block = tile // 6
    mates = sorted(t for t in range(24) if t // 6 == block and (t in early) == (tile in early))
    return block, mates.index(tile)


def attn_kernel(raw_ref, g_ref, gain_ref, shift_ref, fam_ref, tab_ref, wqkv_ref, wo_ref, *rest, linked):
    hand, rest = (rest[:1], rest[1:]) if linked else ((), rest)
    dn_ref, sums_ref, gqkv_ref, go_ref, heads_ref = rest[:5]
    outs, rest = (rest[5:12], rest[12:]) if linked else ((), rest[5:])
    (x_s, xt_s, c_s, s_s, w_s, wo_s, q_s, k_s, v_s, do_s, kt_s, vt_s, ht_s, dqt_s, dk_s, dv_s, draw_s, dn_s, gq_s, go_s, heads_s,
     famr_s, famc_s, w_sem, wo_sem, gq_sem, go_sem, h_sem) = rest[:28]
    rest = rest[28:]
    step = pl.program_id(0)
    steps = len(ORDER)
    last = steps - 1
    n, d = raw_ref.shape
    lanes = 256
    pairs = d // 128
    slot = step % 2

    def weights(at, slot):
        out = []
        for half in range(2):
            pair = pick(at, [o[half] for o in ORDER])
            for kind in range(3):
                col = pl.multiple_of((kind * pairs + pair) * 128, 128)
                j = kind * 2 + half
                out.append(local_copy(wqkv_ref.at[:, pl.ds(col, 128)], w_s.at[slot, :, pl.ds(j * 128, 128)], w_sem.at[slot, j]))
            row = pl.multiple_of(pair * 128, 128)
            out.append(local_copy(wo_ref.at[pl.ds(row, 128), :], wo_s.at[slot, pl.ds(half * 128, 128), :], wo_sem.at[slot, half]))
        return out

    def results(at):
        out = []
        for half in range(2):
            pair = pick(at, [o[half] for o in ORDER])
            for kind in range(3):
                j = kind * 2 + half
                if linked:
                    col = pick(at, [block * 384 + rank * 128 for block, rank in (tile_place(kind * 8 + o[half]) for o in ORDER)])
                    to = gqkv_ref.at[at // 2, :, :, :, pl.ds(pl.multiple_of(col, 128), 128)]
                else:
                    to = gqkv_ref.at[:, :, :, pl.ds(pl.multiple_of((kind * pairs + pair) * 128, 128), 128)]
                out.append(local_copy(gq_s.at[:, :, :, pl.ds(j * 128, 128)], to, gq_sem.at[j]))
            out.append(local_copy(go_s.at[pl.ds(half * 128, 128), :], go_ref.at[pair // 2, pair % 2], go_sem.at[half]))
        return out

    if linked:
        place = Place()
        head_send, head_recv = rest[:2]
        rest = rest[2:]

        def heads_out(at):
            cols = pl.ds(pl.multiple_of(at * lanes, lanes), lanes)
            span = n // 4
            out = []
            for j, (to, device) in enumerate(place.peers):
                src = heads_s.at[pl.ds(pl.multiple_of(to * span, span), span), :]
                out.append(remote_copy(src, heads_ref.at[place.seq, :, cols], head_send.at[at, j], head_recv.at[at, j], device))
            mine = heads_s.at[pl.ds(pl.multiple_of(place.seq * span, span), span), :]
            return out, local_copy(mine, heads_ref.at[place.seq, :, cols], h_sem.at[0])

        def part_of(source, k, w):
            return lambda y, c: source.at[k, :, :, :, pl.ds(pl.multiple_of((y * 2 + c) * w, 128), w)]

        def done_at(k):
            def done(total):
                if k == 3:
                    outs[6][...] = total
                else:
                    outs[2 * k][...] = total[0:128]
                    outs[2 * k + 1][...] = total[128:256]
            return done

        cut = piece_count(AT_SPLIT)
        made = [Piece(place, part_of(hand[0], 1 + k, 256), done_at(k), AT_SPLIT, rest[k * cut:(k + 1) * cut]) for k in range(3)]
        made.append(Piece(place, part_of(gqkv_ref, 0, 384), done_at(3), EARLY_SPLIT, rest[3 * cut:]))
        plan = {}
        for which, times in enumerate(AT_TICKS):
            for t, at in enumerate(times):
                plan.setdefault(at, []).append((which, t))
    else:
        plan = {}

    def tick(position):
        for at, what in sorted(plan.items()):
            if min(at // 6, last) * 6 + position == at:
                def run(what=what):
                    for which, t in sorted(what, key=lambda w: (-w[1], w[0])):
                        made[which].tick(t)
                pl.when(step == min(at // 6, last))(run)

    @pl.when(step == 0)
    def _():
        for copy in weights(0, 0):
            copy.start()
        if linked:
            place.greet()

    @pl.when(step > 0)
    def _():
        for copy in results(step - 1):
            copy.wait()

    tick(0)

    @pl.when(step == 0)
    def _():
        family = fam_ref[pl.ds(lax.axis_index("seq"), 1), :].astype(F32)
        famr_s[...] = family
        for m in range(n // 128):
            rows = slice(m * 128, m * 128 + 128)
            famc_s[rows, :] = jnp.broadcast_to(family[:, rows], (128, 128)).T
        for a in range(n // 32):
            rows = slice(a * 32, a * 32 + 32)
            ca, sa = tab_ref[0, a:a + 1, :], tab_ref[1, a:a + 1, :]
            cb, sb = tab_ref[2], tab_ref[3]
            c1 = ca * cb - sa * sb
            s1 = sa * cb + ca * sb
            lane = lax.broadcasted_iota(jnp.int32, c1.shape, 1) % HEAD_DIM
            c_s[rows, :] = jnp.where(lane < ROT, c1, 1.0)
            s_s[rows, :] = jnp.where(lane < ROT // 2, -s1, jnp.where(lane < ROT, s1, 0.0))
        @functools.partial(each_band, n // 256)
        def _(rows, m):
            xhat, _ = normalize(raw_ref[rows, :].astype(F32))
            normed = (xhat * gain_ref[...] + shift_ref[...]).astype(BF16)
            x_s[rows, :] = normed
            xt_s[:, rows] = normed.T

    @pl.when(step < last)
    def _():
        for copy in weights(step + 1, 1 - slot):
            copy.start()
    for copy in weights(step, slot):
        copy.wait()

    w_ref, wo1_ref = w_s.at[slot], wo_s.at[slot]
    scaling = HEAD_DIM ** -0.5

    def both(rows):
        c, s = c_s[rows, :], s_s[rows, :]
        return jnp.concatenate([c, c], 1), jnp.concatenate([s, s], 1)

    for m in range(n // 256):
        rows = slice(m * 256, m * 256 + 256)
        raw = dot(x_s[rows, :], w_ref[...])
        c, s = both(rows)
        q_s[rows, :] = (turn(raw[:, 0:lanes], c, s, 1.0) * scaling).astype(BF16)
        keys = turn(raw[:, lanes:2 * lanes], c, s, 1.0).astype(BF16)
        k_s[rows, :] = keys
        kt_s[:, rows] = keys.T
        vals = raw[:, 2 * lanes:].astype(BF16)
        v_s[rows, :] = vals
        vt_s[:, rows] = vals.T
        do_s[rows, :] = dot_nt(g_ref[rows, :], wo1_ref[...]).astype(BF16)

    tick(1)
    tile = TILE
    lane = lax.broadcasted_iota(jnp.int32, (tile, 128), 1)
    work = [(h, i) for i in reversed(range(n // tile)) for h in range(4)]

    def first(h, i):
        span = (i + 1) * tile
        here = slice(i * tile, span)
        cols = slice(h // 2 * 128, h // 2 * 128 + 128)
        mine = (lane < HEAD_DIM) if h % 2 == 0 else (lane >= HEAD_DIM)
        qh = jnp.where(mine, q_s[here, cols], 0).astype(BF16)
        doh = jnp.where(mine, do_s[here, cols], 0).astype(BF16)
        return qh, doh, dot_nt(k_s[0:span, cols], qh), dot_nt(v_s[0:span, cols], doh)

    def second(h, i, qh, doh, st, dpt):
        span = (i + 1) * tile
        here = slice(i * tile, span)
        cols = slice(h // 2 * 128, h // 2 * 128 + 128)
        rows = slice(h * HEAD_DIM, (h + 1) * HEAD_DIM)
        family = famc_s[0:span, :]
        allowed = jnp.concatenate([family] * (tile // 128), 1) == famr_s[:, here]
        key_place = lax.broadcasted_iota(jnp.int32, (span, tile), 0)
        query_place = lax.broadcasted_iota(jnp.int32, (span, tile), 1) + i * tile
        st = jnp.where(allowed & (key_place <= query_place), st, -1e9)
        e = jnp.exp(st - jnp.max(st, 0, keepdims=True))
        p = e * (1.0 / jnp.sum(e, 0, keepdims=True))
        pb = p.astype(BF16)
        ds = (p * (dpt - jnp.sum(p * dpt, 0, keepdims=True))).astype(BF16)
        ht_s[rows, here] = dot(vt_s[rows, 0:span], pb).astype(BF16)
        dqt_s[rows, here] = dot(kt_s[rows, 0:span], ds) * scaling
        dv = dot(pb, doh)
        dk = dot(ds, qh)
        if h % 2 == 0 and i == n // tile - 1:
            dv_s[:, cols] = dv
            dk_s[:, cols] = dk
        else:
            dv_s[0:span, cols] += dv
            dk_s[0:span, cols] += dk

    made_first = first(*work[0])
    for j, (h, i) in enumerate(work):
        later = first(*work[j + 1]) if j + 1 < len(work) else None
        second(h, i, *made_first)
        made_first = later
        if h == 3 and i != 1:
            tick({3: 2, 2: 3, 0: 4}[i])

    @pl.when(step > 0)
    def _():
        if linked:
            sent, mine = heads_out(step - 1)
            for copy in sent:
                copy.wait_send()
            mine.wait()
        else:
            local_copy(heads_s, heads_ref.at[:, pl.ds(pl.multiple_of((step - 1) * lanes, lanes), lanes)], h_sem.at[0]).wait()
    heads_s[...] = ht_s[...].T
    if linked:
        sent, mine = heads_out(step)
        for copy in sent:
            copy.start()
        mine.start()
    else:
        local_copy(heads_s, heads_ref.at[:, pl.ds(pl.multiple_of(step * lanes, lanes), lanes)], h_sem.at[0]).start()

    for m in range(n // 256):
        rows = slice(m * 256, m * 256 + 256)
        c, s = both(rows)
        draw_s[rows, 0:lanes] = turn(dqt_s[:, rows].T, c, s, -1.0).astype(BF16)
        draw_s[rows, lanes:2 * lanes] = turn(dk_s[rows, :], c, s, -1.0).astype(BF16)
        draw_s[rows, 2 * lanes:] = dv_s[rows, :].astype(BF16)

    for m in range(d // 256):
        grads = dot(xt_s[m * 256:(m + 1) * 256, :], draw_s[...]).astype(BF16)
        gq_s[m, 0] = grads[0:128]
        gq_s[m, 1] = grads[128:256]
    go_s[...] = dot(ht_s[...], g_ref[...]).astype(BF16)
    for copy in results(step):
        copy.start()
    tick(5)
    for m in range(n // 256):
        here = slice(m * 256, (m + 1) * 256)
        dn = dot_nt(draw_s[here, :], w_ref[...])

        @pl.when(step == 0)
        def _():
            dn_s[here, :] = dn

        @pl.when(step > 0)
        def _():
            dn_s[here, :] += dn

    @pl.when(step == last)
    def _():
        sums_ref[...] = jnp.zeros_like(sums_ref)

        @functools.partial(each_band, n // 256)
        def _(here, m):
            total = dn_s[here, :]
            xhat, _ = normalize(raw_ref[here, :].astype(F32))
            sums_ref[0:1, :] += jnp.sum(total * xhat, 0, keepdims=True)
            sums_ref[1:2, :] += jnp.sum(total, 0, keepdims=True)
            dn_ref[here, :] = total.astype(BF16)

    tick(6)

    @pl.when(step == last)
    def _():
        for copy in results(step):
            copy.wait()
        if linked:
            for at in range(steps):
                for copy in heads_out(at)[0]:
                    copy.wait_recv()
            for copy in heads_out(step)[0]:
                copy.wait_send()
            heads_out(step)[1].wait()
        else:
            local_copy(heads_s, heads_ref.at[:, pl.ds(pl.multiple_of(step * lanes, lanes), lanes)], h_sem.at[0]).wait()


def attend(raw, g, gain, shift, wqkv, wo, families, linked, grads=None):
    n, d = raw.shape
    pair_lane = np.arange(128) % HEAD_DIM % (ROT // 2)
    freq = 10000.0 ** (-2.0 * pair_lane / ROT)
    high, low = np.arange(n // 32)[:, None] * 32.0 * freq, np.arange(32)[:, None] * freq
    tab = jnp.asarray(np.stack([np.cos(high), np.sin(high), np.cos(low), np.sin(low)]), F32)
    sd, vm = jax.ShapeDtypeStruct, pltpu.VMEM
    out_shape = [sd((n, d), BF16), sd((8, d), F32), sd((2, 4, 2, 128, 3 * d // 2) if linked else (4, 2, 128, 3 * d), BF16),
                 sd((4, 2, 128, d), BF16), sd((4, n // 4, d) if linked else (n, d), BF16)]
    out_specs = [whole((n, d)), whole((8, d))] + [ANYWHERE] * 3
    scratch = [vm((n, d), BF16), vm((d, n), BF16), vm((n, 128), F32), vm((n, 128), F32), vm((2, d, 768), BF16), vm((2, 256, d), BF16)]
    scratch += [vm((n, 256), BF16)] * 4 + [vm((256, n), BF16)] * 3
    scratch += [vm((256, n), F32), vm((n, 256), F32), vm((n, 256), F32), vm((n, 768), BF16), vm((n, d), F32), vm((4, 2, 128, 768), BF16),
                vm((256, d), BF16), vm((n, 256), BF16), vm((1, n), F32), vm((n, 128), F32), DMA((2, 6)), DMA((2, 2)), DMA((6,)), DMA((2,)), DMA((1,))]
    params, more = {}, []
    if linked:
        more = [grads]
        out_shape += [sd((128, 256), F32)] * 6 + [sd((128, 384), F32)]
        out_specs += [whole((128, 256))] * 6 + [whole((128, 384))]
        scratch += [DMA((4, 3)), DMA((4, 3))]
        scratch += piece_scratch(256, AT_SPLIT) * 3 + piece_scratch(384, EARLY_SPLIT)
        params = dict(collective_id=1, has_side_effects=True)
    return pl.pallas_call(
        functools.partial(attn_kernel, linked=linked), out_shape=out_shape, grid=(len(ORDER),),
        in_specs=[whole((n, d)), whole((n, d)), whole((1, d)), whole((1, d)), whole(families.shape), whole((4, 32, 128)), ANYWHERE, ANYWHERE]
        + [ANYWHERE] * len(more),
        out_specs=out_specs, scratch_shapes=scratch,
        compiler_params=pltpu.CompilerParams(vmem_limit_bytes=60 * 2**20, **params),
        cost_estimate=pl.CostEstimate(flops=70_000_000_000, bytes_accessed=30_000_000, transcendentals=20_000_000),
    )(raw, g, gain.reshape(1, d), shift.reshape(1, d), families, tab, wqkv, wo, *more)


class SmallSum:
    def __init__(self, place, held, heard, by_z, send, recv):
        self.p, self.held, self.heard, self.by_z, self.send, self.recv = place, held, heard, by_z, send, recv

    def copies(self, t):
        p = self.p
        if t < 3:
            to = (p.twin, p.beside_y, p.beside_x)[t]
            return [remote_copy(self.held, self.heard.at[t], self.send.at[t], self.recv.at[t], to)]
        return [remote_copy(self.by_z.at[p.z], self.by_z.at[p.z], self.send.at[3 + j], self.recv.at[3 + j], to)
                for j, to in enumerate(p.along_z)]

    def tick(self, t):
        if t > 0:
            for copy in self.copies(t - 1):
                copy.wait()
        if 0 < t < 4:
            total = self.held[...] + self.heard[t - 1]
            if t < 3:
                self.held[...] = total
            else:
                self.by_z[self.p.z] = total
        if t < 4:
            for copy in self.copies(t):
                copy.start()
        return None if t < 4 else self.by_z[0] + self.by_z[1] + self.by_z[2] + self.by_z[3]


def tail_kernel(dat_ref, heads_ref, gq_ref, go_ref, inp_ref, cot_ref, act_ref, wd_ref, dn_ref, wo_ref, part_ref, gain_ref, dbias_ref, sums_ff_ref, sums_at_ref,
                ub_ref, early_ref, lo_ref, ig_ref, qkv_ref, out_ref, gain_o, shift_o, ub_o, db_o,
                back_s, inp_s, g_s, heads_s, y_s, dn_s, wo_s, lo_s, ig_s, small_s, heard_s, by_z_s, act_s, wd_s, act_sem, wd_sem,
                load_sem, wo_sem, back_send, back_recv, own_sem, small_send, small_recv, lo_sem, ig_sem, *pieces):
    place = Place()
    d = wo_s.shape[0]
    place.greet()
    swaps = [remote_copy(dat_ref.at[to], back_s.at[place.seq], back_send.at[j], back_recv.at[j], device)
             for j, (to, device) in enumerate(place.peers)]
    own = local_copy(dat_ref.at[place.seq], back_s.at[place.seq], own_sem.at[0])
    blocks = {}

    def part(source, w, row0, rows):
        return lambda y, c: source.at[:, :, pl.ds(row0, rows), pl.ds(pl.multiple_of((y * 2 + c) * w, 128), w)]

    def out_done(total):
        out_ref[...] = total

    def qkv_done(row0):
        def done(total):
            rows = slice(row0, row0 + total.shape[0])
            early = early_ref[rows, :]
            first = jnp.where(place.c == 0, early, total)
            second = jnp.where(place.c == 0, total, early)
            order = ((first, 0), (second, 0), (second, 1), (first, 1), (first, 2), (second, 2))
            for k, (source, at) in enumerate(order):
                qkv_ref[rows, k * 128:(k + 1) * 128] = source[:, at * 128:(at + 1) * 128]
        return done

    cuts = [0, piece_count(TAIL_SPLITS[0])]
    for split in TAIL_SPLITS[1:]:
        cuts.append(cuts[-1] + piece_count(split))
    late = gq_ref.at[1]
    row1 = sum(TAIL_SPLITS[1])
    made = [Piece(place, part(go_ref, 256, 0, 128), out_done, TAIL_SPLITS[0], pieces[:cuts[1]]),
            Piece(place, part(late, 384, 0, row1), qkv_done(0), TAIL_SPLITS[1], pieces[cuts[1]:cuts[2]]),
            Piece(place, part(late, 384, row1, 128 - row1), qkv_done(row1), TAIL_SPLITS[2], pieces[cuts[2]:])]
    small = SmallSum(place, small_s, heard_s, by_z_s, small_send, small_recv)
    small_s[0:3, :] = sums_ff_ref[0:3, :]
    small_s[0:2, :] += sums_at_ref[0:2, :]
    small_s[3:4, :] = jnp.zeros((1, d), F32)
    for k in range(4):
        small_s[4 + k:5 + k, :] = ub_ref[:, k * d:(k + 1) * d]
    for piece in made:
        piece.tick(0)
    for copy in swaps:
        copy.start()
    small.tick(0)
    loads = [local_copy(a, b, load_sem.at[k]) for k, (a, b) in enumerate(
        ((heads_ref, heads_s), (inp_ref, inp_s), (cot_ref, g_s), (dn_ref, dn_s)))]
    for pair in range(d // 128):
        at = [p for two in ORDER for p in two].index(pair)
        blocks[at] = local_copy(wo_ref.at[pl.ds(pair * 128, 128), :], wo_s.at[pl.ds(at * 128, 128), :], wo_sem.at[at])
    for copy in [loads[0]] + list(blocks.values()) + loads[1:] + [own]:
        copy.start()

    def lo_out(r):
        return local_copy(lo_s.at[r], lo_ref.at[r], lo_sem.at[r])

    def ig_out(r):
        return local_copy(ig_s.at[r], ig_ref.at[r], ig_sem.at[r])

    def forward(r, carry):
        total = inp_s[r].astype(F32) + dot(heads_s[r], wo_s[...]) + y_s[r]
        lo_s[r] = total.astype(BF16)
        lo_out(r).start()
        return carry

    def backward(r):
        xhat, scale = normalize(inp_s[r].astype(F32))
        dx = (dn_s[r] + back_s[r].astype(F32)) * gain_ref[...]
        ig_s[r] = g_s[lax.rem(part_ref[r], 4)].astype(F32) + (dx - jnp.mean(dx, -1, keepdims=True) - xhat * jnp.mean(dx * xhat, -1, keepdims=True)) * scale
        ig_out(r).start()

    hidden = wd_ref.shape[0]
    chunks = hidden // 512

    def chunk(at, slot):
        out = [local_copy(act_ref.at[at], act_s.at[slot], act_sem.at[slot])]
        for k, f in hidden_runs(at, hidden):
            f = pl.multiple_of(f, 128)
            out.append(local_copy(wd_ref.at[pl.ds(f, 128), :], wd_s.at[slot, pl.ds(k * 128, 128), :], wd_sem.at[slot, k]))
        return out

    for copy in chunk(0, 0):
        copy.start()

    def down(at, carry):
        slot = at % 2

        @pl.when(at + 1 < chunks)
        def _():
            for copy in chunk(at + 1, 1 - slot):
                copy.start()

        @pl.when(at == TAIL_FIRST)
        def _():
            for piece in made:
                piece.tick(1)
            small.tick(1)

        @pl.when(at == TAIL_FIRST + 4)
        def _():
            small.tick(2)

        for copy in chunk(at, slot):
            copy.wait()
        for r in range(4):
            y_s[r] += dot(act_s[slot, r * 256:(r + 1) * 256, :], wd_s[slot])
        return carry

    for r in range(4):
        y_s[r] = jnp.broadcast_to(dbias_ref[...], y_s.shape[1:])
    lax.fori_loop(0, chunks, down, 0)
    for copy in list(blocks.values()) + loads[:2]:
        copy.wait()
    lax.fori_loop(0, 2, forward, 0)
    made[0].tick(2)
    lax.fori_loop(2, 4, forward, 0)
    made[1].tick(2)
    made[2].tick(2)
    small.tick(3)
    loads[2].wait()
    loads[3].wait()
    own.wait()
    made[0].tick(3)
    backward(place.seq)
    for j in range(3):
        swaps[j].wait_send()
    swaps[2].wait_recv()
    backward((place.seq + 1) % 4)
    made[1].tick(3)
    made[2].tick(3)
    swaps[1].wait_recv()
    swaps[0].wait_recv()
    lax.fori_loop(2, 4, lambda j, carry: (backward((place.seq + j) % 4), carry)[1], 0)
    total = small.tick(4)
    for piece in made:
        piece.tick(4)
    gain_o[...] = total[0:1]
    shift_o[...] = total[1:2]
    db_o[...] = total[2:3]
    for k in range(4):
        ub_o[:, k * d:(k + 1) * d] = total[4 + k:5 + k]
    for r in range(4):
        lo_out(r).wait()
        ig_out(r).wait()


def finish(dat, heads, gq, go, inp, cot, act, wd, dn, wo, partners, gain, dbias, sums_ff, sums_at, ub, early):
    sd, vm = jax.ShapeDtypeStruct, pltpu.VMEM
    shape, d = inp.shape, inp.shape[2]
    vmem = pl.BlockSpec(memory_space=pltpu.VMEM)
    return pl.pallas_call(
        tail_kernel,
        out_shape=[sd(shape, BF16), sd(shape, F32), sd((128, 768), F32), sd((128, 256), F32), sd((1, d), F32), sd((1, d), F32), sd((1, 4 * d), F32),
                   sd((1, d), F32)],
        in_specs=[ANYWHERE] * 10 + [pl.BlockSpec(memory_space=pltpu.SMEM)] + [vmem] * 6, out_specs=[ANYWHERE] * 2 + [vmem] * 6,
        scratch_shapes=[vm(shape, BF16)] * 4 + [vm(shape, F32)] * 2 + [vm((d, d), BF16), vm(shape, BF16), vm(shape, F32),
                        vm((8, d), F32), vm((3, 8, d), F32), vm((4, 8, d), F32), vm((2, 1024, 512), BF16), vm((2, 512, d), BF16), DMA((2,)), DMA((2, 4)),
                        DMA((4,)), DMA((8,)), DMA((3,)), DMA((3,)), DMA((1,)), DMA((6,)), DMA((6,)), DMA((4,)), DMA((4,))]
        + piece_scratch(256, TAIL_SPLITS[0]) + piece_scratch(384, TAIL_SPLITS[1]) + piece_scratch(384, TAIL_SPLITS[2]),
        compiler_params=pltpu.CompilerParams(collective_id=2, has_side_effects=True, vmem_limit_bytes=56 * 2**20),
    )(dat.reshape(shape), heads, gq, go, inp, cot, act, wd, dn.reshape(shape), wo, partners, gain.reshape(1, d), dbias.reshape(1, d), sums_ff, sums_at,
      ub, early)


def copy_kernel(*refs, moves, count):
    ins, outs, held, (in_sem, out_sem) = refs[:count], refs[count:count + 10], refs[count + 10:2 * count + 10], refs[2 * count + 10:]
    loads = [local_copy(ins[a].at[at], held[a].at[at], in_sem.at[k]) for k, (a, at, _) in enumerate(moves)]
    for copy in loads:
        copy.start()
    stores = []
    for k, (a, at, places) in enumerate(moves):
        loads[k].wait()
        for source, b, to in places:
            stores.append(local_copy(held[a].at[source], outs[b].at[to], out_sem.at[len(stores)]))
            stores[-1].start()
    for copy in stores:
        copy.wait()


def gather_up(*parts):
    sd, every = jax.ShapeDtypeStruct, (slice(None), slice(None))
    shapes = [sd(p.shape, p.dtype) for p in parts[:8]] + [sd((128, 1024), F32), sd((512, 256), F32)]
    moves = [(a, r, [(r, a, r)]) for r in range(4) for a in (1, 0)]
    for k in range(4):
        moves.append((8 + k, every, [((slice(None), slice(half * 128, half * 128 + 128)), 8, (slice(None), slice(half * 512 + k * 128, half * 512 + k * 128 + 128)))
                                     for half in range(2)]))
        moves.append((12 + k, every, [(every, 9, (slice(k * 128, k * 128 + 128), slice(None)))]))
    moves += [(a, every, [(every, a, every)]) for a in range(2, 8)]
    return pl.pallas_call(
        functools.partial(copy_kernel, moves=moves, count=len(parts)), out_shape=shapes, in_specs=[ANYWHERE] * len(parts), out_specs=[ANYWHERE] * 10,
        scratch_shapes=[pltpu.VMEM(p.shape, p.dtype) for p in parts] + [DMA((len(moves),)), DMA((sum(len(m[2]) for m in moves),))],
        compiler_params=pltpu.CompilerParams(vmem_limit_bytes=60 * 2**20),
    )(*parts)


def on_device(inputs, norm_gain, norm_shift, qkv_weight, out_weight, up_weight, up_bias, down_weight, down_bias, partners, families, cotangent, linked):
    row_count, place_count, width = inputs.shape
    tokens = row_count * place_count
    branch_args = norm_gain, norm_shift, qkv_weight, out_weight, families, linked
    if linked:
        act, dn, sums_ff, ub, grads, row_inputs, row_grad, up0, down0 = feed_forward(
            inputs, cotangent, partners, norm_gain, norm_shift, up_bias, up_weight, down_weight, True)
        dat, sums_at, gq, go, heads, up1, down1, up2, down2, up3, down3, early = attend(
            row_inputs.reshape(tokens, width), row_grad.reshape(tokens, width), *branch_args, grads)
        layer_out, input_grad, qkv_sum, out_sum, gain_sum, shift_sum, ub_sum, db_sum = finish(
            dat, heads, gq, go, inputs, cotangent, act, down_weight, dn, out_weight, partners, norm_gain, down_bias, sums_ff, sums_at, ub, early)
        layer_out, input_grad, qkv_sum, out_sum, gain_sum, shift_sum, ub_sum, db_sum, up_sum, down_sum = gather_up(
            layer_out, input_grad, qkv_sum, out_sum, gain_sum, shift_sum, ub_sum, db_sum, up0, up1, up2, up3, down0, down1, down2, down3)
        return (layer_out.reshape(inputs.shape), input_grad.reshape(inputs.shape), gain_sum.reshape(width), shift_sum.reshape(width), qkv_sum, out_sum,
                up_sum, ub_sum.reshape(-1), down_sum, db_sum.reshape(width))
    local_rows = partners - lax.axis_index("dp") * row_count
    grad = jnp.take(cotangent, local_rows, axis=0, mode="clip")
    swap = functools.partial(lax.all_to_all, axis_name="seq", split_axis=0, concat_axis=0, tiled=True)
    row_inputs, row_grad = swap(inputs).reshape(tokens, width), swap(grad).reshape(tokens, width)
    y, dn, sums_ff, ub, up_grad, down_grad = feed_forward(
        inputs, cotangent, partners, norm_gain, norm_shift, up_bias, up_weight, down_weight, False)
    dat, sums_at, qkv_grad, out_grad, heads = attend(row_inputs, row_grad, *branch_args)

    def scatter(parts, columns):
        part = lax.psum_scatter(parts.reshape(-1, columns), "seq", scatter_dimension=1, tiled=True)
        return lax.psum_scatter(part, "dp", scatter_dimension=0, tiled=True).astype(F32)

    qkv_sum, out_sum = scatter(qkv_grad, 3 * width), scatter(out_grad, width)
    up_sum, down_sum = scatter(up_grad, up_bias.shape[0]), scatter(down_grad, width)
    heads = swap(heads.reshape(inputs.shape)).reshape(tokens, width)
    order = np.array([p for two in ORDER for p in two])
    attn_out = dot(heads, out_weight.reshape(-1, 128, width)[order].reshape(width, width))
    values = inputs.astype(F32).reshape(tokens, width)
    layer_out = (values + attn_out + (y + down_bias)).astype(BF16).reshape(inputs.shape)
    xhat, scale = normalize(values)
    dx = (dn + swap(dat.reshape(inputs.shape)).reshape(tokens, width).astype(F32)) * norm_gain
    input_grad = grad.reshape(tokens, width).astype(F32) + (dx - jnp.mean(dx, -1, keepdims=True) - xhat * jnp.mean(dx * xhat, -1, keepdims=True)) * scale
    gain_sum, shift_sum, up_bias_sum, down_bias_sum = lax.psum((sums_ff[0] + sums_at[0], sums_ff[1] + sums_at[1], ub[0], sums_ff[2]), ("dp", "seq"))
    return (layer_out, input_grad.reshape(inputs.shape), gain_sum, shift_sum, qkv_sum, out_sum, up_sum, up_bias_sum, down_sum, down_bias_sum)


def solution(mesh):
    rows = P("dp", "seq", None)
    placed = (rows,) + (P(),) * 8 + (P("dp"), P("dp", None), rows)
    grads = P("dp", "seq")
    linked = (mesh.shape["dp"], mesh.shape["seq"]) == (8, 4)
    return jax.shard_map(functools.partial(on_device, linked=linked), mesh=mesh, in_specs=placed,
                         out_specs=(rows, rows, P(), P(), grads, grads, grads, P(), grads, P()), check_vma=False)
```

```python
import functools

import jax
import jax.numpy as jnp
import numpy as np
from jax import lax
from jax.experimental import pallas as pl
from jax.experimental.pallas import tpu as pltpu
from jax.sharding import PartitionSpec as P

F32 = jnp.float32
BF16 = jnp.bfloat16
HEAD_DIM = 64
ROT = 32
EPS = 1e-05
C0 = 0.7978845608028654
C1 = C0 * 0.044715
TILE = 256
FF_SPLIT = 0, 176, 80
AT_SPLIT = 64, 128, 64
EARLY_SPLIT = 48, 64, 16
TAIL_FIRST = 2
TAIL_SPLITS = (0, 80, 48), (0, 48, 16), (0, 32, 32)
FF_TICKS = 6, 10, 18, 21, 24
AT_TICKS = (0, 2, 7, 10, 14), (4, 7, 12, 15, 19), (8, 12, 17, 20, 23), (13, 17, 21, 23, 24)
ORDER = ((0, 3), (4, 7), (1, 2), (5, 6))
MESH_ID = pl.DeviceIdType.MESH
ANYWHERE = pl.BlockSpec(memory_space=pl.ANY)
DMA = pltpu.SemaphoreType.DMA


def dot(a, b):
    return lax.dot_general(a, b, (((1,), (0,)), ((), ())), preferred_element_type=F32)


def dot_nt(a, b):
    return lax.dot_general(a, b, (((1,), (1,)), ((), ())), preferred_element_type=F32)


def dot_tn(a, b):
    return lax.dot_general(a, b, (((0,), (0,)), ((), ())), preferred_element_type=F32)


def whole(shape):
    return pl.BlockSpec(shape, lambda p: (0,) * len(shape), pipeline_mode=pl.Buffered(1))


def pick(step, values):
    out = jnp.int32(values[0])
    for i, value in enumerate(values[1:], 1):
        out = jnp.where(step == i, value, out)
    return out


def normalize(values):
    centered = values - jnp.mean(values, -1, keepdims=True)
    scale = lax.rsqrt(jnp.mean(centered * centered, -1, keepdims=True) + EPS)
    return centered * scale, scale


def each_band(count, body):
    def step(m, carry):
        body(pl.ds(pl.multiple_of(m * 256, 256), 256), m)
        return carry

    lax.fori_loop(0, count, step, 0)


def local_copy(src, dst, sem):
    return pltpu.make_async_copy(src, dst, sem)


def remote_copy(src, dst, send, recv, to):
    return pltpu.make_async_remote_copy(src_ref=src, dst_ref=dst, send_sem=send, recv_sem=recv, device_id=to,
                                        device_id_type=MESH_ID)


class Place:
    def __init__(self):
        self.dp, self.seq = lax.axis_index("dp"), lax.axis_index("seq")
        self.z, self.x, self.y, self.c = self.dp // 2, self.dp % 2, self.seq // 2, self.seq % 2
        self.twin = (self.dp, self.y * 2 + 1 - self.c)
        self.beside_y = (self.dp, (1 - self.y) * 2 + self.c)
        self.across = (self.dp, (1 - self.y) * 2 + 1 - self.c)
        self.beside_x = (self.z * 2 + 1 - self.x, self.seq)
        self.along_z = [(((self.z + j) % 4) * 2 + self.x, self.seq) for j in (1, 2, 3)]
        self.peers = [((self.seq + j) % 4, (self.dp, (self.seq + j) % 4)) for j in (1, 2, 3)]
        self.partners = [self.twin, self.beside_y, self.beside_x] + self.along_z

    def greet(self):
        for partner in self.partners + [self.across]:
            pl.semaphore_signal(pltpu.get_barrier_semaphore(), inc=1, device_id=partner, device_id_type=MESH_ID)

    def meet(self):
        pl.semaphore_wait(pltpu.get_barrier_semaphore(), len(self.partners) + 1)


def add_into(dst, src, lead):
    rows, w = src.shape[-2:]
    band = rows
    while band * w > 65536 and band % 32 == 0:
        band //= 2
    count = 1
    for n in lead:
        count *= n

    def body(t, carry):
        block, part = t // (rows // band), t % (rows // band)
        index = []
        for n in reversed(lead):
            index.insert(0, block % n)
            block = block // n
        at = tuple(index) + (pl.ds(pl.multiple_of(part * band, band), band), slice(None))
        dst[at] = dst[at] + src[at]
        return carry

    lax.fori_loop(0, count * (rows // band), body, 0)


def piece_scratch(w, split):
    ra, rb, rc = split
    r = sum(split)
    out = [((2, 4, 2, r), 1), ((2, 4, 2, r), 1), ((4, 2, ra), ra), ((2, 4, rb), rb), ((3, 2, 2, rc), rc), ((4, ra), ra), ((4, rb), rb), ((2, rc), rc),
           ((3, ra + rb), ra + rb), ((rc,), rc)]
    return [pltpu.VMEM(shape + (w,), BF16) for shape, used in out if used] + [DMA((14,)), DMA((14,)), DMA((2,))]


def piece_count(split):
    return len(piece_scratch(128, split))


class Piece:
    def __init__(self, place, part, done, split, scratch):
        self.p, self.part, self.done, self.split = place, part, done, split
        ra, rb, rc = split
        names = [("a", 1), ("from_twin", 1), ("ya", ra), ("xb", rb), ("zc", rc), ("xa", ra), ("yb", rb), ("xc", rc), ("zab", ra + rb), ("yc", rc)]
        scratch = list(scratch)
        for name, used in names:
            setattr(self, name, scratch.pop(0) if used else None)
        self.ss, self.rs, self.ls = scratch
        self.rows_a, self.rows_b, self.rows_ab, self.rows_c = pl.ds(0, ra), pl.ds(ra, rb), pl.ds(0, ra + rb), pl.ds(ra + rb, rc)

    def copies(self, stage):
        p, a, (ra, rb, rc) = self.p, self.a, self.split
        out = []
        slot = (0, 2, 7, 10)[stage]

        def send(src, dst, to):
            k = slot + len(out)
            out.append(remote_copy(src, dst, self.ss.at[k], self.rs.at[k], to))

        zs = [((p.z + 1 + j) % 4, p.along_z[j]) for j in range(3)]
        if stage == 0:
            for k in (0, 1):
                send(self.part(k, 1 - p.c), self.from_twin.at[k], p.twin)
        if stage == 1:
            if ra:
                send(a.at[1 - p.y, :, :, self.rows_a, :], self.ya, p.beside_y)
            if rb:
                send(a.at[:, :, 1 - p.x, self.rows_b, :], self.xb, p.beside_x)
            for j in range(3 if rc else 0):
                send(a.at[:, zs[j][0], :, self.rows_c, :], self.zc.at[j], zs[j][1])
        if stage == 2:
            if ra:
                send(a.at[p.y, :, 1 - p.x, self.rows_a, :], self.xa, p.beside_x)
            if rb:
                send(a.at[1 - p.y, :, p.x, self.rows_b, :], self.yb, p.beside_y)
            if rc:
                send(a.at[:, p.z, 1 - p.x, self.rows_c, :], self.xc, p.beside_x)
        if stage == 3:
            for j in range(3 if ra + rb else 0):
                send(a.at[p.y, zs[j][0], p.x, self.rows_ab, :], self.zab.at[j], zs[j][1])
            if rc:
                send(a.at[1 - p.y, p.z, p.x, self.rows_c, :], self.yc, p.beside_y)
        return out

    def own(self):
        return [local_copy(self.part(k, self.p.c), self.a.at[k], self.ls.at[k]) for k in (0, 1)]

    def tick(self, t):
        p, a, (ra, rb, rc) = self.p, self.a, self.split
        if t > 0:
            for copy in self.copies(t - 1):
                copy.wait()
        if t == 0:
            for copy in self.copies(0) + self.own():
                copy.start()
        if t == 1:
            for copy in self.own():
                copy.wait()
            add_into(a, self.from_twin, (2, 4, 2))
        if t == 2:
            if ra:
                add_into(a.at[p.y, :, :, self.rows_a, :], self.ya, (4, 2))
            if rb:
                add_into(a.at[:, :, p.x, self.rows_b, :], self.xb, (2, 4))
            for j in range(3 if rc else 0):
                add_into(a.at[:, p.z, :, self.rows_c, :], self.zc.at[j], (2, 2))
        if t == 3:
            if ra:
                add_into(a.at[p.y, :, p.x, self.rows_a, :], self.xa, (4,))
            if rb:
                add_into(a.at[p.y, :, p.x, self.rows_b, :], self.yb, (4,))
            if rc:
                add_into(a.at[:, p.z, p.x, self.rows_c, :], self.xc, (2,))
        if t in (1, 2, 3):
            for copy in self.copies(t):
                copy.start()
        if t == 4:
            mine = a.at[p.y, p.z, p.x]
            parts = []
            if ra + rb:
                total = mine[self.rows_ab, :].astype(F32)
                for j in range(3):
                    total += self.zab[j].astype(F32)
                parts.append(total)
            if rc:
                parts.append(mine[self.rows_c, :].astype(F32) + self.yc[...].astype(F32))
            self.done(jnp.concatenate(parts, 0) if len(parts) > 1 else parts[0])


def hidden_runs(at, hidden):
    return [(s, (2 * s + at % 2) * (hidden // 8) + at // 2 * 128) for s in range(4)]


def ff_kernel(part_ref, inp_ref, cot_ref, gain_ref, shift_ref, bias_ref, wu_ref, wd_ref, *rest, linked):
    hand, rest = (rest[:1], rest[1:]) if linked else ((), rest)
    y_ref, dn_ref, sums_ref, ub_ref = rest[:4]
    outs, rest = (rest[4:9], rest[9:]) if linked else (rest[4:6], rest[6:])
    x_s, xt_s, act_s, dh_s, wu_s, wd_s, gu_s, gd_s, g_ref, wu_sem, wd_sem, gu_sem, gd_sem, act_sem = rest[:14]
    rest = rest[14:]
    step = pl.program_id(0)
    last = pl.num_programs(0) - 1
    n, d = x_s.shape
    hidden = bias_ref.shape[1]
    tile = 512
    slot = step % 2

    def places(at):
        return hidden_runs(at, hidden)

    def weights(at, slot):
        out = []
        for s, f in places(at):
            f = pl.multiple_of(f, 128)
            out.append(local_copy(wu_ref.at[:, pl.ds(f, 128)], wu_s.at[slot, :, pl.ds(s * 128, 128)], wu_sem.at[slot, s]))
            out.append(local_copy(wd_ref.at[pl.ds(f, 128), :], wd_s.at[slot, pl.ds(s * 128, 128), :], wd_sem.at[slot, s]))
        return out

    def results(at):
        out = []
        k, j = at // 2, at % 2
        for s, f in places(at):
            f = pl.multiple_of(f, 128)
            up, down = gu_s.at[:, :, :, pl.ds(s * 128, 128)], gd_s.at[pl.ds(s * 128, 128), :]
            if linked:
                col = pl.multiple_of(s * 256 + j * 128, 128)
                to = outs[0].at[k, :, :, pl.ds(0, 128), pl.ds(col, 128)], outs[0].at[k, s, j, pl.ds(128, 128), :]
            else:
                to = outs[0].at[:, :, :, pl.ds(f, 128)], outs[1].at[pl.ds(f, 128), :]
            out.append(local_copy(up, to[0], gu_sem.at[s]))
            out.append(local_copy(down, to[1], gd_sem.at[s]))
        return out

    def keep(at):
        return [local_copy(act_s, y_ref.at[at], act_sem.at[0])] if linked else []

    if linked:
        place = Place()
        row_send, row_recv, own_sem = rest[:3]
        rest = rest[3:]

        def swaps(a):
            span = n // 4

            def row(at):
                return g_ref.at[pl.ds(pl.multiple_of(at * span, span), span), :] if a else hand[0].at[at]

            out = [remote_copy(row(to), outs[1 + a].at[place.seq], row_send.at[a, j], row_recv.at[a, j], device)
                   for j, (to, device) in enumerate(place.peers)]
            return out + [local_copy(row(place.seq), outs[1 + a].at[place.seq], own_sem.at[a])]

        def part_of(k):
            return lambda y, c: outs[0].at[k, :, :, :, pl.ds(pl.multiple_of((y * 2 + c) * 256, 256), 256)]

        def done_at(k):
            def done(total):
                outs[3 + 2 * k][...] = total[0:128]
                outs[4 + 2 * k][...] = total[128:256]
            return done

        made = [Piece(place, part_of(0), done_at(0), FF_SPLIT, rest)]

    def tick(position):
        for which, times in enumerate((FF_TICKS,) if linked else ()):
            for t, at in enumerate(times):
                if min(at // 3, 7) * 3 + position == at:
                    pl.when(step == min(at // 3, 7))(functools.partial(made[which].tick, t))

    @pl.when(step == 0)
    def _():
        for copy in weights(0, 0):
            copy.start()
        if linked:
            place.greet()
        count, span, _ = cot_ref.shape
        for r in range(count):
            g_ref[r * span:(r + 1) * span, :] = cot_ref[lax.rem(part_ref[r], count)]
        if linked:
            place.meet()
            for copy in swaps(0) + swaps(1):
                copy.start()
        sums_ref[...] = jnp.zeros_like(sums_ref)

        @functools.partial(each_band, n // 256)
        def _(rows, m):
            xhat, _ = normalize(inp_ref[rows, :].astype(F32))
            normed = (xhat * gain_ref[...] + shift_ref[...]).astype(BF16)
            x_s[rows, :] = normed
            xt_s[:, rows] = normed.T
            sums_ref[2:3, :] += jnp.sum(g_ref[rows, :].astype(F32), 0, keepdims=True)

    @pl.when(step > 0)
    def _():
        for copy in results(step - 1) + keep(step - 1):
            copy.wait()

    tick(0)

    @pl.when(step < last)
    def _():
        for copy in weights(step + 1, 1 - slot):
            copy.start()
    for copy in weights(step, slot):
        copy.wait()
    w_up, w_down = wu_s.at[slot], wd_s.at[slot]
    bias = jnp.concatenate([bias_ref[:, pl.ds(pl.multiple_of(f, 128), 128)] for _, f in places(step)], 1)
    unit_sums = None
    for m in range(n // tile):
        here = slice(m * tile, (m + 1) * tile)
        v = dot(x_s[here, :], w_up[...]) + bias
        vv = v * v
        a = 0.5 + 0.5 * jnp.tanh(v * (C0 + C1 * vv))
        act = v * a
        slope = a + act * (1.0 - a) * (2 * C0 + 6 * C1 * vv)
        act_s[here, :] = act.astype(BF16)
        dh = (dot_nt(g_ref[here, :], w_down[...]) * slope).astype(BF16)
        dh_s[here, :] = dh
        total = jnp.sum(dh.astype(F32), 0, keepdims=True)
        unit_sums = total if unit_sums is None else unit_sums + total
    for copy in keep(step):
        copy.start()
    for s, f in places(step):
        ub_ref[:, pl.ds(pl.multiple_of(f, 128), 128)] = unit_sums[:, s * 128:(s + 1) * 128]

    tick(1)
    for m in range(d // 256):
        grads = dot(xt_s[m * 256:(m + 1) * 256, :], dh_s[...]).astype(BF16)
        gu_s[m, 0] = grads[0:128]
        gu_s[m, 1] = grads[128:256]
    gd_s[...] = dot_tn(act_s[...], g_ref[...]).astype(BF16)
    for copy in results(step):
        copy.start()
    tick(2)
    for m in range(n // tile):
        here = slice(m * tile, (m + 1) * tile)
        y = None if linked else dot(act_s[here, :], w_down[...])
        dn = dot_nt(dh_s[here, :], w_up[...])

        @pl.when(step == 0)
        def _():
            if not linked:
                y_ref[here, :] = y
            dn_ref[here, :] = dn

        @pl.when(step > 0)
        def _():
            if not linked:
                y_ref[here, :] += y
            dn_ref[here, :] += dn

    tick(3)

    @pl.when(step == last)
    def _():
        @functools.partial(each_band, n // 256)
        def _(here, m):
            total = dn_ref[here, :]
            xhat, _ = normalize(inp_ref[here, :].astype(F32))
            sums_ref[0:1, :] += jnp.sum(total * xhat, 0, keepdims=True)
            sums_ref[1:2, :] += jnp.sum(total, 0, keepdims=True)

        for copy in results(step) + keep(step):
            copy.wait()
        if linked:
            for copy in swaps(0) + swaps(1):
                copy.wait()


def feed_forward(inp, cot, partners, gain, shift, bias, wu, wd, linked):
    rows, span, d = inp.shape
    n, hidden = rows * span, bias.shape[0]
    sd, vm = jax.ShapeDtypeStruct, pltpu.VMEM
    out_shape = [sd((hidden // 512, n, 512), BF16) if linked else sd((n, d), F32), sd((n, d), F32), sd((8, d), F32), sd((1, hidden), F32)]
    out_specs = [ANYWHERE if linked else whole((n, d)), whole((n, d)), whole((8, d)), whole((1, hidden))]
    scratch = [vm((n, d), BF16), vm((d, n), BF16), vm((n, 512), BF16), vm((n, 512), BF16), vm((2, d, 512), BF16), vm((2, 512, d), BF16),
               vm((4, 2, 128, 512), BF16), vm((512, d), BF16), vm((n, d), BF16), DMA((2, 4)), DMA((2, 4)), DMA((4,)), DMA((4,)), DMA((1,))]
    more, params = [], {}
    if linked:
        more = [inp]
        out_shape += [sd((4, 4, 2, 256, d), BF16), sd(inp.shape, BF16), sd(inp.shape, BF16), *[sd((128, 256), F32)] * 2]
        out_specs += [ANYWHERE] * 3 + [whole((128, 256))] * 2
        scratch += [DMA((2, 3)), DMA((2, 3)), DMA((2,))] + piece_scratch(256, FF_SPLIT)
        params = dict(collective_id=0, has_side_effects=True)
    else:
        out_shape += [sd((4, 2, 128, hidden), BF16), sd((hidden, d), BF16)]
        out_specs += [ANYWHERE] * 2
    return pl.pallas_call(
        functools.partial(ff_kernel, linked=linked), out_shape=out_shape, grid=(hidden // 512,),
        in_specs=[pl.BlockSpec(memory_space=pltpu.SMEM), whole((n, d)), whole(cot.shape), whole((1, d)), whole((1, d)), whole((1, hidden)), ANYWHERE, ANYWHERE] + [ANYWHERE] * len(more),
        out_specs=out_specs, scratch_shapes=scratch,
        compiler_params=pltpu.CompilerParams(vmem_limit_bytes=58 * 2**20, **params),
        cost_estimate=pl.CostEstimate(flops=52_000_000_000, bytes_accessed=50_000_000, transcendentals=4_000_000),
    )(partners, inp.reshape(n, d), cot, gain.reshape(1, d), shift.reshape(1, d), bias.reshape(1, hidden), wu, wd, *more)


def turn(x, c, s, sign):
    lanes = x.shape[1]
    lane = lax.broadcasted_iota(jnp.int32, x.shape, 1) % HEAD_DIM
    other = jnp.where(lane < ROT // 2, pltpu.roll(x, lanes - ROT // 2, 1), pltpu.roll(x, ROT // 2, 1))
    return x * c + (sign * other) * s


def tile_place(tile):
    early = [kind * 8 + pair for two in ORDER[:2] for pair in two for kind in range(3)]
    block = tile // 6
    mates = sorted(t for t in range(24) if t // 6 == block and (t in early) == (tile in early))
    return block, mates.index(tile)


def attn_kernel(raw_ref, g_ref, gain_ref, shift_ref, fam_ref, tab_ref, wqkv_ref, wo_ref, *rest, linked):
    hand, rest = (rest[:1], rest[1:]) if linked else ((), rest)
    dn_ref, sums_ref, gqkv_ref, go_ref, heads_ref = rest[:5]
    outs, rest = (rest[5:12], rest[12:]) if linked else ((), rest[5:])
    (x_s, xt_s, c_s, s_s, w_s, wo_s, q_s, k_s, v_s, do_s, kt_s, vt_s, ht_s, dqt_s, dk_s, dv_s, draw_s, dn_s, gq_s, go_s, heads_s,
     famr_s, famc_s, w_sem, wo_sem, gq_sem, go_sem, h_sem) = rest[:28]
    rest = rest[28:]
    step = pl.program_id(0)
    steps = len(ORDER)
    last = steps - 1
    n, d = raw_ref.shape
    lanes = 256
    pairs = d // 128
    slot = step % 2

    def weights(at, slot):
        out = []
        for half in range(2):
            pair = pick(at, [o[half] for o in ORDER])
            for kind in range(3):
                col = pl.multiple_of((kind * pairs + pair) * 128, 128)
                j = kind * 2 + half
                out.append(local_copy(wqkv_ref.at[:, pl.ds(col, 128)], w_s.at[slot, :, pl.ds(j * 128, 128)], w_sem.at[slot, j]))
            row = pl.multiple_of(pair * 128, 128)
            out.append(local_copy(wo_ref.at[pl.ds(row, 128), :], wo_s.at[slot, pl.ds(half * 128, 128), :], wo_sem.at[slot, half]))
        return out

    def results(at):
        out = []
        for half in range(2):
            pair = pick(at, [o[half] for o in ORDER])
            for kind in range(3):
                j = kind * 2 + half
                if linked:
                    col = pick(at, [block * 384 + rank * 128 for block, rank in (tile_place(kind * 8 + o[half]) for o in ORDER)])
                    to = gqkv_ref.at[at // 2, :, :, :, pl.ds(pl.multiple_of(col, 128), 128)]
                else:
                    to = gqkv_ref.at[:, :, :, pl.ds(pl.multiple_of((kind * pairs + pair) * 128, 128), 128)]
                out.append(local_copy(gq_s.at[:, :, :, pl.ds(j * 128, 128)], to, gq_sem.at[j]))
            out.append(local_copy(go_s.at[pl.ds(half * 128, 128), :], go_ref.at[pair // 2, pair % 2], go_sem.at[half]))
        return out

    if linked:
        place = Place()
        head_send, head_recv = rest[:2]
        rest = rest[2:]

        def heads_out(at):
            cols = pl.ds(pl.multiple_of(at * lanes, lanes), lanes)
            span = n // 4
            out = []
            for j, (to, device) in enumerate(place.peers):
                src = heads_s.at[pl.ds(pl.multiple_of(to * span, span), span), :]
                out.append(remote_copy(src, heads_ref.at[place.seq, :, cols], head_send.at[at, j], head_recv.at[at, j], device))
            mine = heads_s.at[pl.ds(pl.multiple_of(place.seq * span, span), span), :]
            return out, local_copy(mine, heads_ref.at[place.seq, :, cols], h_sem.at[0])

        def part_of(source, k, w):
            return lambda y, c: source.at[k, :, :, :, pl.ds(pl.multiple_of((y * 2 + c) * w, 128), w)]

        def done_at(k):
            def done(total):
                if k == 3:
                    outs[6][...] = total
                else:
                    outs[2 * k][...] = total[0:128]
                    outs[2 * k + 1][...] = total[128:256]
            return done

        cut = piece_count(AT_SPLIT)
        made = [Piece(place, part_of(hand[0], 1 + k, 256), done_at(k), AT_SPLIT, rest[k * cut:(k + 1) * cut]) for k in range(3)]
        made.append(Piece(place, part_of(gqkv_ref, 0, 384), done_at(3), EARLY_SPLIT, rest[3 * cut:]))
        plan = {}
        for which, times in enumerate(AT_TICKS):
            for t, at in enumerate(times):
                plan.setdefault(at, []).append((which, t))
    else:
        plan = {}

    def tick(position):
        for at, what in sorted(plan.items()):
            if min(at // 6, last) * 6 + position == at:
                def run(what=what):
                    for which, t in sorted(what, key=lambda w: (-w[1], w[0])):
                        made[which].tick(t)
                pl.when(step == min(at // 6, last))(run)

    @pl.when(step == 0)
    def _():
        for copy in weights(0, 0):
            copy.start()
        if linked:
            place.greet()
        family = fam_ref[pl.ds(lax.axis_index("seq"), 1), :].astype(F32)
        famr_s[...] = family
        for m in range(n // 128):
            rows = slice(m * 128, m * 128 + 128)
            famc_s[rows, :] = jnp.broadcast_to(family[:, rows], (128, 128)).T
        for a in range(n // 32):
            rows = slice(a * 32, a * 32 + 32)
            ca, sa = tab_ref[0, a:a + 1, :], tab_ref[1, a:a + 1, :]
            cb, sb = tab_ref[2], tab_ref[3]
            c1 = ca * cb - sa * sb
            s1 = sa * cb + ca * sb
            lane = lax.broadcasted_iota(jnp.int32, c1.shape, 1) % HEAD_DIM
            c_s[rows, :] = jnp.where(lane < ROT, c1, 1.0)
            s_s[rows, :] = jnp.where(lane < ROT // 2, -s1, jnp.where(lane < ROT, s1, 0.0))
        @functools.partial(each_band, n // 256)
        def _(rows, m):
            xhat, _ = normalize(raw_ref[rows, :].astype(F32))
            normed = (xhat * gain_ref[...] + shift_ref[...]).astype(BF16)
            x_s[rows, :] = normed
            xt_s[:, rows] = normed.T
        if linked:
            place.meet()

    @pl.when(step > 0)
    def _():
        for copy in results(step - 1):
            copy.wait()

    tick(0)

    @pl.when(step < last)
    def _():
        for copy in weights(step + 1, 1 - slot):
            copy.start()
    for copy in weights(step, slot):
        copy.wait()

    w_ref, wo1_ref = w_s.at[slot], wo_s.at[slot]
    scaling = HEAD_DIM ** -0.5

    def both(rows):
        c, s = c_s[rows, :], s_s[rows, :]
        return jnp.concatenate([c, c], 1), jnp.concatenate([s, s], 1)

    for m in range(n // 256):
        rows = slice(m * 256, m * 256 + 256)
        raw = dot(x_s[rows, :], w_ref[...])
        c, s = both(rows)
        q_s[rows, :] = (turn(raw[:, 0:lanes], c, s, 1.0) * scaling).astype(BF16)
        keys = turn(raw[:, lanes:2 * lanes], c, s, 1.0).astype(BF16)
        k_s[rows, :] = keys
        kt_s[:, rows] = keys.T
        vals = raw[:, 2 * lanes:].astype(BF16)
        v_s[rows, :] = vals
        vt_s[:, rows] = vals.T
        do_s[rows, :] = dot_nt(g_ref[rows, :], wo1_ref[...]).astype(BF16)

    tick(1)
    tile = TILE
    lane = lax.broadcasted_iota(jnp.int32, (tile, 128), 1)
    work = [(h, i) for i in reversed(range(n // tile)) for h in range(4)]

    def first(h, i):
        span = (i + 1) * tile
        here = slice(i * tile, span)
        cols = slice(h // 2 * 128, h // 2 * 128 + 128)
        mine = (lane < HEAD_DIM) if h % 2 == 0 else (lane >= HEAD_DIM)
        qh = jnp.where(mine, q_s[here, cols], 0).astype(BF16)
        doh = jnp.where(mine, do_s[here, cols], 0).astype(BF16)
        return qh, doh, dot_nt(k_s[0:span, cols], qh), dot_nt(v_s[0:span, cols], doh)

    def second(h, i, qh, doh, st, dpt):
        span = (i + 1) * tile
        here = slice(i * tile, span)
        cols = slice(h // 2 * 128, h // 2 * 128 + 128)
        rows = slice(h * HEAD_DIM, (h + 1) * HEAD_DIM)
        family = famc_s[0:span, :]
        allowed = jnp.concatenate([family] * (tile // 128), 1) == famr_s[:, here]
        key_place = lax.broadcasted_iota(jnp.int32, (span, tile), 0)
        query_place = lax.broadcasted_iota(jnp.int32, (span, tile), 1) + i * tile
        st = jnp.where(allowed & (key_place <= query_place), st, -1e9)
        e = jnp.exp(st - jnp.max(st, 0, keepdims=True))
        p = e * (1.0 / jnp.sum(e, 0, keepdims=True))
        pb = p.astype(BF16)
        ds = (p * (dpt - jnp.sum(p * dpt, 0, keepdims=True))).astype(BF16)
        ht_s[rows, here] = dot(vt_s[rows, 0:span], pb).astype(BF16)
        dqt_s[rows, here] = dot(kt_s[rows, 0:span], ds) * scaling
        dv = dot(pb, doh)
        dk = dot(ds, qh)
        if h % 2 == 0 and i == n // tile - 1:
            dv_s[:, cols] = dv
            dk_s[:, cols] = dk
        else:
            dv_s[0:span, cols] += dv
            dk_s[0:span, cols] += dk

    made_first = first(*work[0])
    for j, (h, i) in enumerate(work):
        later = first(*work[j + 1]) if j + 1 < len(work) else None
        second(h, i, *made_first)
        made_first = later
        if h == 3 and i != 1:
            tick({3: 2, 2: 3, 0: 4}[i])

    @pl.when(step > 0)
    def _():
        if linked:
            sent, mine = heads_out(step - 1)
            for copy in sent:
                copy.wait_send()
            mine.wait()
        else:
            local_copy(heads_s, heads_ref.at[:, pl.ds(pl.multiple_of((step - 1) * lanes, lanes), lanes)], h_sem.at[0]).wait()
    heads_s[...] = ht_s[...].T
    if linked:
        sent, mine = heads_out(step)
        for copy in sent:
            copy.start()
        mine.start()
    else:
        local_copy(heads_s, heads_ref.at[:, pl.ds(pl.multiple_of(step * lanes, lanes), lanes)], h_sem.at[0]).start()

    for m in range(n // 256):
        rows = slice(m * 256, m * 256 + 256)
        c, s = both(rows)
        draw_s[rows, 0:lanes] = turn(dqt_s[:, rows].T, c, s, -1.0).astype(BF16)
        draw_s[rows, lanes:2 * lanes] = turn(dk_s[rows, :], c, s, -1.0).astype(BF16)
        draw_s[rows, 2 * lanes:] = dv_s[rows, :].astype(BF16)

    for m in range(d // 256):
        grads = dot(xt_s[m * 256:(m + 1) * 256, :], draw_s[...]).astype(BF16)
        gq_s[m, 0] = grads[0:128]
        gq_s[m, 1] = grads[128:256]
    go_s[...] = dot(ht_s[...], g_ref[...]).astype(BF16)
    for copy in results(step):
        copy.start()
    tick(5)
    for m in range(n // 256):
        here = slice(m * 256, (m + 1) * 256)
        dn = dot_nt(draw_s[here, :], w_ref[...])

        @pl.when(step == 0)
        def _():
            dn_s[here, :] = dn

        @pl.when(step > 0)
        def _():
            dn_s[here, :] += dn

    @pl.when(step == last)
    def _():
        sums_ref[...] = jnp.zeros_like(sums_ref)

        @functools.partial(each_band, n // 256)
        def _(here, m):
            total = dn_s[here, :]
            xhat, _ = normalize(raw_ref[here, :].astype(F32))
            sums_ref[0:1, :] += jnp.sum(total * xhat, 0, keepdims=True)
            sums_ref[1:2, :] += jnp.sum(total, 0, keepdims=True)
            dn_ref[here, :] = total.astype(BF16)

    tick(6)

    @pl.when(step == last)
    def _():
        for copy in results(step):
            copy.wait()
        if linked:
            for at in range(steps):
                for copy in heads_out(at)[0]:
                    copy.wait_recv()
            for copy in heads_out(step)[0]:
                copy.wait_send()
            heads_out(step)[1].wait()
        else:
            local_copy(heads_s, heads_ref.at[:, pl.ds(pl.multiple_of(step * lanes, lanes), lanes)], h_sem.at[0]).wait()


def attend(raw, g, gain, shift, wqkv, wo, families, linked, grads=None):
    n, d = raw.shape
    pair_lane = np.arange(128) % HEAD_DIM % (ROT // 2)
    freq = 10000.0 ** (-2.0 * pair_lane / ROT)
    high, low = np.arange(n // 32)[:, None] * 32.0 * freq, np.arange(32)[:, None] * freq
    tab = jnp.asarray(np.stack([np.cos(high), np.sin(high), np.cos(low), np.sin(low)]), F32)
    sd, vm = jax.ShapeDtypeStruct, pltpu.VMEM
    out_shape = [sd((n, d), BF16), sd((8, d), F32), sd((2, 4, 2, 128, 3 * d // 2) if linked else (4, 2, 128, 3 * d), BF16),
                 sd((4, 2, 128, d), BF16), sd((4, n // 4, d) if linked else (n, d), BF16)]
    out_specs = [whole((n, d)), whole((8, d))] + [ANYWHERE] * 3
    scratch = [vm((n, d), BF16), vm((d, n), BF16), vm((n, 128), F32), vm((n, 128), F32), vm((2, d, 768), BF16), vm((2, 256, d), BF16)]
    scratch += [vm((n, 256), BF16)] * 4 + [vm((256, n), BF16)] * 3
    scratch += [vm((256, n), F32), vm((n, 256), F32), vm((n, 256), F32), vm((n, 768), BF16), vm((n, d), F32), vm((4, 2, 128, 768), BF16),
                vm((256, d), BF16), vm((n, 256), BF16), vm((1, n), F32), vm((n, 128), F32), DMA((2, 6)), DMA((2, 2)), DMA((6,)), DMA((2,)), DMA((1,))]
    params, more = {}, []
    if linked:
        more = [grads]
        out_shape += [sd((128, 256), F32)] * 6 + [sd((128, 384), F32)]
        out_specs += [whole((128, 256))] * 6 + [whole((128, 384))]
        scratch += [DMA((4, 3)), DMA((4, 3))]
        scratch += piece_scratch(256, AT_SPLIT) * 3 + piece_scratch(384, EARLY_SPLIT)
        params = dict(collective_id=1, has_side_effects=True)
    return pl.pallas_call(
        functools.partial(attn_kernel, linked=linked), out_shape=out_shape, grid=(len(ORDER),),
        in_specs=[whole((n, d)), whole((n, d)), whole((1, d)), whole((1, d)), whole(families.shape), whole((4, 32, 128)), ANYWHERE, ANYWHERE]
        + [ANYWHERE] * len(more),
        out_specs=out_specs, scratch_shapes=scratch,
        compiler_params=pltpu.CompilerParams(vmem_limit_bytes=60 * 2**20, **params),
        cost_estimate=pl.CostEstimate(flops=70_000_000_000, bytes_accessed=30_000_000, transcendentals=20_000_000),
    )(raw, g, gain.reshape(1, d), shift.reshape(1, d), families, tab, wqkv, wo, *more)


class SmallSum:
    def __init__(self, place, held, heard, by_z, send, recv):
        self.p, self.held, self.heard, self.by_z, self.send, self.recv = place, held, heard, by_z, send, recv

    def copies(self, t):
        p = self.p
        if t < 3:
            to = (p.twin, p.beside_y, p.beside_x)[t]
            return [remote_copy(self.held, self.heard.at[t], self.send.at[t], self.recv.at[t], to)]
        return [remote_copy(self.by_z.at[p.z], self.by_z.at[p.z], self.send.at[3 + j], self.recv.at[3 + j], to)
                for j, to in enumerate(p.along_z)]

    def tick(self, t):
        if t > 0:
            for copy in self.copies(t - 1):
                copy.wait()
        if 0 < t < 4:
            total = self.held[...] + self.heard[t - 1]
            if t < 3:
                self.held[...] = total
            else:
                self.by_z[self.p.z] = total
        if t < 4:
            for copy in self.copies(t):
                copy.start()
        return None if t < 4 else self.by_z[0] + self.by_z[1] + self.by_z[2] + self.by_z[3]


def tail_kernel(dat_ref, heads_ref, gq_ref, go_ref, inp_ref, cot_ref, act_ref, wd_ref, dn_ref, wo_ref, part_ref, gain_ref, dbias_ref, sums_ff_ref, sums_at_ref,
                ub_ref, early_ref, lo_ref, ig_ref, qkv_ref, out_ref, gain_o, shift_o, ub_o, db_o,
                back_s, inp_s, g_s, heads_s, y_s, dn_s, wo_s, lo_s, ig_s, small_s, heard_s, by_z_s, act_s, wd_s, act_sem, wd_sem,
                load_sem, wo_sem, back_send, back_recv, own_sem, small_send, small_recv, lo_sem, ig_sem, *pieces):
    place = Place()
    d = wo_s.shape[0]
    place.greet()
    swaps = [remote_copy(dat_ref.at[to], back_s.at[place.seq], back_send.at[j], back_recv.at[j], device)
             for j, (to, device) in enumerate(place.peers)]
    own = local_copy(dat_ref.at[place.seq], back_s.at[place.seq], own_sem.at[0])
    blocks = {}

    def part(source, w, row0, rows):
        return lambda y, c: source.at[:, :, pl.ds(row0, rows), pl.ds(pl.multiple_of((y * 2 + c) * w, 128), w)]

    def out_done(total):
        out_ref[...] = total

    def qkv_done(row0):
        def done(total):
            rows = slice(row0, row0 + total.shape[0])
            early = early_ref[rows, :]
            first = jnp.where(place.c == 0, early, total)
            second = jnp.where(place.c == 0, total, early)
            order = ((first, 0), (second, 0), (second, 1), (first, 1), (first, 2), (second, 2))
            for k, (source, at) in enumerate(order):
                qkv_ref[rows, k * 128:(k + 1) * 128] = source[:, at * 128:(at + 1) * 128]
        return done

    cuts = [0, piece_count(TAIL_SPLITS[0])]
    for split in TAIL_SPLITS[1:]:
        cuts.append(cuts[-1] + piece_count(split))
    late = gq_ref.at[1]
    row1 = sum(TAIL_SPLITS[1])
    made = [Piece(place, part(go_ref, 256, 0, 128), out_done, TAIL_SPLITS[0], pieces[:cuts[1]]),
            Piece(place, part(late, 384, 0, row1), qkv_done(0), TAIL_SPLITS[1], pieces[cuts[1]:cuts[2]]),
            Piece(place, part(late, 384, row1, 128 - row1), qkv_done(row1), TAIL_SPLITS[2], pieces[cuts[2]:])]
    small = SmallSum(place, small_s, heard_s, by_z_s, small_send, small_recv)
    small_s[0:3, :] = sums_ff_ref[0:3, :]
    small_s[0:2, :] += sums_at_ref[0:2, :]
    small_s[3:4, :] = jnp.zeros((1, d), F32)
    for k in range(4):
        small_s[4 + k:5 + k, :] = ub_ref[:, k * d:(k + 1) * d]
    place.meet()
    for piece in made:
        piece.tick(0)
    for copy in swaps:
        copy.start()
    small.tick(0)
    loads = [local_copy(a, b, load_sem.at[k]) for k, (a, b) in enumerate(
        ((heads_ref, heads_s), (inp_ref, inp_s), (cot_ref, g_s), (dn_ref, dn_s)))]
    for pair in range(d // 128):
        at = [p for two in ORDER for p in two].index(pair)
        blocks[at] = local_copy(wo_ref.at[pl.ds(pair * 128, 128), :], wo_s.at[pl.ds(at * 128, 128), :], wo_sem.at[at])
    for copy in [loads[0]] + list(blocks.values()) + loads[1:] + [own]:
        copy.start()

    def lo_out(r):
        return local_copy(lo_s.at[r], lo_ref.at[r], lo_sem.at[r])

    def ig_out(r):
        return local_copy(ig_s.at[r], ig_ref.at[r], ig_sem.at[r])

    def forward(r, carry):
        total = inp_s[r].astype(F32) + dot(heads_s[r], wo_s[...]) + y_s[r]
        lo_s[r] = total.astype(BF16)
        lo_out(r).start()
        return carry

    def backward(r):
        xhat, scale = normalize(inp_s[r].astype(F32))
        dx = (dn_s[r] + back_s[r].astype(F32)) * gain_ref[...]
        ig_s[r] = g_s[lax.rem(part_ref[r], 4)].astype(F32) + (dx - jnp.mean(dx, -1, keepdims=True) - xhat * jnp.mean(dx * xhat, -1, keepdims=True)) * scale
        ig_out(r).start()

    hidden = wd_ref.shape[0]
    chunks = hidden // 512

    def chunk(at, slot):
        out = [local_copy(act_ref.at[at], act_s.at[slot], act_sem.at[slot])]
        for k, f in hidden_runs(at, hidden):
            f = pl.multiple_of(f, 128)
            out.append(local_copy(wd_ref.at[pl.ds(f, 128), :], wd_s.at[slot, pl.ds(k * 128, 128), :], wd_sem.at[slot, k]))
        return out

    for copy in chunk(0, 0):
        copy.start()

    def down(at, carry):
        slot = at % 2

        @pl.when(at + 1 < chunks)
        def _():
            for copy in chunk(at + 1, 1 - slot):
                copy.start()

        @pl.when(at == TAIL_FIRST)
        def _():
            for piece in made:
                piece.tick(1)
            small.tick(1)

        @pl.when(at == TAIL_FIRST + 4)
        def _():
            small.tick(2)

        for copy in chunk(at, slot):
            copy.wait()
        for r in range(4):
            y_s[r] += dot(act_s[slot, r * 256:(r + 1) * 256, :], wd_s[slot])
        return carry

    for r in range(4):
        y_s[r] = jnp.broadcast_to(dbias_ref[...], y_s.shape[1:])
    lax.fori_loop(0, chunks, down, 0)
    for copy in list(blocks.values()) + loads[:2]:
        copy.wait()
    lax.fori_loop(0, 2, forward, 0)
    made[0].tick(2)
    lax.fori_loop(2, 4, forward, 0)
    made[1].tick(2)
    made[2].tick(2)
    small.tick(3)
    loads[2].wait()
    loads[3].wait()
    own.wait()
    made[0].tick(3)
    backward(place.seq)
    for j in range(3):
        swaps[j].wait_send()
    swaps[2].wait_recv()
    backward((place.seq + 1) % 4)
    made[1].tick(3)
    made[2].tick(3)
    swaps[1].wait_recv()
    swaps[0].wait_recv()
    lax.fori_loop(2, 4, lambda j, carry: (backward((place.seq + j) % 4), carry)[1], 0)
    total = small.tick(4)
    for piece in made:
        piece.tick(4)
    gain_o[...] = total[0:1]
    shift_o[...] = total[1:2]
    db_o[...] = total[2:3]
    for k in range(4):
        ub_o[:, k * d:(k + 1) * d] = total[4 + k:5 + k]
    for r in range(4):
        lo_out(r).wait()
        ig_out(r).wait()


def finish(dat, heads, gq, go, inp, cot, act, wd, dn, wo, partners, gain, dbias, sums_ff, sums_at, ub, early):
    sd, vm = jax.ShapeDtypeStruct, pltpu.VMEM
    shape, d = inp.shape, inp.shape[2]
    vmem = pl.BlockSpec(memory_space=pltpu.VMEM)
    return pl.pallas_call(
        tail_kernel,
        out_shape=[sd(shape, BF16), sd(shape, F32), sd((128, 768), F32), sd((128, 256), F32), sd((1, d), F32), sd((1, d), F32), sd((1, 4 * d), F32),
                   sd((1, d), F32)],
        in_specs=[ANYWHERE] * 10 + [pl.BlockSpec(memory_space=pltpu.SMEM)] + [vmem] * 6, out_specs=[ANYWHERE] * 2 + [vmem] * 6,
        scratch_shapes=[vm(shape, BF16)] * 4 + [vm(shape, F32)] * 2 + [vm((d, d), BF16), vm(shape, BF16), vm(shape, F32),
                        vm((8, d), F32), vm((3, 8, d), F32), vm((4, 8, d), F32), vm((2, 1024, 512), BF16), vm((2, 512, d), BF16), DMA((2,)), DMA((2, 4)),
                        DMA((4,)), DMA((8,)), DMA((3,)), DMA((3,)), DMA((1,)), DMA((6,)), DMA((6,)), DMA((4,)), DMA((4,))]
        + piece_scratch(256, TAIL_SPLITS[0]) + piece_scratch(384, TAIL_SPLITS[1]) + piece_scratch(384, TAIL_SPLITS[2]),
        compiler_params=pltpu.CompilerParams(collective_id=2, has_side_effects=True, vmem_limit_bytes=56 * 2**20),
    )(dat.reshape(shape), heads, gq, go, inp, cot, act, wd, dn.reshape(shape), wo, partners, gain.reshape(1, d), dbias.reshape(1, d), sums_ff, sums_at,
      ub, early)


def copy_kernel(*refs, moves, count):
    ins, outs, held, (in_sem, out_sem) = refs[:count], refs[count:count + 10], refs[count + 10:2 * count + 10], refs[2 * count + 10:]
    loads = [local_copy(ins[a].at[at], held[a].at[at], in_sem.at[k]) for k, (a, at, _) in enumerate(moves)]
    for copy in loads:
        copy.start()
    stores = []
    for k, (a, at, places) in enumerate(moves):
        loads[k].wait()
        for source, b, to in places:
            stores.append(local_copy(held[a].at[source], outs[b].at[to], out_sem.at[len(stores)]))
            stores[-1].start()
    for copy in stores:
        copy.wait()


def gather_up(*parts):
    sd, every = jax.ShapeDtypeStruct, (slice(None), slice(None))
    shapes = [sd(p.shape, p.dtype) for p in parts[:8]] + [sd((128, 1024), F32), sd((512, 256), F32)]
    moves = [(a, r, [(r, a, r)]) for r in range(4) for a in (1, 0)]
    for k in range(4):
        moves.append((8 + k, every, [((slice(None), slice(half * 128, half * 128 + 128)), 8, (slice(None), slice(half * 512 + k * 128, half * 512 + k * 128 + 128)))
                                     for half in range(2)]))
        moves.append((12 + k, every, [(every, 9, (slice(k * 128, k * 128 + 128), slice(None)))]))
    moves += [(a, every, [(every, a, every)]) for a in range(2, 8)]
    return pl.pallas_call(
        functools.partial(copy_kernel, moves=moves, count=len(parts)), out_shape=shapes, in_specs=[ANYWHERE] * len(parts), out_specs=[ANYWHERE] * 10,
        scratch_shapes=[pltpu.VMEM(p.shape, p.dtype) for p in parts] + [DMA((len(moves),)), DMA((sum(len(m[2]) for m in moves),))],
        compiler_params=pltpu.CompilerParams(vmem_limit_bytes=60 * 2**20),
    )(*parts)


def on_device(inputs, norm_gain, norm_shift, qkv_weight, out_weight, up_weight, up_bias, down_weight, down_bias, partners, families, cotangent, linked):
    row_count, place_count, width = inputs.shape
    tokens = row_count * place_count
    branch_args = norm_gain, norm_shift, qkv_weight, out_weight, families, linked
    if linked:
        act, dn, sums_ff, ub, grads, row_inputs, row_grad, up0, down0 = feed_forward(
            inputs, cotangent, partners, norm_gain, norm_shift, up_bias, up_weight, down_weight, True)
        dat, sums_at, gq, go, heads, up1, down1, up2, down2, up3, down3, early = attend(
            row_inputs.reshape(tokens, width), row_grad.reshape(tokens, width), *branch_args, grads)
        layer_out, input_grad, qkv_sum, out_sum, gain_sum, shift_sum, ub_sum, db_sum = finish(
            dat, heads, gq, go, inputs, cotangent, act, down_weight, dn, out_weight, partners, norm_gain, down_bias, sums_ff, sums_at, ub, early)
        layer_out, input_grad, qkv_sum, out_sum, gain_sum, shift_sum, ub_sum, db_sum, up_sum, down_sum = gather_up(
            layer_out, input_grad, qkv_sum, out_sum, gain_sum, shift_sum, ub_sum, db_sum, up0, up1, up2, up3, down0, down1, down2, down3)
        return (layer_out.reshape(inputs.shape), input_grad.reshape(inputs.shape), gain_sum.reshape(width), shift_sum.reshape(width), qkv_sum, out_sum,
                up_sum, ub_sum.reshape(-1), down_sum, db_sum.reshape(width))
    local_rows = partners - lax.axis_index("dp") * row_count
    grad = jnp.take(cotangent, local_rows, axis=0, mode="clip")
    swap = functools.partial(lax.all_to_all, axis_name="seq", split_axis=0, concat_axis=0, tiled=True)
    row_inputs, row_grad = swap(inputs).reshape(tokens, width), swap(grad).reshape(tokens, width)
    y, dn, sums_ff, ub, up_grad, down_grad = feed_forward(
        inputs, cotangent, partners, norm_gain, norm_shift, up_bias, up_weight, down_weight, False)
    dat, sums_at, qkv_grad, out_grad, heads = attend(row_inputs, row_grad, *branch_args)

    def scatter(parts, columns):
        part = lax.psum_scatter(parts.reshape(-1, columns), "seq", scatter_dimension=1, tiled=True)
        return lax.psum_scatter(part, "dp", scatter_dimension=0, tiled=True).astype(F32)

    qkv_sum, out_sum = scatter(qkv_grad, 3 * width), scatter(out_grad, width)
    up_sum, down_sum = scatter(up_grad, up_bias.shape[0]), scatter(down_grad, width)
    heads = swap(heads.reshape(inputs.shape)).reshape(tokens, width)
    order = np.array([p for two in ORDER for p in two])
    attn_out = dot(heads, out_weight.reshape(-1, 128, width)[order].reshape(width, width))
    values = inputs.astype(F32).reshape(tokens, width)
    layer_out = (values + attn_out + (y + down_bias)).astype(BF16).reshape(inputs.shape)
    xhat, scale = normalize(values)
    dx = (dn + swap(dat.reshape(inputs.shape)).reshape(tokens, width).astype(F32)) * norm_gain
    input_grad = grad.reshape(tokens, width).astype(F32) + (dx - jnp.mean(dx, -1, keepdims=True) - xhat * jnp.mean(dx * xhat, -1, keepdims=True)) * scale
    gain_sum, shift_sum, up_bias_sum, down_bias_sum = lax.psum((sums_ff[0] + sums_at[0], sums_ff[1] + sums_at[1], ub[0], sums_ff[2]), ("dp", "seq"))
    return (layer_out, input_grad.reshape(inputs.shape), gain_sum, shift_sum, qkv_sum, out_sum, up_sum, up_bias_sum, down_sum, down_bias_sum)


def solution(mesh):
    rows = P("dp", "seq", None)
    placed = (rows,) + (P(),) * 8 + (P("dp"), P("dp", None), rows)
    grads = P("dp", "seq")
    linked = (mesh.shape["dp"], mesh.shape["seq"]) == (8, 4)
    return jax.shard_map(functools.partial(on_device, linked=linked), mesh=mesh, in_specs=placed,
                         out_specs=(rows, rows, P(), P(), grads, grads, grads, P(), grads, P()), check_vma=False)
```

```python
import functools

import jax
import jax.numpy as jnp
import numpy as np
from jax import lax
from jax.experimental import pallas as pl
from jax.experimental.pallas import tpu as pltpu
from jax.sharding import PartitionSpec as P

F32 = jnp.float32
BF16 = jnp.bfloat16
HEAD_DIM = 64
ROT = 32
EPS = 1e-05
C0 = 0.7978845608028654
C1 = C0 * 0.044715
TILE = 256
FF_SPLIT = 0, 176, 80
AT_SPLIT = 64, 128, 64
EARLY_SPLIT = 48, 64, 16
TAIL_FIRST = 2
TAIL_SPLITS = (0, 80, 48), (0, 48, 16), (0, 32, 32)
FF_TICKS = 6, 10, 18, 21, 24
AT_TICKS = (0, 2, 7, 10, 14), (4, 7, 12, 15, 19), (8, 12, 17, 20, 23), (13, 17, 21, 23, 24)
ORDER = ((0, 3), (4, 7), (1, 2), (5, 6))
MESH_ID = pl.DeviceIdType.MESH
ANYWHERE = pl.BlockSpec(memory_space=pl.ANY)
DMA = pltpu.SemaphoreType.DMA


def dot(a, b):
    return lax.dot_general(a, b, (((1,), (0,)), ((), ())), preferred_element_type=F32)


def dot_nt(a, b):
    return lax.dot_general(a, b, (((1,), (1,)), ((), ())), preferred_element_type=F32)


def dot_tn(a, b):
    return lax.dot_general(a, b, (((0,), (0,)), ((), ())), preferred_element_type=F32)


def whole(shape):
    return pl.BlockSpec(shape, lambda p: (0,) * len(shape), pipeline_mode=pl.Buffered(1))


def pick(step, values):
    out = jnp.int32(values[0])
    for i, value in enumerate(values[1:], 1):
        out = jnp.where(step == i, value, out)
    return out


def normalize(values):
    centered = values - jnp.mean(values, -1, keepdims=True)
    scale = lax.rsqrt(jnp.mean(centered * centered, -1, keepdims=True) + EPS)
    return centered * scale, scale


def each_band(count, body):
    def step(m, carry):
        body(pl.ds(pl.multiple_of(m * 256, 256), 256), m)
        return carry

    lax.fori_loop(0, count, step, 0)


def local_copy(src, dst, sem):
    return pltpu.make_async_copy(src, dst, sem)


def remote_copy(src, dst, send, recv, to):
    return pltpu.make_async_remote_copy(src_ref=src, dst_ref=dst, send_sem=send, recv_sem=recv, device_id=to,
                                        device_id_type=MESH_ID)


class Place:
    def __init__(self):
        self.dp, self.seq = lax.axis_index("dp"), lax.axis_index("seq")
        self.z, self.x, self.y, self.c = self.dp // 2, self.dp % 2, self.seq // 2, self.seq % 2
        self.twin = (self.dp, self.y * 2 + 1 - self.c)
        self.beside_y = (self.dp, (1 - self.y) * 2 + self.c)
        self.across = (self.dp, (1 - self.y) * 2 + 1 - self.c)
        self.beside_x = (self.z * 2 + 1 - self.x, self.seq)
        self.along_z = [(((self.z + j) % 4) * 2 + self.x, self.seq) for j in (1, 2, 3)]
        self.peers = [((self.seq + j) % 4, (self.dp, (self.seq + j) % 4)) for j in (1, 2, 3)]
        self.partners = [self.twin, self.beside_y, self.beside_x] + self.along_z

    def greet(self):
        for partner in self.partners + [self.across]:
            pl.semaphore_signal(pltpu.get_barrier_semaphore(), inc=1, device_id=partner, device_id_type=MESH_ID)

    def meet(self):
        pl.semaphore_wait(pltpu.get_barrier_semaphore(), len(self.partners) + 1)


def add_into(dst, src, lead):
    rows, w = src.shape[-2:]
    band = rows
    while band * w > 65536 and band % 32 == 0:
        band //= 2
    count = 1
    for n in lead:
        count *= n

    def body(t, carry):
        block, part = t // (rows // band), t % (rows // band)
        index = []
        for n in reversed(lead):
            index.insert(0, block % n)
            block = block // n
        at = tuple(index) + (pl.ds(pl.multiple_of(part * band, band), band), slice(None))
        dst[at] = dst[at] + src[at]
        return carry

    lax.fori_loop(0, count * (rows // band), body, 0)


def piece_scratch(w, split):
    ra, rb, rc = split
    r = sum(split)
    out = [((2, 4, 2, r), 1), ((2, 4, 2, r), 1), ((4, 2, ra), ra), ((2, 4, rb), rb), ((3, 2, 2, rc), rc), ((4, ra), ra), ((4, rb), rb), ((2, rc), rc),
           ((3, ra + rb), ra + rb), ((rc,), rc)]
    return [pltpu.VMEM(shape + (w,), BF16) for shape, used in out if used] + [DMA((14,)), DMA((14,)), DMA((2,))]


def piece_count(split):
    return len(piece_scratch(128, split))


class Piece:
    def __init__(self, place, part, done, split, scratch):
        self.p, self.part, self.done, self.split = place, part, done, split
        ra, rb, rc = split
        names = [("a", 1), ("from_twin", 1), ("ya", ra), ("xb", rb), ("zc", rc), ("xa", ra), ("yb", rb), ("xc", rc), ("zab", ra + rb), ("yc", rc)]
        scratch = list(scratch)
        for name, used in names:
            setattr(self, name, scratch.pop(0) if used else None)
        self.ss, self.rs, self.ls = scratch
        self.rows_a, self.rows_b, self.rows_ab, self.rows_c = pl.ds(0, ra), pl.ds(ra, rb), pl.ds(0, ra + rb), pl.ds(ra + rb, rc)

    def copies(self, stage):
        p, a, (ra, rb, rc) = self.p, self.a, self.split
        out = []
        slot = (0, 2, 7, 10)[stage]

        def send(src, dst, to):
            k = slot + len(out)
            out.append(remote_copy(src, dst, self.ss.at[k], self.rs.at[k], to))

        zs = [((p.z + 1 + j) % 4, p.along_z[j]) for j in range(3)]
        if stage == 0:
            for k in (0, 1):
                send(self.part(k, 1 - p.c), self.from_twin.at[k], p.twin)
        if stage == 1:
            if ra:
                send(a.at[1 - p.y, :, :, self.rows_a, :], self.ya, p.beside_y)
            if rb:
                send(a.at[:, :, 1 - p.x, self.rows_b, :], self.xb, p.beside_x)
            for j in range(3 if rc else 0):
                send(a.at[:, zs[j][0], :, self.rows_c, :], self.zc.at[j], zs[j][1])
        if stage == 2:
            if ra:
                send(a.at[p.y, :, 1 - p.x, self.rows_a, :], self.xa, p.beside_x)
            if rb:
                send(a.at[1 - p.y, :, p.x, self.rows_b, :], self.yb, p.beside_y)
            if rc:
                send(a.at[:, p.z, 1 - p.x, self.rows_c, :], self.xc, p.beside_x)
        if stage == 3:
            for j in range(3 if ra + rb else 0):
                send(a.at[p.y, zs[j][0], p.x, self.rows_ab, :], self.zab.at[j], zs[j][1])
            if rc:
                send(a.at[1 - p.y, p.z, p.x, self.rows_c, :], self.yc, p.beside_y)
        return out

    def own(self):
        return [local_copy(self.part(k, self.p.c), self.a.at[k], self.ls.at[k]) for k in (0, 1)]

    def tick(self, t):
        p, a, (ra, rb, rc) = self.p, self.a, self.split
        if t > 0:
            for copy in self.copies(t - 1):
                copy.wait()
        if t == 0:
            for copy in self.copies(0) + self.own():
                copy.start()
        if t == 1:
            for copy in self.own():
                copy.wait()
            add_into(a, self.from_twin, (2, 4, 2))
        if t == 2:
            if ra:
                add_into(a.at[p.y, :, :, self.rows_a, :], self.ya, (4, 2))
            if rb:
                add_into(a.at[:, :, p.x, self.rows_b, :], self.xb, (2, 4))
            for j in range(3 if rc else 0):
                add_into(a.at[:, p.z, :, self.rows_c, :], self.zc.at[j], (2, 2))
        if t == 3:
            if ra:
                add_into(a.at[p.y, :, p.x, self.rows_a, :], self.xa, (4,))
            if rb:
                add_into(a.at[p.y, :, p.x, self.rows_b, :], self.yb, (4,))
            if rc:
                add_into(a.at[:, p.z, p.x, self.rows_c, :], self.xc, (2,))
        if t in (1, 2, 3):
            for copy in self.copies(t):
                copy.start()
        if t == 4:
            mine = a.at[p.y, p.z, p.x]
            parts = []
            if ra + rb:
                total = mine[self.rows_ab, :].astype(F32)
                for j in range(3):
                    total += self.zab[j].astype(F32)
                parts.append(total)
            if rc:
                parts.append(mine[self.rows_c, :].astype(F32) + self.yc[...].astype(F32))
            self.done(jnp.concatenate(parts, 0) if len(parts) > 1 else parts[0])


def hidden_runs(at, hidden):
    return [(s, (2 * s + at % 2) * (hidden // 8) + at // 2 * 128) for s in range(4)]


def ff_kernel(part_ref, inp_ref, cot_ref, gain_ref, shift_ref, bias_ref, wu_ref, wd_ref, *rest, linked):
    hand, rest = (rest[:1], rest[1:]) if linked else ((), rest)
    y_ref, dn_ref, sums_ref, ub_ref = rest[:4]
    outs, rest = (rest[4:9], rest[9:]) if linked else (rest[4:6], rest[6:])
    x_s, xt_s, act_s, dh_s, wu_s, wd_s, gu_s, gd_s, g_ref, wu_sem, wd_sem, gu_sem, gd_sem, act_sem = rest[:14]
    rest = rest[14:]
    step = pl.program_id(0)
    last = pl.num_programs(0) - 1
    n, d = x_s.shape
    hidden = bias_ref.shape[1]
    tile = 512
    slot = step % 2

    def places(at):
        return hidden_runs(at, hidden)

    def weights(at, slot):
        out = []
        for s, f in places(at):
            f = pl.multiple_of(f, 128)
            out.append(local_copy(wu_ref.at[:, pl.ds(f, 128)], wu_s.at[slot, :, pl.ds(s * 128, 128)], wu_sem.at[slot, s]))
            out.append(local_copy(wd_ref.at[pl.ds(f, 128), :], wd_s.at[slot, pl.ds(s * 128, 128), :], wd_sem.at[slot, s]))
        return out

    def results(at):
        out = []
        k, j = at // 2, at % 2
        for s, f in places(at):
            f = pl.multiple_of(f, 128)
            up, down = gu_s.at[:, :, :, pl.ds(s * 128, 128)], gd_s.at[pl.ds(s * 128, 128), :]
            if linked:
                col = pl.multiple_of(s * 256 + j * 128, 128)
                to = outs[0].at[k, :, :, pl.ds(0, 128), pl.ds(col, 128)], outs[0].at[k, s, j, pl.ds(128, 128), :]
            else:
                to = outs[0].at[:, :, :, pl.ds(f, 128)], outs[1].at[pl.ds(f, 128), :]
            out.append(local_copy(up, to[0], gu_sem.at[s]))
            out.append(local_copy(down, to[1], gd_sem.at[s]))
        return out

    def keep(at):
        return [local_copy(act_s, y_ref.at[at], act_sem.at[0])] if linked else []

    if linked:
        place = Place()
        row_send, row_recv, own_sem = rest[:3]
        rest = rest[3:]

        def swaps(a):
            span = n // 4

            def row(at):
                return g_ref.at[pl.ds(pl.multiple_of(at * span, span), span), :] if a else hand[0].at[at]

            out = [remote_copy(row(to), outs[1 + a].at[place.seq], row_send.at[a, j], row_recv.at[a, j], device)
                   for j, (to, device) in enumerate(place.peers)]
            return out + [local_copy(row(place.seq), outs[1 + a].at[place.seq], own_sem.at[a])]

        def part_of(k):
            return lambda y, c: outs[0].at[k, :, :, :, pl.ds(pl.multiple_of((y * 2 + c) * 256, 256), 256)]

        def done_at(k):
            def done(total):
                outs[3 + 2 * k][...] = total[0:128]
                outs[4 + 2 * k][...] = total[128:256]
            return done

        made = [Piece(place, part_of(0), done_at(0), FF_SPLIT, rest)]

    def tick(position):
        for which, times in enumerate((FF_TICKS,) if linked else ()):
            for t, at in enumerate(times):
                if min(at // 3, 7) * 3 + position == at:
                    pl.when(step == min(at // 3, 7))(functools.partial(made[which].tick, t))

    @pl.when(step == 0)
    def _():
        for copy in weights(0, 0):
            copy.start()
        if linked:
            place.greet()
        count, span, _ = cot_ref.shape
        for r in range(count):
            g_ref[r * span:(r + 1) * span, :] = cot_ref[lax.rem(part_ref[r], count)]
        if linked:
            place.meet()
            for copy in swaps(0) + swaps(1):
                copy.start()
        sums_ref[...] = jnp.zeros_like(sums_ref)

        @functools.partial(each_band, n // 256)
        def _(rows, m):
            xhat, _ = normalize(inp_ref[rows, :].astype(F32))
            normed = (xhat * gain_ref[...] + shift_ref[...]).astype(BF16)
            x_s[rows, :] = normed
            xt_s[:, rows] = normed.T
            sums_ref[2:3, :] += jnp.sum(g_ref[rows, :].astype(F32), 0, keepdims=True)

    @pl.when(step > 0)
    def _():
        for copy in results(step - 1) + keep(step - 1):
            copy.wait()

    tick(0)

    @pl.when(step < last)
    def _():
        for copy in weights(step + 1, 1 - slot):
            copy.start()
    for copy in weights(step, slot):
        copy.wait()
    w_up, w_down = wu_s.at[slot], wd_s.at[slot]
    bias = jnp.concatenate([bias_ref[:, pl.ds(pl.multiple_of(f, 128), 128)] for _, f in places(step)], 1)
    unit_sums = None
    for m in range(n // tile):
        here = slice(m * tile, (m + 1) * tile)
        v = dot(x_s[here, :], w_up[...]) + bias
        vv = v * v
        a = 0.5 + 0.5 * jnp.tanh(v * (C0 + C1 * vv))
        act = v * a
        slope = a + act * (1.0 - a) * (2 * C0 + 6 * C1 * vv)
        act_s[here, :] = act.astype(BF16)
        dh = (dot_nt(g_ref[here, :], w_down[...]) * slope).astype(BF16)
        dh_s[here, :] = dh
        total = jnp.sum(dh.astype(F32), 0, keepdims=True)
        unit_sums = total if unit_sums is None else unit_sums + total
    for copy in keep(step):
        copy.start()
    for s, f in places(step):
        ub_ref[:, pl.ds(pl.multiple_of(f, 128), 128)] = unit_sums[:, s * 128:(s + 1) * 128]

    tick(1)
    for m in range(d // 256):
        grads = dot(xt_s[m * 256:(m + 1) * 256, :], dh_s[...]).astype(BF16)
        gu_s[m, 0] = grads[0:128]
        gu_s[m, 1] = grads[128:256]
    gd_s[...] = dot_tn(act_s[...], g_ref[...]).astype(BF16)
    for copy in results(step):
        copy.start()
    tick(2)
    for m in range(n // tile):
        here = slice(m * tile, (m + 1) * tile)
        y = None if linked else dot(act_s[here, :], w_down[...])
        dn = dot_nt(dh_s[here, :], w_up[...])

        @pl.when(step == 0)
        def _():
            if not linked:
                y_ref[here, :] = y
            dn_ref[here, :] = dn

        @pl.when(step > 0)
        def _():
            if not linked:
                y_ref[here, :] += y
            dn_ref[here, :] += dn

    tick(3)

    @pl.when(step == last)
    def _():
        @functools.partial(each_band, n // 256)
        def _(here, m):
            total = dn_ref[here, :]
            xhat, _ = normalize(inp_ref[here, :].astype(F32))
            sums_ref[0:1, :] += jnp.sum(total * xhat, 0, keepdims=True)
            sums_ref[1:2, :] += jnp.sum(total, 0, keepdims=True)

        for copy in results(step) + keep(step):
            copy.wait()
        if linked:
            for copy in swaps(0) + swaps(1):
                copy.wait()


def feed_forward(inp, cot, partners, gain, shift, bias, wu, wd, linked):
    rows, span, d = inp.shape
    n, hidden = rows * span, bias.shape[0]
    sd, vm = jax.ShapeDtypeStruct, pltpu.VMEM
    out_shape = [sd((hidden // 512, n, 512), BF16) if linked else sd((n, d), F32), sd((n, d), F32), sd((8, d), F32), sd((1, hidden), F32)]
    out_specs = [ANYWHERE if linked else whole((n, d)), whole((n, d)), whole((8, d)), whole((1, hidden))]
    scratch = [vm((n, d), BF16), vm((d, n), BF16), vm((n, 512), BF16), vm((n, 512), BF16), vm((2, d, 512), BF16), vm((2, 512, d), BF16),
               vm((4, 2, 128, 512), BF16), vm((512, d), BF16), vm((n, d), BF16), DMA((2, 4)), DMA((2, 4)), DMA((4,)), DMA((4,)), DMA((1,))]
    more, params = [], {}
    if linked:
        more = [inp]
        out_shape += [sd((4, 4, 2, 256, d), BF16), sd(inp.shape, BF16), sd(inp.shape, BF16), *[sd((128, 256), F32)] * 2]
        out_specs += [ANYWHERE] * 3 + [whole((128, 256))] * 2
        scratch += [DMA((2, 3)), DMA((2, 3)), DMA((2,))] + piece_scratch(256, FF_SPLIT)
        params = dict(collective_id=0, has_side_effects=True)
    else:
        out_shape += [sd((4, 2, 128, hidden), BF16), sd((hidden, d), BF16)]
        out_specs += [ANYWHERE] * 2
    return pl.pallas_call(
        functools.partial(ff_kernel, linked=linked), out_shape=out_shape, grid=(hidden // 512,),
        in_specs=[pl.BlockSpec(memory_space=pltpu.SMEM), whole((n, d)), whole(cot.shape), whole((1, d)), whole((1, d)), whole((1, hidden)), ANYWHERE, ANYWHERE] + [ANYWHERE] * len(more),
        out_specs=out_specs, scratch_shapes=scratch,
        compiler_params=pltpu.CompilerParams(vmem_limit_bytes=58 * 2**20, **params),
        cost_estimate=pl.CostEstimate(flops=52_000_000_000, bytes_accessed=50_000_000, transcendentals=4_000_000),
    )(partners, inp.reshape(n, d), cot, gain.reshape(1, d), shift.reshape(1, d), bias.reshape(1, hidden), wu, wd, *more)


def turn(x, c, s, sign):
    lanes = x.shape[1]
    lane = lax.broadcasted_iota(jnp.int32, x.shape, 1) % HEAD_DIM
    other = jnp.where(lane < ROT // 2, pltpu.roll(x, lanes - ROT // 2, 1), pltpu.roll(x, ROT // 2, 1))
    return x * c + (sign * other) * s


def tile_place(tile):
    early = [kind * 8 + pair for two in ORDER[:2] for pair in two for kind in range(3)]
    block = tile // 6
    mates = sorted(t for t in range(24) if t // 6 == block and (t in early) == (tile in early))
    return block, mates.index(tile)


def attn_kernel(raw_ref, g_ref, gain_ref, shift_ref, fam_ref, tab_ref, wqkv_ref, wo_ref, *rest, linked):
    hand, rest = (rest[:1], rest[1:]) if linked else ((), rest)
    dn_ref, sums_ref, gqkv_ref, go_ref, heads_ref = rest[:5]
    outs, rest = (rest[5:12], rest[12:]) if linked else ((), rest[5:])
    (x_s, xt_s, c_s, s_s, w_s, wo_s, q_s, k_s, v_s, do_s, kt_s, vt_s, ht_s, dqt_s, dk_s, dv_s, draw_s, dn_s, gq_s, go_s, heads_s,
     famr_s, famc_s, w_sem, wo_sem, gq_sem, go_sem, h_sem) = rest[:28]
    rest = rest[28:]
    step = pl.program_id(0)
    steps = len(ORDER)
    last = steps - 1
    n, d = raw_ref.shape
    lanes = 256
    pairs = d // 128
    slot = step % 2

    def weights(at, slot):
        out = []
        for half in range(2):
            pair = pick(at, [o[half] for o in ORDER])
            for kind in range(3):
                col = pl.multiple_of((kind * pairs + pair) * 128, 128)
                j = kind * 2 + half
                out.append(local_copy(wqkv_ref.at[:, pl.ds(col, 128)], w_s.at[slot, :, pl.ds(j * 128, 128)], w_sem.at[slot, j]))
            row = pl.multiple_of(pair * 128, 128)
            out.append(local_copy(wo_ref.at[pl.ds(row, 128), :], wo_s.at[slot, pl.ds(half * 128, 128), :], wo_sem.at[slot, half]))
        return out

    def results(at):
        out = []
        for half in range(2):
            pair = pick(at, [o[half] for o in ORDER])
            for kind in range(3):
                j = kind * 2 + half
                if linked:
                    col = pick(at, [block * 384 + rank * 128 for block, rank in (tile_place(kind * 8 + o[half]) for o in ORDER)])
                    to = gqkv_ref.at[at // 2, :, :, :, pl.ds(pl.multiple_of(col, 128), 128)]
                else:
                    to = gqkv_ref.at[:, :, :, pl.ds(pl.multiple_of((kind * pairs + pair) * 128, 128), 128)]
                out.append(local_copy(gq_s.at[:, :, :, pl.ds(j * 128, 128)], to, gq_sem.at[j]))
            out.append(local_copy(go_s.at[pl.ds(half * 128, 128), :], go_ref.at[pair // 2, pair % 2], go_sem.at[half]))
        return out

    if linked:
        place = Place()
        head_send, head_recv = rest[:2]
        rest = rest[2:]

        def heads_out(at):
            cols = pl.ds(pl.multiple_of(at * lanes, lanes), lanes)
            span = n // 4
            out = []
            for j, (to, device) in enumerate(place.peers):
                src = heads_s.at[pl.ds(pl.multiple_of(to * span, span), span), :]
                out.append(remote_copy(src, heads_ref.at[place.seq, :, cols], head_send.at[at, j], head_recv.at[at, j], device))
            mine = heads_s.at[pl.ds(pl.multiple_of(place.seq * span, span), span), :]
            return out, local_copy(mine, heads_ref.at[place.seq, :, cols], h_sem.at[0])

        def part_of(source, k, w):
            return lambda y, c: source.at[k, :, :, :, pl.ds(pl.multiple_of((y * 2 + c) * w, 128), w)]

        def done_at(k):
            def done(total):
                if k == 3:
                    outs[6][...] = total
                else:
                    outs[2 * k][...] = total[0:128]
                    outs[2 * k + 1][...] = total[128:256]
            return done

        cut = piece_count(AT_SPLIT)
        made = [Piece(place, part_of(hand[0], 1 + k, 256), done_at(k), AT_SPLIT, rest[k * cut:(k + 1) * cut]) for k in range(3)]
        made.append(Piece(place, part_of(gqkv_ref, 0, 384), done_at(3), EARLY_SPLIT, rest[3 * cut:]))
        plan = {}
        for which, times in enumerate(AT_TICKS):
            for t, at in enumerate(times):
                plan.setdefault(at, []).append((which, t))
    else:
        plan = {}

    def tick(position):
        for at, what in sorted(plan.items()):
            if min(at // 6, last) * 6 + position == at:
                def run(what=what):
                    for which, t in sorted(what, key=lambda w: (-w[1], w[0])):
                        made[which].tick(t)
                pl.when(step == min(at // 6, last))(run)

    @pl.when(step == 0)
    def _():
        for copy in weights(0, 0):
            copy.start()
        if linked:
            place.greet()
        family = fam_ref[pl.ds(lax.axis_index("seq"), 1), :].astype(F32)
        famr_s[...] = family
        for m in range(n // 128):
            rows = slice(m * 128, m * 128 + 128)
            famc_s[rows, :] = jnp.broadcast_to(family[:, rows], (128, 128)).T
        for a in range(n // 32):
            rows = slice(a * 32, a * 32 + 32)
            ca, sa = tab_ref[0, a:a + 1, :], tab_ref[1, a:a + 1, :]
            cb, sb = tab_ref[2], tab_ref[3]
            c1 = ca * cb - sa * sb
            s1 = sa * cb + ca * sb
            lane = lax.broadcasted_iota(jnp.int32, c1.shape, 1) % HEAD_DIM
            c_s[rows, :] = jnp.where(lane < ROT, c1, 1.0)
            s_s[rows, :] = jnp.where(lane < ROT // 2, -s1, jnp.where(lane < ROT, s1, 0.0))
        @functools.partial(each_band, n // 256)
        def _(rows, m):
            xhat, _ = normalize(raw_ref[rows, :].astype(F32))
            normed = (xhat * gain_ref[...] + shift_ref[...]).astype(BF16)
            x_s[rows, :] = normed
            xt_s[:, rows] = normed.T
        if linked:
            place.meet()

    @pl.when(step > 0)
    def _():
        for copy in results(step - 1):
            copy.wait()

    tick(0)

    @pl.when(step < last)
    def _():
        for copy in weights(step + 1, 1 - slot):
            copy.start()
    for copy in weights(step, slot):
        copy.wait()

    w_ref, wo1_ref = w_s.at[slot], wo_s.at[slot]
    scaling = HEAD_DIM ** -0.5

    def both(rows):
        c, s = c_s[rows, :], s_s[rows, :]
        return jnp.concatenate([c, c], 1), jnp.concatenate([s, s], 1)

    for m in range(n // 256):
        rows = slice(m * 256, m * 256 + 256)
        raw = dot(x_s[rows, :], w_ref[...])
        c, s = both(rows)
        q_s[rows, :] = (turn(raw[:, 0:lanes], c, s, 1.0) * scaling).astype(BF16)
        keys = turn(raw[:, lanes:2 * lanes], c, s, 1.0).astype(BF16)
        k_s[rows, :] = keys
        kt_s[:, rows] = keys.T
        vals = raw[:, 2 * lanes:].astype(BF16)
        v_s[rows, :] = vals
        vt_s[:, rows] = vals.T
        do_s[rows, :] = dot_nt(g_ref[rows, :], wo1_ref[...]).astype(BF16)

    tick(1)
    tile = TILE
    lane = lax.broadcasted_iota(jnp.int32, (tile, 128), 1)
    work = [(h, i) for i in reversed(range(n // tile)) for h in range(4)]

    def first(h, i):
        span = (i + 1) * tile
        here = slice(i * tile, span)
        cols = slice(h // 2 * 128, h // 2 * 128 + 128)
        mine = (lane < HEAD_DIM) if h % 2 == 0 else (lane >= HEAD_DIM)
        qh = jnp.where(mine, q_s[here, cols], 0).astype(BF16)
        doh = jnp.where(mine, do_s[here, cols], 0).astype(BF16)
        return qh, doh, dot_nt(k_s[0:span, cols], qh), dot_nt(v_s[0:span, cols], doh)

    def second(h, i, qh, doh, st, dpt):
        span = (i + 1) * tile
        here = slice(i * tile, span)
        cols = slice(h // 2 * 128, h // 2 * 128 + 128)
        rows = slice(h * HEAD_DIM, (h + 1) * HEAD_DIM)
        family = famc_s[0:span, :]
        allowed = jnp.concatenate([family] * (tile // 128), 1) == famr_s[:, here]
        key_place = lax.broadcasted_iota(jnp.int32, (span, tile), 0)
        query_place = lax.broadcasted_iota(jnp.int32, (span, tile), 1) + i * tile
        st = jnp.where(allowed & (key_place <= query_place), st, -1e9)
        e = jnp.exp(st - jnp.max(st, 0, keepdims=True))
        p = e * (1.0 / jnp.sum(e, 0, keepdims=True))
        pb = p.astype(BF16)
        ds = (p * (dpt - jnp.sum(p * dpt, 0, keepdims=True))).astype(BF16)
        ht_s[rows, here] = dot(vt_s[rows, 0:span], pb).astype(BF16)
        dqt_s[rows, here] = dot(kt_s[rows, 0:span], ds) * scaling
        dv = dot(pb, doh)
        dk = dot(ds, qh)
        if h % 2 == 0 and i == n // tile - 1:
            dv_s[:, cols] = dv
            dk_s[:, cols] = dk
        else:
            dv_s[0:span, cols] += dv
            dk_s[0:span, cols] += dk

    made_first = first(*work[0])
    for j, (h, i) in enumerate(work):
        later = first(*work[j + 1]) if j + 1 < len(work) else None
        second(h, i, *made_first)
        made_first = later
        if h == 3 and i != 1:
            tick({3: 2, 2: 3, 0: 4}[i])

    @pl.when(step > 0)
    def _():
        if linked:
            sent, mine = heads_out(step - 1)
            for copy in sent:
                copy.wait_send()
            mine.wait()
        else:
            local_copy(heads_s, heads_ref.at[:, pl.ds(pl.multiple_of((step - 1) * lanes, lanes), lanes)], h_sem.at[0]).wait()
    heads_s[...] = ht_s[...].T
    if linked:
        sent, mine = heads_out(step)
        for copy in sent:
            copy.start()
        mine.start()
    else:
        local_copy(heads_s, heads_ref.at[:, pl.ds(pl.multiple_of(step * lanes, lanes), lanes)], h_sem.at[0]).start()

    for m in range(n // 256):
        rows = slice(m * 256, m * 256 + 256)
        c, s = both(rows)
        draw_s[rows, 0:lanes] = turn(dqt_s[:, rows].T, c, s, -1.0).astype(BF16)
        draw_s[rows, lanes:2 * lanes] = turn(dk_s[rows, :], c, s, -1.0).astype(BF16)
        draw_s[rows, 2 * lanes:] = dv_s[rows, :].astype(BF16)

    for m in range(d // 256):
        grads = dot(xt_s[m * 256:(m + 1) * 256, :], draw_s[...]).astype(BF16)
        gq_s[m, 0] = grads[0:128]
        gq_s[m, 1] = grads[128:256]
    go_s[...] = dot(ht_s[...], g_ref[...]).astype(BF16)
    for copy in results(step):
        copy.start()
    tick(5)
    for m in range(n // 256):
        here = slice(m * 256, (m + 1) * 256)
        dn = dot_nt(draw_s[here, :], w_ref[...])

        @pl.when(step == 0)
        def _():
            dn_s[here, :] = dn

        @pl.when(step > 0)
        def _():
            dn_s[here, :] += dn

    @pl.when(step == last)
    def _():
        sums_ref[...] = jnp.zeros_like(sums_ref)

        @functools.partial(each_band, n // 256)
        def _(here, m):
            total = dn_s[here, :]
            xhat, _ = normalize(raw_ref[here, :].astype(F32))
            sums_ref[0:1, :] += jnp.sum(total * xhat, 0, keepdims=True)
            sums_ref[1:2, :] += jnp.sum(total, 0, keepdims=True)
            dn_ref[here, :] = total.astype(BF16)

    tick(6)

    @pl.when(step == last)
    def _():
        for copy in results(step):
            copy.wait()
        if linked:
            for at in range(steps):
                for copy in heads_out(at)[0]:
                    copy.wait_recv()
            for copy in heads_out(step)[0]:
                copy.wait_send()
            heads_out(step)[1].wait()
        else:
            local_copy(heads_s, heads_ref.at[:, pl.ds(pl.multiple_of(step * lanes, lanes), lanes)], h_sem.at[0]).wait()


def attend(raw, g, gain, shift, wqkv, wo, families, linked, grads=None):
    n, d = raw.shape
    pair_lane = np.arange(128) % HEAD_DIM % (ROT // 2)
    freq = 10000.0 ** (-2.0 * pair_lane / ROT)
    high, low = np.arange(n // 32)[:, None] * 32.0 * freq, np.arange(32)[:, None] * freq
    tab = jnp.asarray(np.stack([np.cos(high), np.sin(high), np.cos(low), np.sin(low)]), F32)
    sd, vm = jax.ShapeDtypeStruct, pltpu.VMEM
    out_shape = [sd((n, d), BF16), sd((8, d), F32), sd((2, 4, 2, 128, 3 * d // 2) if linked else (4, 2, 128, 3 * d), BF16),
                 sd((4, 2, 128, d), BF16), sd((4, n // 4, d) if linked else (n, d), BF16)]
    out_specs = [whole((n, d)), whole((8, d))] + [ANYWHERE] * 3
    scratch = [vm((n, d), BF16), vm((d, n), BF16), vm((n, 128), F32), vm((n, 128), F32), vm((2, d, 768), BF16), vm((2, 256, d), BF16)]
    scratch += [vm((n, 256), BF16)] * 4 + [vm((256, n), BF16)] * 3
    scratch += [vm((256, n), F32), vm((n, 256), F32), vm((n, 256), F32), vm((n, 768), BF16), vm((n, d), F32), vm((4, 2, 128, 768), BF16),
                vm((256, d), BF16), vm((n, 256), BF16), vm((1, n), F32), vm((n, 128), F32), DMA((2, 6)), DMA((2, 2)), DMA((6,)), DMA((2,)), DMA((1,))]
    params, more = {}, []
    if linked:
        more = [grads]
        out_shape += [sd((128, 256), F32)] * 6 + [sd((128, 384), F32)]
        out_specs += [whole((128, 256))] * 6 + [whole((128, 384))]
        scratch += [DMA((4, 3)), DMA((4, 3))]
        scratch += piece_scratch(256, AT_SPLIT) * 3 + piece_scratch(384, EARLY_SPLIT)
        params = dict(collective_id=1, has_side_effects=True)
    return pl.pallas_call(
        functools.partial(attn_kernel, linked=linked), out_shape=out_shape, grid=(len(ORDER),),
        in_specs=[whole((n, d)), whole((n, d)), whole((1, d)), whole((1, d)), whole(families.shape), whole((4, 32, 128)), ANYWHERE, ANYWHERE]
        + [ANYWHERE] * len(more),
        out_specs=out_specs, scratch_shapes=scratch,
        compiler_params=pltpu.CompilerParams(vmem_limit_bytes=60 * 2**20, **params),
        cost_estimate=pl.CostEstimate(flops=70_000_000_000, bytes_accessed=30_000_000, transcendentals=20_000_000),
    )(raw, g, gain.reshape(1, d), shift.reshape(1, d), families, tab, wqkv, wo, *more)


class SmallSum:
    def __init__(self, place, held, heard, by_z, send, recv):
        self.p, self.held, self.heard, self.by_z, self.send, self.recv = place, held, heard, by_z, send, recv

    def copies(self, t):
        p = self.p
        if t < 3:
            to = (p.twin, p.beside_y, p.beside_x)[t]
            return [remote_copy(self.held, self.heard.at[t], self.send.at[t], self.recv.at[t], to)]
        return [remote_copy(self.by_z.at[p.z], self.by_z.at[p.z], self.send.at[3 + j], self.recv.at[3 + j], to)
                for j, to in enumerate(p.along_z)]

    def tick(self, t):
        if t > 0:
            for copy in self.copies(t - 1):
                copy.wait()
        if 0 < t < 4:
            total = self.held[...] + self.heard[t - 1]
            if t < 3:
                self.held[...] = total
            else:
                self.by_z[self.p.z] = total
        if t < 4:
            for copy in self.copies(t):
                copy.start()
        return None if t < 4 else self.by_z[0] + self.by_z[1] + self.by_z[2] + self.by_z[3]


def tail_kernel(dat_ref, heads_ref, gq_ref, go_ref, inp_ref, cot_ref, act_ref, wd_ref, dn_ref, wo_ref, part_ref, gain_ref, dbias_ref, sums_ff_ref, sums_at_ref,
                ub_ref, early_ref, lo_ref, ig_ref, qkv_ref, out_ref, gain_o, shift_o, ub_o, db_o,
                back_s, inp_s, g_s, heads_s, y_s, dn_s, wo_s, lo_s, ig_s, small_s, heard_s, by_z_s, act_s, wd_s, act_sem, wd_sem,
                load_sem, wo_sem, back_send, back_recv, own_sem, small_send, small_recv, lo_sem, ig_sem, *pieces):
    place = Place()
    d = wo_s.shape[0]
    place.greet()
    swaps = [remote_copy(dat_ref.at[to], back_s.at[place.seq], back_send.at[j], back_recv.at[j], device)
             for j, (to, device) in enumerate(place.peers)]
    own = local_copy(dat_ref.at[place.seq], back_s.at[place.seq], own_sem.at[0])
    blocks = {}

    def part(source, w, row0, rows):
        return lambda y, c: source.at[:, :, pl.ds(row0, rows), pl.ds(pl.multiple_of((y * 2 + c) * w, 128), w)]

    def out_done(total):
        out_ref[...] = total

    def qkv_done(row0):
        def done(total):
            rows = slice(row0, row0 + total.shape[0])
            early = early_ref[rows, :]
            first = jnp.where(place.c == 0, early, total)
            second = jnp.where(place.c == 0, total, early)
            order = ((first, 0), (second, 0), (second, 1), (first, 1), (first, 2), (second, 2))
            for k, (source, at) in enumerate(order):
                qkv_ref[rows, k * 128:(k + 1) * 128] = source[:, at * 128:(at + 1) * 128]
        return done

    cuts = [0, piece_count(TAIL_SPLITS[0])]
    for split in TAIL_SPLITS[1:]:
        cuts.append(cuts[-1] + piece_count(split))
    late = gq_ref.at[1]
    row1 = sum(TAIL_SPLITS[1])
    made = [Piece(place, part(go_ref, 256, 0, 128), out_done, TAIL_SPLITS[0], pieces[:cuts[1]]),
            Piece(place, part(late, 384, 0, row1), qkv_done(0), TAIL_SPLITS[1], pieces[cuts[1]:cuts[2]]),
            Piece(place, part(late, 384, row1, 128 - row1), qkv_done(row1), TAIL_SPLITS[2], pieces[cuts[2]:])]
    small = SmallSum(place, small_s, heard_s, by_z_s, small_send, small_recv)
    small_s[0:3, :] = sums_ff_ref[0:3, :]
    small_s[0:2, :] += sums_at_ref[0:2, :]
    small_s[3:4, :] = jnp.zeros((1, d), F32)
    for k in range(4):
        small_s[4 + k:5 + k, :] = ub_ref[:, k * d:(k + 1) * d]
    loads = [local_copy(a, b, load_sem.at[k]) for k, (a, b) in enumerate(
        ((heads_ref, heads_s), (inp_ref, inp_s), (cot_ref, g_s), (dn_ref, dn_s)))]
    for pair in range(d // 128):
        at = [p for two in ORDER for p in two].index(pair)
        blocks[at] = local_copy(wo_ref.at[pl.ds(pair * 128, 128), :], wo_s.at[pl.ds(at * 128, 128), :], wo_sem.at[at])
    for copy in [loads[0]] + list(blocks.values()) + loads[1:] + [own]:
        copy.start()
    place.meet()
    for piece in made:
        piece.tick(0)
    for copy in swaps:
        copy.start()
    small.tick(0)

    def lo_out(r):
        return local_copy(lo_s.at[r], lo_ref.at[r], lo_sem.at[r])

    def ig_out(r):
        return local_copy(ig_s.at[r], ig_ref.at[r], ig_sem.at[r])

    def forward(r, carry):
        total = inp_s[r].astype(F32) + dot(heads_s[r], wo_s[...]) + y_s[r]
        lo_s[r] = total.astype(BF16)
        lo_out(r).start()
        return carry

    def backward(r):
        xhat, scale = normalize(inp_s[r].astype(F32))
        dx = (dn_s[r] + back_s[r].astype(F32)) * gain_ref[...]
        ig_s[r] = g_s[lax.rem(part_ref[r], 4)].astype(F32) + (dx - jnp.mean(dx, -1, keepdims=True) - xhat * jnp.mean(dx * xhat, -1, keepdims=True)) * scale
        ig_out(r).start()

    hidden = wd_ref.shape[0]
    chunks = hidden // 512

    def chunk(at, slot):
        out = [local_copy(act_ref.at[at], act_s.at[slot], act_sem.at[slot])]
        for k, f in hidden_runs(at, hidden):
            f = pl.multiple_of(f, 128)
            out.append(local_copy(wd_ref.at[pl.ds(f, 128), :], wd_s.at[slot, pl.ds(k * 128, 128), :], wd_sem.at[slot, k]))
        return out

    for copy in chunk(0, 0):
        copy.start()

    def down(at, carry):
        slot = at % 2

        @pl.when(at + 1 < chunks)
        def _():
            for copy in chunk(at + 1, 1 - slot):
                copy.start()

        @pl.when(at == TAIL_FIRST)
        def _():
            for piece in made:
                piece.tick(1)
            small.tick(1)

        @pl.when(at == TAIL_FIRST + 4)
        def _():
            small.tick(2)

        for copy in chunk(at, slot):
            copy.wait()
        for r in range(4):
            y_s[r] += dot(act_s[slot, r * 256:(r + 1) * 256, :], wd_s[slot])
        return carry

    for r in range(4):
        y_s[r] = jnp.broadcast_to(dbias_ref[...], y_s.shape[1:])
    lax.fori_loop(0, chunks, down, 0)
    for copy in list(blocks.values()) + loads[:2]:
        copy.wait()
    lax.fori_loop(0, 2, forward, 0)
    made[0].tick(2)
    lax.fori_loop(2, 4, forward, 0)
    made[1].tick(2)
    made[2].tick(2)
    small.tick(3)
    loads[2].wait()
    loads[3].wait()
    own.wait()
    made[0].tick(3)
    backward(place.seq)
    for j in range(3):
        swaps[j].wait_send()
    swaps[2].wait_recv()
    backward((place.seq + 1) % 4)
    made[1].tick(3)
    made[2].tick(3)
    swaps[1].wait_recv()
    swaps[0].wait_recv()
    lax.fori_loop(2, 4, lambda j, carry: (backward((place.seq + j) % 4), carry)[1], 0)
    total = small.tick(4)
    for piece in made:
        piece.tick(4)
    gain_o[...] = total[0:1]
    shift_o[...] = total[1:2]
    db_o[...] = total[2:3]
    for k in range(4):
        ub_o[:, k * d:(k + 1) * d] = total[4 + k:5 + k]
    for r in range(4):
        lo_out(r).wait()
        ig_out(r).wait()


def finish(dat, heads, gq, go, inp, cot, act, wd, dn, wo, partners, gain, dbias, sums_ff, sums_at, ub, early):
    sd, vm = jax.ShapeDtypeStruct, pltpu.VMEM
    shape, d = inp.shape, inp.shape[2]
    vmem = pl.BlockSpec(memory_space=pltpu.VMEM)
    return pl.pallas_call(
        tail_kernel,
        out_shape=[sd(shape, BF16), sd(shape, F32), sd((128, 768), F32), sd((128, 256), F32), sd((1, d), F32), sd((1, d), F32), sd((1, 4 * d), F32),
                   sd((1, d), F32)],
        in_specs=[ANYWHERE] * 10 + [pl.BlockSpec(memory_space=pltpu.SMEM)] + [vmem] * 6, out_specs=[ANYWHERE] * 2 + [vmem] * 6,
        scratch_shapes=[vm(shape, BF16)] * 4 + [vm(shape, F32)] * 2 + [vm((d, d), BF16), vm(shape, BF16), vm(shape, F32),
                        vm((8, d), F32), vm((3, 8, d), F32), vm((4, 8, d), F32), vm((2, 1024, 512), BF16), vm((2, 512, d), BF16), DMA((2,)), DMA((2, 4)),
                        DMA((4,)), DMA((8,)), DMA((3,)), DMA((3,)), DMA((1,)), DMA((6,)), DMA((6,)), DMA((4,)), DMA((4,))]
        + piece_scratch(256, TAIL_SPLITS[0]) + piece_scratch(384, TAIL_SPLITS[1]) + piece_scratch(384, TAIL_SPLITS[2]),
        compiler_params=pltpu.CompilerParams(collective_id=2, has_side_effects=True, vmem_limit_bytes=56 * 2**20),
    )(dat.reshape(shape), heads, gq, go, inp, cot, act, wd, dn.reshape(shape), wo, partners, gain.reshape(1, d), dbias.reshape(1, d), sums_ff, sums_at,
      ub, early)


def copy_kernel(*refs, moves, count):
    ins, outs, held, (in_sem, out_sem) = refs[:count], refs[count:count + 10], refs[count + 10:2 * count + 10], refs[2 * count + 10:]
    loads = [local_copy(ins[a].at[at], held[a].at[at], in_sem.at[k]) for k, (a, at, _) in enumerate(moves)]
    for copy in loads:
        copy.start()
    stores = []
    for k, (a, at, places) in enumerate(moves):
        loads[k].wait()
        for source, b, to in places:
            stores.append(local_copy(held[a].at[source], outs[b].at[to], out_sem.at[len(stores)]))
            stores[-1].start()
    for copy in stores:
        copy.wait()


def gather_up(*parts):
    sd, every = jax.ShapeDtypeStruct, (slice(None), slice(None))
    shapes = [sd(p.shape, p.dtype) for p in parts[:8]] + [sd((128, 1024), F32), sd((512, 256), F32)]
    moves = [(a, r, [(r, a, r)]) for r in range(4) for a in (1, 0)]
    for k in range(4):
        moves.append((8 + k, every, [((slice(None), slice(half * 128, half * 128 + 128)), 8, (slice(None), slice(half * 512 + k * 128, half * 512 + k * 128 + 128)))
                                     for half in range(2)]))
        moves.append((12 + k, every, [(every, 9, (slice(k * 128, k * 128 + 128), slice(None)))]))
    moves += [(a, every, [(every, a, every)]) for a in range(2, 8)]
    return pl.pallas_call(
        functools.partial(copy_kernel, moves=moves, count=len(parts)), out_shape=shapes, in_specs=[ANYWHERE] * len(parts), out_specs=[ANYWHERE] * 10,
        scratch_shapes=[pltpu.VMEM(p.shape, p.dtype) for p in parts] + [DMA((len(moves),)), DMA((sum(len(m[2]) for m in moves),))],
        compiler_params=pltpu.CompilerParams(vmem_limit_bytes=60 * 2**20),
    )(*parts)


def on_device(inputs, norm_gain, norm_shift, qkv_weight, out_weight, up_weight, up_bias, down_weight, down_bias, partners, families, cotangent, linked):
    row_count, place_count, width = inputs.shape
    tokens = row_count * place_count
    branch_args = norm_gain, norm_shift, qkv_weight, out_weight, families, linked
    if linked:
        act, dn, sums_ff, ub, grads, row_inputs, row_grad, up0, down0 = feed_forward(
            inputs, cotangent, partners, norm_gain, norm_shift, up_bias, up_weight, down_weight, True)
        dat, sums_at, gq, go, heads, up1, down1, up2, down2, up3, down3, early = attend(
            row_inputs.reshape(tokens, width), row_grad.reshape(tokens, width), *branch_args, grads)
        layer_out, input_grad, qkv_sum, out_sum, gain_sum, shift_sum, ub_sum, db_sum = finish(
            dat, heads, gq, go, inputs, cotangent, act, down_weight, dn, out_weight, partners, norm_gain, down_bias, sums_ff, sums_at, ub, early)
        layer_out, input_grad, qkv_sum, out_sum, gain_sum, shift_sum, ub_sum, db_sum, up_sum, down_sum = gather_up(
            layer_out, input_grad, qkv_sum, out_sum, gain_sum, shift_sum, ub_sum, db_sum, up0, up1, up2, up3, down0, down1, down2, down3)
        return (layer_out.reshape(inputs.shape), input_grad.reshape(inputs.shape), gain_sum.reshape(width), shift_sum.reshape(width), qkv_sum, out_sum,
                up_sum, ub_sum.reshape(-1), down_sum, db_sum.reshape(width))
    local_rows = partners - lax.axis_index("dp") * row_count
    grad = jnp.take(cotangent, local_rows, axis=0, mode="clip")
    swap = functools.partial(lax.all_to_all, axis_name="seq", split_axis=0, concat_axis=0, tiled=True)
    row_inputs, row_grad = swap(inputs).reshape(tokens, width), swap(grad).reshape(tokens, width)
    y, dn, sums_ff, ub, up_grad, down_grad = feed_forward(
        inputs, cotangent, partners, norm_gain, norm_shift, up_bias, up_weight, down_weight, False)
    dat, sums_at, qkv_grad, out_grad, heads = attend(row_inputs, row_grad, *branch_args)

    def scatter(parts, columns):
        part = lax.psum_scatter(parts.reshape(-1, columns), "seq", scatter_dimension=1, tiled=True)
        return lax.psum_scatter(part, "dp", scatter_dimension=0, tiled=True).astype(F32)

    qkv_sum, out_sum = scatter(qkv_grad, 3 * width), scatter(out_grad, width)
    up_sum, down_sum = scatter(up_grad, up_bias.shape[0]), scatter(down_grad, width)
    heads = swap(heads.reshape(inputs.shape)).reshape(tokens, width)
    order = np.array([p for two in ORDER for p in two])
    attn_out = dot(heads, out_weight.reshape(-1, 128, width)[order].reshape(width, width))
    values = inputs.astype(F32).reshape(tokens, width)
    layer_out = (values + attn_out + (y + down_bias)).astype(BF16).reshape(inputs.shape)
    xhat, scale = normalize(values)
    dx = (dn + swap(dat.reshape(inputs.shape)).reshape(tokens, width).astype(F32)) * norm_gain
    input_grad = grad.reshape(tokens, width).astype(F32) + (dx - jnp.mean(dx, -1, keepdims=True) - xhat * jnp.mean(dx * xhat, -1, keepdims=True)) * scale
    gain_sum, shift_sum, up_bias_sum, down_bias_sum = lax.psum((sums_ff[0] + sums_at[0], sums_ff[1] + sums_at[1], ub[0], sums_ff[2]), ("dp", "seq"))
    return (layer_out, input_grad.reshape(inputs.shape), gain_sum, shift_sum, qkv_sum, out_sum, up_sum, up_bias_sum, down_sum, down_bias_sum)


def solution(mesh):
    rows = P("dp", "seq", None)
    placed = (rows,) + (P(),) * 8 + (P("dp"), P("dp", None), rows)
    grads = P("dp", "seq")
    linked = (mesh.shape["dp"], mesh.shape["seq"]) == (8, 4)
    return jax.shard_map(functools.partial(on_device, linked=linked), mesh=mesh, in_specs=placed,
                         out_specs=(rows, rows, P(), P(), grads, grads, grads, P(), grads, P()), check_vma=False)
```
